32 devices in a mesh: dp: 4 (over y, x), fsdp: 8 (over z, core).
Axes of the slice: x: 2, y: 2, z: 4, core: 2. Of those that a mesh axis runs over, the one named last changes fastest.
Arguments:
- frames: bfloat16 [4096, 1024], P(('dp', 'fsdp')), may hold values from -6 to 6
- segments: int32 [4096], P(('dp', 'fsdp')), may hold values from 0 to 3, as said below
- cotangent: bfloat16 [4096, 1024], P(('dp', 'fsdp')), may hold values from -6 to 6
- early_gain: bfloat16 [1024], P(('dp', 'fsdp')), may hold values from 0.5 to 1.5
- early_shift: bfloat16 [1024], P(('dp', 'fsdp')), may hold values from -1.25 to 1.25
- early_up: bfloat16 [1024, 4096], P(('dp', 'fsdp')), may hold values from -0.1875 to 0.1875
- early_lift: bfloat16 [4096], P(('dp', 'fsdp')), may hold values from -1.25 to 1.25
- early_down: bfloat16 [4096, 1024], P(('dp', 'fsdp')), may hold values from -0.09375 to 0.09375
- early_drop: bfloat16 [1024], P(('dp', 'fsdp')), may hold values from -1.25 to 1.25
- mixer_gain: bfloat16 [1024], P(('dp', 'fsdp')), may hold values from 0.5 to 1.5
- mixer_shift: bfloat16 [1024], P(('dp', 'fsdp')), may hold values from -1.25 to 1.25
- mixer_project: bfloat16 [1024, 3072], P(('dp', 'fsdp')), may hold values from -0.1875 to 0.1875
- query_bias: bfloat16 [1024], P(('dp', 'fsdp')), may hold values from -1.25 to 1.25
- value_bias: bfloat16 [1024], P(('dp', 'fsdp')), may hold values from -1.25 to 1.25
- mixer_output: bfloat16 [1024, 1024], P(('dp', 'fsdp')), may hold values from -1.5 to 1.5
- mixer_drop: bfloat16 [1024], P(('dp', 'fsdp')), may hold values from -1.25 to 1.25
- distance_table: bfloat16 [256, 16], P(('dp', 'fsdp')), may hold values from -6 to 6
- filter_gain: bfloat16 [1024], P(('dp', 'fsdp')), may hold values from 0.5 to 1.5
- filter_shift: bfloat16 [1024], P(('dp', 'fsdp')), may hold values from -1.25 to 1.25
- filter_up: bfloat16 [1024, 2048], P(('dp', 'fsdp')), may hold values from -0.1875 to 0.1875
- filter_lift: bfloat16 [2048], P(('dp', 'fsdp')), may hold values from -1.25 to 1.25
- depth_weight: bfloat16 [1024, 31], P(('dp', 'fsdp')), may hold values from -1 to 1
- depth_bias: bfloat16 [1024], P(('dp', 'fsdp')), may hold values from -1.75 to 1.75
- middle_gain: bfloat16 [1024], P(('dp', 'fsdp')), may hold values from 0.5 to 1.5
- middle_shift: bfloat16 [1024], P(('dp', 'fsdp')), may hold values from -1.25 to 1.25
- filter_down: bfloat16 [1024, 1024], P(('dp', 'fsdp')), may hold values from -0.1875 to 0.1875
- filter_drop: bfloat16 [1024], P(('dp', 'fsdp')), may hold values from -1.25 to 1.25
- late_gain: bfloat16 [1024], P(('dp', 'fsdp')), may hold values from 0.5 to 1.5
- late_shift: bfloat16 [1024], P(('dp', 'fsdp')), may hold values from -1.25 to 1.25
- late_up: bfloat16 [1024, 4096], P(('dp', 'fsdp')), may hold values from -0.1875 to 0.1875
- late_lift: bfloat16 [4096], P(('dp', 'fsdp')), may hold values from -1.25 to 1.25
- late_down: bfloat16 [4096, 1024], P(('dp', 'fsdp')), may hold values from -0.09375 to 0.09375
- late_drop: bfloat16 [1024], P(('dp', 'fsdp')), may hold values from -2.5 to 2.5
- final_gain: bfloat16 [1024], P(('dp', 'fsdp')), may hold values from 0.5 to 1.5
- final_shift: bfloat16 [1024], P(('dp', 'fsdp')), may hold values from -1.25 to 1.25
Outputs:
- layer_out: float32 [4096, 1024], P(('dp', 'fsdp'))
- slope_frames: float32 [4096, 1024], P(('dp', 'fsdp'))
- slope_early_gain: float32 [1024], P(('dp', 'fsdp'))
- slope_early_shift: float32 [1024], P(('dp', 'fsdp'))
- slope_early_up: float32 [1024, 4096], P(('dp', 'fsdp'))
- slope_early_lift: float32 [4096], P(('dp', 'fsdp'))
- slope_early_down: float32 [4096, 1024], P(('dp', 'fsdp'))
- slope_early_drop: float32 [1024], P(('dp', 'fsdp'))
- slope_mixer_gain: float32 [1024], P(('dp', 'fsdp'))
- slope_mixer_shift: float32 [1024], P(('dp', 'fsdp'))
- slope_mixer_project: float32 [1024, 3072], P(('dp', 'fsdp'))
- slope_query_bias: float32 [1024], P(('dp', 'fsdp'))
- slope_value_bias: float32 [1024], P(('dp', 'fsdp'))
- slope_mixer_output: float32 [1024, 1024], P(('dp', 'fsdp'))
- slope_mixer_drop: float32 [1024], P(('dp', 'fsdp'))
- slope_distance_table: float32 [256, 16], P(('dp', 'fsdp'))
- slope_filter_gain: float32 [1024], P(('dp', 'fsdp'))
- slope_filter_shift: float32 [1024], P(('dp', 'fsdp'))
- slope_filter_up: float32 [1024, 2048], P(('dp', 'fsdp'))
- slope_filter_lift: float32 [2048], P(('dp', 'fsdp'))
- slope_depth_weight: float32 [1024, 31], P(('dp', 'fsdp'))
- slope_depth_bias: float32 [1024], P(('dp', 'fsdp'))
- slope_middle_gain: float32 [1024], P(('dp', 'fsdp'))
- slope_middle_shift: float32 [1024], P(('dp', 'fsdp'))
- slope_filter_down: float32 [1024, 1024], P(('dp', 'fsdp'))
- slope_filter_drop: float32 [1024], P(('dp', 'fsdp'))
- slope_late_gain: float32 [1024], P(('dp', 'fsdp'))
- slope_late_shift: float32 [1024], P(('dp', 'fsdp'))
- slope_late_up: float32 [1024, 4096], P(('dp', 'fsdp'))
- slope_late_lift: float32 [4096], P(('dp', 'fsdp'))
- slope_late_down: float32 [4096, 1024], P(('dp', 'fsdp'))
- slope_late_drop: float32 [1024], P(('dp', 'fsdp'))
- slope_final_gain: float32 [1024], P(('dp', 'fsdp'))
- slope_final_shift: float32 [1024], P(('dp', 'fsdp'))
The draws below stay inside these ranges and needn't reach their ends.
Inputs may be any that keep to these rules, and one draw needn't show every extreme that they name: `segments`: within each device's 4096 / 32 frames the numbers start at 0 and never fall; a device holds one utterance (all 0) or four, each one frame or longer; some device holds four.
All inputs are finite; a program needn't handle non-finite values.
Results may differ from the reference program's by a relative error of at most 0.017.
Values may be sent and summed in bfloat16 or wider, within the bound.
A program may use at most 384 MiB of HBM per device.

```python
import jax
import jax.numpy as jnp
from jax import lax

D = 1024
FF = 4096
HEADS = 16
HEAD = 64
KW = 31
NREL = 256
TOK_DEV = 128
TOKENS = 4096


def draw_segments(key, part):
    device_count = TOKENS // TOK_DEV
    kind_key, cut_key, force_key = jax.random.split(key, 3)
    several = jax.random.randint(kind_key, (device_count,), 0, 2)
    forced = jax.random.randint(force_key, (), 0, device_count)
    several = several.at[forced].set(1)
    scores = jax.random.randint(cut_key, (device_count, TOK_DEV - 1), 0, 1 << 20) * TOK_DEV
    scores = scores + jnp.arange(TOK_DEV - 1, dtype=jnp.int32)[None, :]
    cut_points = lax.top_k(scores, 3)[1] + 1
    places = jnp.arange(TOK_DEV, dtype=jnp.int32)
    crossed = jnp.sum((places[None, :, None] >= cut_points[:, None, :]).astype(jnp.int32), axis=-1)
    return (crossed * several[:, None]).reshape(-1).astype(jnp.int32)


def steps_of(own_key, shape, cuts, smallest, top_value):
    loudness = 1.0
    for axis_at, shards_of in cuts:
        steps = jax.random.uniform(jax.random.fold_in(jax.random.fold_in(own_key, 6), axis_at), (shards_of,), jnp.float32, smallest / len(cuts), top_value / len(cuts))
        loudness = loudness * jnp.repeat(jnp.exp(steps), shape[axis_at] // shards_of).reshape((-1,) + (1,) * (len(shape) - 1 - axis_at))
    return loudness


def scatter_about(rng, shape, spread, most, pieces=(), kind=jnp.bfloat16):
    gain = steps_of(rng, shape, pieces, -0.22, 0.18) if pieces else 1.0
    entries = jax.random.normal(rng, shape, jnp.float32) * spread * gain
    return jnp.minimum(jnp.maximum(entries, -most), most).astype(kind)


def setup_inputs(seed: int = 0) -> dict:
    seeds = jax.random.split(jax.random.key(seed), 36)
    return {
        "frames": scatter_about(seeds[0], (TOKENS, D), 1.0, 6.0, ((0, 32),)),
        "segments": draw_segments(jax.random.fold_in(seeds[35], 71), 0),
        "cotangent": scatter_about(seeds[2], (TOKENS, D), 1.0, 6.0, ((0, 32),)),
        "early_gain": jnp.clip(1.0 + 0.1 * jax.random.normal(seeds[3], (D,), jnp.float32), 0.5, 1.5).astype(jnp.bfloat16),
        "early_shift": scatter_about(seeds[4], (D,), 0.2, 1.25, ((0, 32),)),
        "early_up": scatter_about(seeds[5], (D, FF), D ** -0.5, 0.1875, ((0, 32),)),
        "early_lift": scatter_about(seeds[6], (FF,), 0.2, 1.25, ((0, 32),)),
        "early_down": scatter_about(seeds[7], (FF, D), FF ** -0.5, 0.09375, ((0, 32),)),
        "early_drop": scatter_about(seeds[8], (D,), 0.2, 1.25, ((0, 32),)),
        "mixer_gain": jnp.clip(1.0 + 0.1 * jax.random.normal(seeds[9], (D,), jnp.float32), 0.5, 1.5).astype(jnp.bfloat16),
        "mixer_shift": scatter_about(seeds[10], (D,), 0.2, 1.25, ((0, 32),)),
        "mixer_project": scatter_about(seeds[11], (D, 3 * D), D ** -0.5, 0.1875, ((0, 32),)),
        "query_bias": scatter_about(seeds[12], (D,), 0.2, 1.25, ((0, 32),)),
        "value_bias": scatter_about(seeds[13], (D,), 0.2, 1.25, ((0, 32),)),
        "mixer_output": scatter_about(seeds[14], (D, D), (D // 64) ** -0.5, 1.5, ((0, 32),)),
        "mixer_drop": scatter_about(seeds[15], (D,), 0.2, 1.25, ((0, 32),)),
        "distance_table": scatter_about(seeds[16], (NREL, HEADS), 1.0, 6.0, ((0, 32),)),
        "filter_gain": jnp.clip(1.0 + 0.1 * jax.random.normal(seeds[17], (D,), jnp.float32), 0.5, 1.5).astype(jnp.bfloat16),
        "filter_shift": scatter_about(seeds[18], (D,), 0.2, 1.25, ((0, 32),)),
        "filter_up": scatter_about(seeds[19], (D, 2 * D), D ** -0.5, 0.1875, ((0, 32),)),
        "filter_lift": scatter_about(seeds[20], (2 * D,), 0.2, 1.25, ((0, 32),)),
        "depth_weight": scatter_about(seeds[21], (D, KW), KW ** -0.5, 1.0, ((0, 32),)),
        "depth_bias": scatter_about(seeds[22], (D,), 0.3, 1.75, ((0, 32),)),
        "middle_gain": jnp.clip(1.0 + 0.1 * jax.random.normal(seeds[23], (D,), jnp.float32), 0.5, 1.5).astype(jnp.bfloat16),
        "middle_shift": scatter_about(seeds[24], (D,), 0.2, 1.25, ((0, 32),)),
        "filter_down": scatter_about(seeds[25], (D, D), D ** -0.5, 0.1875, ((0, 32),)),
        "filter_drop": scatter_about(seeds[26], (D,), 0.2, 1.25, ((0, 32),)),
        "late_gain": jnp.clip(1.0 + 0.1 * jax.random.normal(seeds[27], (D,), jnp.float32), 0.5, 1.5).astype(jnp.bfloat16),
        "late_shift": scatter_about(seeds[28], (D,), 0.2, 1.25, ((0, 32),)),
        "late_up": scatter_about(seeds[29], (D, FF), D ** -0.5, 0.1875, ((0, 32),)),
        "late_lift": scatter_about(seeds[30], (FF,), 0.2, 1.25, ((0, 32),)),
        "late_down": scatter_about(seeds[31], (FF, D), FF ** -0.5, 0.09375, ((0, 32),)),
        "late_drop": scatter_about(seeds[32], (D,), 0.4, 2.5, ((0, 32),)),
        "final_gain": jnp.clip(1.0 + 0.1 * jax.random.normal(seeds[33], (D,), jnp.float32), 0.5, 1.5).astype(jnp.bfloat16),
        "final_shift": scatter_about(seeds[34], (D,), 0.2, 1.25, ((0, 32),)),
    }


@jax.custom_vjp
def reduced_precision(v):
    return lax.optimization_barrier(v.astype(jnp.bfloat16)).astype(jnp.float32)

@jax.custom_vjp
def reduced_precision_backward(v):
    return v

def low_keep(v):
    return (reduced_precision(v), None)

def low_pass(kept, grad):
    return (grad,)

def back_keep(v):
    return (v, None)

def back_low(kept, grad):
    return (reduced_precision(grad),)
reduced_precision.defvjp(low_keep, low_pass)
reduced_precision_backward.defvjp(back_keep, back_low)
EPSILON = 1e-05
MASKED = -1e+30

def exact_dot(left_rows, right_rows):
    return jnp.dot(left_rows, right_rows, precision=lax.Precision.HIGHEST, preferred_element_type=jnp.float32)

def layer_norm(values, norm_gain, norm_shift):
    centered = values - lax.optimization_barrier(jnp.mean(values, axis=-1, keepdims=True))
    inverse = lax.rsqrt(lax.optimization_barrier(jnp.mean(centered * centered, axis=-1, keepdims=True)) + EPSILON)
    return centered * inverse * norm_gain + norm_shift

def swish(values):
    return values * jax.nn.sigmoid(values)

def feed_forward(values, weights):
    hidden = reduced_precision(layer_norm(values, weights[0], weights[1]))
    widened = reduced_precision_backward(exact_dot(hidden, weights[2])) + weights[3]
    active = reduced_precision(swish(widened))
    return values + 0.5 * (reduced_precision_backward(exact_dot(active, weights[4])) + weights[5])

def attention(values, segment_ids, weights):
    frame_count = values.shape[0]
    hidden = reduced_precision(layer_norm(values, weights[0], weights[1]))
    projected = reduced_precision_backward(exact_dot(hidden, weights[2]))
    query_rows = reduced_precision(projected[:, :D] + weights[3]).reshape(frame_count, HEADS, HEAD)
    key_matrix_rows = reduced_precision(projected[:, D:2 * D]).reshape(frame_count, HEADS, HEAD)
    value_matrix_rows = reduced_precision(projected[:, 2 * D:] + weights[4]).reshape(frame_count, HEADS, HEAD)
    unnormalized_scores = reduced_precision_backward(jnp.einsum('jug,fug->ujf', query_rows, key_matrix_rows, precision=lax.Precision.HIGHEST))
    places = jnp.arange(frame_count, dtype=jnp.int32)
    bucket = jnp.clip(places[:, None] - places[None, :], -(NREL // 2), NREL // 2 - 1) + NREL // 2
    relative = jnp.transpose(weights[7][bucket], (2, 0, 1))
    same_utterance = (segment_ids[:, None] == segment_ids[None, :])[None]
    scores = jnp.where(same_utterance, HEAD ** (-0.5) * unnormalized_scores + relative, MASKED)
    row_peak = lax.optimization_barrier(jnp.max(scores, axis=-1, keepdims=True))
    powered = jnp.exp(scores - row_peak)
    softmax_rows = reduced_precision(powered / lax.optimization_barrier(jnp.sum(powered, axis=-1, keepdims=True)))
    attention_blend = reduced_precision(reduced_precision_backward(jnp.einsum('ief,fiv->eiv', softmax_rows, value_matrix_rows, precision=lax.Precision.HIGHEST)))
    attention_blend = attention_blend.reshape(frame_count, D)
    return values + (reduced_precision_backward(exact_dot(attention_blend, weights[5])) + weights[6])

def convolution(values, segment_ids, weights):
    frame_count = values.shape[0]
    margin = (KW - 1) // 2
    hidden = reduced_precision(layer_norm(values, weights[0], weights[1]))
    widened = reduced_precision_backward(exact_dot(hidden, weights[2])) + weights[3]
    gated_rows = widened[:, :D] * jax.nn.sigmoid(widened[:, D:])
    padded = jnp.pad(gated_rows, ((margin, margin), (0, 0)))
    padded_ids = jnp.pad(segment_ids, (margin, margin), constant_values=-1)
    running = jnp.zeros_like(gated_rows)
    for offset in range(KW):
        matching = (padded_ids[offset:offset + frame_count] == segment_ids)[:, None]
        running = running + jnp.where(matching, padded[offset:offset + frame_count] * weights[4][:, offset], 0.0)
    filtered = running + weights[5]
    swished = reduced_precision(swish(layer_norm(filtered, weights[6], weights[7])))
    return values + (reduced_precision_backward(exact_dot(swished, weights[8])) + weights[9])

def layer(values, segment_ids, params):
    first_rows = feed_forward(values, params[0:6])
    second_rows = attention(first_rows, segment_ids, params[6:14])
    third_rows = convolution(second_rows, segment_ids, params[14:24])
    fourth_rows = feed_forward(third_rows, params[24:30])
    return layer_norm(fourth_rows, params[30], params[31])

def reference(frames, segments, cotangent, early_gain, early_shift, early_up, early_lift, early_down, early_drop, mixer_gain, mixer_shift, mixer_project, query_bias, value_bias, mixer_output, mixer_drop, distance_table, filter_gain, filter_shift, filter_up, filter_lift, depth_weight, depth_bias, middle_gain, middle_shift, filter_down, filter_drop, late_gain, late_shift, late_up, late_lift, late_down, late_drop, final_gain, final_shift):
    stored = (early_gain, early_shift, early_up, early_lift, early_down, early_drop, mixer_gain, mixer_shift, mixer_project, query_bias, value_bias, mixer_output, mixer_drop, distance_table, filter_gain, filter_shift, filter_up, filter_lift, depth_weight, depth_bias, middle_gain, middle_shift, filter_down, filter_drop, late_gain, late_shift, late_up, late_lift, late_down, late_drop, final_gain, final_shift)
    params = tuple((entry.astype(jnp.float32) for entry in stored))
    blocks = frames.astype(jnp.float32).reshape(-1, TOK_DEV, D)
    id_blocks = segments.reshape(-1, TOK_DEV)
    upstream_blocks = cotangent.astype(jnp.float32).reshape(-1, TOK_DEV, D)

    def one_block(carried, inputs):
        piece_rows, piece_ids, piece_upstream = inputs

        def local_layer(local_values, local_params):
            return layer(local_values, piece_ids, local_params)
        outcome, pullback = jax.vjp(local_layer, piece_rows, params)
        piece_grad, param_grads = pullback(piece_upstream)
        return (jax.tree.map(jnp.add, carried, param_grads), (outcome, piece_grad))
    starting = tuple((jnp.zeros_like(entry) for entry in params))
    totals, (outcomes, frame_grads) = lax.scan(one_block, starting, (blocks, id_blocks, upstream_blocks))
    return (outcomes.reshape(TOKENS, D), frame_grads.reshape(TOKENS, D), totals[0], totals[1], totals[2], totals[3], totals[4], totals[5], totals[6], totals[7], totals[8], totals[9], totals[10], totals[11], totals[12], totals[13], totals[14], totals[15], totals[16], totals[17], totals[18], totals[19], totals[20], totals[21], totals[22], totals[23], totals[24], totals[25], totals[26], totals[27], totals[28], totals[29], totals[30], totals[31])
```

```python
import functools

import jax
import jax.numpy as jnp
from jax import lax
from jax.experimental import pallas as pl
from jax.experimental.pallas import tpu as pltpu
from jax.sharding import PartitionSpec as P

D = 1024
HEADS = 16
HEAD = 64
KW = 31
NREL = 256


EPSILON = 1e-05
MASKED = -1e30
UTTERANCE_LIMIT = 4
MESH = pl.DeviceIdType.MESH


def flat_dot(left_rows, right_rows):
    return jnp.dot(left_rows, right_rows, preferred_element_type=jnp.float32)


def lead_dot(left_rows, right_rows):
    return lax.dot_general(
        left_rows, right_rows, (((0,), (0,)), ((), ())), preferred_element_type=jnp.float32
    )


def back_dot(left_rows, right_rows):
    return lax.dot_general(
        left_rows, right_rows, (((1,), (1,)), ((), ())), preferred_element_type=jnp.float32
    )


def norm_apply(values, norm_gain, norm_shift):
    centered = values - jnp.mean(values, axis=-1, keepdims=True)
    inverse = lax.rsqrt(jnp.mean(centered * centered, axis=-1, keepdims=True) + EPSILON)
    normed_unit = centered * inverse
    return (
        normed_unit * norm_gain.astype(jnp.float32) + norm_shift.astype(jnp.float32),
        normed_unit,
        inverse,
    )


def norm_back(upstream, normed_unit, inverse, norm_gain):
    scaled = upstream * norm_gain.astype(jnp.float32)
    adjusted = scaled - jnp.mean(scaled, axis=-1, keepdims=True)
    adjusted = adjusted - normed_unit * jnp.mean(scaled * normed_unit, axis=-1, keepdims=True)
    return (inverse * adjusted, jnp.sum(upstream * normed_unit, axis=0), jnp.sum(upstream, axis=0))


def swish_back(upstream, before):
    sigmoid_rows = jax.nn.sigmoid(before)
    return upstream * sigmoid_rows * (1.0 + before * (1.0 - sigmoid_rows))


def depthwise(gated_rows, kernel, segment_ids):
    margin = (KW - 1) // 2
    channels = gated_rows.shape[1]
    taps = jnp.transpose(kernel)[:, None, :]
    running = jnp.zeros_like(gated_rows)
    for utterance in range(UTTERANCE_LIMIT):
        inside = (segment_ids == utterance)[:, None]
        masked_rows = jnp.where(inside, gated_rows, 0.0)
        convolved = lax.conv_general_dilated(
            masked_rows[None],
            taps,
            (1,),
            ((margin, margin),),
            dimension_numbers=("NWC", "WIO", "NWC"),
            feature_group_count=channels,
            precision=lax.Precision.HIGHEST,
        )[0]
        running = running + jnp.where(inside, convolved, 0.0)
    return running


def fetch_feed(norm_gain, norm_shift, w_up, up_shift, w_down, down_shift):
    return (
        lax.all_gather(norm_gain, ("dp", "fsdp"), axis=0, tiled=True),
        lax.all_gather(norm_shift, ("dp", "fsdp"), axis=0, tiled=True),
        lax.all_gather(w_up, ("dp", "fsdp"), axis=0, tiled=True),
        lax.all_gather(up_shift, ("dp", "fsdp"), axis=0, tiled=True),
        lax.all_gather(w_down, ("dp", "fsdp"), axis=0, tiled=True),
        lax.all_gather(down_shift, ("dp", "fsdp"), axis=0, tiled=True),
    )


def reduce_feed(norm_gain, norm_shift, w_up, up_shift, w_down, down_shift):
    return (
        lax.psum_scatter(norm_gain, ("dp", "fsdp"), scatter_dimension=0, tiled=True),
        lax.psum_scatter(norm_shift, ("dp", "fsdp"), scatter_dimension=0, tiled=True),
        lax.psum_scatter(w_up, ("dp", "fsdp"), scatter_dimension=0, tiled=True),
        lax.psum_scatter(up_shift, ("dp", "fsdp"), scatter_dimension=0, tiled=True),
        lax.psum_scatter(w_down, ("dp", "fsdp"), scatter_dimension=0, tiled=True),
        lax.psum_scatter(down_shift, ("dp", "fsdp"), scatter_dimension=0, tiled=True),
    )


def fetch_mixer(
    norm_gain, norm_shift, w_project, query_shift, value_shift, w_output, output_shift, table_rows
):
    return (
        lax.all_gather(norm_gain, ("dp", "fsdp"), axis=0, tiled=True),
        lax.all_gather(norm_shift, ("dp", "fsdp"), axis=0, tiled=True),
        lax.all_gather(w_project, ("dp", "fsdp"), axis=0, tiled=True),
        lax.all_gather(query_shift, ("dp", "fsdp"), axis=0, tiled=True),
        lax.all_gather(value_shift, ("dp", "fsdp"), axis=0, tiled=True),
        lax.all_gather(w_output, ("dp", "fsdp"), axis=0, tiled=True),
        lax.all_gather(output_shift, ("dp", "fsdp"), axis=0, tiled=True),
        lax.all_gather(table_rows, ("dp", "fsdp"), axis=0, tiled=True),
    )


def reduce_mixer(
    norm_gain, norm_shift, w_project, query_shift, value_shift, w_output, output_shift, table_rows
):
    return (
        lax.psum_scatter(norm_gain, ("dp", "fsdp"), scatter_dimension=0, tiled=True),
        lax.psum_scatter(norm_shift, ("dp", "fsdp"), scatter_dimension=0, tiled=True),
        lax.psum_scatter(w_project, ("dp", "fsdp"), scatter_dimension=0, tiled=True),
        lax.psum_scatter(query_shift, ("dp", "fsdp"), scatter_dimension=0, tiled=True),
        lax.psum_scatter(value_shift, ("dp", "fsdp"), scatter_dimension=0, tiled=True),
        lax.psum_scatter(w_output, ("dp", "fsdp"), scatter_dimension=0, tiled=True),
        lax.psum_scatter(output_shift, ("dp", "fsdp"), scatter_dimension=0, tiled=True),
        lax.psum_scatter(table_rows, ("dp", "fsdp"), scatter_dimension=0, tiled=True),
    )


def fetch_filter(
    norm_gain,
    norm_shift,
    w_up,
    up_shift,
    depth_taps,
    depth_shift,
    middle_gain,
    middle_shift,
    w_down,
    down_shift,
    last_gain,
    last_shift,
):
    return (
        lax.all_gather(norm_gain, ("dp", "fsdp"), axis=0, tiled=True),
        lax.all_gather(norm_shift, ("dp", "fsdp"), axis=0, tiled=True),
        lax.all_gather(w_up, ("dp", "fsdp"), axis=0, tiled=True),
        lax.all_gather(up_shift, ("dp", "fsdp"), axis=0, tiled=True),
        lax.all_gather(depth_taps, ("dp", "fsdp"), axis=0, tiled=True),
        lax.all_gather(depth_shift, ("dp", "fsdp"), axis=0, tiled=True),
        lax.all_gather(middle_gain, ("dp", "fsdp"), axis=0, tiled=True),
        lax.all_gather(middle_shift, ("dp", "fsdp"), axis=0, tiled=True),
        lax.all_gather(w_down, ("dp", "fsdp"), axis=0, tiled=True),
        lax.all_gather(down_shift, ("dp", "fsdp"), axis=0, tiled=True),
        lax.all_gather(last_gain, ("dp", "fsdp"), axis=0, tiled=True),
        lax.all_gather(last_shift, ("dp", "fsdp"), axis=0, tiled=True),
    )


def reduce_filter(
    norm_gain,
    norm_shift,
    w_up,
    up_shift,
    depth_taps,
    depth_shift,
    middle_gain,
    middle_shift,
    w_down,
    down_shift,
    last_gain,
    last_shift,
):
    return (
        lax.psum_scatter(norm_gain, ("dp", "fsdp"), scatter_dimension=0, tiled=True),
        lax.psum_scatter(norm_shift, ("dp", "fsdp"), scatter_dimension=0, tiled=True),
        lax.psum_scatter(w_up, ("dp", "fsdp"), scatter_dimension=0, tiled=True),
        lax.psum_scatter(up_shift, ("dp", "fsdp"), scatter_dimension=0, tiled=True),
        lax.psum_scatter(depth_taps, ("dp", "fsdp"), scatter_dimension=0, tiled=True),
        lax.psum_scatter(depth_shift, ("dp", "fsdp"), scatter_dimension=0, tiled=True),
        lax.psum_scatter(middle_gain, ("dp", "fsdp"), scatter_dimension=0, tiled=True),
        lax.psum_scatter(middle_shift, ("dp", "fsdp"), scatter_dimension=0, tiled=True),
        lax.psum_scatter(w_down, ("dp", "fsdp"), scatter_dimension=0, tiled=True),
        lax.psum_scatter(down_shift, ("dp", "fsdp"), scatter_dimension=0, tiled=True),
        lax.psum_scatter(last_gain, ("dp", "fsdp"), scatter_dimension=0, tiled=True),
        lax.psum_scatter(last_shift, ("dp", "fsdp"), scatter_dimension=0, tiled=True),
    )


def feed_forward(values, weights):
    normed, normed_unit, inverse = norm_apply(values, weights[0], weights[1])
    hidden = normed.astype(jnp.bfloat16)
    widened = flat_dot(hidden, weights[2]) + weights[3].astype(jnp.float32)
    active = (widened * jax.nn.sigmoid(widened)).astype(jnp.bfloat16)
    result = values + 0.5 * (flat_dot(active, weights[4]) + weights[5].astype(jnp.float32))
    return (result, (normed_unit, inverse, hidden, widened, active))


def feed_backward(upstream, saved, weights):
    normed_unit, inverse, hidden, widened, active = saved
    half_grad = 0.5 * upstream
    half_low = half_grad.astype(jnp.bfloat16)
    down_slope = lead_dot(active, half_low)
    widened_grad = swish_back(back_dot(half_low, weights[4]), widened)
    widened_low = widened_grad.astype(jnp.bfloat16)
    up_slope = lead_dot(hidden, widened_low)
    hidden_grad = back_dot(widened_low, weights[2])
    input_grad, gain_slope, shift_slope = norm_back(hidden_grad, normed_unit, inverse, weights[0])
    slopes = (
        gain_slope,
        shift_slope,
        up_slope,
        jnp.sum(widened_grad, axis=0),
        down_slope,
        jnp.sum(half_grad, axis=0),
    )
    return (upstream + input_grad, slopes)


def bucket_table(frame_count):
    offsets = jnp.arange(2 * frame_count - 1, dtype=jnp.int32) - (frame_count - 1)
    buckets = jnp.clip(offsets, -(NREL // 2), NREL // 2 - 1) + NREL // 2
    return (buckets[:, None] == jnp.arange(NREL, dtype=jnp.int32)[None, :]).astype(jnp.float32)


def relative_bias(table_rows, frame_count):
    diagonals = jnp.dot(
        bucket_table(frame_count),
        table_rows.astype(jnp.float32),
        precision=lax.Precision.HIGHEST,
        preferred_element_type=jnp.float32,
    )
    flipped = jnp.concatenate(
        [jnp.transpose(diagonals[::-1]), jnp.zeros((HEADS, 1), jnp.float32)], axis=1
    )
    spread = jnp.broadcast_to(flipped[:, None, :], (HEADS, frame_count, 2 * frame_count))
    spread = spread.reshape(HEADS, 2 * frame_count * frame_count)
    sheared = spread[:, : frame_count * (2 * frame_count - 1)].reshape(
        HEADS, frame_count, 2 * frame_count - 1
    )
    return sheared[:, :, frame_count - 1 :]


def relative_slope(score_grad, frame_count):
    placed = jnp.pad(score_grad, ((0, 0), (0, 0), (frame_count - 1, 0)))
    flattened = jnp.pad(
        placed.reshape(HEADS, frame_count * (2 * frame_count - 1)), ((0, 0), (0, frame_count))
    )
    columns = jnp.sum(flattened.reshape(HEADS, frame_count, 2 * frame_count), axis=1)
    diagonals = columns[:, 2 * frame_count - 2 :: -1]
    return lax.dot_general(
        bucket_table(frame_count),
        diagonals,
        (((0,), (1,)), ((), ())),
        precision=lax.Precision.HIGHEST,
        preferred_element_type=jnp.float32,
    )


def mixer_scores(query_rows, key_matrix_rows, relative, same_utterance):
    unnormalized_scores = jnp.einsum(
        "jug,fug->ujf", query_rows, key_matrix_rows, preferred_element_type=jnp.float32
    )
    return jnp.where(same_utterance[None], HEAD ** (-0.5) * unnormalized_scores + relative, MASKED)


def mixer_forward(values, segment_ids, weights):
    frame_count = values.shape[0]
    normed, normed_unit, inverse = norm_apply(values, weights[0], weights[1])
    hidden = normed.astype(jnp.bfloat16)
    projected = flat_dot(hidden, weights[2])
    query_rows = (projected[:, :D] + weights[3].astype(jnp.float32)).astype(jnp.bfloat16)
    query_rows = query_rows.reshape(frame_count, HEADS, HEAD)
    key_matrix_rows = projected[:, D : 2 * D].astype(jnp.bfloat16).reshape(frame_count, HEADS, HEAD)
    value_matrix_rows = (projected[:, 2 * D :] + weights[4].astype(jnp.float32)).astype(
        jnp.bfloat16
    )
    value_matrix_rows = value_matrix_rows.reshape(frame_count, HEADS, HEAD)
    relative = relative_bias(weights[7], frame_count)
    same_utterance = segment_ids[:, None] == segment_ids[None, :]
    scores = mixer_scores(query_rows, key_matrix_rows, relative, same_utterance)
    row_peak = jnp.max(scores, axis=-1, keepdims=True)
    powered = jnp.exp(scores - row_peak)
    row_total = jnp.sum(powered, axis=-1, keepdims=True)
    log_total = row_peak + jnp.log(row_total)
    softmax_rows = (powered / row_total).astype(jnp.bfloat16)
    attention_blend = jnp.einsum(
        "ief,fiv->eiv", softmax_rows, value_matrix_rows, preferred_element_type=jnp.float32
    )
    attention_blend = attention_blend.reshape(frame_count, D).astype(jnp.bfloat16)
    result = values + (flat_dot(attention_blend, weights[5]) + weights[6].astype(jnp.float32))
    return (
        result,
        (
            normed_unit,
            inverse,
            hidden,
            query_rows,
            key_matrix_rows,
            value_matrix_rows,
            log_total,
            attention_blend,
            relative,
            same_utterance,
        ),
    )


def mixer_backward(upstream, saved, weights):
    (
        normed_unit,
        inverse,
        hidden,
        query_rows,
        key_matrix_rows,
        value_matrix_rows,
        log_total,
        attention_blend,
        relative,
        same_utterance,
    ) = saved
    frame_count = upstream.shape[0]
    upstream_low = upstream.astype(jnp.bfloat16)
    output_slope = lead_dot(attention_blend, upstream_low)
    attention_blend_gradient = (
        back_dot(upstream_low, weights[5]).astype(jnp.bfloat16).reshape(frame_count, HEADS, HEAD)
    )
    scores = mixer_scores(query_rows, key_matrix_rows, relative, same_utterance)
    soft_full = jnp.exp(scores - log_total)
    value_grad = jnp.einsum(
        "ybr,byq->ryq",
        soft_full.astype(jnp.bfloat16),
        attention_blend_gradient,
        preferred_element_type=jnp.float32,
    ).reshape(frame_count, D)
    soft_grad = jnp.einsum(
        "jug,fug->ujf",
        attention_blend_gradient,
        value_matrix_rows,
        preferred_element_type=jnp.float32,
    )
    score_grad = soft_full * (soft_grad - jnp.sum(soft_full * soft_grad, axis=-1, keepdims=True))
    table_slope = relative_slope(score_grad, frame_count)
    score_reduced_precision = (HEAD ** (-0.5) * score_grad).astype(jnp.bfloat16)
    query_grad = jnp.einsum(
        "ief,fiv->eiv", score_reduced_precision, key_matrix_rows, preferred_element_type=jnp.float32
    ).reshape(frame_count, D)
    key_grad = jnp.einsum(
        "ybr,byq->ryq", score_reduced_precision, query_rows, preferred_element_type=jnp.float32
    ).reshape(frame_count, D)
    projected_low = jnp.concatenate([query_grad, key_grad, value_grad], axis=1).astype(jnp.bfloat16)
    project_slope = lead_dot(hidden, projected_low)
    hidden_grad = back_dot(projected_low, weights[2])
    input_grad, gain_slope, shift_slope = norm_back(hidden_grad, normed_unit, inverse, weights[0])
    slopes = (
        gain_slope,
        shift_slope,
        project_slope,
        jnp.sum(query_grad, axis=0),
        jnp.sum(value_grad, axis=0),
        output_slope,
        jnp.sum(upstream, axis=0),
        table_slope,
    )
    return (upstream + input_grad, slopes)


def filter_forward(values, segment_ids, weights):
    normed, normed_unit, inverse = norm_apply(values, weights[0], weights[1])
    hidden = normed.astype(jnp.bfloat16)
    widened = flat_dot(hidden, weights[2]) + weights[3].astype(jnp.float32)
    gated_rows = widened[:, :D] * jax.nn.sigmoid(widened[:, D:])
    filtered = depthwise(gated_rows, weights[4].astype(jnp.float32), segment_ids) + weights[
        5
    ].astype(jnp.float32)
    middle, middle_unit, middle_inverse = norm_apply(filtered, weights[6], weights[7])
    swished = (middle * jax.nn.sigmoid(middle)).astype(jnp.bfloat16)
    result = values + (flat_dot(swished, weights[8]) + weights[9].astype(jnp.float32))
    return (
        result,
        (
            normed_unit,
            inverse,
            hidden,
            widened,
            gated_rows,
            middle_unit,
            middle_inverse,
            middle,
            swished,
        ),
    )


def filter_backward(upstream, saved, weights, segment_ids):
    (
        normed_unit,
        inverse,
        hidden,
        widened,
        gated_rows,
        middle_unit,
        middle_inverse,
        middle,
        swished,
    ) = saved
    upstream_low = upstream.astype(jnp.bfloat16)
    down_slope = lead_dot(swished, upstream_low)
    middle_grad = swish_back(back_dot(upstream_low, weights[8]), middle)
    filtered_grad, middle_gain_slope, middle_shift_slope = norm_back(
        middle_grad, middle_unit, middle_inverse, weights[6]
    )

    def local_filter(local_rows, local_kernel):
        return depthwise(local_rows, local_kernel, segment_ids)

    unused, pullback = jax.vjp(local_filter, gated_rows, weights[4].astype(jnp.float32))
    gated_grad, kernel_slope = pullback(filtered_grad)
    opened = jax.nn.sigmoid(widened[:, D:])
    widened_grad = jnp.concatenate(
        [gated_grad * opened, gated_grad * widened[:, :D] * opened * (1.0 - opened)], axis=1
    )
    widened_low = widened_grad.astype(jnp.bfloat16)
    up_slope = lead_dot(hidden, widened_low)
    hidden_grad = back_dot(widened_low, weights[2])
    input_grad, gain_slope, shift_slope = norm_back(hidden_grad, normed_unit, inverse, weights[0])
    slopes = (
        gain_slope,
        shift_slope,
        up_slope,
        jnp.sum(widened_grad, axis=0),
        kernel_slope,
        jnp.sum(filtered_grad, axis=0),
        middle_gain_slope,
        middle_shift_slope,
        down_slope,
        jnp.sum(upstream, axis=0),
    )
    return (upstream + input_grad, slopes)


def body(
    frames,
    segments,
    cotangent,
    early_gain,
    early_shift,
    early_up,
    early_lift,
    early_down,
    early_drop,
    mixer_gain,
    mixer_shift,
    mixer_project,
    query_bias,
    value_bias,
    mixer_output,
    mixer_drop,
    distance_table,
    filter_gain,
    filter_shift,
    filter_up,
    filter_lift,
    depth_weight,
    depth_bias,
    middle_gain,
    middle_shift,
    filter_down,
    filter_drop,
    late_gain,
    late_shift,
    late_up,
    late_lift,
    late_down,
    late_drop,
    final_gain,
    final_shift,
):
    start_rows = frames.astype(jnp.float32)
    final_upstream = cotangent.astype(jnp.float32)
    early_full = fetch_feed(early_gain, early_shift, early_up, early_lift, early_down, early_drop)
    first_rows, early_kept = feed_forward(start_rows, early_full)
    mixer_full = fetch_mixer(
        mixer_gain,
        mixer_shift,
        mixer_project,
        query_bias,
        value_bias,
        mixer_output,
        mixer_drop,
        distance_table,
    )
    second_rows, mixer_kept = mixer_forward(first_rows, segments, mixer_full)
    filter_full = fetch_filter(
        filter_gain,
        filter_shift,
        filter_up,
        filter_lift,
        depth_weight,
        depth_bias,
        middle_gain,
        middle_shift,
        filter_down,
        filter_drop,
        final_gain,
        final_shift,
    )
    third_rows, filter_kept = filter_forward(second_rows, segments, filter_full)
    late_full = fetch_feed(late_gain, late_shift, late_up, late_lift, late_down, late_drop)
    fourth_rows, late_kept = feed_forward(third_rows, late_full)
    layer_out, final_unit, final_inverse = norm_apply(fourth_rows, filter_full[10], filter_full[11])
    final_stats = (final_unit, final_inverse)
    upstream, final_gain_slope, final_shift_slope = norm_back(
        final_upstream, final_stats[0], final_stats[1], filter_full[10]
    )
    upstream, late_slopes = feed_backward(upstream, late_kept, late_full)
    late_summed = reduce_feed(
        late_slopes[0],
        late_slopes[1],
        late_slopes[2],
        late_slopes[3],
        late_slopes[4],
        late_slopes[5],
    )
    upstream, filter_grads = filter_backward(upstream, filter_kept, filter_full, segments)
    filter_summed = reduce_filter(
        filter_grads[0],
        filter_grads[1],
        filter_grads[2],
        filter_grads[3],
        filter_grads[4],
        filter_grads[5],
        filter_grads[6],
        filter_grads[7],
        filter_grads[8],
        filter_grads[9],
        final_gain_slope,
        final_shift_slope,
    )
    upstream, mixer_grads = mixer_backward(upstream, mixer_kept, mixer_full)
    mixer_summed = reduce_mixer(
        mixer_grads[0],
        mixer_grads[1],
        mixer_grads[2],
        mixer_grads[3],
        mixer_grads[4],
        mixer_grads[5],
        mixer_grads[6],
        mixer_grads[7],
    )
    upstream, early_slopes = feed_backward(upstream, early_kept, early_full)
    early_summed = reduce_feed(
        early_slopes[0],
        early_slopes[1],
        early_slopes[2],
        early_slopes[3],
        early_slopes[4],
        early_slopes[5],
    )
    return (
        layer_out,
        upstream,
        early_summed[0],
        early_summed[1],
        early_summed[2],
        early_summed[3],
        early_summed[4],
        early_summed[5],
        mixer_summed[0],
        mixer_summed[1],
        mixer_summed[2],
        mixer_summed[3],
        mixer_summed[4],
        mixer_summed[5],
        mixer_summed[6],
        mixer_summed[7],
        filter_summed[0],
        filter_summed[1],
        filter_summed[2],
        filter_summed[3],
        filter_summed[4],
        filter_summed[5],
        filter_summed[6],
        filter_summed[7],
        filter_summed[8],
        filter_summed[9],
        late_summed[0],
        late_summed[1],
        late_summed[2],
        late_summed[3],
        late_summed[4],
        late_summed[5],
        filter_summed[10],
        filter_summed[11],
    )


def near(me, n):
    if n == 4:
        row, column = me // 2, me % 2
        flip_row, flip_column = (1 - row) * 2 + column, row * 2 + 1 - column
        across = (1 - row) * 2 + 1 - column
        return [(flip_column, flip_column), (flip_row, flip_row), (across, across)]
    return [((me + step) % n, (me + n - step) % n) for step in range(1, n)]


def greet(targets):
    barrier = pltpu.get_barrier_semaphore()
    for target in targets:
        pl.semaphore_signal(barrier, inc=1, device_id={"dp": target}, device_id_type=MESH)
    pl.semaphore_wait(barrier, len(targets))


def greet_all(n, m):
    me, lane = lax.axis_index("dp"), lax.axis_index("fsdp")
    barrier = pltpu.get_barrier_semaphore()

    def say(step, carry):
        target = {"dp": (me + step // m) % n, "fsdp": (lane + step % m) % m}
        pl.semaphore_signal(barrier, inc=1, device_id=target, device_id_type=MESH)
        return carry

    lax.fori_loop(1, n * m, say, 0)
    pl.semaphore_wait(barrier, n * m - 1)


def remote(src, dst, send, recv, target):
    return pltpu.make_async_remote_copy(
        src_ref=src, dst_ref=dst, send_sem=send, recv_sem=recv, device_id=target, device_id_type=MESH
    )


def columns(start, width):
    return pl.ds(pl.multiple_of(start * width, width), width)


def column_pieces(index, sizes):
    pieces = []
    for place, (groups, width) in enumerate(sizes):
        whole = width * index[2]
        for group in range(groups):
            wide = pl.ds(pl.multiple_of(group * whole + index[0] * width, width), width)
            pieces.append((place, wide, pl.ds(group * width, width)))
    return pieces


def exchange_kernel(n, m, sizes, *refs):
    count = len(sizes)
    wides = refs[:count]
    small, segs = refs[count : count + 2]
    narrows = refs[count + 2 : 2 * count + 2]
    small_all, segs_all, local, send, recv, small_send, small_recv = refs[2 * count + 2 :]
    me, lane = lax.axis_index("dp"), lax.axis_index("fsdp")
    here = me * m + lane
    greet_all(n, m)
    others = near(me, n)

    def to_device(step):
        target = {"dp": (me + step // m) % n, "fsdp": (lane + step % m) % m}
        return remote(small, small_all.at[here], small_send.at[step], small_recv.at[step], target)

    def start_small(step, carry):
        to_device(step).start()
        return carry

    def wait_small(step, carry):
        to_device(step).wait()
        return carry

    copies = []
    for peer, (target, unused) in enumerate(others):
        for at, (place, wide, narrow) in enumerate(column_pieces((target, 0, n), sizes)):
            copies.append(
                (at, remote(wides[place].at[:, wide], narrows[place].at[me, :, narrow], send.at[peer, at], recv.at[peer, at], {"dp": target}))
            )
        copies.append((-1, remote(segs, segs_all.at[me], send.at[peer, at + 1], recv.at[peer, at + 1], {"dp": target})))
    owns = [pltpu.make_async_copy(small, small_all.at[here], local.at[0]), pltpu.make_async_copy(segs, segs_all.at[me], local.at[1])]
    for at, (place, wide, narrow) in enumerate(column_pieces((me, 0, n), sizes)):
        owns.append(pltpu.make_async_copy(wides[place].at[:, wide], narrows[place].at[me, :, narrow], local.at[2 + at]))
    for order, copy in copies:
        if order <= 0:
            copy.start()
    lax.fori_loop(1, n * m, start_small, 0)
    for order, copy in copies:
        if order > 0:
            copy.start()
    for copy in owns:
        copy.start()
    for copy in owns:
        copy.wait()
    for order, copy in copies:
        copy.wait()
    lax.fori_loop(1, n * m, wait_small, 0)


def exchange(n, m, wides, sizes, small, segs):
    rows = small.shape[0]
    total = sum(groups for groups, width in sizes)
    outs = [jax.ShapeDtypeStruct((n, rows, groups * width), jnp.bfloat16) for groups, width in sizes]
    outs.append(jax.ShapeDtypeStruct((n * m,) + small.shape, small.dtype))
    outs.append(jax.ShapeDtypeStruct((n,) + segs.shape, segs.dtype))
    anywhere = pl.BlockSpec(memory_space=pl.ANY)
    return pl.pallas_call(
        functools.partial(exchange_kernel, n, m, sizes),
        out_shape=outs,
        in_specs=[anywhere] * (len(wides) + 2),
        out_specs=[anywhere] * len(outs),
        scratch_shapes=[
            pltpu.SemaphoreType.DMA((total + 2,)),
            pltpu.SemaphoreType.DMA((n - 1, total + 1)),
            pltpu.SemaphoreType.DMA((n - 1, total + 1)),
            pltpu.SemaphoreType.DMA((n * m,)),
            pltpu.SemaphoreType.DMA((n * m,)),
        ],
        compiler_params=pltpu.CompilerParams(collective_id=0, has_side_effects=True),
        name="exchange",
    )(*wides, small, segs)


def giveback_kernel(n, sizes, *refs):
    count = len(sizes)
    narrows, wides = refs[:count], refs[count : 2 * count]
    local, send, recv = refs[2 * count :]
    me = lax.axis_index("dp")
    others = near(me, n)
    greet([target for target, unused in others])
    copies = []
    for peer, (target, unused) in enumerate(others):
        for at, (place, wide, narrow) in enumerate(column_pieces((me, 0, n), sizes)):
            copies.append(
                remote(narrows[place].at[target, :, narrow], wides[place].at[:, wide], send.at[peer, at], recv.at[peer, at], {"dp": target})
            )
    for at, (place, wide, narrow) in enumerate(column_pieces((me, 0, n), sizes)):
        copies.append(pltpu.make_async_copy(narrows[place].at[me, :, narrow], wides[place].at[:, wide], local.at[at]))
    for copy in copies:
        copy.start()
    for copy in copies:
        copy.wait()


def giveback(n, narrows, sizes, number):
    rows = narrows[0].shape[1]
    total = sum(groups for groups, width in sizes)
    outs = [jax.ShapeDtypeStruct((rows, groups * width * n), jnp.bfloat16) for groups, width in sizes]
    anywhere = pl.BlockSpec(memory_space=pl.ANY)
    return pl.pallas_call(
        functools.partial(giveback_kernel, n, sizes),
        out_shape=outs,
        in_specs=[anywhere] * len(narrows),
        out_specs=[anywhere] * len(outs),
        scratch_shapes=[
            pltpu.SemaphoreType.DMA((total,)),
            pltpu.SemaphoreType.DMA((n - 1, total)),
            pltpu.SemaphoreType.DMA((n - 1, total)),
        ],
        compiler_params=pltpu.CompilerParams(collective_id=number, has_side_effects=True),
        name="giveback",
    )(*narrows)


def share_kernel(n, mine, shared, local, send, recv):
    me = lax.axis_index("dp")
    others = near(me, n)
    greet([target for target, unused in others])
    copies = [pltpu.make_async_copy(mine, shared.at[me], local)]
    for peer, (target, unused) in enumerate(others):
        copies.append(remote(mine, shared.at[me], send.at[peer], recv.at[peer], {"dp": target}))
    for copy in copies:
        copy.start()
    for copy in copies:
        copy.wait()


def share(n, mine, number):
    inside = pl.BlockSpec(memory_space=pltpu.VMEM)
    return pl.pallas_call(
        functools.partial(share_kernel, n),
        out_shape=jax.ShapeDtypeStruct((n,) + mine.shape, mine.dtype),
        in_specs=[inside],
        out_specs=inside,
        scratch_shapes=[
            pltpu.SemaphoreType.DMA,
            pltpu.SemaphoreType.DMA((n - 1,)),
            pltpu.SemaphoreType.DMA((n - 1,)),
        ],
        compiler_params=pltpu.CompilerParams(collective_id=number, has_side_effects=True),
        name="share",
    )(mine)


def collect_kernel(n, m, wide, group, wide_all, group_all, local, send, recv, group_send, group_recv):
    me, lane = lax.axis_index("dp"), lax.axis_index("fsdp")
    here = me * m + lane
    greet_all(n, m)

    def to_device(step):
        other, beside = (me + step // m) % n, (lane + step % m) % m
        return remote(
            wide.at[other * m + beside], wide_all.at[here], send.at[step], recv.at[step], {"dp": other, "fsdp": beside}
        )

    def to_group(step):
        beside = (lane + step) % m
        return remote(group.at[beside], group_all.at[lane], group_send.at[step], group_recv.at[step], {"fsdp": beside})

    def start_wide(step, carry):
        to_device(step).start()
        return carry

    def start_group(step, carry):
        to_group(step).start()
        return carry

    def wait_wide(step, carry):
        to_device(step).wait()
        return carry

    def wait_group(step, carry):
        to_group(step).wait()
        return carry

    own = pltpu.make_async_copy(wide.at[here], wide_all.at[here], local.at[0])
    own_group = pltpu.make_async_copy(group.at[lane], group_all.at[lane], local.at[1])
    own.start()
    own_group.start()
    lax.fori_loop(1, n * m, start_wide, 0)
    lax.fori_loop(1, m, start_group, 0)
    own.wait()
    own_group.wait()
    lax.fori_loop(1, n * m, wait_wide, 0)
    lax.fori_loop(1, m, wait_group, 0)


def collect(n, m, wide, group, number):
    inside = pl.BlockSpec(memory_space=pltpu.VMEM)
    return pl.pallas_call(
        functools.partial(collect_kernel, n, m),
        out_shape=[jax.ShapeDtypeStruct(wide.shape, wide.dtype), jax.ShapeDtypeStruct(group.shape, group.dtype)],
        in_specs=[inside] * 2,
        out_specs=[inside] * 2,
        scratch_shapes=[
            pltpu.SemaphoreType.DMA((2,)),
            pltpu.SemaphoreType.DMA((n * m,)),
            pltpu.SemaphoreType.DMA((n * m,)),
            pltpu.SemaphoreType.DMA((m,)),
            pltpu.SemaphoreType.DMA((m,)),
        ],
        compiler_params=pltpu.CompilerParams(collective_id=number, has_side_effects=True),
        name="collect",
    )(wide, group)


def unit_of(values):
    centered = values - jnp.mean(values, axis=-1, keepdims=True)
    inverse = lax.rsqrt(jnp.mean(centered * centered, axis=-1, keepdims=True) + EPSILON)
    return centered * inverse, inverse


def unit_back(upstream, unit, inverse, gain):
    scaled = upstream * gain
    adjusted = scaled - jnp.mean(scaled, axis=-1, keepdims=True)
    return inverse * (adjusted - unit * jnp.mean(scaled * unit, axis=-1, keepdims=True))


def step_first(total, states, vectors):
    unit, inverse = unit_of(states[0])
    return [], unit * vectors[0] + vectors[1], []


def step_forward(scale, total, states, vectors):
    values = states[0] + scale * (total + vectors[0])
    unit, inverse = unit_of(values)
    return [values], unit * vectors[1] + vectors[2], []


def step_turn(total, states, vectors):
    values = states[0] + 0.5 * (total + vectors[0])
    upstream = states[1]
    unit, inverse = unit_of(values)
    layer_out = unit * vectors[1] + vectors[2]
    grad = unit_back(upstream, unit, inverse, vectors[1])
    half = 0.5 * grad
    return [layer_out, grad], half, [upstream * unit, upstream, half]


def step_backward(scale, total, states, vectors):
    unit, inverse = unit_of(states[1])
    grad = states[0] + unit_back(total, unit, inverse, vectors[0])
    sent = scale * grad
    return [grad], sent, [total * unit, total, sent]


def step_last(total, states, vectors):
    unit, inverse = unit_of(states[1])
    grad = states[0] + unit_back(total, unit, inverse, vectors[0])
    return [grad], None, [total * unit, total]


PIECES = 4
BLOCK = 16


def boundary_kernel(n, step, shape, *refs):
    summed, gathered, state_count, out_count, sum_count, vector_count = shape
    refs = list(refs)
    take = lambda count: [refs.pop(0) for unused in range(count)]
    part = take(1)[0] if summed else None
    states = take(state_count)
    vectors = take(1)[0]
    outs = take(out_count)
    spread = take(1)[0] if gathered else None
    sums = take(1)[0] if sum_count else None
    if summed:
        arrived, own, own_sem, send, recv = take(5)
    if gathered:
        held, held_sem, out_send, out_recv = take(4)
    partials = take(1)[0] if sum_count else None
    me = lax.axis_index("dp")
    others = near(me, n)
    rows = states[0].shape[0]
    height = rows // PIECES
    greet([target for target, unused in others])
    incoming = {}
    if summed:
        own_copy = pltpu.make_async_copy(part.at[me], own, own_sem)
        for piece in range(PIECES):
            span = pl.ds(piece * height, height)
            for peer, (target, unused) in enumerate(others):
                copy = remote(
                    part.at[target, span], arrived.at[peer, span], send.at[peer, piece], recv.at[peer, piece], {"dp": target}
                )
                copy.start()
                incoming[peer, piece] = copy
        own_copy.start()
        own_copy.wait()
    if sum_count:
        partials[...] = jnp.zeros_like(partials)
    outgoing = []
    rows_of = [vectors[pl.ds(index, 1), :] for index in range(vector_count)]
    for piece in range(PIECES):
        if summed:
            for peer in range(n - 1):
                incoming[peer, piece].wait_recv()

        def work(block, carry):
            span = pl.ds(pl.multiple_of(piece * height + block * BLOCK, BLOCK), BLOCK)
            total = None
            if summed:
                total = own[span, :].astype(jnp.float32)
                for peer in range(n - 1):
                    total = total + arrived[peer, span, :].astype(jnp.float32)
            made, sent, terms = step(total, [state[span, :] for state in states], rows_of)
            for out, value in zip(outs, made):
                out[span, :] = value
            if gathered:
                held[span, :] = sent.astype(jnp.bfloat16)
            for index, term in enumerate(terms):
                partials[index] += sum(term[8 * low : 8 * low + 8] for low in range(BLOCK // 8))
            return carry

        lax.fori_loop(0, height // BLOCK, work, 0)
        if gathered:
            span = pl.ds(piece * height, height)
            for peer, (target, unused) in enumerate(others):
                copy = remote(
                    held.at[span], spread.at[me, span], out_send.at[peer, piece], out_recv.at[peer, piece], {"dp": target}
                )
                copy.start()
                outgoing.append(copy)
    if gathered:
        keep = pltpu.make_async_copy(held, spread.at[me], held_sem)
        keep.start()
    for index in range(sum_count):
        sums[pl.ds(index, 1), :] = jnp.sum(partials[index], axis=0, keepdims=True)
    for copy in incoming.values():
        copy.wait_send()
    for copy in outgoing:
        copy.wait()
    if gathered:
        keep.wait()


def boundary(n, step, part, states, vectors, out_count, sum_count, number, gathered=True):
    rows, width = states[0].shape
    summed = part is not None
    inside = pl.BlockSpec(memory_space=pltpu.VMEM)
    anywhere = pl.BlockSpec(memory_space=pl.ANY)
    shape = (summed, gathered, len(states), out_count, sum_count, len(vectors))
    operands, in_specs, outs, out_specs, scratch = [], [], [], [], []
    if summed:
        operands.append(part)
        in_specs.append(anywhere)
        scratch += [
            pltpu.VMEM((n - 1, rows, width), jnp.bfloat16),
            pltpu.VMEM((rows, width), jnp.bfloat16),
            pltpu.SemaphoreType.DMA,
            pltpu.SemaphoreType.DMA((n - 1, PIECES)),
            pltpu.SemaphoreType.DMA((n - 1, PIECES)),
        ]
    operands += list(states) + [jnp.stack(vectors)]
    in_specs += [inside] * (len(states) + 1)
    outs += [jax.ShapeDtypeStruct((rows, width), jnp.float32)] * out_count
    out_specs += [inside] * out_count
    if gathered:
        outs.append(jax.ShapeDtypeStruct((n, rows, width), jnp.bfloat16))
        out_specs.append(anywhere)
        scratch += [
            pltpu.VMEM((rows, width), jnp.bfloat16),
            pltpu.SemaphoreType.DMA,
            pltpu.SemaphoreType.DMA((n - 1, PIECES)),
            pltpu.SemaphoreType.DMA((n - 1, PIECES)),
        ]
    if sum_count:
        outs.append(jax.ShapeDtypeStruct((sum_count, width), jnp.float32))
        out_specs.append(inside)
        scratch.append(pltpu.VMEM((sum_count, 8, width), jnp.float32))
    return pl.pallas_call(
        functools.partial(boundary_kernel, n, step, shape),
        out_shape=outs,
        in_specs=in_specs,
        out_specs=out_specs,
        scratch_shapes=scratch,
        compiler_params=pltpu.CompilerParams(collective_id=number, has_side_effects=True),
        name="boundary",
    )(*operands)


def toeplitz(line, frame_count):
    wide = jnp.broadcast_to(line, (frame_count, NREL))
    return pltpu.roll(wide, NREL - frame_count + 1, 1, stride=1, stride_axis=0)[:, :frame_count]


def head_scores(packed, head, heads, same, bias):
    size = heads * HEAD
    query_rows = packed[:, head * HEAD : (head + 1) * HEAD]
    key_rows = packed[:, size + head * HEAD : size + (head + 1) * HEAD]
    value_rows = packed[:, 2 * size + head * HEAD : 2 * size + (head + 1) * HEAD]
    scores = jnp.where(same, HEAD ** (-0.5) * back_dot(query_rows, key_rows) + bias, MASKED)
    powered = jnp.exp(scores - jnp.max(scores, axis=-1, keepdims=True))
    soft = powered / jnp.sum(powered, axis=-1, keepdims=True)
    return query_rows, key_rows, value_rows, soft


def attend_kernel(heads, packed, segment_rows, segment_columns, table, blended, bias):
    frame_count = packed.shape[1]

    @pl.when(pl.program_id(0) == 0)
    def _():
        for head in range(heads):
            bias[head] = toeplitz(table[pl.ds(head, 1), :], frame_count)

    same = segment_columns[0] == segment_rows[0]
    block = packed[0]
    results = []
    for head in range(heads):
        unused, unused_too, value_rows, soft = head_scores(block, head, heads, same, bias[head])
        results.append(flat_dot(soft.astype(jnp.bfloat16), value_rows).astype(jnp.bfloat16))
    blended[0] = jnp.concatenate(results, axis=1)


def attend(packed, segment_rows, segment_columns, table):
    blocks, frame_count, width = packed.shape
    heads = table.shape[0]
    return pl.pallas_call(
        functools.partial(attend_kernel, heads),
        grid=(blocks,),
        out_shape=jax.ShapeDtypeStruct((blocks, frame_count, width // 3), jnp.bfloat16),
        in_specs=[
            pl.BlockSpec((1, frame_count, width), lambda i: (i, 0, 0)),
            pl.BlockSpec((1, 1, frame_count), lambda i: (i, 0, 0)),
            pl.BlockSpec((1, frame_count, 1), lambda i: (i, 0, 0)),
            pl.BlockSpec((heads, NREL), lambda i: (0, 0)),
        ],
        out_specs=pl.BlockSpec((1, frame_count, width // 3), lambda i: (i, 0, 0)),
        scratch_shapes=[pltpu.VMEM((heads, frame_count, frame_count), jnp.float32)],
        name="attend",
    )(packed, segment_rows, segment_columns, table)


def unattend_kernel(heads, packed, upstream, segment_rows, segment_columns, table, grads, sums, slope, bias, gathered):
    frame_count = packed.shape[1]
    size = heads * HEAD
    at = pl.program_id(0)

    @pl.when(at == 0)
    def _():
        for head in range(heads):
            bias[head] = toeplitz(table[pl.ds(head, 1), :], frame_count)
        gathered[...] = jnp.zeros_like(gathered)
        sums[...] = jnp.zeros_like(sums)

    same = segment_columns[0] == segment_rows[0]
    block = packed[0]
    above = upstream[0]
    query_grads, key_grads, value_grads = [], [], []
    for head in range(heads):
        query_rows, key_rows, value_rows, soft = head_scores(block, head, heads, same, bias[head])
        blend_grad = above[:, head * HEAD : (head + 1) * HEAD]
        value_grads.append(lead_dot(soft.astype(jnp.bfloat16), blend_grad))
        soft_grad = back_dot(blend_grad, value_rows)
        score_grad = soft * (soft_grad - jnp.sum(soft * soft_grad, axis=-1, keepdims=True))
        gathered[head] += score_grad
        low = (HEAD ** (-0.5) * score_grad).astype(jnp.bfloat16)
        query_grads.append(flat_dot(low, key_rows))
        key_grads.append(lead_dot(low, query_rows))
    query_grad = jnp.concatenate(query_grads, axis=1)
    value_grad = jnp.concatenate(value_grads, axis=1)
    grads[0, :, 0:size] = query_grad.astype(jnp.bfloat16)
    grads[0, :, size : 2 * size] = jnp.concatenate(key_grads, axis=1).astype(jnp.bfloat16)
    grads[0, :, 2 * size :] = value_grad.astype(jnp.bfloat16)
    sums[0:1, :] += jnp.sum(query_grad, axis=0, keepdims=True)
    sums[1:2, :] += jnp.sum(value_grad, axis=0, keepdims=True)

    @pl.when(at == pl.num_programs(0) - 1)
    def _():
        places = lax.broadcasted_iota(jnp.int32, (frame_count, NREL), 0)
        for head in range(heads):
            wide = jnp.concatenate(
                [gathered[head], jnp.zeros((frame_count, NREL - frame_count), jnp.float32)], axis=1
            )
            stride = 1
            while stride < frame_count:
                moved = pltpu.roll(wide, NREL - stride, 1)
                wide = jnp.where((places // stride) % 2 == 1, moved, wide)
                stride *= 2
            slope[pl.ds(head, 1), :] = jnp.sum(wide, axis=0, keepdims=True)


def unattend(packed, upstream, segment_rows, segment_columns, table):
    blocks, frame_count, width = packed.shape
    heads = table.shape[0]
    return pl.pallas_call(
        functools.partial(unattend_kernel, heads),
        grid=(blocks,),
        out_shape=[
            jax.ShapeDtypeStruct((blocks, frame_count, width), jnp.bfloat16),
            jax.ShapeDtypeStruct((2, width // 3), jnp.float32),
            jax.ShapeDtypeStruct((heads, NREL), jnp.float32),
        ],
        in_specs=[
            pl.BlockSpec((1, frame_count, width), lambda i: (i, 0, 0)),
            pl.BlockSpec((1, frame_count, width // 3), lambda i: (i, 0, 0)),
            pl.BlockSpec((1, 1, frame_count), lambda i: (i, 0, 0)),
            pl.BlockSpec((1, frame_count, 1), lambda i: (i, 0, 0)),
            pl.BlockSpec((heads, NREL), lambda i: (0, 0)),
        ],
        out_specs=[
            pl.BlockSpec((1, frame_count, width), lambda i: (i, 0, 0)),
            pl.BlockSpec((2, width // 3), lambda i: (0, 0)),
            pl.BlockSpec((heads, NREL), lambda i: (0, 0)),
        ],
        scratch_shapes=[
            pltpu.VMEM((heads, frame_count, frame_count), jnp.float32),
            pltpu.VMEM((heads, frame_count, frame_count), jnp.float32),
        ],
        name="unattend",
    )(packed, upstream, segment_rows, segment_columns, table)


MARGIN = 16
LANES = 128


def reach_mask(offset, behind, ahead):
    if offset < 0:
        return behind >= -offset
    return ahead >= offset


def convolve_kernel(opened, behind, ahead, taps, bias, gated, filtered, padded):
    frame_count, channels = gated.shape[1:]
    gates = opened[0, :, 0:channels] * jax.nn.sigmoid(opened[0, :, channels:])
    gated[0] = gates
    padded[pl.ds(0, MARGIN), :] = jnp.zeros((MARGIN, channels), jnp.float32)
    padded[pl.ds(MARGIN + frame_count, MARGIN), :] = jnp.zeros((MARGIN, channels), jnp.float32)
    padded[pl.ds(MARGIN, frame_count), :] = gates
    back = jnp.broadcast_to(behind[0], (frame_count, LANES))
    front = jnp.broadcast_to(ahead[0], (frame_count, LANES))
    for low in range(0, channels, LANES):
        lanes = slice(low, low + LANES)
        running = jnp.broadcast_to(bias[:, lanes], (frame_count, LANES))
        for tap in range(KW):
            offset = tap - (KW - 1) // 2
            moved = padded[pl.ds(MARGIN + offset, frame_count), lanes]
            if offset:
                moved = jnp.where(reach_mask(offset, back, front), moved, 0.0)
            running = running + moved * taps[pl.ds(tap, 1), lanes]
        filtered[0, :, lanes] = running


def convolve(opened, behind, ahead, taps, bias):
    blocks, frame_count, width = opened.shape
    channels = width // 2
    rows = pl.BlockSpec((1, frame_count, channels), lambda i: (i, 0, 0))
    places = pl.BlockSpec((1, frame_count, 1), lambda i: (i, 0, 0))
    return pl.pallas_call(
        convolve_kernel,
        grid=(blocks,),
        out_shape=[jax.ShapeDtypeStruct((blocks, frame_count, channels), jnp.float32)] * 2,
        in_specs=[
            pl.BlockSpec((1, frame_count, width), lambda i: (i, 0, 0)),
            places,
            places,
            pl.BlockSpec((KW, channels), lambda i: (0, 0)),
            pl.BlockSpec((1, channels), lambda i: (0, 0)),
        ],
        out_specs=[rows, rows],
        scratch_shapes=[pltpu.VMEM((frame_count + 2 * MARGIN, channels), jnp.float32)],
        name="convolve",
    )(opened, behind, ahead, taps, bias)


def unconvolve_kernel(opened, gated, upstream, behind, ahead, taps, grads, lifts, slopes, padded, padded_grad):
    frame_count, channels = gated.shape[1:]

    @pl.when(pl.program_id(0) == 0)
    def _():
        lifts[...] = jnp.zeros_like(lifts)
        slopes[...] = jnp.zeros_like(slopes)

    for store, value in ((padded, gated[0]), (padded_grad, upstream[0])):
        store[pl.ds(0, MARGIN), :] = jnp.zeros((MARGIN, channels), jnp.float32)
        store[pl.ds(MARGIN + frame_count, MARGIN), :] = jnp.zeros((MARGIN, channels), jnp.float32)
        store[pl.ds(MARGIN, frame_count), :] = value
    back = jnp.broadcast_to(behind[0], (frame_count, LANES))
    front = jnp.broadcast_to(ahead[0], (frame_count, LANES))
    for low in range(0, channels, LANES):
        lanes = slice(low, low + LANES)
        above = upstream[0, :, lanes]
        running = jnp.zeros((frame_count, LANES), jnp.float32)
        for tap in range(KW):
            offset = tap - (KW - 1) // 2
            moved = padded[pl.ds(MARGIN + offset, frame_count), lanes]
            moved_grad = padded_grad[pl.ds(MARGIN + offset, frame_count), lanes]
            if offset:
                mask = reach_mask(offset, back, front)
                moved = jnp.where(mask, moved, 0.0)
                moved_grad = jnp.where(mask, moved_grad, 0.0)
            running = running + moved_grad * taps[pl.ds(KW - 1 - tap, 1), lanes]
            slopes[pl.ds(tap, 1), lanes] += jnp.sum(moved * above, axis=0, keepdims=True)
        slopes[pl.ds(KW, 1), lanes] += jnp.sum(above, axis=0, keepdims=True)
        wide = slice(channels + low, channels + low + LANES)
        left, gate = opened[0, :, lanes], jax.nn.sigmoid(opened[0, :, wide])
        left_grad = running * gate
        gate_grad = running * left * gate * (1.0 - gate)
        grads[0, :, lanes] = left_grad.astype(jnp.bfloat16)
        grads[0, :, wide] = gate_grad.astype(jnp.bfloat16)
        lifts[:, lanes] += jnp.sum(left_grad, axis=0, keepdims=True)
        lifts[:, wide] += jnp.sum(gate_grad, axis=0, keepdims=True)


def unconvolve(opened, gated, upstream, behind, ahead, taps):
    blocks, frame_count, width = opened.shape
    channels = width // 2
    wide = pl.BlockSpec((1, frame_count, width), lambda i: (i, 0, 0))
    rows = pl.BlockSpec((1, frame_count, channels), lambda i: (i, 0, 0))
    places = pl.BlockSpec((1, frame_count, 1), lambda i: (i, 0, 0))
    return pl.pallas_call(
        unconvolve_kernel,
        grid=(blocks,),
        out_shape=[
            jax.ShapeDtypeStruct((blocks, frame_count, width), jnp.bfloat16),
            jax.ShapeDtypeStruct((1, width), jnp.float32),
            jax.ShapeDtypeStruct((KW + 1, channels), jnp.float32),
        ],
        in_specs=[wide, rows, rows, places, places, pl.BlockSpec((KW, channels), lambda i: (0, 0))],
        out_specs=[
            wide,
            pl.BlockSpec((1, width), lambda i: (0, 0)),
            pl.BlockSpec((KW + 1, channels), lambda i: (0, 0)),
        ],
        scratch_shapes=[pltpu.VMEM((frame_count + 2 * MARGIN, channels), jnp.float32)] * 2,
        name="unconvolve",
    )(opened, gated, upstream, behind, ahead, taps)


def gather_rows(value):
    return lax.all_gather(value, "fsdp", axis=0, tiled=True)


def gather_split(value):
    full = lax.all_gather(value, "fsdp", axis=1, tiled=True)
    return full.reshape(-1, full.shape[-1])


def scatter_rows(value):
    return lax.psum_scatter(value.astype(jnp.bfloat16), "fsdp", scatter_dimension=0, tiled=True)


def scatter_split(value, n):
    value = value.astype(jnp.bfloat16).reshape(n, value.shape[0] // n, value.shape[1])
    return lax.psum_scatter(value, "fsdp", scatter_dimension=1, tiled=True)


def flat(value):
    return value.reshape(-1, value.shape[-1])


def split_body(
    n,
    m,
    frames,
    segments,
    cotangent,
    early_gain,
    early_shift,
    early_up,
    early_lift,
    early_down,
    early_drop,
    mixer_gain,
    mixer_shift,
    mixer_project,
    query_bias,
    value_bias,
    mixer_output,
    mixer_drop,
    distance_table,
    filter_gain,
    filter_shift,
    filter_up,
    filter_lift,
    depth_weight,
    depth_bias,
    middle_gain,
    middle_shift,
    filter_down,
    filter_drop,
    late_gain,
    late_shift,
    late_up,
    late_lift,
    late_down,
    late_drop,
    final_gain,
    final_shift,
):
    me = lax.axis_index("dp")
    frame_count = frames.shape[0]
    rows = early_gain.shape[0]
    hidden = early_up.shape[1] // n
    inner = D // n
    heads = HEADS // n
    start_rows = frames.astype(jnp.float32)
    final_upstream = cotangent.astype(jnp.float32)
    singles = [
        early_gain, early_shift, early_drop, mixer_gain, mixer_shift, query_bias, value_bias, mixer_drop,
        filter_gain, filter_shift, depth_bias, middle_gain, middle_shift, filter_drop, late_gain, late_shift,
        late_drop, final_gain, final_shift,
    ]
    at_lift = len(singles) + KW
    spans = hidden * n // D
    small = jnp.concatenate(
        [
            jnp.transpose(jnp.stack(singles)),
            depth_weight,
            early_lift.reshape(rows, spans),
            late_lift.reshape(rows, spans),
            filter_lift.reshape(rows, 2),
            distance_table.reshape(rows, -1),
        ],
        axis=1,
    )
    small = jnp.pad(small, ((0, 0), (0, LANES - small.shape[1])))
    sizes = [(1, hidden), (1, hidden), (3, inner), (2, inner)]
    early_up_split, late_up_split, project_split, filter_up_split, small_all, segments_all = exchange(
        n, m, [early_up, late_up, mixer_project, filter_up], sizes, small, segments.reshape(1, frame_count)
    )
    w_early_down = gather_rows(early_down)
    w_early_up = gather_split(early_up_split)
    w_project = gather_split(project_split)
    w_output = gather_rows(mixer_output)
    w_filter_up = gather_split(filter_up_split)
    w_filter_down = gather_rows(filter_down)
    w_late_up = gather_split(late_up_split)
    w_late_down = gather_rows(late_down)

    listed = small_all.reshape(D, LANES)
    vectors = jnp.transpose(listed).astype(jnp.float32)
    own_vectors = lax.dynamic_slice(vectors, (0, me * inner), (LANES, inner))

    def whole(low, count):
        return listed[:, low : low + count].astype(jnp.float32).reshape(-1)

    early_lifts = lax.dynamic_slice(whole(at_lift, spans), (me * hidden,), (hidden,))
    late_lifts = lax.dynamic_slice(whole(at_lift + spans, spans), (me * hidden,), (hidden,))
    filter_lifts = lax.dynamic_slice(
        whole(at_lift + 2 * spans, 2).reshape(2, D), (0, me * inner), (2, inner)
    ).reshape(2 * inner)
    at_table = at_lift + 2 * spans + 2
    table = whole(at_table, NREL * HEADS // D).reshape(NREL, HEADS)
    table = jnp.transpose(lax.dynamic_slice(table, (0, me * heads), (NREL, heads)))[:, ::-1]
    taps = own_vectors[len(singles) : len(singles) + KW]
    attention_shift = jnp.concatenate([own_vectors[5], jnp.zeros((inner,), jnp.float32), own_vectors[6]])
    segment_rows = segments_all
    segment_columns = segments_all.reshape(n, frame_count, 1)
    places = jnp.arange(frame_count, dtype=jnp.int32)[None, :]
    lower = (segment_rows < segment_columns).astype(jnp.int32)
    upto = (segment_rows <= segment_columns).astype(jnp.int32)
    behind = (places - jnp.sum(lower, axis=-1)).reshape(n, frame_count, 1)
    ahead = (jnp.sum(upto, axis=-1) - 1 - places).reshape(n, frame_count, 1)

    def blocks(value):
        return value.reshape(n, frame_count, value.shape[-1])

    def feed(hidden_rows, w_up, lifts, w_down):
        widened = flat_dot(flat(hidden_rows), w_up) + lifts
        active = (widened * jax.nn.sigmoid(widened)).astype(jnp.bfloat16)
        return widened, active, blocks(flat_dot(active, w_down).astype(jnp.bfloat16))

    def feed_back(low, hidden_rows, widened, active, w_up, w_down):
        low = flat(low)
        down_slope = scatter_rows(lead_dot(active, low))
        widened_grad = swish_back(back_dot(low, w_down), widened)
        widened_low = widened_grad.astype(jnp.bfloat16)
        up_slope = scatter_split(lead_dot(flat(hidden_rows), widened_low), n)
        part = blocks(back_dot(widened_low, w_up).astype(jnp.bfloat16))
        return part, down_slope, up_slope, jnp.sum(widened_grad, axis=0)

    (early_hidden,) = boundary(n, step_first, None, [start_rows], [vectors[0], vectors[1]], 0, 0, 1)
    early_wide, early_active, part = feed(early_hidden, w_early_up, early_lifts, w_early_down)
    first_rows, mixer_hidden = boundary(
        n, functools.partial(step_forward, 0.5), part, [start_rows], [vectors[2], vectors[3], vectors[4]], 1, 0, 2
    )
    packed = blocks((flat_dot(flat(mixer_hidden), w_project) + attention_shift).astype(jnp.bfloat16))
    blended = attend(packed, segment_rows, segment_columns, table)
    part = blocks(flat_dot(flat(blended), w_output).astype(jnp.bfloat16))
    second_rows, filter_hidden = boundary(
        n, functools.partial(step_forward, 1.0), part, [first_rows], [vectors[7], vectors[8], vectors[9]], 1, 0, 3
    )
    opened = blocks(flat_dot(flat(filter_hidden), w_filter_up) + filter_lifts)
    gated, filtered = convolve(opened, behind, ahead, taps, own_vectors[10:11])
    filtered = flat(filtered)
    local_mean = jnp.mean(filtered, axis=-1)
    local_square = jnp.sum((filtered - local_mean[:, None]) ** 2, axis=-1)
    shared = share(
        n, jnp.concatenate([local_mean.reshape(n, frame_count), local_square.reshape(n, frame_count)]), 4
    )
    means, squares = shared[:, :n], shared[:, n:]
    middle_mean = jnp.mean(means, axis=0)
    spread = jnp.sum(squares, axis=0) + inner * jnp.sum((means - middle_mean) ** 2, axis=0)
    middle_inverse = lax.rsqrt(spread / D + EPSILON).reshape(-1, 1)
    middle_unit = (filtered - middle_mean.reshape(-1, 1)) * middle_inverse
    middle = middle_unit * own_vectors[11] + own_vectors[12]
    swished = (middle * jax.nn.sigmoid(middle)).astype(jnp.bfloat16)
    part = blocks(flat_dot(swished, w_filter_down).astype(jnp.bfloat16))
    third_rows, late_hidden = boundary(
        n, functools.partial(step_forward, 1.0), part, [second_rows], [vectors[13], vectors[14], vectors[15]], 1, 0, 5
    )
    late_wide, late_active, part = feed(late_hidden, w_late_up, late_lifts, w_late_down)
    layer_out, grad, low, turn_sums = boundary(
        n, step_turn, part, [third_rows, final_upstream], [vectors[16], vectors[17], vectors[18]], 2, 3, 6
    )

    part, late_down_slope, late_up_slope, late_lift_slope = feed_back(
        low, late_hidden, late_wide, late_active, w_late_up, w_late_down
    )
    grad, low, late_sums = boundary(
        n, functools.partial(step_backward, 1.0), part, [grad, third_rows], [vectors[14]], 1, 3, 7
    )
    low = flat(low)
    filter_down_slope = scatter_rows(lead_dot(swished, low))
    middle_grad = swish_back(back_dot(low, w_filter_down), middle)
    middle_gain_slope = jnp.sum(middle_grad * middle_unit, axis=0)
    middle_shift_slope = jnp.sum(middle_grad, axis=0)
    scaled = middle_grad * own_vectors[11]
    shared = share(
        n,
        jnp.concatenate(
            [
                jnp.sum(scaled, axis=-1).reshape(n, frame_count),
                jnp.sum(scaled * middle_unit, axis=-1).reshape(n, frame_count),
            ]
        ),
        8,
    )
    totals = jnp.sum(shared, axis=0) / D
    filtered_grad = middle_inverse * (
        scaled - totals[:n].reshape(-1, 1) - middle_unit * totals[n:].reshape(-1, 1)
    )
    opened_low, filter_lift_slope, depth_slope = unconvolve(
        opened, gated, blocks(filtered_grad), behind, ahead, taps
    )
    opened_low = flat(opened_low)
    filter_up_slope = scatter_split(lead_dot(flat(filter_hidden), opened_low), n)
    part = blocks(back_dot(opened_low, w_filter_up).astype(jnp.bfloat16))
    grad, low, filter_sums = boundary(
        n, functools.partial(step_backward, 1.0), part, [grad, second_rows], [vectors[8]], 1, 3, 9
    )
    low = flat(low)
    output_slope = scatter_rows(lead_dot(flat(blended), low))
    blend_grad = blocks(back_dot(low, w_output).astype(jnp.bfloat16))
    packed_low, shift_sums, table_slope = unattend(packed, blend_grad, segment_rows, segment_columns, table)
    packed_low = flat(packed_low)
    project_slope = scatter_split(lead_dot(flat(mixer_hidden), packed_low), n)
    part = blocks(back_dot(packed_low, w_project).astype(jnp.bfloat16))
    grad, low, mixer_sums = boundary(
        n, functools.partial(step_backward, 0.5), part, [grad, first_rows], [vectors[3]], 1, 3, 10
    )
    part, early_down_slope, early_up_slope, early_lift_slope = feed_back(
        low, early_hidden, early_wide, early_active, w_early_up, w_early_down
    )
    slope_frames, early_sums = boundary(
        n, step_last, part, [grad, start_rows], [vectors[0]], 1, 2, 11, gathered=False
    )

    table_slope = jnp.roll(table_slope[:, ::-1], 1 - NREL // 2, axis=1)
    table_rows = NREL // (n * m)
    wide = jnp.concatenate([turn_sums, late_sums, filter_sums, mixer_sums, early_sums])
    wide_count = wide.shape[0]
    wide = jnp.transpose(wide.reshape(wide_count, n * m, rows), (1, 0, 2)).reshape(n * m, wide_count * rows)
    wide = jnp.concatenate(
        [wide, jnp.transpose(table_slope.reshape(heads, n * m, table_rows), (1, 0, 2)).reshape(n * m, -1)], axis=1
    )
    lift_full = lax.dynamic_update_slice(
        jnp.zeros((2, D), jnp.float32), filter_lift_slope.reshape(2, inner), (0, me * inner)
    ).reshape(n * m, -1)
    table_used = wide.shape[1]
    wide = jnp.concatenate([wide, lift_full], axis=1)
    wide_used = wide.shape[1]
    wide = jnp.pad(wide, ((0, 0), (0, -wide_used % LANES))).reshape(n * m, -1, LANES)
    group = jnp.concatenate(
        [
            shift_sums,
            middle_gain_slope[None],
            middle_shift_slope[None],
            depth_slope,
            jnp.transpose(early_lift_slope.reshape(inner, spans)),
            jnp.transpose(late_lift_slope.reshape(inner, spans)),
        ]
    )
    group_count = group.shape[0]
    group = jnp.transpose(group.reshape(group_count, m, rows), (1, 0, 2)).reshape(m, group_count * rows)
    group_used = group.shape[1]
    group = jnp.pad(group, ((0, 0), (0, -group_used % LANES))).reshape(m, -1, LANES)
    wide_all, group_all = collect(n, m, wide, group, 12)
    tables = wide_all.reshape(n, m, -1)[:, :, wide_count * rows : table_used]
    wide = jnp.sum(wide_all, axis=0).reshape(-1)
    lift_total = wide[table_used:wide_used]
    wide = wide[: wide_count * rows].reshape(wide_count, rows)
    tables = jnp.transpose(jnp.sum(tables, axis=1).reshape(HEADS, table_rows))
    group = jnp.sum(group_all, axis=0).reshape(-1)[:group_used].reshape(group_count, rows)
    late_up_wide, project_wide, filter_up_wide = giveback(
        n, [late_up_slope, project_slope, filter_up_slope], sizes[1:], 13
    )
    (early_up_wide,) = giveback(n, [early_up_slope], sizes[:1], 14)

    def final(value):
        return value.astype(jnp.float32)

    lift_slopes = KW + 5
    return (
        layer_out,
        slope_frames,
        wide[12],
        wide[13],
        final(early_up_wide),
        jnp.transpose(group[lift_slopes : lift_slopes + spans]).reshape(-1),
        final(early_down_slope),
        wide[11],
        wide[9],
        wide[10],
        final(project_wide),
        group[0],
        group[1],
        final(output_slope),
        wide[8],
        tables,
        wide[6],
        wide[7],
        final(filter_up_wide),
        lift_total,
        jnp.transpose(group[4 : 4 + KW]),
        group[4 + KW],
        group[2],
        group[3],
        final(filter_down_slope),
        wide[5],
        wide[3],
        wide[4],
        final(late_up_wide),
        jnp.transpose(group[lift_slopes + spans : lift_slopes + 2 * spans]).reshape(-1),
        final(late_down_slope),
        wide[2],
        wide[0],
        wide[1],
    )


def solution(mesh):
    in_specs = (
        P(("dp", "fsdp"), None),
        P(("dp", "fsdp")),
        P(("dp", "fsdp"), None),
        P(("dp", "fsdp")),
        P(("dp", "fsdp")),
        P(("dp", "fsdp"), None),
        P(("dp", "fsdp")),
        P(("dp", "fsdp"), None),
        P(("dp", "fsdp")),
        P(("dp", "fsdp")),
        P(("dp", "fsdp")),
        P(("dp", "fsdp"), None),
        P(("dp", "fsdp")),
        P(("dp", "fsdp")),
        P(("dp", "fsdp"), None),
        P(("dp", "fsdp")),
        P(("dp", "fsdp"), None),
        P(("dp", "fsdp")),
        P(("dp", "fsdp")),
        P(("dp", "fsdp"), None),
        P(("dp", "fsdp")),
        P(("dp", "fsdp"), None),
        P(("dp", "fsdp")),
        P(("dp", "fsdp")),
        P(("dp", "fsdp")),
        P(("dp", "fsdp"), None),
        P(("dp", "fsdp")),
        P(("dp", "fsdp")),
        P(("dp", "fsdp")),
        P(("dp", "fsdp"), None),
        P(("dp", "fsdp")),
        P(("dp", "fsdp"), None),
        P(("dp", "fsdp")),
        P(("dp", "fsdp")),
        P(("dp", "fsdp")),
    )
    out_specs = (
        P(("dp", "fsdp"), None),
        P(("dp", "fsdp"), None),
        P(("dp", "fsdp")),
        P(("dp", "fsdp")),
        P(("dp", "fsdp"), None),
        P(("dp", "fsdp")),
        P(("dp", "fsdp"), None),
        P(("dp", "fsdp")),
        P(("dp", "fsdp")),
        P(("dp", "fsdp")),
        P(("dp", "fsdp"), None),
        P(("dp", "fsdp")),
        P(("dp", "fsdp")),
        P(("dp", "fsdp"), None),
        P(("dp", "fsdp")),
        P(("dp", "fsdp"), None),
        P(("dp", "fsdp")),
        P(("dp", "fsdp")),
        P(("dp", "fsdp"), None),
        P(("dp", "fsdp")),
        P(("dp", "fsdp"), None),
        P(("dp", "fsdp")),
        P(("dp", "fsdp")),
        P(("dp", "fsdp")),
        P(("dp", "fsdp"), None),
        P(("dp", "fsdp")),
        P(("dp", "fsdp")),
        P(("dp", "fsdp")),
        P(("dp", "fsdp"), None),
        P(("dp", "fsdp")),
        P(("dp", "fsdp"), None),
        P(("dp", "fsdp")),
        P(("dp", "fsdp")),
        P(("dp", "fsdp")),
    )
    n, m = mesh.shape["dp"], mesh.shape["fsdp"]
    run = functools.partial(split_body, n, m) if n == 4 and D // (n * m) == 32 else body
    return jax.shard_map(run, mesh=mesh, in_specs=in_specs, out_specs=out_specs, check_vma=False)
```

```python
import functools

import jax
import jax.numpy as jnp
from jax import lax
from jax.experimental import pallas as pl
from jax.experimental.pallas import tpu as pltpu
from jax.sharding import PartitionSpec as P

D = 1024
HEADS = 16
HEAD = 64
KW = 31
NREL = 256


EPSILON = 1e-05
MASKED = -1e30
UTTERANCE_LIMIT = 4
MESH = pl.DeviceIdType.MESH
PIECES = 4
BLOCK = 16
MARGIN = 16
LANES = 128


def flat_dot(left_rows, right_rows):
    return jnp.dot(left_rows, right_rows, preferred_element_type=jnp.float32)


def lead_dot(left_rows, right_rows):
    return lax.dot_general(
        left_rows, right_rows, (((0,), (0,)), ((), ())), preferred_element_type=jnp.float32
    )


def back_dot(left_rows, right_rows):
    return lax.dot_general(
        left_rows, right_rows, (((1,), (1,)), ((), ())), preferred_element_type=jnp.float32
    )


def norm_apply(values, norm_gain, norm_shift):
    centered = values - jnp.mean(values, axis=-1, keepdims=True)
    inverse = lax.rsqrt(jnp.mean(centered * centered, axis=-1, keepdims=True) + EPSILON)
    normed_unit = centered * inverse
    return (
        normed_unit * norm_gain.astype(jnp.float32) + norm_shift.astype(jnp.float32),
        normed_unit,
        inverse,
    )


def norm_back(upstream, normed_unit, inverse, norm_gain):
    scaled = upstream * norm_gain.astype(jnp.float32)
    adjusted = scaled - jnp.mean(scaled, axis=-1, keepdims=True)
    adjusted = adjusted - normed_unit * jnp.mean(scaled * normed_unit, axis=-1, keepdims=True)
    return (inverse * adjusted, jnp.sum(upstream * normed_unit, axis=0), jnp.sum(upstream, axis=0))


def swish_back(upstream, before):
    sigmoid_rows = jax.nn.sigmoid(before)
    return upstream * sigmoid_rows * (1.0 + before * (1.0 - sigmoid_rows))


def depthwise(gated_rows, kernel, segment_ids):
    margin = (KW - 1) // 2
    channels = gated_rows.shape[1]
    taps = jnp.transpose(kernel)[:, None, :]
    running = jnp.zeros_like(gated_rows)
    for utterance in range(UTTERANCE_LIMIT):
        inside = (segment_ids == utterance)[:, None]
        masked_rows = jnp.where(inside, gated_rows, 0.0)
        convolved = lax.conv_general_dilated(
            masked_rows[None],
            taps,
            (1,),
            ((margin, margin),),
            dimension_numbers=("NWC", "WIO", "NWC"),
            feature_group_count=channels,
            precision=lax.Precision.HIGHEST,
        )[0]
        running = running + jnp.where(inside, convolved, 0.0)
    return running


def fetch_feed(norm_gain, norm_shift, w_up, up_shift, w_down, down_shift):
    return (
        lax.all_gather(norm_gain, ("dp", "fsdp"), axis=0, tiled=True),
        lax.all_gather(norm_shift, ("dp", "fsdp"), axis=0, tiled=True),
        lax.all_gather(w_up, ("dp", "fsdp"), axis=0, tiled=True),
        lax.all_gather(up_shift, ("dp", "fsdp"), axis=0, tiled=True),
        lax.all_gather(w_down, ("dp", "fsdp"), axis=0, tiled=True),
        lax.all_gather(down_shift, ("dp", "fsdp"), axis=0, tiled=True),
    )


def reduce_feed(norm_gain, norm_shift, w_up, up_shift, w_down, down_shift):
    return (
        lax.psum_scatter(norm_gain, ("dp", "fsdp"), scatter_dimension=0, tiled=True),
        lax.psum_scatter(norm_shift, ("dp", "fsdp"), scatter_dimension=0, tiled=True),
        lax.psum_scatter(w_up, ("dp", "fsdp"), scatter_dimension=0, tiled=True),
        lax.psum_scatter(up_shift, ("dp", "fsdp"), scatter_dimension=0, tiled=True),
        lax.psum_scatter(w_down, ("dp", "fsdp"), scatter_dimension=0, tiled=True),
        lax.psum_scatter(down_shift, ("dp", "fsdp"), scatter_dimension=0, tiled=True),
    )


def fetch_mixer(
    norm_gain, norm_shift, w_project, query_shift, value_shift, w_output, output_shift, table_rows
):
    return (
        lax.all_gather(norm_gain, ("dp", "fsdp"), axis=0, tiled=True),
        lax.all_gather(norm_shift, ("dp", "fsdp"), axis=0, tiled=True),
        lax.all_gather(w_project, ("dp", "fsdp"), axis=0, tiled=True),
        lax.all_gather(query_shift, ("dp", "fsdp"), axis=0, tiled=True),
        lax.all_gather(value_shift, ("dp", "fsdp"), axis=0, tiled=True),
        lax.all_gather(w_output, ("dp", "fsdp"), axis=0, tiled=True),
        lax.all_gather(output_shift, ("dp", "fsdp"), axis=0, tiled=True),
        lax.all_gather(table_rows, ("dp", "fsdp"), axis=0, tiled=True),
    )


def reduce_mixer(
    norm_gain, norm_shift, w_project, query_shift, value_shift, w_output, output_shift, table_rows
):
    return (
        lax.psum_scatter(norm_gain, ("dp", "fsdp"), scatter_dimension=0, tiled=True),
        lax.psum_scatter(norm_shift, ("dp", "fsdp"), scatter_dimension=0, tiled=True),
        lax.psum_scatter(w_project, ("dp", "fsdp"), scatter_dimension=0, tiled=True),
        lax.psum_scatter(query_shift, ("dp", "fsdp"), scatter_dimension=0, tiled=True),
        lax.psum_scatter(value_shift, ("dp", "fsdp"), scatter_dimension=0, tiled=True),
        lax.psum_scatter(w_output, ("dp", "fsdp"), scatter_dimension=0, tiled=True),
        lax.psum_scatter(output_shift, ("dp", "fsdp"), scatter_dimension=0, tiled=True),
        lax.psum_scatter(table_rows, ("dp", "fsdp"), scatter_dimension=0, tiled=True),
    )


def fetch_filter(
    norm_gain,
    norm_shift,
    w_up,
    up_shift,
    depth_taps,
    depth_shift,
    middle_gain,
    middle_shift,
    w_down,
    down_shift,
    last_gain,
    last_shift,
):
    return (
        lax.all_gather(norm_gain, ("dp", "fsdp"), axis=0, tiled=True),
        lax.all_gather(norm_shift, ("dp", "fsdp"), axis=0, tiled=True),
        lax.all_gather(w_up, ("dp", "fsdp"), axis=0, tiled=True),
        lax.all_gather(up_shift, ("dp", "fsdp"), axis=0, tiled=True),
        lax.all_gather(depth_taps, ("dp", "fsdp"), axis=0, tiled=True),
        lax.all_gather(depth_shift, ("dp", "fsdp"), axis=0, tiled=True),
        lax.all_gather(middle_gain, ("dp", "fsdp"), axis=0, tiled=True),
        lax.all_gather(middle_shift, ("dp", "fsdp"), axis=0, tiled=True),
        lax.all_gather(w_down, ("dp", "fsdp"), axis=0, tiled=True),
        lax.all_gather(down_shift, ("dp", "fsdp"), axis=0, tiled=True),
        lax.all_gather(last_gain, ("dp", "fsdp"), axis=0, tiled=True),
        lax.all_gather(last_shift, ("dp", "fsdp"), axis=0, tiled=True),
    )


def reduce_filter(
    norm_gain,
    norm_shift,
    w_up,
    up_shift,
    depth_taps,
    depth_shift,
    middle_gain,
    middle_shift,
    w_down,
    down_shift,
    last_gain,
    last_shift,
):
    return (
        lax.psum_scatter(norm_gain, ("dp", "fsdp"), scatter_dimension=0, tiled=True),
        lax.psum_scatter(norm_shift, ("dp", "fsdp"), scatter_dimension=0, tiled=True),
        lax.psum_scatter(w_up, ("dp", "fsdp"), scatter_dimension=0, tiled=True),
        lax.psum_scatter(up_shift, ("dp", "fsdp"), scatter_dimension=0, tiled=True),
        lax.psum_scatter(depth_taps, ("dp", "fsdp"), scatter_dimension=0, tiled=True),
        lax.psum_scatter(depth_shift, ("dp", "fsdp"), scatter_dimension=0, tiled=True),
        lax.psum_scatter(middle_gain, ("dp", "fsdp"), scatter_dimension=0, tiled=True),
        lax.psum_scatter(middle_shift, ("dp", "fsdp"), scatter_dimension=0, tiled=True),
        lax.psum_scatter(w_down, ("dp", "fsdp"), scatter_dimension=0, tiled=True),
        lax.psum_scatter(down_shift, ("dp", "fsdp"), scatter_dimension=0, tiled=True),
        lax.psum_scatter(last_gain, ("dp", "fsdp"), scatter_dimension=0, tiled=True),
        lax.psum_scatter(last_shift, ("dp", "fsdp"), scatter_dimension=0, tiled=True),
    )


def feed_forward(values, weights):
    normed, normed_unit, inverse = norm_apply(values, weights[0], weights[1])
    hidden = normed.astype(jnp.bfloat16)
    widened = flat_dot(hidden, weights[2]) + weights[3].astype(jnp.float32)
    active = (widened * jax.nn.sigmoid(widened)).astype(jnp.bfloat16)
    result = values + 0.5 * (flat_dot(active, weights[4]) + weights[5].astype(jnp.float32))
    return (result, (normed_unit, inverse, hidden, widened, active))


def feed_backward(upstream, saved, weights):
    normed_unit, inverse, hidden, widened, active = saved
    half_grad = 0.5 * upstream
    half_low = half_grad.astype(jnp.bfloat16)
    down_slope = lead_dot(active, half_low)
    widened_grad = swish_back(back_dot(half_low, weights[4]), widened)
    widened_low = widened_grad.astype(jnp.bfloat16)
    up_slope = lead_dot(hidden, widened_low)
    hidden_grad = back_dot(widened_low, weights[2])
    input_grad, gain_slope, shift_slope = norm_back(hidden_grad, normed_unit, inverse, weights[0])
    slopes = (
        gain_slope,
        shift_slope,
        up_slope,
        jnp.sum(widened_grad, axis=0),
        down_slope,
        jnp.sum(half_grad, axis=0),
    )
    return (upstream + input_grad, slopes)


def bucket_table(frame_count):
    offsets = jnp.arange(2 * frame_count - 1, dtype=jnp.int32) - (frame_count - 1)
    buckets = jnp.clip(offsets, -(NREL // 2), NREL // 2 - 1) + NREL // 2
    return (buckets[:, None] == jnp.arange(NREL, dtype=jnp.int32)[None, :]).astype(jnp.float32)


def relative_bias(table_rows, frame_count):
    diagonals = jnp.dot(
        bucket_table(frame_count),
        table_rows.astype(jnp.float32),
        precision=lax.Precision.HIGHEST,
        preferred_element_type=jnp.float32,
    )
    flipped = jnp.concatenate(
        [jnp.transpose(diagonals[::-1]), jnp.zeros((HEADS, 1), jnp.float32)], axis=1
    )
    spread = jnp.broadcast_to(flipped[:, None, :], (HEADS, frame_count, 2 * frame_count))
    spread = spread.reshape(HEADS, 2 * frame_count * frame_count)
    sheared = spread[:, : frame_count * (2 * frame_count - 1)].reshape(
        HEADS, frame_count, 2 * frame_count - 1
    )
    return sheared[:, :, frame_count - 1 :]


def relative_slope(score_grad, frame_count):
    placed = jnp.pad(score_grad, ((0, 0), (0, 0), (frame_count - 1, 0)))
    flattened = jnp.pad(
        placed.reshape(HEADS, frame_count * (2 * frame_count - 1)), ((0, 0), (0, frame_count))
    )
    columns = jnp.sum(flattened.reshape(HEADS, frame_count, 2 * frame_count), axis=1)
    diagonals = columns[:, 2 * frame_count - 2 :: -1]
    return lax.dot_general(
        bucket_table(frame_count),
        diagonals,
        (((0,), (1,)), ((), ())),
        precision=lax.Precision.HIGHEST,
        preferred_element_type=jnp.float32,
    )


def mixer_scores(query_rows, key_matrix_rows, relative, same_utterance):
    unnormalized_scores = jnp.einsum(
        "jug,fug->ujf", query_rows, key_matrix_rows, preferred_element_type=jnp.float32
    )
    return jnp.where(same_utterance[None], HEAD ** (-0.5) * unnormalized_scores + relative, MASKED)


def mixer_forward(values, segment_ids, weights):
    frame_count = values.shape[0]
    normed, normed_unit, inverse = norm_apply(values, weights[0], weights[1])
    hidden = normed.astype(jnp.bfloat16)
    projected = flat_dot(hidden, weights[2])
    query_rows = (projected[:, :D] + weights[3].astype(jnp.float32)).astype(jnp.bfloat16)
    query_rows = query_rows.reshape(frame_count, HEADS, HEAD)
    key_matrix_rows = projected[:, D : 2 * D].astype(jnp.bfloat16).reshape(frame_count, HEADS, HEAD)
    value_matrix_rows = (projected[:, 2 * D :] + weights[4].astype(jnp.float32)).astype(
        jnp.bfloat16
    )
    value_matrix_rows = value_matrix_rows.reshape(frame_count, HEADS, HEAD)
    relative = relative_bias(weights[7], frame_count)
    same_utterance = segment_ids[:, None] == segment_ids[None, :]
    scores = mixer_scores(query_rows, key_matrix_rows, relative, same_utterance)
    row_peak = jnp.max(scores, axis=-1, keepdims=True)
    powered = jnp.exp(scores - row_peak)
    row_total = jnp.sum(powered, axis=-1, keepdims=True)
    log_total = row_peak + jnp.log(row_total)
    softmax_rows = (powered / row_total).astype(jnp.bfloat16)
    attention_blend = jnp.einsum(
        "ief,fiv->eiv", softmax_rows, value_matrix_rows, preferred_element_type=jnp.float32
    )
    attention_blend = attention_blend.reshape(frame_count, D).astype(jnp.bfloat16)
    result = values + (flat_dot(attention_blend, weights[5]) + weights[6].astype(jnp.float32))
    return (
        result,
        (
            normed_unit,
            inverse,
            hidden,
            query_rows,
            key_matrix_rows,
            value_matrix_rows,
            log_total,
            attention_blend,
            relative,
            same_utterance,
        ),
    )


def mixer_backward(upstream, saved, weights):
    (
        normed_unit,
        inverse,
        hidden,
        query_rows,
        key_matrix_rows,
        value_matrix_rows,
        log_total,
        attention_blend,
        relative,
        same_utterance,
    ) = saved
    frame_count = upstream.shape[0]
    upstream_low = upstream.astype(jnp.bfloat16)
    output_slope = lead_dot(attention_blend, upstream_low)
    attention_blend_gradient = (
        back_dot(upstream_low, weights[5]).astype(jnp.bfloat16).reshape(frame_count, HEADS, HEAD)
    )
    scores = mixer_scores(query_rows, key_matrix_rows, relative, same_utterance)
    soft_full = jnp.exp(scores - log_total)
    value_grad = jnp.einsum(
        "ybr,byq->ryq",
        soft_full.astype(jnp.bfloat16),
        attention_blend_gradient,
        preferred_element_type=jnp.float32,
    ).reshape(frame_count, D)
    soft_grad = jnp.einsum(
        "jug,fug->ujf",
        attention_blend_gradient,
        value_matrix_rows,
        preferred_element_type=jnp.float32,
    )
    score_grad = soft_full * (soft_grad - jnp.sum(soft_full * soft_grad, axis=-1, keepdims=True))
    table_slope = relative_slope(score_grad, frame_count)
    score_reduced_precision = (HEAD ** (-0.5) * score_grad).astype(jnp.bfloat16)
    query_grad = jnp.einsum(
        "ief,fiv->eiv", score_reduced_precision, key_matrix_rows, preferred_element_type=jnp.float32
    ).reshape(frame_count, D)
    key_grad = jnp.einsum(
        "ybr,byq->ryq", score_reduced_precision, query_rows, preferred_element_type=jnp.float32
    ).reshape(frame_count, D)
    projected_low = jnp.concatenate([query_grad, key_grad, value_grad], axis=1).astype(jnp.bfloat16)
    project_slope = lead_dot(hidden, projected_low)
    hidden_grad = back_dot(projected_low, weights[2])
    input_grad, gain_slope, shift_slope = norm_back(hidden_grad, normed_unit, inverse, weights[0])
    slopes = (
        gain_slope,
        shift_slope,
        project_slope,
        jnp.sum(query_grad, axis=0),
        jnp.sum(value_grad, axis=0),
        output_slope,
        jnp.sum(upstream, axis=0),
        table_slope,
    )
    return (upstream + input_grad, slopes)


def filter_forward(values, segment_ids, weights):
    normed, normed_unit, inverse = norm_apply(values, weights[0], weights[1])
    hidden = normed.astype(jnp.bfloat16)
    widened = flat_dot(hidden, weights[2]) + weights[3].astype(jnp.float32)
    gated_rows = widened[:, :D] * jax.nn.sigmoid(widened[:, D:])
    filtered = depthwise(gated_rows, weights[4].astype(jnp.float32), segment_ids) + weights[
        5
    ].astype(jnp.float32)
    middle, middle_unit, middle_inverse = norm_apply(filtered, weights[6], weights[7])
    swished = (middle * jax.nn.sigmoid(middle)).astype(jnp.bfloat16)
    result = values + (flat_dot(swished, weights[8]) + weights[9].astype(jnp.float32))
    return (
        result,
        (
            normed_unit,
            inverse,
            hidden,
            widened,
            gated_rows,
            middle_unit,
            middle_inverse,
            middle,
            swished,
        ),
    )


def filter_backward(upstream, saved, weights, segment_ids):
    (
        normed_unit,
        inverse,
        hidden,
        widened,
        gated_rows,
        middle_unit,
        middle_inverse,
        middle,
        swished,
    ) = saved
    upstream_low = upstream.astype(jnp.bfloat16)
    down_slope = lead_dot(swished, upstream_low)
    middle_grad = swish_back(back_dot(upstream_low, weights[8]), middle)
    filtered_grad, middle_gain_slope, middle_shift_slope = norm_back(
        middle_grad, middle_unit, middle_inverse, weights[6]
    )

    def local_filter(local_rows, local_kernel):
        return depthwise(local_rows, local_kernel, segment_ids)

    unused, pullback = jax.vjp(local_filter, gated_rows, weights[4].astype(jnp.float32))
    gated_grad, kernel_slope = pullback(filtered_grad)
    opened = jax.nn.sigmoid(widened[:, D:])
    widened_grad = jnp.concatenate(
        [gated_grad * opened, gated_grad * widened[:, :D] * opened * (1.0 - opened)], axis=1
    )
    widened_low = widened_grad.astype(jnp.bfloat16)
    up_slope = lead_dot(hidden, widened_low)
    hidden_grad = back_dot(widened_low, weights[2])
    input_grad, gain_slope, shift_slope = norm_back(hidden_grad, normed_unit, inverse, weights[0])
    slopes = (
        gain_slope,
        shift_slope,
        up_slope,
        jnp.sum(widened_grad, axis=0),
        kernel_slope,
        jnp.sum(filtered_grad, axis=0),
        middle_gain_slope,
        middle_shift_slope,
        down_slope,
        jnp.sum(upstream, axis=0),
    )
    return (upstream + input_grad, slopes)


def body(
    frames,
    segments,
    cotangent,
    early_gain,
    early_shift,
    early_up,
    early_lift,
    early_down,
    early_drop,
    mixer_gain,
    mixer_shift,
    mixer_project,
    query_bias,
    value_bias,
    mixer_output,
    mixer_drop,
    distance_table,
    filter_gain,
    filter_shift,
    filter_up,
    filter_lift,
    depth_weight,
    depth_bias,
    middle_gain,
    middle_shift,
    filter_down,
    filter_drop,
    late_gain,
    late_shift,
    late_up,
    late_lift,
    late_down,
    late_drop,
    final_gain,
    final_shift,
):
    start_rows = frames.astype(jnp.float32)
    final_upstream = cotangent.astype(jnp.float32)
    early_full = fetch_feed(early_gain, early_shift, early_up, early_lift, early_down, early_drop)
    first_rows, early_kept = feed_forward(start_rows, early_full)
    mixer_full = fetch_mixer(
        mixer_gain,
        mixer_shift,
        mixer_project,
        query_bias,
        value_bias,
        mixer_output,
        mixer_drop,
        distance_table,
    )
    second_rows, mixer_kept = mixer_forward(first_rows, segments, mixer_full)
    filter_full = fetch_filter(
        filter_gain,
        filter_shift,
        filter_up,
        filter_lift,
        depth_weight,
        depth_bias,
        middle_gain,
        middle_shift,
        filter_down,
        filter_drop,
        final_gain,
        final_shift,
    )
    third_rows, filter_kept = filter_forward(second_rows, segments, filter_full)
    late_full = fetch_feed(late_gain, late_shift, late_up, late_lift, late_down, late_drop)
    fourth_rows, late_kept = feed_forward(third_rows, late_full)
    layer_out, final_unit, final_inverse = norm_apply(fourth_rows, filter_full[10], filter_full[11])
    final_stats = (final_unit, final_inverse)
    upstream, final_gain_slope, final_shift_slope = norm_back(
        final_upstream, final_stats[0], final_stats[1], filter_full[10]
    )
    upstream, late_slopes = feed_backward(upstream, late_kept, late_full)
    late_summed = reduce_feed(
        late_slopes[0],
        late_slopes[1],
        late_slopes[2],
        late_slopes[3],
        late_slopes[4],
        late_slopes[5],
    )
    upstream, filter_grads = filter_backward(upstream, filter_kept, filter_full, segments)
    filter_summed = reduce_filter(
        filter_grads[0],
        filter_grads[1],
        filter_grads[2],
        filter_grads[3],
        filter_grads[4],
        filter_grads[5],
        filter_grads[6],
        filter_grads[7],
        filter_grads[8],
        filter_grads[9],
        final_gain_slope,
        final_shift_slope,
    )
    upstream, mixer_grads = mixer_backward(upstream, mixer_kept, mixer_full)
    mixer_summed = reduce_mixer(
        mixer_grads[0],
        mixer_grads[1],
        mixer_grads[2],
        mixer_grads[3],
        mixer_grads[4],
        mixer_grads[5],
        mixer_grads[6],
        mixer_grads[7],
    )
    upstream, early_slopes = feed_backward(upstream, early_kept, early_full)
    early_summed = reduce_feed(
        early_slopes[0],
        early_slopes[1],
        early_slopes[2],
        early_slopes[3],
        early_slopes[4],
        early_slopes[5],
    )
    return (
        layer_out,
        upstream,
        early_summed[0],
        early_summed[1],
        early_summed[2],
        early_summed[3],
        early_summed[4],
        early_summed[5],
        mixer_summed[0],
        mixer_summed[1],
        mixer_summed[2],
        mixer_summed[3],
        mixer_summed[4],
        mixer_summed[5],
        mixer_summed[6],
        mixer_summed[7],
        filter_summed[0],
        filter_summed[1],
        filter_summed[2],
        filter_summed[3],
        filter_summed[4],
        filter_summed[5],
        filter_summed[6],
        filter_summed[7],
        filter_summed[8],
        filter_summed[9],
        late_summed[0],
        late_summed[1],
        late_summed[2],
        late_summed[3],
        late_summed[4],
        late_summed[5],
        filter_summed[10],
        filter_summed[11],
    )


def near(me, n):
    if n == 4:
        row, column = me // 2, me % 2
        flip_row, flip_column = (1 - row) * 2 + column, row * 2 + 1 - column
        across = (1 - row) * 2 + 1 - column
        return [(flip_column, flip_column), (flip_row, flip_row), (across, across)]
    return [((me + step) % n, (me + n - step) % n) for step in range(1, n)]


def greet(targets):
    barrier = pltpu.get_barrier_semaphore()
    for target in targets:
        pl.semaphore_signal(barrier, inc=1, device_id={"dp": target}, device_id_type=MESH)
    pl.semaphore_wait(barrier, len(targets))


def greet_all(n, m):
    me, lane = lax.axis_index("dp"), lax.axis_index("fsdp")
    barrier = pltpu.get_barrier_semaphore()

    def say(step, carry):
        target = {"dp": (me + step // m) % n, "fsdp": (lane + step % m) % m}
        pl.semaphore_signal(barrier, inc=1, device_id=target, device_id_type=MESH)
        return carry

    lax.fori_loop(1, n * m, say, 0)
    pl.semaphore_wait(barrier, n * m - 1)


def remote(src, dst, send, recv, target):
    return pltpu.make_async_remote_copy(
        src_ref=src, dst_ref=dst, send_sem=send, recv_sem=recv, device_id=target, device_id_type=MESH
    )


def columns(start, width):
    return pl.ds(pl.multiple_of(start * width, width), width)


def column_pieces(index, n, sizes):
    pieces = []
    for place, (groups, width) in enumerate(sizes):
        for group in range(groups):
            wide = pl.ds(pl.multiple_of((group * n + index) * width, width), width)
            pieces.append((place, wide, pl.ds(group * width, width)))
    return pieces


def row_of(shards, first):
    rows = shards.shape[0]
    lines = shards[:, 0, :]
    lanes = lax.broadcasted_iota(jnp.int32, lines.shape, 1) // 32
    places = lax.broadcasted_iota(jnp.int32, lines.shape, 0) % 4
    merged = jnp.zeros_like(lines)
    for quarter in range(4):
        shift = (32 * quarter - 32 * first) % LANES
        moved = pltpu.roll(lines, shift, 1) if shift else lines
        merged = merged + jnp.where((lanes == quarter) & (places == quarter), moved, 0.0)
    return [
        jnp.sum(merged[4 * tile : 4 * tile + 4], axis=0, keepdims=True) for tile in range(rows // 4)
    ]


def pack_small(small, singles, lifts, table):
    rows = singles[0].shape[0]
    small[...] = jnp.zeros_like(small)
    for at, single in enumerate(singles):
        line, low = at * rows // LANES, at * rows % LANES
        small[line : line + 1, low : low + rows] = single[...].astype(jnp.float32).reshape(1, rows)
    for at, lift in enumerate(lifts):
        line, count = 5 + at, lift.shape[0]
        small[line : line + 1, 0:count] = lift[...].astype(jnp.float32).reshape(1, count)
    small[8 : 8 + table.shape[0], 0 : table.shape[1]] = table[...].astype(jnp.float32)


def exchange_kernel(n, m, width, inner, *refs):
    early_up, late_up, project, filter_up, output, filter_down, depth, segs, frames = refs[:9]
    singles, lifts, table = refs[9:28], refs[28:31], refs[31]
    early_full, late_split, mixer_split, filter_split, small_all, depth_all, segs_all, spread = refs[32:40]
    scratch = refs[40:]
    small, gains, held, local, send, recv, small_send, small_recv = scratch[:8]
    up_send, up_recv, pass_send, pass_recv, out_send, out_recv, depth_send, depth_recv = scratch[8:]
    pack_small(small, singles, lifts, table)
    me, lane = lax.axis_index("dp"), lax.axis_index("fsdp")
    here = me * m + lane
    half = m // 2
    beside = lane + 1 - 2 * (lane % 2)
    others = near(me, n)
    greet_all(n, m)

    def to_device(step):
        target = {"dp": (me + step // m) % n, "fsdp": (lane + step % m) % m}
        return remote(small, small_all.at[here], small_send.at[step], small_recv.at[step], target)

    def to_lane(step):
        return remote(
            depth, depth_all.at[lane], depth_send.at[step], depth_recv.at[step], {"fsdp": (lane + step) % m}
        )

    def start_depth(step, carry):
        to_lane(step).start()
        return carry

    def wait_depth(step, carry):
        to_lane(step).wait()
        return carry

    def to_column(step):
        other, above = (me + step // half) % n, (lane + 2 * (step % half)) % m
        target = {"dp": other, "fsdp": above}
        return remote(
            early_up.at[:, columns(other, width)], early_full.at[here], up_send.at[step], up_recv.at[step], target
        )

    def to_partner(step):
        source = ((me + n - step // half) % n) * m + (lane + m - 2 * (step % half)) % m
        return remote(
            early_full.at[source], early_full.at[source], pass_send.at[step], pass_recv.at[step], {"fsdp": beside}
        )

    def start_small(step, carry):
        to_device(step).start()
        return carry

    def wait_small(step, carry):
        to_device(step).wait()
        return carry

    def start_column(step, carry):
        to_column(step).start()
        return carry

    def relay_column(step, carry):
        to_column(step).wait_recv()
        to_partner(step).start()
        return carry

    def wait_column(step, carry):
        to_column(step).wait_send()
        to_partner(step).wait()
        return carry

    def pieces(index):
        found = [(late_up.at[:, columns(index, width)], late_split.at[me])]
        for group in range(3):
            wide = pl.ds(pl.multiple_of(group * inner * n + index * inner, inner), inner)
            found.append((project.at[:, wide], mixer_split.at[me, :, pl.ds(group * inner, inner)]))
        for group in range(2):
            wide = pl.ds(pl.multiple_of(group * inner * n + index * inner, inner), inner)
            found.append((filter_up.at[:, wide], filter_split.at[me, :, pl.ds(group * inner, inner)]))
        found.append((segs, segs_all.at[me]))
        return found

    lax.fori_loop(1, n * m, start_small, 0)
    own_small = pltpu.make_async_copy(small, small_all.at[here], local.at[0])
    own_small.start()
    own_up = pltpu.make_async_copy(early_up.at[:, columns(me, width)], early_full.at[here], local.at[1])
    own_up.start()
    lax.fori_loop(1, n * half, start_column, 0)
    copies = []
    for peer, (target, unused) in enumerate(others):
        for at, (src, dst) in enumerate(pieces(target)):
            copies.append(remote(src, dst, send.at[peer, at], recv.at[peer, at], {"dp": target}))
    owns = []
    for src, dst in pieces(me):
        owns.append((src, dst))
    for group in range(n):
        wide = pl.ds(group * inner, inner)
        owns.append((output.at[:, wide], mixer_split.at[group, :, pl.ds(3 * inner, inner)]))
        owns.append((filter_down.at[:, wide], filter_split.at[group, :, pl.ds(2 * inner, inner)]))
    owns = [pltpu.make_async_copy(src, dst, local.at[2 + at]) for at, (src, dst) in enumerate(owns)]
    owns.append(pltpu.make_async_copy(depth, depth_all.at[lane], local.at[2 + len(owns)]))
    for copy in copies + owns:
        copy.start()
    lax.fori_loop(1, m, start_depth, 0)
    own_up.wait()
    to_partner(0).start()
    own_small.wait()
    lax.fori_loop(1, n * m, wait_small, 0)
    for index in range(2):
        for tile, line in enumerate(row_of(small_all, index)):
            gains[pl.ds(index, 1), pl.ds(tile * LANES, LANES)] = line
    gain, shift = gains[0:1, :], gains[1:2, :]

    def work(block, carry):
        span = pl.ds(pl.multiple_of(block * BLOCK, BLOCK), BLOCK)
        unit, inverse = unit_of(frames[span, :].astype(jnp.float32))
        held[span, :] = (unit * gain + shift).astype(jnp.bfloat16)
        return carry

    lax.fori_loop(0, frames.shape[0] // BLOCK, work, 0)
    keep = pltpu.make_async_copy(held, spread.at[me], local.at[len(owns) + 2])
    keep.start()
    outgoing = []
    for peer, (target, unused) in enumerate(others):
        outgoing.append(remote(held, spread.at[me], out_send.at[peer], out_recv.at[peer], {"dp": target}))
    for copy in outgoing:
        copy.start()
    lax.fori_loop(1, n * half, relay_column, 0)
    for copy in owns + copies + outgoing:
        copy.wait()
    keep.wait()
    to_partner(0).wait()
    lax.fori_loop(1, n * half, wait_column, 0)
    lax.fori_loop(1, m, wait_depth, 0)


def exchange(n, m, early_up, late_up, project, filter_up, output, filter_down, depth, segs, frames, singles, lifts, table):
    rows, width = early_up.shape[0], early_up.shape[1] // n
    inner = output.shape[1] // n
    frame_count, deep = frames.shape
    low = jnp.bfloat16
    packed = (16, LANES)
    outs = [
        jax.ShapeDtypeStruct((n * m, rows, width), low),
        jax.ShapeDtypeStruct((n, rows, width), low),
        jax.ShapeDtypeStruct((n, rows, 4 * inner), low),
        jax.ShapeDtypeStruct((n, rows, 3 * inner), low),
        jax.ShapeDtypeStruct((n * m,) + packed, jnp.float32),
        jax.ShapeDtypeStruct((m,) + depth.shape, low),
        jax.ShapeDtypeStruct((n,) + segs.shape, segs.dtype),
        jax.ShapeDtypeStruct((n, frame_count, deep), low),
    ]
    anywhere = pl.BlockSpec(memory_space=pl.ANY)
    inside = pl.BlockSpec(memory_space=pltpu.VMEM)
    dma = pltpu.SemaphoreType.DMA
    return pl.pallas_call(
        functools.partial(exchange_kernel, n, m, width, inner),
        out_shape=outs,
        in_specs=[anywhere] * 8 + [inside] * (2 + len(singles) + len(lifts)),
        out_specs=[anywhere] * 4 + [inside] + [anywhere] * 3,
        scratch_shapes=[
            pltpu.VMEM(packed, jnp.float32),
            pltpu.VMEM((2, deep), jnp.float32),
            pltpu.VMEM((frame_count, deep), low),
            dma((2 * n + 8 + 3,)),
            dma((n - 1, 7)),
            dma((n - 1, 7)),
            dma((n * m,)),
            dma((n * m,)),
            dma((n * m // 2,)),
            dma((n * m // 2,)),
            dma((n * m // 2,)),
            dma((n * m // 2,)),
            dma((n - 1,)),
            dma((n - 1,)),
            dma((m,)),
            dma((m,)),
        ],
        compiler_params=pltpu.CompilerParams(collective_id=0, has_side_effects=True),
        name="exchange",
    )(early_up, late_up, project, filter_up, output, filter_down, depth, segs, frames, *singles, *lifts, table)


def giveback_kernel(n, sizes, *refs):
    count = len(sizes)
    narrows, wides = refs[:count], refs[count : 2 * count]
    local, send, recv = refs[2 * count :]
    me = lax.axis_index("dp")
    others = near(me, n)
    greet([target for target, unused in others])
    copies = []
    for peer, (target, unused) in enumerate(others):
        for at, (place, wide, narrow) in enumerate(column_pieces(me, n, sizes)):
            copies.append(
                remote(narrows[place].at[target, :, narrow], wides[place].at[:, wide], send.at[peer, at], recv.at[peer, at], {"dp": target})
            )
    for at, (place, wide, narrow) in enumerate(column_pieces(me, n, sizes)):
        copies.append(pltpu.make_async_copy(narrows[place].at[me, :, narrow], wides[place].at[:, wide], local.at[at]))
    for copy in copies:
        copy.start()
    for copy in copies:
        copy.wait()


def giveback(n, narrows, sizes, number):
    rows = narrows[0].shape[1]
    total = sum(groups for groups, width in sizes)
    outs = [jax.ShapeDtypeStruct((rows, groups * width * n), jnp.bfloat16) for groups, width in sizes]
    anywhere = pl.BlockSpec(memory_space=pl.ANY)
    return pl.pallas_call(
        functools.partial(giveback_kernel, n, sizes),
        out_shape=outs,
        in_specs=[anywhere] * len(narrows),
        out_specs=[anywhere] * len(outs),
        scratch_shapes=[
            pltpu.SemaphoreType.DMA((total,)),
            pltpu.SemaphoreType.DMA((n - 1, total)),
            pltpu.SemaphoreType.DMA((n - 1, total)),
        ],
        compiler_params=pltpu.CompilerParams(collective_id=number, has_side_effects=True),
        name="giveback",
    )(*narrows)


def share_kernel(n, mine, shared, local, send, recv):
    me = lax.axis_index("dp")
    others = near(me, n)
    greet([target for target, unused in others])
    copies = [pltpu.make_async_copy(mine, shared.at[me], local)]
    for peer, (target, unused) in enumerate(others):
        copies.append(remote(mine, shared.at[me], send.at[peer], recv.at[peer], {"dp": target}))
    for copy in copies:
        copy.start()
    for copy in copies:
        copy.wait()


def share(n, mine, number):
    inside = pl.BlockSpec(memory_space=pltpu.VMEM)
    return pl.pallas_call(
        functools.partial(share_kernel, n),
        out_shape=jax.ShapeDtypeStruct((n,) + mine.shape, mine.dtype),
        in_specs=[inside],
        out_specs=inside,
        scratch_shapes=[
            pltpu.SemaphoreType.DMA,
            pltpu.SemaphoreType.DMA((n - 1,)),
            pltpu.SemaphoreType.DMA((n - 1,)),
        ],
        compiler_params=pltpu.CompilerParams(collective_id=number, has_side_effects=True),
        name="share",
    )(mine)


def collect_kernel(n, m, wide, group, wide_all, group_all, local, send, recv, group_send, group_recv):
    me, lane = lax.axis_index("dp"), lax.axis_index("fsdp")
    here = me * m + lane
    greet_all(n, m)

    def to_device(step):
        other, beside = (me + step // m) % n, (lane + step % m) % m
        return remote(
            wide.at[other * m + beside], wide_all.at[here], send.at[step], recv.at[step], {"dp": other, "fsdp": beside}
        )

    def to_group(step):
        beside = (lane + step) % m
        return remote(group.at[beside], group_all.at[lane], group_send.at[step], group_recv.at[step], {"fsdp": beside})

    def start_wide(step, carry):
        to_device(step).start()
        return carry

    def start_group(step, carry):
        to_group(step).start()
        return carry

    def wait_wide(step, carry):
        to_device(step).wait()
        return carry

    def wait_group(step, carry):
        to_group(step).wait()
        return carry

    own = pltpu.make_async_copy(wide.at[here], wide_all.at[here], local.at[0])
    own_group = pltpu.make_async_copy(group.at[lane], group_all.at[lane], local.at[1])
    own.start()
    own_group.start()
    lax.fori_loop(1, n * m, start_wide, 0)
    lax.fori_loop(1, m, start_group, 0)
    own.wait()
    own_group.wait()
    lax.fori_loop(1, n * m, wait_wide, 0)
    lax.fori_loop(1, m, wait_group, 0)


def collect(n, m, wide, group, number):
    inside = pl.BlockSpec(memory_space=pltpu.VMEM)
    return pl.pallas_call(
        functools.partial(collect_kernel, n, m),
        out_shape=[jax.ShapeDtypeStruct(wide.shape, wide.dtype), jax.ShapeDtypeStruct(group.shape, group.dtype)],
        in_specs=[inside] * 2,
        out_specs=[inside] * 2,
        scratch_shapes=[
            pltpu.SemaphoreType.DMA((2,)),
            pltpu.SemaphoreType.DMA((n * m,)),
            pltpu.SemaphoreType.DMA((n * m,)),
            pltpu.SemaphoreType.DMA((m,)),
            pltpu.SemaphoreType.DMA((m,)),
        ],
        compiler_params=pltpu.CompilerParams(collective_id=number, has_side_effects=True),
        name="collect",
    )(wide, group)


def unit_of(values):
    centered = values - jnp.mean(values, axis=-1, keepdims=True)
    inverse = lax.rsqrt(jnp.mean(centered * centered, axis=-1, keepdims=True) + EPSILON)
    return centered * inverse, inverse


def unit_back(upstream, unit, inverse, gain):
    scaled = upstream * gain
    adjusted = scaled - jnp.mean(scaled, axis=-1, keepdims=True)
    return inverse * (adjusted - unit * jnp.mean(scaled * unit, axis=-1, keepdims=True))


def step_forward(scale, total, states, vectors):
    values = states[0] + scale * (total + vectors[0])
    unit, inverse = unit_of(values)
    return [values], unit * vectors[1] + vectors[2], []


def step_turn(total, states, vectors):
    values = states[0] + 0.5 * (total + vectors[0])
    upstream = states[1]
    unit, inverse = unit_of(values)
    layer_out = unit * vectors[1] + vectors[2]
    grad = unit_back(upstream, unit, inverse, vectors[1])
    half = 0.5 * grad
    return [layer_out, grad], half, [upstream * unit, upstream, half]


def step_backward(scale, total, states, vectors):
    unit, inverse = unit_of(states[1])
    grad = states[0] + unit_back(total, unit, inverse, vectors[0])
    sent = scale * grad
    return [grad], sent, [total * unit, total, sent]


def step_last(total, states, vectors):
    unit, inverse = unit_of(states[1])
    grad = states[0] + unit_back(total, unit, inverse, vectors[0])
    return [grad], None, [total * unit, total]


def boundary_kernel(n, step, shape, *refs):
    summed, gathered, state_count, out_count, sum_count, vector_count = shape
    refs = list(refs)
    take = lambda count: [refs.pop(0) for unused in range(count)]
    part = take(1)[0] if summed else None
    states = take(state_count)
    vectors = take(1)[0]
    outs = take(out_count)
    spread = take(1)[0] if gathered else None
    sums = take(1)[0] if sum_count else None
    if summed:
        arrived, own, own_sem, send, recv = take(5)
    if gathered:
        held, held_sem, out_send, out_recv = take(4)
    partials = take(1)[0] if sum_count else None
    me = lax.axis_index("dp")
    others = near(me, n)
    rows = states[0].shape[0]
    height = rows // PIECES
    greet([target for target, unused in others])
    incoming = {}
    if summed:
        own_copy = pltpu.make_async_copy(part.at[me], own, own_sem)
        for piece in range(PIECES):
            span = pl.ds(piece * height, height)
            for peer, (target, unused) in enumerate(others):
                copy = remote(
                    part.at[target, span], arrived.at[peer, span], send.at[peer, piece], recv.at[peer, piece], {"dp": target}
                )
                copy.start()
                incoming[peer, piece] = copy
        own_copy.start()
        own_copy.wait()
    if sum_count:
        partials[...] = jnp.zeros_like(partials)
    outgoing = []
    rows_of = [vectors[pl.ds(index, 1), :] for index in range(vector_count)]
    for piece in range(PIECES):
        if summed:
            for peer in range(n - 1):
                incoming[peer, piece].wait_recv()

        def work(block, carry):
            span = pl.ds(pl.multiple_of(piece * height + block * BLOCK, BLOCK), BLOCK)
            total = None
            if summed:
                total = own[span, :].astype(jnp.float32)
                for peer in range(n - 1):
                    total = total + arrived[peer, span, :].astype(jnp.float32)
            made, sent, terms = step(total, [state[span, :] for state in states], rows_of)
            for out, value in zip(outs, made):
                out[span, :] = value
            if gathered:
                held[span, :] = sent.astype(jnp.bfloat16)
            for index, term in enumerate(terms):
                partials[index] += sum(term[8 * low : 8 * low + 8] for low in range(BLOCK // 8))
            return carry

        lax.fori_loop(0, height // BLOCK, work, 0)
        if gathered:
            span = pl.ds(piece * height, height)
            for peer, (target, unused) in enumerate(others):
                copy = remote(
                    held.at[span], spread.at[me, span], out_send.at[peer, piece], out_recv.at[peer, piece], {"dp": target}
                )
                copy.start()
                outgoing.append(copy)
    if gathered:
        keep = pltpu.make_async_copy(held, spread.at[me], held_sem)
        keep.start()
    for index in range(sum_count):
        sums[pl.ds(index, 1), :] = jnp.sum(partials[index], axis=0, keepdims=True)
    for copy in incoming.values():
        copy.wait_send()
    for copy in outgoing:
        copy.wait()
    if gathered:
        keep.wait()


def boundary(n, step, part, states, vectors, out_count, sum_count, number, gathered=True):
    rows, width = states[0].shape
    summed = part is not None
    inside = pl.BlockSpec(memory_space=pltpu.VMEM)
    anywhere = pl.BlockSpec(memory_space=pl.ANY)
    shape = (summed, gathered, len(states), out_count, sum_count, len(vectors))
    operands, in_specs, outs, out_specs, scratch = [], [], [], [], []
    if summed:
        operands.append(part)
        in_specs.append(anywhere)
        scratch += [
            pltpu.VMEM((n - 1, rows, width), jnp.bfloat16),
            pltpu.VMEM((rows, width), jnp.bfloat16),
            pltpu.SemaphoreType.DMA,
            pltpu.SemaphoreType.DMA((n - 1, PIECES)),
            pltpu.SemaphoreType.DMA((n - 1, PIECES)),
        ]
    operands += list(states) + [jnp.stack(vectors)]
    in_specs += [inside] * (len(states) + 1)
    outs += [jax.ShapeDtypeStruct((rows, width), jnp.float32)] * out_count
    out_specs += [inside] * out_count
    if gathered:
        outs.append(jax.ShapeDtypeStruct((n, rows, width), jnp.bfloat16))
        out_specs.append(anywhere)
        scratch += [
            pltpu.VMEM((rows, width), jnp.bfloat16),
            pltpu.SemaphoreType.DMA,
            pltpu.SemaphoreType.DMA((n - 1, PIECES)),
            pltpu.SemaphoreType.DMA((n - 1, PIECES)),
        ]
    if sum_count:
        outs.append(jax.ShapeDtypeStruct((sum_count, width), jnp.float32))
        out_specs.append(inside)
        scratch.append(pltpu.VMEM((sum_count, 8, width), jnp.float32))
    return pl.pallas_call(
        functools.partial(boundary_kernel, n, step, shape),
        out_shape=outs,
        in_specs=in_specs,
        out_specs=out_specs,
        scratch_shapes=scratch,
        compiler_params=pltpu.CompilerParams(collective_id=number, has_side_effects=True),
        name="boundary",
    )(*operands)


def toeplitz(line, frame_count):
    wide = jnp.broadcast_to(line, (frame_count, NREL))
    return pltpu.roll(wide, NREL - frame_count + 1, 1, stride=1, stride_axis=0)[:, :frame_count]


def head_scores(packed, head, heads, same, bias):
    size = heads * HEAD
    query_rows = packed[:, head * HEAD : (head + 1) * HEAD]
    key_rows = packed[:, size + head * HEAD : size + (head + 1) * HEAD]
    value_rows = packed[:, 2 * size + head * HEAD : 2 * size + (head + 1) * HEAD]
    scores = jnp.where(same, HEAD ** (-0.5) * back_dot(query_rows, key_rows) + bias, MASKED)
    powered = jnp.exp(scores - jnp.max(scores, axis=-1, keepdims=True))
    soft = powered / jnp.sum(powered, axis=-1, keepdims=True)
    return query_rows, key_rows, value_rows, soft


def attend_kernel(heads, packed, segment_rows, segment_columns, table, blended, bias):
    frame_count = packed.shape[1]

    @pl.when(pl.program_id(0) == 0)
    def _():
        for head in range(heads):
            bias[head] = toeplitz(table[pl.ds(head, 1), :], frame_count)

    same = segment_columns[0] == segment_rows[0]
    block = packed[0]
    results = []
    for head in range(heads):
        unused, unused_too, value_rows, soft = head_scores(block, head, heads, same, bias[head])
        results.append(flat_dot(soft.astype(jnp.bfloat16), value_rows).astype(jnp.bfloat16))
    blended[0] = jnp.concatenate(results, axis=1)


def attend(packed, segment_rows, segment_columns, table):
    blocks, frame_count, width = packed.shape
    heads = table.shape[0]
    return pl.pallas_call(
        functools.partial(attend_kernel, heads),
        grid=(blocks,),
        out_shape=jax.ShapeDtypeStruct((blocks, frame_count, width // 3), jnp.bfloat16),
        in_specs=[
            pl.BlockSpec((1, frame_count, width), lambda i: (i, 0, 0)),
            pl.BlockSpec((1, 1, frame_count), lambda i: (i, 0, 0)),
            pl.BlockSpec((1, frame_count, 1), lambda i: (i, 0, 0)),
            pl.BlockSpec((heads, NREL), lambda i: (0, 0)),
        ],
        out_specs=pl.BlockSpec((1, frame_count, width // 3), lambda i: (i, 0, 0)),
        scratch_shapes=[pltpu.VMEM((heads, frame_count, frame_count), jnp.float32)],
        name="attend",
    )(packed, segment_rows, segment_columns, table)


def unattend_kernel(heads, packed, upstream, segment_rows, segment_columns, table, grads, sums, slope, bias, gathered):
    frame_count = packed.shape[1]
    size = heads * HEAD
    at = pl.program_id(0)

    @pl.when(at == 0)
    def _():
        for head in range(heads):
            bias[head] = toeplitz(table[pl.ds(head, 1), :], frame_count)
        gathered[...] = jnp.zeros_like(gathered)
        sums[...] = jnp.zeros_like(sums)

    same = segment_columns[0] == segment_rows[0]
    block = packed[0]
    above = upstream[0]
    query_grads, key_grads, value_grads = [], [], []
    for head in range(heads):
        query_rows, key_rows, value_rows, soft = head_scores(block, head, heads, same, bias[head])
        blend_grad = above[:, head * HEAD : (head + 1) * HEAD]
        value_grads.append(lead_dot(soft.astype(jnp.bfloat16), blend_grad))
        soft_grad = back_dot(blend_grad, value_rows)
        score_grad = soft * (soft_grad - jnp.sum(soft * soft_grad, axis=-1, keepdims=True))
        gathered[head] += score_grad
        low = (HEAD ** (-0.5) * score_grad).astype(jnp.bfloat16)
        query_grads.append(flat_dot(low, key_rows))
        key_grads.append(lead_dot(low, query_rows))
    query_grad = jnp.concatenate(query_grads, axis=1)
    value_grad = jnp.concatenate(value_grads, axis=1)
    grads[0, :, 0:size] = query_grad.astype(jnp.bfloat16)
    grads[0, :, size : 2 * size] = jnp.concatenate(key_grads, axis=1).astype(jnp.bfloat16)
    grads[0, :, 2 * size :] = value_grad.astype(jnp.bfloat16)
    sums[0:1, :] += jnp.sum(query_grad, axis=0, keepdims=True)
    sums[1:2, :] += jnp.sum(value_grad, axis=0, keepdims=True)

    @pl.when(at == pl.num_programs(0) - 1)
    def _():
        places = lax.broadcasted_iota(jnp.int32, (frame_count, NREL), 0)
        for head in range(heads):
            wide = jnp.concatenate(
                [gathered[head], jnp.zeros((frame_count, NREL - frame_count), jnp.float32)], axis=1
            )
            stride = 1
            while stride < frame_count:
                moved = pltpu.roll(wide, NREL - stride, 1)
                wide = jnp.where((places // stride) % 2 == 1, moved, wide)
                stride *= 2
            slope[pl.ds(head, 1), :] = jnp.sum(wide, axis=0, keepdims=True)


def unattend(packed, upstream, segment_rows, segment_columns, table):
    blocks, frame_count, width = packed.shape
    heads = table.shape[0]
    return pl.pallas_call(
        functools.partial(unattend_kernel, heads),
        grid=(blocks,),
        out_shape=[
            jax.ShapeDtypeStruct((blocks, frame_count, width), jnp.bfloat16),
            jax.ShapeDtypeStruct((2, width // 3), jnp.float32),
            jax.ShapeDtypeStruct((heads, NREL), jnp.float32),
        ],
        in_specs=[
            pl.BlockSpec((1, frame_count, width), lambda i: (i, 0, 0)),
            pl.BlockSpec((1, frame_count, width // 3), lambda i: (i, 0, 0)),
            pl.BlockSpec((1, 1, frame_count), lambda i: (i, 0, 0)),
            pl.BlockSpec((1, frame_count, 1), lambda i: (i, 0, 0)),
            pl.BlockSpec((heads, NREL), lambda i: (0, 0)),
        ],
        out_specs=[
            pl.BlockSpec((1, frame_count, width), lambda i: (i, 0, 0)),
            pl.BlockSpec((2, width // 3), lambda i: (0, 0)),
            pl.BlockSpec((heads, NREL), lambda i: (0, 0)),
        ],
        scratch_shapes=[
            pltpu.VMEM((heads, frame_count, frame_count), jnp.float32),
            pltpu.VMEM((heads, frame_count, frame_count), jnp.float32),
        ],
        name="unattend",
    )(packed, upstream, segment_rows, segment_columns, table)


def reach_mask(offset, behind, ahead):
    if offset < 0:
        return behind >= -offset
    return ahead >= offset


def convolve_kernel(opened, behind, ahead, taps, bias, gated, filtered, padded):
    frame_count, channels = gated.shape[1:]
    gates = opened[0, :, 0:channels] * jax.nn.sigmoid(opened[0, :, channels:])
    gated[0] = gates
    padded[pl.ds(0, MARGIN), :] = jnp.zeros((MARGIN, channels), jnp.float32)
    padded[pl.ds(MARGIN + frame_count, MARGIN), :] = jnp.zeros((MARGIN, channels), jnp.float32)
    padded[pl.ds(MARGIN, frame_count), :] = gates
    back = jnp.broadcast_to(behind[0], (frame_count, LANES))
    front = jnp.broadcast_to(ahead[0], (frame_count, LANES))
    for low in range(0, channels, LANES):
        lanes = slice(low, low + LANES)
        running = jnp.broadcast_to(bias[:, lanes], (frame_count, LANES))
        for tap in range(KW):
            offset = tap - (KW - 1) // 2
            moved = padded[pl.ds(MARGIN + offset, frame_count), lanes]
            if offset:
                moved = jnp.where(reach_mask(offset, back, front), moved, 0.0)
            running = running + moved * taps[pl.ds(tap, 1), lanes]
        filtered[0, :, lanes] = running


def convolve(opened, behind, ahead, taps, bias):
    blocks, frame_count, width = opened.shape
    channels = width // 2
    rows = pl.BlockSpec((1, frame_count, channels), lambda i: (i, 0, 0))
    places = pl.BlockSpec((1, frame_count, 1), lambda i: (i, 0, 0))
    return pl.pallas_call(
        convolve_kernel,
        grid=(blocks,),
        out_shape=[jax.ShapeDtypeStruct((blocks, frame_count, channels), jnp.float32)] * 2,
        in_specs=[
            pl.BlockSpec((1, frame_count, width), lambda i: (i, 0, 0)),
            places,
            places,
            pl.BlockSpec((KW, channels), lambda i: (0, 0)),
            pl.BlockSpec((1, channels), lambda i: (0, 0)),
        ],
        out_specs=[rows, rows],
        scratch_shapes=[pltpu.VMEM((frame_count + 2 * MARGIN, channels), jnp.float32)],
        name="convolve",
    )(opened, behind, ahead, taps, bias)


def unconvolve_kernel(opened, gated, upstream, behind, ahead, taps, grads, lifts, slopes, padded, padded_grad):
    frame_count, channels = gated.shape[1:]

    @pl.when(pl.program_id(0) == 0)
    def _():
        lifts[...] = jnp.zeros_like(lifts)
        slopes[...] = jnp.zeros_like(slopes)

    for store, value in ((padded, gated[0]), (padded_grad, upstream[0])):
        store[pl.ds(0, MARGIN), :] = jnp.zeros((MARGIN, channels), jnp.float32)
        store[pl.ds(MARGIN + frame_count, MARGIN), :] = jnp.zeros((MARGIN, channels), jnp.float32)
        store[pl.ds(MARGIN, frame_count), :] = value
    back = jnp.broadcast_to(behind[0], (frame_count, LANES))
    front = jnp.broadcast_to(ahead[0], (frame_count, LANES))
    for low in range(0, channels, LANES):
        lanes = slice(low, low + LANES)
        above = upstream[0, :, lanes]
        running = jnp.zeros((frame_count, LANES), jnp.float32)
        for tap in range(KW):
            offset = tap - (KW - 1) // 2
            moved = padded[pl.ds(MARGIN + offset, frame_count), lanes]
            moved_grad = padded_grad[pl.ds(MARGIN + offset, frame_count), lanes]
            if offset:
                mask = reach_mask(offset, back, front)
                moved = jnp.where(mask, moved, 0.0)
                moved_grad = jnp.where(mask, moved_grad, 0.0)
            running = running + moved_grad * taps[pl.ds(KW - 1 - tap, 1), lanes]
            slopes[pl.ds(tap, 1), lanes] += jnp.sum(moved * above, axis=0, keepdims=True)
        slopes[pl.ds(KW, 1), lanes] += jnp.sum(above, axis=0, keepdims=True)
        wide = slice(channels + low, channels + low + LANES)
        left, gate = opened[0, :, lanes], jax.nn.sigmoid(opened[0, :, wide])
        left_grad = running * gate
        gate_grad = running * left * gate * (1.0 - gate)
        grads[0, :, lanes] = left_grad.astype(jnp.bfloat16)
        grads[0, :, wide] = gate_grad.astype(jnp.bfloat16)
        lifts[:, lanes] += jnp.sum(left_grad, axis=0, keepdims=True)
        lifts[:, wide] += jnp.sum(gate_grad, axis=0, keepdims=True)


def unconvolve(opened, gated, upstream, behind, ahead, taps):
    blocks, frame_count, width = opened.shape
    channels = width // 2
    wide = pl.BlockSpec((1, frame_count, width), lambda i: (i, 0, 0))
    rows = pl.BlockSpec((1, frame_count, channels), lambda i: (i, 0, 0))
    places = pl.BlockSpec((1, frame_count, 1), lambda i: (i, 0, 0))
    return pl.pallas_call(
        unconvolve_kernel,
        grid=(blocks,),
        out_shape=[
            jax.ShapeDtypeStruct((blocks, frame_count, width), jnp.bfloat16),
            jax.ShapeDtypeStruct((1, width), jnp.float32),
            jax.ShapeDtypeStruct((KW + 1, channels), jnp.float32),
        ],
        in_specs=[wide, rows, rows, places, places, pl.BlockSpec((KW, channels), lambda i: (0, 0))],
        out_specs=[
            wide,
            pl.BlockSpec((1, width), lambda i: (0, 0)),
            pl.BlockSpec((KW + 1, channels), lambda i: (0, 0)),
        ],
        scratch_shapes=[pltpu.VMEM((frame_count + 2 * MARGIN, channels), jnp.float32)] * 2,
        name="unconvolve",
    )(opened, gated, upstream, behind, ahead, taps)


def gather_rows(value):
    return lax.all_gather(value, "fsdp", axis=0, tiled=True)


def gather_split(value):
    full = lax.all_gather(value, "fsdp", axis=1, tiled=True)
    return full.reshape(-1, full.shape[-1])


def scatter_rows(value):
    return lax.psum_scatter(value.astype(jnp.bfloat16), "fsdp", scatter_dimension=0, tiled=True)


def scatter_split(value, n):
    value = value.astype(jnp.bfloat16).reshape(n, value.shape[0] // n, value.shape[1])
    return lax.psum_scatter(value, "fsdp", scatter_dimension=1, tiled=True)


def pair_slopes(up_slope, down_slope, n):
    inner = down_slope.shape[0]
    up_slope = up_slope.reshape(n, inner, -1)
    down_slope = jnp.transpose(down_slope.reshape(inner, n, inner), (1, 0, 2))
    return jnp.concatenate([up_slope, down_slope], axis=2)


def flat(value):
    return value.reshape(-1, value.shape[-1])


def split_body(
    n,
    m,
    frames,
    segments,
    cotangent,
    early_gain,
    early_shift,
    early_up,
    early_lift,
    early_down,
    early_drop,
    mixer_gain,
    mixer_shift,
    mixer_project,
    query_bias,
    value_bias,
    mixer_output,
    mixer_drop,
    distance_table,
    filter_gain,
    filter_shift,
    filter_up,
    filter_lift,
    depth_weight,
    depth_bias,
    middle_gain,
    middle_shift,
    filter_down,
    filter_drop,
    late_gain,
    late_shift,
    late_up,
    late_lift,
    late_down,
    late_drop,
    final_gain,
    final_shift,
):
    me = lax.axis_index("dp")
    frame_count = frames.shape[0]
    rows = early_gain.shape[0]
    hidden = early_up.shape[1] // n
    inner = D // n
    heads = HEADS // n
    start_rows = frames.astype(jnp.float32)
    final_upstream = cotangent.astype(jnp.float32)
    singles = [
        early_gain, early_shift, early_drop, mixer_gain, mixer_shift, query_bias, value_bias, mixer_drop,
        filter_gain, filter_shift, depth_bias, middle_gain, middle_shift, filter_drop, late_gain, late_shift,
        late_drop, final_gain, final_shift,
    ]
    spans = hidden * n // D
    w_early_down = gather_rows(early_down)
    w_early_up, late_up_split, mixer_split, filter_split, small_all, depth_all, segments_all, early_hidden = exchange(
        n, m, early_up, late_up, mixer_project, filter_up, mixer_output, filter_down, depth_weight,
        segments.reshape(1, frame_count), frames, singles, [early_lift, late_lift, filter_lift], distance_table,
    )
    w_early_up = w_early_up.reshape(D, hidden)
    w_mixer = lax.all_gather(mixer_split, "fsdp", axis=1, tiled=True)
    w_filter = lax.all_gather(filter_split, "fsdp", axis=1, tiled=True)
    w_late_up = gather_split(late_up_split)
    w_late_down = gather_rows(late_down)

    lines = -(-len(singles) * rows // LANES)
    vectors = jnp.transpose(small_all[:, :lines].reshape(n * m, lines, LANES // rows, rows), (1, 2, 0, 3)).reshape(-1, D)
    own_vectors = lax.dynamic_slice(vectors, (0, me * inner), (vectors.shape[0], inner))
    own_lifts = lax.dynamic_slice(small_all, (me * m, lines, 0), (m, 2, LANES))
    early_lifts, late_lifts = own_lifts[:, 0].reshape(-1), own_lifts[:, 1].reshape(-1)
    filter_lifts = small_all[:, lines + 2, : 2 * D // (n * m)].reshape(2, D)
    filter_lifts = lax.dynamic_slice(filter_lifts, (0, me * inner), (2, inner)).reshape(2 * inner)
    table = small_all[:, 8 : 8 + distance_table.shape[0], :HEADS].reshape(NREL, HEADS)
    table = jnp.transpose(lax.dynamic_slice(table, (0, me * heads), (NREL, heads)))[:, ::-1]
    taps = jnp.transpose(depth_all.reshape(inner, KW)).astype(jnp.float32)
    attention_shift = jnp.concatenate([own_vectors[5], jnp.zeros((inner,), jnp.float32), own_vectors[6]])
    segment_rows = segments_all
    segment_columns = segments_all.reshape(n, frame_count, 1)
    places = jnp.arange(frame_count, dtype=jnp.int32)[None, :]
    lower = (segment_rows < segment_columns).astype(jnp.int32)
    upto = (segment_rows <= segment_columns).astype(jnp.int32)
    behind = (places - jnp.sum(lower, axis=-1)).reshape(n, frame_count, 1)
    ahead = (jnp.sum(upto, axis=-1) - 1 - places).reshape(n, frame_count, 1)

    def blocks(value):
        return value.reshape(n, frame_count, value.shape[-1])

    def feed(hidden_rows, w_up, lifts, w_down):
        widened = flat_dot(flat(hidden_rows), w_up) + lifts
        active = (widened * jax.nn.sigmoid(widened)).astype(jnp.bfloat16)
        return widened, active, blocks(flat_dot(active, w_down).astype(jnp.bfloat16))

    def feed_back(low, hidden_rows, widened, active, w_up, w_down):
        low = flat(low)
        down_slope = lead_dot(active, low).astype(jnp.bfloat16)
        widened_grad = swish_back(back_dot(low, w_down), widened)
        widened_low = widened_grad.astype(jnp.bfloat16)
        up_slope = lead_dot(flat(hidden_rows), widened_low).astype(jnp.bfloat16)
        part = blocks(back_dot(widened_low, w_up).astype(jnp.bfloat16))
        part, down_slope, up_slope = lax.optimization_barrier((part, down_slope, up_slope))
        return part, down_slope, up_slope, jnp.sum(widened_grad, axis=0)

    early_wide, early_active, part = feed(early_hidden, w_early_up, early_lifts, w_early_down)
    first_rows, mixer_hidden = boundary(
        n, functools.partial(step_forward, 0.5), part, [start_rows], [vectors[2], vectors[3], vectors[4]], 1, 0, 2
    )
    mixer_hidden, w_mixer = lax.optimization_barrier((mixer_hidden, w_mixer))
    w_project = w_mixer[:, :, : 3 * inner].reshape(D, 3 * inner)
    w_output = jnp.transpose(w_mixer[:, :, 3 * inner :], (1, 0, 2)).reshape(inner, D)
    packed = blocks((flat_dot(flat(mixer_hidden), w_project) + attention_shift).astype(jnp.bfloat16))
    blended = attend(packed, segment_rows, segment_columns, table)
    part = blocks(flat_dot(flat(blended), w_output).astype(jnp.bfloat16))
    second_rows, filter_hidden = boundary(
        n, functools.partial(step_forward, 1.0), part, [first_rows], [vectors[7], vectors[8], vectors[9]], 1, 0, 3
    )
    filter_hidden, w_filter = lax.optimization_barrier((filter_hidden, w_filter))
    w_filter_up = w_filter[:, :, : 2 * inner].reshape(D, 2 * inner)
    w_filter_down = jnp.transpose(w_filter[:, :, 2 * inner :], (1, 0, 2)).reshape(inner, D)
    opened = blocks(flat_dot(flat(filter_hidden), w_filter_up) + filter_lifts)
    gated, filtered = convolve(opened, behind, ahead, taps, own_vectors[10:11])
    filtered = flat(filtered)
    local_mean = jnp.mean(filtered, axis=-1)
    local_square = jnp.sum((filtered - local_mean[:, None]) ** 2, axis=-1)
    shared = share(
        n, jnp.concatenate([local_mean.reshape(n, frame_count), local_square.reshape(n, frame_count)]), 4
    )
    means, squares = shared[:, :n], shared[:, n:]
    middle_mean = jnp.mean(means, axis=0)
    spread = jnp.sum(squares, axis=0) + inner * jnp.sum((means - middle_mean) ** 2, axis=0)
    middle_inverse = lax.rsqrt(spread / D + EPSILON).reshape(-1, 1)
    middle_unit = (filtered - middle_mean.reshape(-1, 1)) * middle_inverse
    middle = middle_unit * own_vectors[11] + own_vectors[12]
    swished = (middle * jax.nn.sigmoid(middle)).astype(jnp.bfloat16)
    part = blocks(flat_dot(swished, w_filter_down).astype(jnp.bfloat16))
    third_rows, late_hidden = boundary(
        n, functools.partial(step_forward, 1.0), part, [second_rows], [vectors[13], vectors[14], vectors[15]], 1, 0, 5
    )
    late_hidden, w_late_up, w_late_down = lax.optimization_barrier((late_hidden, w_late_up, w_late_down))
    late_wide, late_active, part = feed(late_hidden, w_late_up, late_lifts, w_late_down)
    layer_out, grad, low, turn_sums = boundary(
        n, step_turn, part, [third_rows, final_upstream], [vectors[16], vectors[17], vectors[18]], 2, 3, 6
    )

    part, late_down_slope, late_up_slope, late_lift_slope = feed_back(
        low, late_hidden, late_wide, late_active, w_late_up, w_late_down
    )
    late_down_slope = scatter_rows(late_down_slope)
    late_up_slope = scatter_split(late_up_slope, n)
    grad, low, late_sums = boundary(
        n, functools.partial(step_backward, 1.0), part, [grad, third_rows], [vectors[14]], 1, 3, 7
    )
    low = flat(low)
    filter_down_slope = lead_dot(swished, low).astype(jnp.bfloat16)
    middle_grad = swish_back(back_dot(low, w_filter_down), middle)
    middle_gain_slope = jnp.sum(middle_grad * middle_unit, axis=0)
    middle_shift_slope = jnp.sum(middle_grad, axis=0)
    scaled = middle_grad * own_vectors[11]
    shared = share(
        n,
        jnp.concatenate(
            [
                jnp.sum(scaled, axis=-1).reshape(n, frame_count),
                jnp.sum(scaled * middle_unit, axis=-1).reshape(n, frame_count),
            ]
        ),
        8,
    )
    totals = jnp.sum(shared, axis=0) / D
    filtered_grad = middle_inverse * (
        scaled - totals[:n].reshape(-1, 1) - middle_unit * totals[n:].reshape(-1, 1)
    )
    opened_low, filter_lift_slope, depth_slope = unconvolve(
        opened, gated, blocks(filtered_grad), behind, ahead, taps
    )
    opened_low = flat(opened_low)
    filter_up_slope = lead_dot(flat(filter_hidden), opened_low).astype(jnp.bfloat16)
    part = blocks(back_dot(opened_low, w_filter_up).astype(jnp.bfloat16))
    part, filter_slope = lax.optimization_barrier((part, pair_slopes(filter_up_slope, filter_down_slope, n)))
    filter_slope = lax.psum_scatter(filter_slope, "fsdp", scatter_dimension=1, tiled=True)
    grad, low, filter_sums = boundary(
        n, functools.partial(step_backward, 1.0), part, [grad, second_rows], [vectors[8]], 1, 3, 9
    )
    low = flat(low)
    output_slope = lead_dot(flat(blended), low).astype(jnp.bfloat16)
    blend_grad = blocks(back_dot(low, w_output).astype(jnp.bfloat16))
    packed_low, shift_sums, table_slope = unattend(packed, blend_grad, segment_rows, segment_columns, table)
    packed_low = flat(packed_low)
    project_slope = lead_dot(flat(mixer_hidden), packed_low).astype(jnp.bfloat16)
    part = blocks(back_dot(packed_low, w_project).astype(jnp.bfloat16))
    part, mixer_slope, late_down_slope, late_up_slope = lax.optimization_barrier(
        (part, pair_slopes(project_slope, output_slope, n), late_down_slope, late_up_slope)
    )
    mixer_slope = lax.psum_scatter(mixer_slope, "fsdp", scatter_dimension=1, tiled=True)
    grad, low, mixer_sums = boundary(
        n, functools.partial(step_backward, 0.5), part, [grad, first_rows], [vectors[3]], 1, 3, 10
    )
    part, early_down_slope, early_up_slope, early_lift_slope = feed_back(
        low, early_hidden, early_wide, early_active, w_early_up, w_early_down
    )
    early_down_slope = jnp.transpose(early_down_slope.reshape(m, spans, rows, D), (1, 0, 2, 3))
    early_slope = jnp.concatenate(
        [early_up_slope.reshape(n, D // n, hidden), early_down_slope.reshape(spans, m * rows, D)]
    )
    part, early_slope, filter_slope = lax.optimization_barrier((part, early_slope, filter_slope))
    early_slope = lax.psum_scatter(early_slope, "fsdp", scatter_dimension=1, tiled=True)
    early_up_slope, early_down_slope = early_slope[:n], early_slope[n:].reshape(spans * rows, D)
    slope_frames, early_sums = boundary(
        n, step_last, part, [grad, start_rows], [vectors[0]], 1, 2, 11, gathered=False
    )

    table_slope = jnp.roll(table_slope[:, ::-1], 1 - NREL // 2, axis=1)
    table_rows = NREL // (n * m)
    wide = jnp.concatenate([turn_sums, late_sums, filter_sums, mixer_sums, early_sums])
    wide_count = wide.shape[0]
    wide = jnp.transpose(wide.reshape(wide_count, n * m, rows), (1, 0, 2)).reshape(n * m, wide_count * rows)
    wide = jnp.concatenate(
        [wide, jnp.transpose(table_slope.reshape(heads, n * m, table_rows), (1, 0, 2)).reshape(n * m, -1)], axis=1
    )
    lift_full = lax.dynamic_update_slice(
        jnp.zeros((2, D), jnp.float32), filter_lift_slope.reshape(2, inner), (0, me * inner)
    ).reshape(n * m, -1)
    table_used = wide.shape[1]
    wide = jnp.concatenate([wide, lift_full], axis=1)
    wide_used = wide.shape[1]
    wide = jnp.pad(wide, ((0, 0), (0, -wide_used % LANES))).reshape(n * m, -1, LANES)
    group = jnp.concatenate(
        [
            shift_sums,
            middle_gain_slope[None],
            middle_shift_slope[None],
            depth_slope,
            jnp.transpose(early_lift_slope.reshape(inner, spans)),
            jnp.transpose(late_lift_slope.reshape(inner, spans)),
        ]
    )
    group_count = group.shape[0]
    group = jnp.transpose(group.reshape(group_count, m, rows), (1, 0, 2)).reshape(m, group_count * rows)
    group_used = group.shape[1]
    group = jnp.pad(group, ((0, 0), (0, -group_used % LANES))).reshape(m, -1, LANES)
    wide_all, group_all = collect(n, m, wide, group, 12)
    wide_all, mixer_slope = lax.optimization_barrier((wide_all, mixer_slope))
    tables = wide_all.reshape(n, m, -1)[:, :, wide_count * rows : table_used]
    wide = jnp.sum(wide_all, axis=0).reshape(-1)
    lift_total = wide[table_used:wide_used]
    wide = wide[: wide_count * rows].reshape(wide_count, rows)
    tables = jnp.transpose(jnp.sum(tables, axis=1).reshape(HEADS, table_rows))
    group = jnp.sum(group_all, axis=0).reshape(-1)[:group_used].reshape(group_count, rows)
    late_up_wide, project_wide, filter_up_wide = giveback(
        n, [late_up_slope, mixer_slope, filter_slope], [(1, hidden), (3, inner), (2, inner)], 13
    )
    (early_up_wide,) = giveback(n, [early_up_slope], [(1, hidden)], 14)

    def rejoin(value, low):
        return final(jnp.transpose(value[:, :, low:], (1, 0, 2)).reshape(rows, D))

    def final(value):
        return value.astype(jnp.float32)

    lift_slopes = KW + 5
    return (
        layer_out,
        slope_frames,
        wide[12],
        wide[13],
        final(early_up_wide),
        jnp.transpose(group[lift_slopes : lift_slopes + spans]).reshape(-1),
        final(early_down_slope),
        wide[11],
        wide[9],
        wide[10],
        final(project_wide),
        group[0],
        group[1],
        rejoin(mixer_slope, 3 * inner),
        wide[8],
        tables,
        wide[6],
        wide[7],
        final(filter_up_wide),
        lift_total,
        jnp.transpose(group[4 : 4 + KW]),
        group[4 + KW],
        group[2],
        group[3],
        rejoin(filter_slope, 2 * inner),
        wide[5],
        wide[3],
        wide[4],
        final(late_up_wide),
        jnp.transpose(group[lift_slopes + spans : lift_slopes + 2 * spans]).reshape(-1),
        final(late_down_slope),
        wide[2],
        wide[0],
        wide[1],
    )


def solution(mesh):
    in_specs = (
        P(("dp", "fsdp"), None),
        P(("dp", "fsdp")),
        P(("dp", "fsdp"), None),
        P(("dp", "fsdp")),
        P(("dp", "fsdp")),
        P(("dp", "fsdp"), None),
        P(("dp", "fsdp")),
        P(("dp", "fsdp"), None),
        P(("dp", "fsdp")),
        P(("dp", "fsdp")),
        P(("dp", "fsdp")),
        P(("dp", "fsdp"), None),
        P(("dp", "fsdp")),
        P(("dp", "fsdp")),
        P(("dp", "fsdp"), None),
        P(("dp", "fsdp")),
        P(("dp", "fsdp"), None),
        P(("dp", "fsdp")),
        P(("dp", "fsdp")),
        P(("dp", "fsdp"), None),
        P(("dp", "fsdp")),
        P(("dp", "fsdp"), None),
        P(("dp", "fsdp")),
        P(("dp", "fsdp")),
        P(("dp", "fsdp")),
        P(("dp", "fsdp"), None),
        P(("dp", "fsdp")),
        P(("dp", "fsdp")),
        P(("dp", "fsdp")),
        P(("dp", "fsdp"), None),
        P(("dp", "fsdp")),
        P(("dp", "fsdp"), None),
        P(("dp", "fsdp")),
        P(("dp", "fsdp")),
        P(("dp", "fsdp")),
    )
    out_specs = (
        P(("dp", "fsdp"), None),
        P(("dp", "fsdp"), None),
        P(("dp", "fsdp")),
        P(("dp", "fsdp")),
        P(("dp", "fsdp"), None),
        P(("dp", "fsdp")),
        P(("dp", "fsdp"), None),
        P(("dp", "fsdp")),
        P(("dp", "fsdp")),
        P(("dp", "fsdp")),
        P(("dp", "fsdp"), None),
        P(("dp", "fsdp")),
        P(("dp", "fsdp")),
        P(("dp", "fsdp"), None),
        P(("dp", "fsdp")),
        P(("dp", "fsdp"), None),
        P(("dp", "fsdp")),
        P(("dp", "fsdp")),
        P(("dp", "fsdp"), None),
        P(("dp", "fsdp")),
        P(("dp", "fsdp"), None),
        P(("dp", "fsdp")),
        P(("dp", "fsdp")),
        P(("dp", "fsdp")),
        P(("dp", "fsdp"), None),
        P(("dp", "fsdp")),
        P(("dp", "fsdp")),
        P(("dp", "fsdp")),
        P(("dp", "fsdp"), None),
        P(("dp", "fsdp")),
        P(("dp", "fsdp"), None),
        P(("dp", "fsdp")),
        P(("dp", "fsdp")),
        P(("dp", "fsdp")),
    )
    n, m = mesh.shape["dp"], mesh.shape["fsdp"]
    run = functools.partial(split_body, n, m) if n == 4 and D // (n * m) == 32 else body
    return jax.shard_map(run, mesh=mesh, in_specs=in_specs, out_specs=out_specs, check_vma=False)
```

```python
import functools

import jax
import jax.numpy as jnp
from jax import lax
from jax.experimental import pallas as pl
from jax.experimental.pallas import tpu as pltpu
from jax.sharding import PartitionSpec as P

D = 1024
HEADS = 16
HEAD = 64
KW = 31
NREL = 256


EPSILON = 1e-05
MASKED = -1e30
UTTERANCE_LIMIT = 4
MESH = pl.DeviceIdType.MESH
PIECES = 2
LAG = 2
BLOCK = 16
MARGIN = 16
LANES = 128


def flat_dot(left_rows, right_rows):
    return jnp.dot(left_rows, right_rows, preferred_element_type=jnp.float32)


def lead_dot(left_rows, right_rows):
    return lax.dot_general(
        left_rows, right_rows, (((0,), (0,)), ((), ())), preferred_element_type=jnp.float32
    )


def back_dot(left_rows, right_rows):
    return lax.dot_general(
        left_rows, right_rows, (((1,), (1,)), ((), ())), preferred_element_type=jnp.float32
    )


def norm_apply(values, norm_gain, norm_shift):
    centered = values - jnp.mean(values, axis=-1, keepdims=True)
    inverse = lax.rsqrt(jnp.mean(centered * centered, axis=-1, keepdims=True) + EPSILON)
    normed_unit = centered * inverse
    return (
        normed_unit * norm_gain.astype(jnp.float32) + norm_shift.astype(jnp.float32),
        normed_unit,
        inverse,
    )


def norm_back(upstream, normed_unit, inverse, norm_gain):
    scaled = upstream * norm_gain.astype(jnp.float32)
    adjusted = scaled - jnp.mean(scaled, axis=-1, keepdims=True)
    adjusted = adjusted - normed_unit * jnp.mean(scaled * normed_unit, axis=-1, keepdims=True)
    return (inverse * adjusted, jnp.sum(upstream * normed_unit, axis=0), jnp.sum(upstream, axis=0))


def swish_back(upstream, before):
    sigmoid_rows = jax.nn.sigmoid(before)
    return upstream * sigmoid_rows * (1.0 + before * (1.0 - sigmoid_rows))


def depthwise(gated_rows, kernel, segment_ids):
    margin = (KW - 1) // 2
    channels = gated_rows.shape[1]
    taps = jnp.transpose(kernel)[:, None, :]
    running = jnp.zeros_like(gated_rows)
    for utterance in range(UTTERANCE_LIMIT):
        inside = (segment_ids == utterance)[:, None]
        masked_rows = jnp.where(inside, gated_rows, 0.0)
        convolved = lax.conv_general_dilated(
            masked_rows[None],
            taps,
            (1,),
            ((margin, margin),),
            dimension_numbers=("NWC", "WIO", "NWC"),
            feature_group_count=channels,
            precision=lax.Precision.HIGHEST,
        )[0]
        running = running + jnp.where(inside, convolved, 0.0)
    return running


def fetch_feed(norm_gain, norm_shift, w_up, up_shift, w_down, down_shift):
    return (
        lax.all_gather(norm_gain, ("dp", "fsdp"), axis=0, tiled=True),
        lax.all_gather(norm_shift, ("dp", "fsdp"), axis=0, tiled=True),
        lax.all_gather(w_up, ("dp", "fsdp"), axis=0, tiled=True),
        lax.all_gather(up_shift, ("dp", "fsdp"), axis=0, tiled=True),
        lax.all_gather(w_down, ("dp", "fsdp"), axis=0, tiled=True),
        lax.all_gather(down_shift, ("dp", "fsdp"), axis=0, tiled=True),
    )


def reduce_feed(norm_gain, norm_shift, w_up, up_shift, w_down, down_shift):
    return (
        lax.psum_scatter(norm_gain, ("dp", "fsdp"), scatter_dimension=0, tiled=True),
        lax.psum_scatter(norm_shift, ("dp", "fsdp"), scatter_dimension=0, tiled=True),
        lax.psum_scatter(w_up, ("dp", "fsdp"), scatter_dimension=0, tiled=True),
        lax.psum_scatter(up_shift, ("dp", "fsdp"), scatter_dimension=0, tiled=True),
        lax.psum_scatter(w_down, ("dp", "fsdp"), scatter_dimension=0, tiled=True),
        lax.psum_scatter(down_shift, ("dp", "fsdp"), scatter_dimension=0, tiled=True),
    )


def fetch_mixer(
    norm_gain, norm_shift, w_project, query_shift, value_shift, w_output, output_shift, table_rows
):
    return (
        lax.all_gather(norm_gain, ("dp", "fsdp"), axis=0, tiled=True),
        lax.all_gather(norm_shift, ("dp", "fsdp"), axis=0, tiled=True),
        lax.all_gather(w_project, ("dp", "fsdp"), axis=0, tiled=True),
        lax.all_gather(query_shift, ("dp", "fsdp"), axis=0, tiled=True),
        lax.all_gather(value_shift, ("dp", "fsdp"), axis=0, tiled=True),
        lax.all_gather(w_output, ("dp", "fsdp"), axis=0, tiled=True),
        lax.all_gather(output_shift, ("dp", "fsdp"), axis=0, tiled=True),
        lax.all_gather(table_rows, ("dp", "fsdp"), axis=0, tiled=True),
    )


def reduce_mixer(
    norm_gain, norm_shift, w_project, query_shift, value_shift, w_output, output_shift, table_rows
):
    return (
        lax.psum_scatter(norm_gain, ("dp", "fsdp"), scatter_dimension=0, tiled=True),
        lax.psum_scatter(norm_shift, ("dp", "fsdp"), scatter_dimension=0, tiled=True),
        lax.psum_scatter(w_project, ("dp", "fsdp"), scatter_dimension=0, tiled=True),
        lax.psum_scatter(query_shift, ("dp", "fsdp"), scatter_dimension=0, tiled=True),
        lax.psum_scatter(value_shift, ("dp", "fsdp"), scatter_dimension=0, tiled=True),
        lax.psum_scatter(w_output, ("dp", "fsdp"), scatter_dimension=0, tiled=True),
        lax.psum_scatter(output_shift, ("dp", "fsdp"), scatter_dimension=0, tiled=True),
        lax.psum_scatter(table_rows, ("dp", "fsdp"), scatter_dimension=0, tiled=True),
    )


def fetch_filter(
    norm_gain,
    norm_shift,
    w_up,
    up_shift,
    depth_taps,
    depth_shift,
    middle_gain,
    middle_shift,
    w_down,
    down_shift,
    last_gain,
    last_shift,
):
    return (
        lax.all_gather(norm_gain, ("dp", "fsdp"), axis=0, tiled=True),
        lax.all_gather(norm_shift, ("dp", "fsdp"), axis=0, tiled=True),
        lax.all_gather(w_up, ("dp", "fsdp"), axis=0, tiled=True),
        lax.all_gather(up_shift, ("dp", "fsdp"), axis=0, tiled=True),
        lax.all_gather(depth_taps, ("dp", "fsdp"), axis=0, tiled=True),
        lax.all_gather(depth_shift, ("dp", "fsdp"), axis=0, tiled=True),
        lax.all_gather(middle_gain, ("dp", "fsdp"), axis=0, tiled=True),
        lax.all_gather(middle_shift, ("dp", "fsdp"), axis=0, tiled=True),
        lax.all_gather(w_down, ("dp", "fsdp"), axis=0, tiled=True),
        lax.all_gather(down_shift, ("dp", "fsdp"), axis=0, tiled=True),
        lax.all_gather(last_gain, ("dp", "fsdp"), axis=0, tiled=True),
        lax.all_gather(last_shift, ("dp", "fsdp"), axis=0, tiled=True),
    )


def reduce_filter(
    norm_gain,
    norm_shift,
    w_up,
    up_shift,
    depth_taps,
    depth_shift,
    middle_gain,
    middle_shift,
    w_down,
    down_shift,
    last_gain,
    last_shift,
):
    return (
        lax.psum_scatter(norm_gain, ("dp", "fsdp"), scatter_dimension=0, tiled=True),
        lax.psum_scatter(norm_shift, ("dp", "fsdp"), scatter_dimension=0, tiled=True),
        lax.psum_scatter(w_up, ("dp", "fsdp"), scatter_dimension=0, tiled=True),
        lax.psum_scatter(up_shift, ("dp", "fsdp"), scatter_dimension=0, tiled=True),
        lax.psum_scatter(depth_taps, ("dp", "fsdp"), scatter_dimension=0, tiled=True),
        lax.psum_scatter(depth_shift, ("dp", "fsdp"), scatter_dimension=0, tiled=True),
        lax.psum_scatter(middle_gain, ("dp", "fsdp"), scatter_dimension=0, tiled=True),
        lax.psum_scatter(middle_shift, ("dp", "fsdp"), scatter_dimension=0, tiled=True),
        lax.psum_scatter(w_down, ("dp", "fsdp"), scatter_dimension=0, tiled=True),
        lax.psum_scatter(down_shift, ("dp", "fsdp"), scatter_dimension=0, tiled=True),
        lax.psum_scatter(last_gain, ("dp", "fsdp"), scatter_dimension=0, tiled=True),
        lax.psum_scatter(last_shift, ("dp", "fsdp"), scatter_dimension=0, tiled=True),
    )


def feed_forward(values, weights):
    normed, normed_unit, inverse = norm_apply(values, weights[0], weights[1])
    hidden = normed.astype(jnp.bfloat16)
    widened = flat_dot(hidden, weights[2]) + weights[3].astype(jnp.float32)
    active = (widened * jax.nn.sigmoid(widened)).astype(jnp.bfloat16)
    result = values + 0.5 * (flat_dot(active, weights[4]) + weights[5].astype(jnp.float32))
    return (result, (normed_unit, inverse, hidden, widened, active))


def feed_backward(upstream, saved, weights):
    normed_unit, inverse, hidden, widened, active = saved
    half_grad = 0.5 * upstream
    half_low = half_grad.astype(jnp.bfloat16)
    down_slope = lead_dot(active, half_low)
    widened_grad = swish_back(back_dot(half_low, weights[4]), widened)
    widened_low = widened_grad.astype(jnp.bfloat16)
    up_slope = lead_dot(hidden, widened_low)
    hidden_grad = back_dot(widened_low, weights[2])
    input_grad, gain_slope, shift_slope = norm_back(hidden_grad, normed_unit, inverse, weights[0])
    slopes = (
        gain_slope,
        shift_slope,
        up_slope,
        jnp.sum(widened_grad, axis=0),
        down_slope,
        jnp.sum(half_grad, axis=0),
    )
    return (upstream + input_grad, slopes)


def bucket_table(frame_count):
    offsets = jnp.arange(2 * frame_count - 1, dtype=jnp.int32) - (frame_count - 1)
    buckets = jnp.clip(offsets, -(NREL // 2), NREL // 2 - 1) + NREL // 2
    return (buckets[:, None] == jnp.arange(NREL, dtype=jnp.int32)[None, :]).astype(jnp.float32)


def relative_bias(table_rows, frame_count):
    diagonals = jnp.dot(
        bucket_table(frame_count),
        table_rows.astype(jnp.float32),
        precision=lax.Precision.HIGHEST,
        preferred_element_type=jnp.float32,
    )
    flipped = jnp.concatenate(
        [jnp.transpose(diagonals[::-1]), jnp.zeros((HEADS, 1), jnp.float32)], axis=1
    )
    spread = jnp.broadcast_to(flipped[:, None, :], (HEADS, frame_count, 2 * frame_count))
    spread = spread.reshape(HEADS, 2 * frame_count * frame_count)
    sheared = spread[:, : frame_count * (2 * frame_count - 1)].reshape(
        HEADS, frame_count, 2 * frame_count - 1
    )
    return sheared[:, :, frame_count - 1 :]


def relative_slope(score_grad, frame_count):
    placed = jnp.pad(score_grad, ((0, 0), (0, 0), (frame_count - 1, 0)))
    flattened = jnp.pad(
        placed.reshape(HEADS, frame_count * (2 * frame_count - 1)), ((0, 0), (0, frame_count))
    )
    columns = jnp.sum(flattened.reshape(HEADS, frame_count, 2 * frame_count), axis=1)
    diagonals = columns[:, 2 * frame_count - 2 :: -1]
    return lax.dot_general(
        bucket_table(frame_count),
        diagonals,
        (((0,), (1,)), ((), ())),
        precision=lax.Precision.HIGHEST,
        preferred_element_type=jnp.float32,
    )


def mixer_scores(query_rows, key_matrix_rows, relative, same_utterance):
    unnormalized_scores = jnp.einsum(
        "jug,fug->ujf", query_rows, key_matrix_rows, preferred_element_type=jnp.float32
    )
    return jnp.where(same_utterance[None], HEAD ** (-0.5) * unnormalized_scores + relative, MASKED)


def mixer_forward(values, segment_ids, weights):
    frame_count = values.shape[0]
    normed, normed_unit, inverse = norm_apply(values, weights[0], weights[1])
    hidden = normed.astype(jnp.bfloat16)
    projected = flat_dot(hidden, weights[2])
    query_rows = (projected[:, :D] + weights[3].astype(jnp.float32)).astype(jnp.bfloat16)
    query_rows = query_rows.reshape(frame_count, HEADS, HEAD)
    key_matrix_rows = projected[:, D : 2 * D].astype(jnp.bfloat16).reshape(frame_count, HEADS, HEAD)
    value_matrix_rows = (projected[:, 2 * D :] + weights[4].astype(jnp.float32)).astype(
        jnp.bfloat16
    )
    value_matrix_rows = value_matrix_rows.reshape(frame_count, HEADS, HEAD)
    relative = relative_bias(weights[7], frame_count)
    same_utterance = segment_ids[:, None] == segment_ids[None, :]
    scores = mixer_scores(query_rows, key_matrix_rows, relative, same_utterance)
    row_peak = jnp.max(scores, axis=-1, keepdims=True)
    powered = jnp.exp(scores - row_peak)
    row_total = jnp.sum(powered, axis=-1, keepdims=True)
    log_total = row_peak + jnp.log(row_total)
    softmax_rows = (powered / row_total).astype(jnp.bfloat16)
    attention_blend = jnp.einsum(
        "ief,fiv->eiv", softmax_rows, value_matrix_rows, preferred_element_type=jnp.float32
    )
    attention_blend = attention_blend.reshape(frame_count, D).astype(jnp.bfloat16)
    result = values + (flat_dot(attention_blend, weights[5]) + weights[6].astype(jnp.float32))
    return (
        result,
        (
            normed_unit,
            inverse,
            hidden,
            query_rows,
            key_matrix_rows,
            value_matrix_rows,
            log_total,
            attention_blend,
            relative,
            same_utterance,
        ),
    )


def mixer_backward(upstream, saved, weights):
    (
        normed_unit,
        inverse,
        hidden,
        query_rows,
        key_matrix_rows,
        value_matrix_rows,
        log_total,
        attention_blend,
        relative,
        same_utterance,
    ) = saved
    frame_count = upstream.shape[0]
    upstream_low = upstream.astype(jnp.bfloat16)
    output_slope = lead_dot(attention_blend, upstream_low)
    attention_blend_gradient = (
        back_dot(upstream_low, weights[5]).astype(jnp.bfloat16).reshape(frame_count, HEADS, HEAD)
    )
    scores = mixer_scores(query_rows, key_matrix_rows, relative, same_utterance)
    soft_full = jnp.exp(scores - log_total)
    value_grad = jnp.einsum(
        "ybr,byq->ryq",
        soft_full.astype(jnp.bfloat16),
        attention_blend_gradient,
        preferred_element_type=jnp.float32,
    ).reshape(frame_count, D)
    soft_grad = jnp.einsum(
        "jug,fug->ujf",
        attention_blend_gradient,
        value_matrix_rows,
        preferred_element_type=jnp.float32,
    )
    score_grad = soft_full * (soft_grad - jnp.sum(soft_full * soft_grad, axis=-1, keepdims=True))
    table_slope = relative_slope(score_grad, frame_count)
    score_reduced_precision = (HEAD ** (-0.5) * score_grad).astype(jnp.bfloat16)
    query_grad = jnp.einsum(
        "ief,fiv->eiv", score_reduced_precision, key_matrix_rows, preferred_element_type=jnp.float32
    ).reshape(frame_count, D)
    key_grad = jnp.einsum(
        "ybr,byq->ryq", score_reduced_precision, query_rows, preferred_element_type=jnp.float32
    ).reshape(frame_count, D)
    projected_low = jnp.concatenate([query_grad, key_grad, value_grad], axis=1).astype(jnp.bfloat16)
    project_slope = lead_dot(hidden, projected_low)
    hidden_grad = back_dot(projected_low, weights[2])
    input_grad, gain_slope, shift_slope = norm_back(hidden_grad, normed_unit, inverse, weights[0])
    slopes = (
        gain_slope,
        shift_slope,
        project_slope,
        jnp.sum(query_grad, axis=0),
        jnp.sum(value_grad, axis=0),
        output_slope,
        jnp.sum(upstream, axis=0),
        table_slope,
    )
    return (upstream + input_grad, slopes)


def filter_forward(values, segment_ids, weights):
    normed, normed_unit, inverse = norm_apply(values, weights[0], weights[1])
    hidden = normed.astype(jnp.bfloat16)
    widened = flat_dot(hidden, weights[2]) + weights[3].astype(jnp.float32)
    gated_rows = widened[:, :D] * jax.nn.sigmoid(widened[:, D:])
    filtered = depthwise(gated_rows, weights[4].astype(jnp.float32), segment_ids) + weights[
        5
    ].astype(jnp.float32)
    middle, middle_unit, middle_inverse = norm_apply(filtered, weights[6], weights[7])
    swished = (middle * jax.nn.sigmoid(middle)).astype(jnp.bfloat16)
    result = values + (flat_dot(swished, weights[8]) + weights[9].astype(jnp.float32))
    return (
        result,
        (
            normed_unit,
            inverse,
            hidden,
            widened,
            gated_rows,
            middle_unit,
            middle_inverse,
            middle,
            swished,
        ),
    )


def filter_backward(upstream, saved, weights, segment_ids):
    (
        normed_unit,
        inverse,
        hidden,
        widened,
        gated_rows,
        middle_unit,
        middle_inverse,
        middle,
        swished,
    ) = saved
    upstream_low = upstream.astype(jnp.bfloat16)
    down_slope = lead_dot(swished, upstream_low)
    middle_grad = swish_back(back_dot(upstream_low, weights[8]), middle)
    filtered_grad, middle_gain_slope, middle_shift_slope = norm_back(
        middle_grad, middle_unit, middle_inverse, weights[6]
    )

    def local_filter(local_rows, local_kernel):
        return depthwise(local_rows, local_kernel, segment_ids)

    unused, pullback = jax.vjp(local_filter, gated_rows, weights[4].astype(jnp.float32))
    gated_grad, kernel_slope = pullback(filtered_grad)
    opened = jax.nn.sigmoid(widened[:, D:])
    widened_grad = jnp.concatenate(
        [gated_grad * opened, gated_grad * widened[:, :D] * opened * (1.0 - opened)], axis=1
    )
    widened_low = widened_grad.astype(jnp.bfloat16)
    up_slope = lead_dot(hidden, widened_low)
    hidden_grad = back_dot(widened_low, weights[2])
    input_grad, gain_slope, shift_slope = norm_back(hidden_grad, normed_unit, inverse, weights[0])
    slopes = (
        gain_slope,
        shift_slope,
        up_slope,
        jnp.sum(widened_grad, axis=0),
        kernel_slope,
        jnp.sum(filtered_grad, axis=0),
        middle_gain_slope,
        middle_shift_slope,
        down_slope,
        jnp.sum(upstream, axis=0),
    )
    return (upstream + input_grad, slopes)


def body(
    frames,
    segments,
    cotangent,
    early_gain,
    early_shift,
    early_up,
    early_lift,
    early_down,
    early_drop,
    mixer_gain,
    mixer_shift,
    mixer_project,
    query_bias,
    value_bias,
    mixer_output,
    mixer_drop,
    distance_table,
    filter_gain,
    filter_shift,
    filter_up,
    filter_lift,
    depth_weight,
    depth_bias,
    middle_gain,
    middle_shift,
    filter_down,
    filter_drop,
    late_gain,
    late_shift,
    late_up,
    late_lift,
    late_down,
    late_drop,
    final_gain,
    final_shift,
):
    start_rows = frames.astype(jnp.float32)
    final_upstream = cotangent.astype(jnp.float32)
    early_full = fetch_feed(early_gain, early_shift, early_up, early_lift, early_down, early_drop)
    first_rows, early_kept = feed_forward(start_rows, early_full)
    mixer_full = fetch_mixer(
        mixer_gain,
        mixer_shift,
        mixer_project,
        query_bias,
        value_bias,
        mixer_output,
        mixer_drop,
        distance_table,
    )
    second_rows, mixer_kept = mixer_forward(first_rows, segments, mixer_full)
    filter_full = fetch_filter(
        filter_gain,
        filter_shift,
        filter_up,
        filter_lift,
        depth_weight,
        depth_bias,
        middle_gain,
        middle_shift,
        filter_down,
        filter_drop,
        final_gain,
        final_shift,
    )
    third_rows, filter_kept = filter_forward(second_rows, segments, filter_full)
    late_full = fetch_feed(late_gain, late_shift, late_up, late_lift, late_down, late_drop)
    fourth_rows, late_kept = feed_forward(third_rows, late_full)
    layer_out, final_unit, final_inverse = norm_apply(fourth_rows, filter_full[10], filter_full[11])
    final_stats = (final_unit, final_inverse)
    upstream, final_gain_slope, final_shift_slope = norm_back(
        final_upstream, final_stats[0], final_stats[1], filter_full[10]
    )
    upstream, late_slopes = feed_backward(upstream, late_kept, late_full)
    late_summed = reduce_feed(
        late_slopes[0],
        late_slopes[1],
        late_slopes[2],
        late_slopes[3],
        late_slopes[4],
        late_slopes[5],
    )
    upstream, filter_grads = filter_backward(upstream, filter_kept, filter_full, segments)
    filter_summed = reduce_filter(
        filter_grads[0],
        filter_grads[1],
        filter_grads[2],
        filter_grads[3],
        filter_grads[4],
        filter_grads[5],
        filter_grads[6],
        filter_grads[7],
        filter_grads[8],
        filter_grads[9],
        final_gain_slope,
        final_shift_slope,
    )
    upstream, mixer_grads = mixer_backward(upstream, mixer_kept, mixer_full)
    mixer_summed = reduce_mixer(
        mixer_grads[0],
        mixer_grads[1],
        mixer_grads[2],
        mixer_grads[3],
        mixer_grads[4],
        mixer_grads[5],
        mixer_grads[6],
        mixer_grads[7],
    )
    upstream, early_slopes = feed_backward(upstream, early_kept, early_full)
    early_summed = reduce_feed(
        early_slopes[0],
        early_slopes[1],
        early_slopes[2],
        early_slopes[3],
        early_slopes[4],
        early_slopes[5],
    )
    return (
        layer_out,
        upstream,
        early_summed[0],
        early_summed[1],
        early_summed[2],
        early_summed[3],
        early_summed[4],
        early_summed[5],
        mixer_summed[0],
        mixer_summed[1],
        mixer_summed[2],
        mixer_summed[3],
        mixer_summed[4],
        mixer_summed[5],
        mixer_summed[6],
        mixer_summed[7],
        filter_summed[0],
        filter_summed[1],
        filter_summed[2],
        filter_summed[3],
        filter_summed[4],
        filter_summed[5],
        filter_summed[6],
        filter_summed[7],
        filter_summed[8],
        filter_summed[9],
        late_summed[0],
        late_summed[1],
        late_summed[2],
        late_summed[3],
        late_summed[4],
        late_summed[5],
        filter_summed[10],
        filter_summed[11],
    )


def near(me, n):
    if n == 4:
        row, column = me // 2, me % 2
        flip_row, flip_column = (1 - row) * 2 + column, row * 2 + 1 - column
        across = (1 - row) * 2 + 1 - column
        return [(flip_column, flip_column), (flip_row, flip_row), (across, across)]
    return [((me + step) % n, (me + n - step) % n) for step in range(1, n)]


def greet(targets):
    barrier = pltpu.get_barrier_semaphore()
    for target in targets:
        pl.semaphore_signal(barrier, inc=1, device_id={"dp": target}, device_id_type=MESH)
    pl.semaphore_wait(barrier, len(targets))


def greet_all(n, m):
    me, lane = lax.axis_index("dp"), lax.axis_index("fsdp")
    barrier = pltpu.get_barrier_semaphore()

    def say(step, carry):
        target = {"dp": (me + step // m) % n, "fsdp": (lane + step % m) % m}
        pl.semaphore_signal(barrier, inc=1, device_id=target, device_id_type=MESH)
        return carry

    lax.fori_loop(1, n * m, say, 0)
    pl.semaphore_wait(barrier, n * m - 1)


def remote(src, dst, send, recv, target):
    return pltpu.make_async_remote_copy(
        src_ref=src, dst_ref=dst, send_sem=send, recv_sem=recv, device_id=target, device_id_type=MESH
    )


def columns(start, width):
    return pl.ds(pl.multiple_of(start * width, width), width)


def column_pieces(index, n, sizes):
    pieces = []
    for place, (groups, width) in enumerate(sizes):
        for group in range(groups):
            wide = pl.ds(pl.multiple_of((group * n + index) * width, width), width)
            pieces.append((place, wide, pl.ds(group * width, width)))
    return pieces


def row_of(shards, line, first):
    rows = shards.shape[0]
    lines = shards[:, line, :]
    lanes = lax.broadcasted_iota(jnp.int32, lines.shape, 1) // 32
    places = lax.broadcasted_iota(jnp.int32, lines.shape, 0) % 4
    merged = jnp.zeros_like(lines)
    for quarter in range(4):
        shift = (32 * quarter - 32 * first) % LANES
        moved = pltpu.roll(lines, shift, 1) if shift else lines
        merged = merged + jnp.where((lanes == quarter) & (places == quarter), moved, 0.0)
    return [
        jnp.sum(merged[4 * tile : 4 * tile + 4], axis=0, keepdims=True) for tile in range(rows // 4)
    ]


def pack_small(small, singles, lifts, table):
    rows = singles[0].shape[0]
    small[...] = jnp.zeros_like(small)
    for at, single in enumerate(singles):
        line, low = at * rows // LANES, at * rows % LANES
        small[line : line + 1, low : low + rows] = single[...].astype(jnp.float32).reshape(1, rows)
    for at, lift in enumerate(lifts):
        line, count = 5 + at, lift.shape[0]
        small[line : line + 1, 0:count] = lift[...].astype(jnp.float32).reshape(1, count)
    small[8 : 8 + table.shape[0], 0 : table.shape[1]] = table[...].astype(jnp.float32)


def exchange_kernel(n, m, width, inner, *refs):
    early_up, late_up, project, filter_up, output, filter_down, depth, segs, frames = refs[:9]
    singles, lifts, table = refs[9:28], refs[28:31], refs[31]
    early_full, late_split, mixer_split, filter_split, small_all, gains, depth_all, segs_all, spread = refs[32:41]
    scratch = refs[41:]
    small, held, local, send, recv, small_send, small_recv = scratch[:7]
    up_send, up_recv, pass_send, pass_recv, out_send, out_recv, depth_send, depth_recv = scratch[7:]
    pack_small(small, singles, lifts, table)
    me, lane = lax.axis_index("dp"), lax.axis_index("fsdp")
    here = me * m + lane
    half = m // 2
    beside = lane + 1 - 2 * (lane % 2)
    others = near(me, n)
    greet_all(n, m)

    def to_device(step):
        target = {"dp": (me + step // m) % n, "fsdp": (lane + step % m) % m}
        return remote(small, small_all.at[here], small_send.at[step], small_recv.at[step], target)

    def to_lane(step):
        return remote(
            depth, depth_all.at[lane], depth_send.at[step], depth_recv.at[step], {"fsdp": (lane + step) % m}
        )

    def start_depth(step, carry):
        to_lane(step).start()
        return carry

    def wait_depth(step, carry):
        to_lane(step).wait()
        return carry

    def to_column(step):
        other, above = (me + step // half) % n, (lane + 2 * (step % half)) % m
        target = {"dp": other, "fsdp": above}
        return remote(
            early_up.at[:, columns(other, width)], early_full.at[here], up_send.at[step], up_recv.at[step], target
        )

    def to_partner(step):
        source = ((me + n - step // half) % n) * m + (lane + m - 2 * (step % half)) % m
        return remote(
            early_full.at[source], early_full.at[source], pass_send.at[step], pass_recv.at[step], {"fsdp": beside}
        )

    def start_small(step, carry):
        to_device(step).start()
        return carry

    def wait_small(step, carry):
        to_device(step).wait()
        return carry

    def start_column(step, carry):
        to_column(step).start()
        return carry

    def relay_column(step, carry):
        to_column(step).wait_recv()
        to_partner(step).start()
        return carry

    def wait_column(step, carry):
        to_column(step).wait_send()
        to_partner(step).wait()
        return carry

    def pieces(index):
        found = [(late_up.at[:, columns(index, width)], late_split.at[me])]
        for group in range(3):
            wide = pl.ds(pl.multiple_of(group * inner * n + index * inner, inner), inner)
            found.append((project.at[:, wide], mixer_split.at[me, :, pl.ds(group * inner, inner)]))
        for group in range(2):
            wide = pl.ds(pl.multiple_of(group * inner * n + index * inner, inner), inner)
            found.append((filter_up.at[:, wide], filter_split.at[me, :, pl.ds(group * inner, inner)]))
        found.append((segs, segs_all.at[me]))
        return found

    lax.fori_loop(1, n * m, start_small, 0)
    own_small = pltpu.make_async_copy(small, small_all.at[here], local.at[0])
    own_small.start()
    own_up = pltpu.make_async_copy(early_up.at[:, columns(me, width)], early_full.at[here], local.at[1])
    own_up.start()
    lax.fori_loop(1, n * half, start_column, 0)
    copies = []
    for peer, (target, unused) in enumerate(others):
        for at, (src, dst) in enumerate(pieces(target)):
            copies.append(remote(src, dst, send.at[peer, at], recv.at[peer, at], {"dp": target}))
    owns = []
    for src, dst in pieces(me):
        owns.append((src, dst))
    for group in range(n):
        wide = pl.ds(group * inner, inner)
        owns.append((output.at[:, wide], mixer_split.at[group, :, pl.ds(3 * inner, inner)]))
        owns.append((filter_down.at[:, wide], filter_split.at[group, :, pl.ds(2 * inner, inner)]))
    owns = [pltpu.make_async_copy(src, dst, local.at[2 + at]) for at, (src, dst) in enumerate(owns)]
    owns.append(pltpu.make_async_copy(depth, depth_all.at[lane], local.at[2 + len(owns)]))
    for copy in copies + owns:
        copy.start()
    lax.fori_loop(1, m, start_depth, 0)
    own_up.wait()
    to_partner(0).start()
    own_small.wait()
    lax.fori_loop(1, n * m, wait_small, 0)
    for index in range(len(singles)):
        for tile, line in enumerate(row_of(small_all, index // 4, index % 4)):
            gains[index : index + 1, tile * LANES : (tile + 1) * LANES] = line
    gain, shift = gains[0:1, :], gains[1:2, :]

    def work(block, carry):
        span = pl.ds(pl.multiple_of(block * BLOCK, BLOCK), BLOCK)
        unit, inverse = unit_of(frames[span, :].astype(jnp.float32))
        held[span, :] = (unit * gain + shift).astype(jnp.bfloat16)
        return carry

    lax.fori_loop(0, frames.shape[0] // BLOCK, work, 0)
    keep = pltpu.make_async_copy(held, spread.at[me], local.at[len(owns) + 2])
    keep.start()
    outgoing = []
    for peer, (target, unused) in enumerate(others):
        outgoing.append(remote(held, spread.at[me], out_send.at[peer], out_recv.at[peer], {"dp": target}))
    for copy in outgoing:
        copy.start()
    lax.fori_loop(1, n * half, relay_column, 0)
    for copy in owns + copies + outgoing:
        copy.wait()
    keep.wait()
    to_partner(0).wait()
    lax.fori_loop(1, n * half, wait_column, 0)
    lax.fori_loop(1, m, wait_depth, 0)


def exchange(n, m, early_up, late_up, project, filter_up, output, filter_down, depth, segs, frames, singles, lifts, table):
    rows, width = early_up.shape[0], early_up.shape[1] // n
    inner = output.shape[1] // n
    frame_count, deep = frames.shape
    low = jnp.bfloat16
    packed = (16, LANES)
    outs = [
        jax.ShapeDtypeStruct((n * m, rows, width), low),
        jax.ShapeDtypeStruct((n, rows, width), low),
        jax.ShapeDtypeStruct((n, rows, 4 * inner), low),
        jax.ShapeDtypeStruct((n, rows, 3 * inner), low),
        jax.ShapeDtypeStruct((n * m,) + packed, jnp.float32),
        jax.ShapeDtypeStruct((len(singles), deep), jnp.float32),
        jax.ShapeDtypeStruct((m,) + depth.shape, low),
        jax.ShapeDtypeStruct((n,) + segs.shape, segs.dtype),
        jax.ShapeDtypeStruct((n, frame_count, deep), low),
    ]
    anywhere = pl.BlockSpec(memory_space=pl.ANY)
    inside = pl.BlockSpec(memory_space=pltpu.VMEM)
    dma = pltpu.SemaphoreType.DMA
    return pl.pallas_call(
        functools.partial(exchange_kernel, n, m, width, inner),
        out_shape=outs,
        in_specs=[anywhere] * 8 + [inside] * (2 + len(singles) + len(lifts)),
        out_specs=[anywhere] * 4 + [inside] * 2 + [anywhere] * 3,
        scratch_shapes=[
            pltpu.VMEM(packed, jnp.float32),
            pltpu.VMEM((frame_count, deep), low),
            dma((2 * n + 8 + 3,)),
            dma((n - 1, 7)),
            dma((n - 1, 7)),
            dma((n * m,)),
            dma((n * m,)),
            dma((n * m // 2,)),
            dma((n * m // 2,)),
            dma((n * m // 2,)),
            dma((n * m // 2,)),
            dma((n - 1,)),
            dma((n - 1,)),
            dma((m,)),
            dma((m,)),
        ],
        compiler_params=pltpu.CompilerParams(collective_id=0, has_side_effects=True),
        name="exchange",
    )(early_up, late_up, project, filter_up, output, filter_down, depth, segs, frames, *singles, *lifts, table)


def giveback_kernel(n, sizes, *refs):
    count = len(sizes)
    narrows, wides = refs[:count], refs[count : 2 * count]
    local, send, recv = refs[2 * count :]
    me = lax.axis_index("dp")
    others = near(me, n)
    greet([target for target, unused in others])
    copies = []
    for peer, (target, unused) in enumerate(others):
        for at, (place, wide, narrow) in enumerate(column_pieces(me, n, sizes)):
            copies.append(
                remote(narrows[place].at[target, :, narrow], wides[place].at[:, wide], send.at[peer, at], recv.at[peer, at], {"dp": target})
            )
    for at, (place, wide, narrow) in enumerate(column_pieces(me, n, sizes)):
        copies.append(pltpu.make_async_copy(narrows[place].at[me, :, narrow], wides[place].at[:, wide], local.at[at]))
    for copy in copies:
        copy.start()
    for copy in copies:
        copy.wait()


def giveback(n, narrows, sizes, number):
    rows = narrows[0].shape[1]
    total = sum(groups for groups, width in sizes)
    outs = [jax.ShapeDtypeStruct((rows, groups * width * n), jnp.bfloat16) for groups, width in sizes]
    anywhere = pl.BlockSpec(memory_space=pl.ANY)
    return pl.pallas_call(
        functools.partial(giveback_kernel, n, sizes),
        out_shape=outs,
        in_specs=[anywhere] * len(narrows),
        out_specs=[anywhere] * len(outs),
        scratch_shapes=[
            pltpu.SemaphoreType.DMA((total,)),
            pltpu.SemaphoreType.DMA((n - 1, total)),
            pltpu.SemaphoreType.DMA((n - 1, total)),
        ],
        compiler_params=pltpu.CompilerParams(collective_id=number, has_side_effects=True),
        name="giveback",
    )(*narrows)


def share_kernel(n, mine, shared, local, send, recv):
    me = lax.axis_index("dp")
    others = near(me, n)
    greet([target for target, unused in others])
    copies = [pltpu.make_async_copy(mine, shared.at[me], local)]
    for peer, (target, unused) in enumerate(others):
        copies.append(remote(mine, shared.at[me], send.at[peer], recv.at[peer], {"dp": target}))
    for copy in copies:
        copy.start()
    for copy in copies:
        copy.wait()


def share(n, mine, number):
    inside = pl.BlockSpec(memory_space=pltpu.VMEM)
    return pl.pallas_call(
        functools.partial(share_kernel, n),
        out_shape=jax.ShapeDtypeStruct((n,) + mine.shape, mine.dtype),
        in_specs=[inside],
        out_specs=inside,
        scratch_shapes=[
            pltpu.SemaphoreType.DMA,
            pltpu.SemaphoreType.DMA((n - 1,)),
            pltpu.SemaphoreType.DMA((n - 1,)),
        ],
        compiler_params=pltpu.CompilerParams(collective_id=number, has_side_effects=True),
        name="share",
    )(mine)


def collect_kernel(n, m, wide, group, wide_all, group_all, local, send, recv, group_send, group_recv):
    me, lane = lax.axis_index("dp"), lax.axis_index("fsdp")
    here = me * m + lane
    greet_all(n, m)

    def to_device(step):
        other, beside = (me + step // m) % n, (lane + step % m) % m
        return remote(
            wide.at[other * m + beside], wide_all.at[here], send.at[step], recv.at[step], {"dp": other, "fsdp": beside}
        )

    def to_group(step):
        beside = (lane + step) % m
        return remote(group.at[beside], group_all.at[lane], group_send.at[step], group_recv.at[step], {"fsdp": beside})

    def start_wide(step, carry):
        to_device(step).start()
        return carry

    def start_group(step, carry):
        to_group(step).start()
        return carry

    def wait_wide(step, carry):
        to_device(step).wait()
        return carry

    def wait_group(step, carry):
        to_group(step).wait()
        return carry

    own = pltpu.make_async_copy(wide.at[here], wide_all.at[here], local.at[0])
    own_group = pltpu.make_async_copy(group.at[lane], group_all.at[lane], local.at[1])
    own.start()
    own_group.start()
    lax.fori_loop(1, n * m, start_wide, 0)
    lax.fori_loop(1, m, start_group, 0)
    own.wait()
    own_group.wait()
    lax.fori_loop(1, n * m, wait_wide, 0)
    lax.fori_loop(1, m, wait_group, 0)


def collect(n, m, wide, group, number):
    inside = pl.BlockSpec(memory_space=pltpu.VMEM)
    return pl.pallas_call(
        functools.partial(collect_kernel, n, m),
        out_shape=[jax.ShapeDtypeStruct(wide.shape, wide.dtype), jax.ShapeDtypeStruct(group.shape, group.dtype)],
        in_specs=[inside] * 2,
        out_specs=[inside] * 2,
        scratch_shapes=[
            pltpu.SemaphoreType.DMA((2,)),
            pltpu.SemaphoreType.DMA((n * m,)),
            pltpu.SemaphoreType.DMA((n * m,)),
            pltpu.SemaphoreType.DMA((m,)),
            pltpu.SemaphoreType.DMA((m,)),
        ],
        compiler_params=pltpu.CompilerParams(collective_id=number, has_side_effects=True),
        name="collect",
    )(wide, group)


def unit_of(values):
    centered = values - jnp.mean(values, axis=-1, keepdims=True)
    inverse = lax.rsqrt(jnp.mean(centered * centered, axis=-1, keepdims=True) + EPSILON)
    return centered * inverse, inverse


def unit_back(upstream, unit, inverse, gain):
    scaled = upstream * gain
    adjusted = scaled - jnp.mean(scaled, axis=-1, keepdims=True)
    return inverse * (adjusted - unit * jnp.mean(scaled * unit, axis=-1, keepdims=True))


def step_forward(scale, total, states, vectors):
    values = states[0] + scale * (total + vectors[0])
    unit, inverse = unit_of(values)
    return [values], unit * vectors[1] + vectors[2], []


def step_turn(total, states, vectors):
    values = states[0] + 0.5 * (total + vectors[0])
    upstream = states[1]
    unit, inverse = unit_of(values)
    layer_out = unit * vectors[1] + vectors[2]
    grad = unit_back(upstream, unit, inverse, vectors[1])
    half = 0.5 * grad
    return [layer_out, grad], half, [upstream * unit, upstream, half]


def step_backward(scale, total, states, vectors):
    unit, inverse = unit_of(states[1])
    grad = states[0] + unit_back(total, unit, inverse, vectors[0])
    sent = scale * grad
    return [grad], sent, [total * unit, total, sent]


def step_last(total, states, vectors):
    unit, inverse = unit_of(states[1])
    grad = states[0] + unit_back(total, unit, inverse, vectors[0])
    return [grad], None, [total * unit, total]


def boundary_kernel(step, shape, *refs):
    gathered, state_count, out_count, sum_count, picked = shape
    refs = list(refs)
    take = lambda count: [refs.pop(0) for unused in range(count)]
    part = take(1)[0]
    states = take(state_count)
    vectors = take(1)[0]
    outs = take(out_count)
    spread = take(1)[0] if gathered else None
    sums = take(1)[0] if sum_count else None
    arrived, passing, mine, merged, own, local = take(6)
    relay_send, relay_recv, direct_send, direct_recv, merge_send, merge_recv = take(6)
    if gathered:
        held, held_sem, out_send, out_recv, pass_send, pass_recv = take(6)
    partials = take(1)[0] if sum_count else None
    me = lax.axis_index("dp")
    row, column = me // 2, me % 2
    sides = [row * 2 + 1 - column, (1 - row) * 2 + column]
    across = (1 - row) * 2 + 1 - column
    half = own.shape[0] // 2
    height = half // PIECES
    both, places = range(2), range(PIECES)

    def span(axis, piece):
        return pl.ds(axis * half + piece * height, height)

    def inner(piece):
        return pl.ds(piece * height, height)

    def relay(axis, piece):
        return remote(
            part.at[across, span(axis, piece)],
            passing.at[axis, inner(piece)],
            relay_send.at[axis, piece],
            relay_recv.at[axis, piece],
            {"dp": sides[axis]},
        )

    def direct(axis, piece):
        return remote(
            part.at[sides[axis], span(axis, piece)],
            arrived.at[axis, span(axis, piece)],
            direct_send.at[axis, piece],
            direct_recv.at[axis, piece],
            {"dp": sides[axis]},
        )

    def merge(axis, piece):
        return remote(
            merged.at[axis, inner(piece)],
            arrived.at[1 - axis, span(axis, piece)],
            merge_send.at[axis, piece],
            merge_recv.at[axis, piece],
            {"dp": sides[1 - axis]},
        )

    def hand(target, axis, piece):
        return remote(
            held.at[span(axis, piece)],
            spread.at[me, span(axis, piece)],
            out_send.at[target, axis, piece],
            out_recv.at[target, axis, piece],
            {"dp": sides[target]},
        )

    def onward(axis, piece):
        block = spread.at[sides[axis], span(axis, piece)]
        return remote(
            block, block, pass_send.at[axis, piece], pass_recv.at[axis, piece], {"dp": sides[1 - axis]}
        )

    def forward(axis, piece):
        hand(axis, axis, piece).wait_recv()
        onward(axis, piece).start()

    greet(sides)
    for piece in places:
        for axis in both:
            relay(axis, piece).start()
    locals_ = [
        pltpu.make_async_copy(part.at[sides[1 - axis], pl.ds(axis * half, half)], mine.at[axis], local.at[axis])
        for axis in both
    ]
    locals_.append(pltpu.make_async_copy(part.at[me], own, local.at[2]))
    for copy in locals_:
        copy.start()
    for piece in places:
        for axis in both:
            direct(axis, piece).start()
    if sum_count:
        partials[...] = jnp.zeros_like(partials)
    for copy in locals_:
        copy.wait()
    for piece in places:
        for axis in both:
            relay(axis, piece).wait_recv()

            def join(block, carry):
                rows = pl.ds(pl.multiple_of(piece * height + block * BLOCK, BLOCK), BLOCK)
                total = passing[axis, rows, :].astype(jnp.float32) + mine[axis, rows, :].astype(jnp.float32)
                merged[axis, rows, :] = total.astype(jnp.bfloat16)
                return carry

            lax.fori_loop(0, height // BLOCK, join, 0)
            merge(axis, piece).start()
    rows_of = [vectors[pl.ds(index, 1), :] for index in picked]
    order = [(axis, piece) for piece in places for axis in both]
    for at, (axis, piece) in enumerate(order):
        direct(axis, piece).wait_recv()
        merge(axis, piece).wait_recv()

        def work(block, carry):
            rows = pl.ds(pl.multiple_of(axis * half + piece * height + block * BLOCK, BLOCK), BLOCK)
            total = own[rows, :].astype(jnp.float32)
            for side in both:
                total = total + arrived[side, rows, :].astype(jnp.float32)
            made, sent, terms = step(total, [state[rows, :].astype(jnp.float32) for state in states], rows_of)
            for out, value in zip(outs, made):
                out[rows, :] = value
            if gathered:
                held[rows, :] = sent.astype(jnp.bfloat16)
            for index, term in enumerate(terms):
                partials[index] += sum(term[8 * low : 8 * low + 8] for low in range(BLOCK // 8))
            return carry

        lax.fori_loop(0, height // BLOCK, work, 0)
        if gathered:
            for target in both:
                hand(target, axis, piece).start()
            if at >= LAG:
                forward(*order[at - LAG])
    if gathered:
        keep = pltpu.make_async_copy(held, spread.at[me], held_sem)
        keep.start()
        for axis, piece in order[len(order) - LAG :]:
            forward(axis, piece)
    for index in range(sum_count):
        sums[pl.ds(index, 1), :] = jnp.sum(partials[index], axis=0, keepdims=True)
    for axis, piece in order:
        relay(axis, piece).wait_send()
        direct(axis, piece).wait_send()
        merge(axis, piece).wait_send()
    if gathered:
        for axis, piece in order:
            hand(axis, axis, piece).wait_send()
            hand(1 - axis, axis, piece).wait()
        for axis, piece in order:
            onward(axis, piece).wait()
        keep.wait()


def boundary(step, part, states, vectors, picked, out_count, sum_count, number, gathered=True):
    n, rows, width = part.shape
    inside = pl.BlockSpec(memory_space=pltpu.VMEM)
    anywhere = pl.BlockSpec(memory_space=pl.ANY)
    dma = pltpu.SemaphoreType.DMA
    shape = (gathered, len(states), out_count, sum_count, picked)
    low = jnp.bfloat16
    scratch = [
        pltpu.VMEM((2, rows, width), low),
        pltpu.VMEM((2, rows // 2, width), low),
        pltpu.VMEM((2, rows // 2, width), low),
        pltpu.VMEM((2, rows // 2, width), low),
        pltpu.VMEM((rows, width), low),
        dma((3,)),
    ]
    scratch += [dma((2, PIECES))] * 6
    outs = [jax.ShapeDtypeStruct((rows, width), jnp.float32)] * out_count
    out_specs = [inside] * out_count
    if gathered:
        outs.append(jax.ShapeDtypeStruct((n, rows, width), low))
        out_specs.append(anywhere)
        scratch += [pltpu.VMEM((rows, width), low), dma]
        scratch += [dma((2, 2, PIECES))] * 2 + [dma((2, PIECES))] * 2
    if sum_count:
        outs.append(jax.ShapeDtypeStruct((sum_count, width), jnp.float32))
        out_specs.append(inside)
        scratch.append(pltpu.VMEM((sum_count, 8, width), jnp.float32))
    return pl.pallas_call(
        functools.partial(boundary_kernel, step, shape),
        out_shape=outs,
        in_specs=[anywhere] + [inside] * (len(states) + 1),
        out_specs=out_specs,
        scratch_shapes=scratch,
        compiler_params=pltpu.CompilerParams(collective_id=number, has_side_effects=True),
        name="boundary",
    )(part, *states, vectors)


def toeplitz(line, frame_count):
    wide = jnp.broadcast_to(line, (frame_count, NREL))
    return pltpu.roll(wide, NREL - frame_count + 1, 1, stride=1, stride_axis=0)[:, :frame_count]


def head_scores(packed, head, heads, same, bias):
    size = heads * HEAD
    query_rows = packed[:, head * HEAD : (head + 1) * HEAD]
    key_rows = packed[:, size + head * HEAD : size + (head + 1) * HEAD]
    value_rows = packed[:, 2 * size + head * HEAD : 2 * size + (head + 1) * HEAD]
    scores = jnp.where(same, HEAD ** (-0.5) * back_dot(query_rows, key_rows) + bias, MASKED)
    powered = jnp.exp(scores - jnp.max(scores, axis=-1, keepdims=True))
    soft = powered / jnp.sum(powered, axis=-1, keepdims=True)
    return query_rows, key_rows, value_rows, soft


def attend_kernel(heads, packed, segment_rows, segment_columns, table, blended, bias):
    frame_count = packed.shape[1]

    @pl.when(pl.program_id(0) == 0)
    def _():
        for head in range(heads):
            bias[head] = toeplitz(table[pl.ds(head, 1), :], frame_count)

    same = segment_columns[0] == segment_rows[0]
    block = packed[0]
    results = []
    for head in range(heads):
        unused, unused_too, value_rows, soft = head_scores(block, head, heads, same, bias[head])
        results.append(flat_dot(soft.astype(jnp.bfloat16), value_rows).astype(jnp.bfloat16))
    blended[0] = jnp.concatenate(results, axis=1)


def attend(packed, segment_rows, segment_columns, table):
    blocks, frame_count, width = packed.shape
    heads = table.shape[0]
    return pl.pallas_call(
        functools.partial(attend_kernel, heads),
        grid=(blocks,),
        out_shape=jax.ShapeDtypeStruct((blocks, frame_count, width // 3), jnp.bfloat16),
        in_specs=[
            pl.BlockSpec((1, frame_count, width), lambda i: (i, 0, 0)),
            pl.BlockSpec((1, 1, frame_count), lambda i: (i, 0, 0)),
            pl.BlockSpec((1, frame_count, 1), lambda i: (i, 0, 0)),
            pl.BlockSpec((heads, NREL), lambda i: (0, 0)),
        ],
        out_specs=pl.BlockSpec((1, frame_count, width // 3), lambda i: (i, 0, 0)),
        scratch_shapes=[pltpu.VMEM((heads, frame_count, frame_count), jnp.float32)],
        name="attend",
    )(packed, segment_rows, segment_columns, table)


def unattend_kernel(heads, packed, upstream, segment_rows, segment_columns, table, grads, sums, slope, bias, gathered):
    frame_count = packed.shape[1]
    size = heads * HEAD
    at = pl.program_id(0)

    @pl.when(at == 0)
    def _():
        for head in range(heads):
            bias[head] = toeplitz(table[pl.ds(head, 1), :], frame_count)
        gathered[...] = jnp.zeros_like(gathered)
        sums[...] = jnp.zeros_like(sums)

    same = segment_columns[0] == segment_rows[0]
    block = packed[0]
    above = upstream[0]
    query_grads, key_grads, value_grads = [], [], []
    for head in range(heads):
        query_rows, key_rows, value_rows, soft = head_scores(block, head, heads, same, bias[head])
        blend_grad = above[:, head * HEAD : (head + 1) * HEAD]
        value_grads.append(lead_dot(soft.astype(jnp.bfloat16), blend_grad))
        soft_grad = back_dot(blend_grad, value_rows)
        score_grad = soft * (soft_grad - jnp.sum(soft * soft_grad, axis=-1, keepdims=True))
        gathered[head] += score_grad
        low = (HEAD ** (-0.5) * score_grad).astype(jnp.bfloat16)
        query_grads.append(flat_dot(low, key_rows))
        key_grads.append(lead_dot(low, query_rows))
    query_grad = jnp.concatenate(query_grads, axis=1)
    value_grad = jnp.concatenate(value_grads, axis=1)
    grads[0, :, 0:size] = query_grad.astype(jnp.bfloat16)
    grads[0, :, size : 2 * size] = jnp.concatenate(key_grads, axis=1).astype(jnp.bfloat16)
    grads[0, :, 2 * size :] = value_grad.astype(jnp.bfloat16)
    sums[0:1, :] += jnp.sum(query_grad, axis=0, keepdims=True)
    sums[1:2, :] += jnp.sum(value_grad, axis=0, keepdims=True)

    @pl.when(at == pl.num_programs(0) - 1)
    def _():
        places = lax.broadcasted_iota(jnp.int32, (frame_count, NREL), 0)
        for head in range(heads):
            wide = jnp.concatenate(
                [gathered[head], jnp.zeros((frame_count, NREL - frame_count), jnp.float32)], axis=1
            )
            stride = 1
            while stride < frame_count:
                moved = pltpu.roll(wide, NREL - stride, 1)
                wide = jnp.where((places // stride) % 2 == 1, moved, wide)
                stride *= 2
            slope[pl.ds(head, 1), :] = jnp.sum(wide, axis=0, keepdims=True)


def unattend(packed, upstream, segment_rows, segment_columns, table):
    blocks, frame_count, width = packed.shape
    heads = table.shape[0]
    return pl.pallas_call(
        functools.partial(unattend_kernel, heads),
        grid=(blocks,),
        out_shape=[
            jax.ShapeDtypeStruct((blocks, frame_count, width), jnp.bfloat16),
            jax.ShapeDtypeStruct((2, width // 3), jnp.float32),
            jax.ShapeDtypeStruct((heads, NREL), jnp.float32),
        ],
        in_specs=[
            pl.BlockSpec((1, frame_count, width), lambda i: (i, 0, 0)),
            pl.BlockSpec((1, frame_count, width // 3), lambda i: (i, 0, 0)),
            pl.BlockSpec((1, 1, frame_count), lambda i: (i, 0, 0)),
            pl.BlockSpec((1, frame_count, 1), lambda i: (i, 0, 0)),
            pl.BlockSpec((heads, NREL), lambda i: (0, 0)),
        ],
        out_specs=[
            pl.BlockSpec((1, frame_count, width), lambda i: (i, 0, 0)),
            pl.BlockSpec((2, width // 3), lambda i: (0, 0)),
            pl.BlockSpec((heads, NREL), lambda i: (0, 0)),
        ],
        scratch_shapes=[
            pltpu.VMEM((heads, frame_count, frame_count), jnp.float32),
            pltpu.VMEM((heads, frame_count, frame_count), jnp.float32),
        ],
        name="unattend",
    )(packed, upstream, segment_rows, segment_columns, table)


def reach_mask(offset, behind, ahead):
    if offset < 0:
        return behind >= -offset
    return ahead >= offset


def convolve_kernel(opened, behind, ahead, taps, bias, gated, filtered, padded):
    frame_count, channels = gated.shape[1:]
    gates = opened[0, :, 0:channels] * jax.nn.sigmoid(opened[0, :, channels:])
    gated[0] = gates
    padded[pl.ds(0, MARGIN), :] = jnp.zeros((MARGIN, channels), jnp.float32)
    padded[pl.ds(MARGIN + frame_count, MARGIN), :] = jnp.zeros((MARGIN, channels), jnp.float32)
    padded[pl.ds(MARGIN, frame_count), :] = gates
    back = jnp.broadcast_to(behind[0], (frame_count, LANES))
    front = jnp.broadcast_to(ahead[0], (frame_count, LANES))
    for low in range(0, channels, LANES):
        lanes = slice(low, low + LANES)
        running = jnp.broadcast_to(bias[:, lanes], (frame_count, LANES))
        for tap in range(KW):
            offset = tap - (KW - 1) // 2
            moved = padded[pl.ds(MARGIN + offset, frame_count), lanes]
            if offset:
                moved = jnp.where(reach_mask(offset, back, front), moved, 0.0)
            running = running + moved * taps[pl.ds(tap, 1), lanes]
        filtered[0, :, lanes] = running


def convolve(opened, behind, ahead, taps, bias):
    blocks, frame_count, width = opened.shape
    channels = width // 2
    rows = pl.BlockSpec((1, frame_count, channels), lambda i: (i, 0, 0))
    places = pl.BlockSpec((1, frame_count, 1), lambda i: (i, 0, 0))
    return pl.pallas_call(
        convolve_kernel,
        grid=(blocks,),
        out_shape=[jax.ShapeDtypeStruct((blocks, frame_count, channels), jnp.float32)] * 2,
        in_specs=[
            pl.BlockSpec((1, frame_count, width), lambda i: (i, 0, 0)),
            places,
            places,
            pl.BlockSpec((KW, channels), lambda i: (0, 0)),
            pl.BlockSpec((1, channels), lambda i: (0, 0)),
        ],
        out_specs=[rows, rows],
        scratch_shapes=[pltpu.VMEM((frame_count + 2 * MARGIN, channels), jnp.float32)],
        name="convolve",
    )(opened, behind, ahead, taps, bias)


def unconvolve_kernel(opened, gated, upstream, behind, ahead, taps, grads, lifts, slopes, padded, padded_grad):
    frame_count, channels = gated.shape[1:]

    @pl.when(pl.program_id(0) == 0)
    def _():
        lifts[...] = jnp.zeros_like(lifts)
        slopes[...] = jnp.zeros_like(slopes)

    for store, value in ((padded, gated[0]), (padded_grad, upstream[0])):
        store[pl.ds(0, MARGIN), :] = jnp.zeros((MARGIN, channels), jnp.float32)
        store[pl.ds(MARGIN + frame_count, MARGIN), :] = jnp.zeros((MARGIN, channels), jnp.float32)
        store[pl.ds(MARGIN, frame_count), :] = value
    back = jnp.broadcast_to(behind[0], (frame_count, LANES))
    front = jnp.broadcast_to(ahead[0], (frame_count, LANES))
    for low in range(0, channels, LANES):
        lanes = slice(low, low + LANES)
        above = upstream[0, :, lanes]
        running = jnp.zeros((frame_count, LANES), jnp.float32)
        for tap in range(KW):
            offset = tap - (KW - 1) // 2
            moved = padded[pl.ds(MARGIN + offset, frame_count), lanes]
            moved_grad = padded_grad[pl.ds(MARGIN + offset, frame_count), lanes]
            if offset:
                mask = reach_mask(offset, back, front)
                moved = jnp.where(mask, moved, 0.0)
                moved_grad = jnp.where(mask, moved_grad, 0.0)
            running = running + moved_grad * taps[pl.ds(KW - 1 - tap, 1), lanes]
            slopes[pl.ds(tap, 1), lanes] += jnp.sum(moved * above, axis=0, keepdims=True)
        slopes[pl.ds(KW, 1), lanes] += jnp.sum(above, axis=0, keepdims=True)
        wide = slice(channels + low, channels + low + LANES)
        left, gate = opened[0, :, lanes], jax.nn.sigmoid(opened[0, :, wide])
        left_grad = running * gate
        gate_grad = running * left * gate * (1.0 - gate)
        grads[0, :, lanes] = left_grad.astype(jnp.bfloat16)
        grads[0, :, wide] = gate_grad.astype(jnp.bfloat16)
        lifts[:, lanes] += jnp.sum(left_grad, axis=0, keepdims=True)
        lifts[:, wide] += jnp.sum(gate_grad, axis=0, keepdims=True)


def unconvolve(opened, gated, upstream, behind, ahead, taps):
    blocks, frame_count, width = opened.shape
    channels = width // 2
    wide = pl.BlockSpec((1, frame_count, width), lambda i: (i, 0, 0))
    rows = pl.BlockSpec((1, frame_count, channels), lambda i: (i, 0, 0))
    places = pl.BlockSpec((1, frame_count, 1), lambda i: (i, 0, 0))
    return pl.pallas_call(
        unconvolve_kernel,
        grid=(blocks,),
        out_shape=[
            jax.ShapeDtypeStruct((blocks, frame_count, width), jnp.bfloat16),
            jax.ShapeDtypeStruct((1, width), jnp.float32),
            jax.ShapeDtypeStruct((KW + 1, channels), jnp.float32),
        ],
        in_specs=[wide, rows, rows, places, places, pl.BlockSpec((KW, channels), lambda i: (0, 0))],
        out_specs=[
            wide,
            pl.BlockSpec((1, width), lambda i: (0, 0)),
            pl.BlockSpec((KW + 1, channels), lambda i: (0, 0)),
        ],
        scratch_shapes=[pltpu.VMEM((frame_count + 2 * MARGIN, channels), jnp.float32)] * 2,
        name="unconvolve",
    )(opened, gated, upstream, behind, ahead, taps)


def gather_rows(value):
    return lax.all_gather(value, "fsdp", axis=0, tiled=True)


def gather_split(value):
    full = lax.all_gather(value, "fsdp", axis=1, tiled=True)
    return full.reshape(-1, full.shape[-1])


def scatter_rows(value):
    return lax.psum_scatter(value.astype(jnp.bfloat16), "fsdp", scatter_dimension=0, tiled=True)


def scatter_split(value, n):
    value = value.astype(jnp.bfloat16).reshape(n, value.shape[0] // n, value.shape[1])
    return lax.psum_scatter(value, "fsdp", scatter_dimension=1, tiled=True)


def pair_slopes(up_slope, down_slope, n):
    inner = down_slope.shape[0]
    up_slope = up_slope.reshape(n, inner, -1)
    down_slope = jnp.transpose(down_slope.reshape(inner, n, inner), (1, 0, 2))
    return jnp.concatenate([up_slope, down_slope], axis=2)


def flat(value):
    return value.reshape(-1, value.shape[-1])


def split_body(
    n,
    m,
    frames,
    segments,
    cotangent,
    early_gain,
    early_shift,
    early_up,
    early_lift,
    early_down,
    early_drop,
    mixer_gain,
    mixer_shift,
    mixer_project,
    query_bias,
    value_bias,
    mixer_output,
    mixer_drop,
    distance_table,
    filter_gain,
    filter_shift,
    filter_up,
    filter_lift,
    depth_weight,
    depth_bias,
    middle_gain,
    middle_shift,
    filter_down,
    filter_drop,
    late_gain,
    late_shift,
    late_up,
    late_lift,
    late_down,
    late_drop,
    final_gain,
    final_shift,
):
    me = lax.axis_index("dp")
    frame_count = frames.shape[0]
    rows = early_gain.shape[0]
    hidden = early_up.shape[1] // n
    inner = D // n
    heads = HEADS // n
    singles = [
        early_gain, early_shift, early_drop, mixer_gain, mixer_shift, query_bias, value_bias, mixer_drop,
        filter_gain, filter_shift, depth_bias, middle_gain, middle_shift, filter_drop, late_gain, late_shift,
        late_drop, final_gain, final_shift,
    ]
    spans = hidden * n // D
    w_early_down = gather_rows(early_down)
    (
        w_early_up, late_up_split, mixer_split, filter_split, small_all, vectors, depth_all, segments_all, early_hidden
    ) = exchange(
        n, m, early_up, late_up, mixer_project, filter_up, mixer_output, filter_down, depth_weight,
        segments.reshape(1, frame_count), frames, singles, [early_lift, late_lift, filter_lift], distance_table,
    )
    w_early_up = w_early_up.reshape(D, hidden)
    w_mixer = lax.all_gather(mixer_split, "fsdp", axis=1, tiled=True)
    w_filter = lax.all_gather(filter_split, "fsdp", axis=1, tiled=True)
    w_late_up = gather_split(late_up_split)
    w_late_down = gather_rows(late_down)

    lines = -(-len(singles) * rows // LANES)
    own_vectors = lax.dynamic_slice(vectors, (0, me * inner), (vectors.shape[0], inner))
    own_lifts = lax.dynamic_slice(small_all, (me * m, lines, 0), (m, 2, LANES))
    early_lifts, late_lifts = own_lifts[:, 0].reshape(-1), own_lifts[:, 1].reshape(-1)
    filter_lifts = small_all[:, lines + 2, : 2 * D // (n * m)].reshape(2, D)
    filter_lifts = lax.dynamic_slice(filter_lifts, (0, me * inner), (2, inner)).reshape(2 * inner)
    table = small_all[:, 8 : 8 + distance_table.shape[0], :HEADS].reshape(NREL, HEADS)
    table = jnp.transpose(lax.dynamic_slice(table, (0, me * heads), (NREL, heads)))[:, ::-1]
    taps = jnp.transpose(depth_all.reshape(inner, KW)).astype(jnp.float32)
    attention_shift = jnp.concatenate([own_vectors[5], jnp.zeros((inner,), jnp.float32), own_vectors[6]])
    segment_rows = segments_all
    segment_columns = segments_all.reshape(n, frame_count, 1)
    places = jnp.arange(frame_count, dtype=jnp.int32)[None, :]
    lower = (segment_rows < segment_columns).astype(jnp.int32)
    upto = (segment_rows <= segment_columns).astype(jnp.int32)
    behind = (places - jnp.sum(lower, axis=-1)).reshape(n, frame_count, 1)
    ahead = (jnp.sum(upto, axis=-1) - 1 - places).reshape(n, frame_count, 1)

    def blocks(value):
        return value.reshape(n, frame_count, value.shape[-1])

    def feed(hidden_rows, w_up, lifts, w_down):
        widened = flat_dot(flat(hidden_rows), w_up) + lifts
        active = (widened * jax.nn.sigmoid(widened)).astype(jnp.bfloat16)
        return widened, active, blocks(flat_dot(active, w_down).astype(jnp.bfloat16))

    def feed_back(low, hidden_rows, widened, active, w_up, w_down):
        low = flat(low)
        down_slope = lead_dot(active, low).astype(jnp.bfloat16)
        widened_grad = swish_back(back_dot(low, w_down), widened)
        widened_low = widened_grad.astype(jnp.bfloat16)
        up_slope = lead_dot(flat(hidden_rows), widened_low).astype(jnp.bfloat16)
        part = blocks(back_dot(widened_low, w_up).astype(jnp.bfloat16))
        down_slope = jnp.transpose(down_slope.reshape(m, spans, rows, D), (1, 0, 2, 3)).reshape(spans, m * rows, D)
        slope = jnp.concatenate([up_slope.reshape(n, D // n, hidden), down_slope])
        part, slope = lax.optimization_barrier((part, slope))
        return part, slope, jnp.sum(widened_grad, axis=0)

    early_wide, early_active, part = feed(early_hidden, w_early_up, early_lifts, w_early_down)
    first_rows, mixer_hidden = boundary(
        functools.partial(step_forward, 0.5), part, [frames], vectors, (2, 3, 4), 1, 0, 2
    )
    mixer_hidden, w_mixer = lax.optimization_barrier((mixer_hidden, w_mixer))
    w_project = w_mixer[:, :, : 3 * inner].reshape(D, 3 * inner)
    w_output = jnp.transpose(w_mixer[:, :, 3 * inner :], (1, 0, 2)).reshape(inner, D)
    packed = blocks((flat_dot(flat(mixer_hidden), w_project) + attention_shift).astype(jnp.bfloat16))
    blended = attend(packed, segment_rows, segment_columns, table)
    part = blocks(flat_dot(flat(blended), w_output).astype(jnp.bfloat16))
    second_rows, filter_hidden = boundary(
        functools.partial(step_forward, 1.0), part, [first_rows], vectors, (7, 8, 9), 1, 0, 3
    )
    filter_hidden, w_filter = lax.optimization_barrier((filter_hidden, w_filter))
    w_filter_up = w_filter[:, :, : 2 * inner].reshape(D, 2 * inner)
    w_filter_down = jnp.transpose(w_filter[:, :, 2 * inner :], (1, 0, 2)).reshape(inner, D)
    opened = blocks(flat_dot(flat(filter_hidden), w_filter_up) + filter_lifts)
    gated, filtered = convolve(opened, behind, ahead, taps, own_vectors[10:11])
    filtered = flat(filtered)
    local_mean = jnp.mean(filtered, axis=-1)
    local_square = jnp.sum((filtered - local_mean[:, None]) ** 2, axis=-1)
    shared = share(
        n, jnp.concatenate([local_mean.reshape(n, frame_count), local_square.reshape(n, frame_count)]), 4
    )
    means, squares = shared[:, :n], shared[:, n:]
    middle_mean = jnp.mean(means, axis=0)
    spread = jnp.sum(squares, axis=0) + inner * jnp.sum((means - middle_mean) ** 2, axis=0)
    middle_inverse = lax.rsqrt(spread / D + EPSILON).reshape(-1, 1)
    middle_unit = (filtered - middle_mean.reshape(-1, 1)) * middle_inverse
    middle = middle_unit * own_vectors[11] + own_vectors[12]
    swished = (middle * jax.nn.sigmoid(middle)).astype(jnp.bfloat16)
    part = blocks(flat_dot(swished, w_filter_down).astype(jnp.bfloat16))
    third_rows, late_hidden = boundary(
        functools.partial(step_forward, 1.0), part, [second_rows], vectors, (13, 14, 15), 1, 0, 5
    )
    late_hidden, w_late_up, w_late_down = lax.optimization_barrier((late_hidden, w_late_up, w_late_down))
    late_wide, late_active, part = feed(late_hidden, w_late_up, late_lifts, w_late_down)
    layer_out, grad, low, turn_sums = boundary(
        step_turn, part, [third_rows, cotangent], vectors, (16, 17, 18), 2, 3, 6
    )

    part, late_slope, late_lift_slope = feed_back(
        low, late_hidden, late_wide, late_active, w_late_up, w_late_down
    )
    late_slope = lax.psum_scatter(late_slope, "fsdp", scatter_dimension=1, tiled=True)
    grad, low, late_sums = boundary(
        functools.partial(step_backward, 1.0), part, [grad, third_rows], vectors, (14,), 1, 3, 7
    )
    low = flat(low)
    filter_down_slope = lead_dot(swished, low).astype(jnp.bfloat16)
    middle_grad = swish_back(back_dot(low, w_filter_down), middle)
    middle_gain_slope = jnp.sum(middle_grad * middle_unit, axis=0)
    middle_shift_slope = jnp.sum(middle_grad, axis=0)
    scaled = middle_grad * own_vectors[11]
    shared = share(
        n,
        jnp.concatenate(
            [
                jnp.sum(scaled, axis=-1).reshape(n, frame_count),
                jnp.sum(scaled * middle_unit, axis=-1).reshape(n, frame_count),
            ]
        ),
        8,
    )
    totals = jnp.sum(shared, axis=0) / D
    filtered_grad = middle_inverse * (
        scaled - totals[:n].reshape(-1, 1) - middle_unit * totals[n:].reshape(-1, 1)
    )
    opened_low, filter_lift_slope, depth_slope = unconvolve(
        opened, gated, blocks(filtered_grad), behind, ahead, taps
    )
    opened_low = flat(opened_low)
    filter_up_slope = lead_dot(flat(filter_hidden), opened_low).astype(jnp.bfloat16)
    part = blocks(back_dot(opened_low, w_filter_up).astype(jnp.bfloat16))
    part, filter_slope = lax.optimization_barrier((part, pair_slopes(filter_up_slope, filter_down_slope, n)))
    filter_slope = lax.psum_scatter(filter_slope, "fsdp", scatter_dimension=1, tiled=True)
    grad, low, filter_sums = boundary(
        functools.partial(step_backward, 1.0), part, [grad, second_rows], vectors, (8,), 1, 3, 9
    )
    low = flat(low)
    output_slope = lead_dot(flat(blended), low).astype(jnp.bfloat16)
    blend_grad = blocks(back_dot(low, w_output).astype(jnp.bfloat16))
    packed_low, shift_sums, table_slope = unattend(packed, blend_grad, segment_rows, segment_columns, table)
    packed_low = flat(packed_low)
    project_slope = lead_dot(flat(mixer_hidden), packed_low).astype(jnp.bfloat16)
    part = blocks(back_dot(packed_low, w_project).astype(jnp.bfloat16))
    part, mixer_slope, late_slope = lax.optimization_barrier(
        (part, pair_slopes(project_slope, output_slope, n), late_slope)
    )
    mixer_slope = lax.psum_scatter(mixer_slope, "fsdp", scatter_dimension=1, tiled=True)
    grad, low, mixer_sums = boundary(
        functools.partial(step_backward, 0.5), part, [grad, first_rows], vectors, (3,), 1, 3, 10
    )
    part, early_slope, early_lift_slope = feed_back(
        low, early_hidden, early_wide, early_active, w_early_up, w_early_down
    )
    part, early_slope, filter_slope = lax.optimization_barrier((part, early_slope, filter_slope))
    early_slope = lax.psum_scatter(early_slope, "fsdp", scatter_dimension=1, tiled=True)
    slope_frames, early_sums = boundary(
        step_last, part, [grad, frames], vectors, (0,), 1, 2, 11, gathered=False
    )

    table_slope = jnp.roll(table_slope[:, ::-1], 1 - NREL // 2, axis=1)
    table_rows = NREL // (n * m)
    wide = jnp.concatenate([turn_sums, late_sums, filter_sums, mixer_sums, early_sums])
    wide_count = wide.shape[0]
    wide = jnp.transpose(wide.reshape(wide_count, n * m, rows), (1, 0, 2)).reshape(n * m, wide_count * rows)
    wide = jnp.concatenate(
        [wide, jnp.transpose(table_slope.reshape(heads, n * m, table_rows), (1, 0, 2)).reshape(n * m, -1)], axis=1
    )
    lift_full = lax.dynamic_update_slice(
        jnp.zeros((2, D), jnp.float32), filter_lift_slope.reshape(2, inner), (0, me * inner)
    ).reshape(n * m, -1)
    table_used = wide.shape[1]
    wide = jnp.concatenate([wide, lift_full], axis=1)
    wide_used = wide.shape[1]
    wide = jnp.pad(wide, ((0, 0), (0, -wide_used % LANES))).reshape(n * m, -1, LANES)
    group = jnp.concatenate(
        [
            shift_sums,
            middle_gain_slope[None],
            middle_shift_slope[None],
            depth_slope,
            jnp.transpose(early_lift_slope.reshape(inner, spans)),
            jnp.transpose(late_lift_slope.reshape(inner, spans)),
        ]
    )
    group_count = group.shape[0]
    group = jnp.transpose(group.reshape(group_count, m, rows), (1, 0, 2)).reshape(m, group_count * rows)
    group_used = group.shape[1]
    group = jnp.pad(group, ((0, 0), (0, -group_used % LANES))).reshape(m, -1, LANES)
    wide_all, group_all = collect(n, m, wide, group, 12)
    wide_all, mixer_slope = lax.optimization_barrier((wide_all, mixer_slope))
    tables = wide_all.reshape(n, m, -1)[:, :, wide_count * rows : table_used]
    wide = jnp.sum(wide_all, axis=0).reshape(-1)
    lift_total = wide[table_used:wide_used]
    wide = wide[: wide_count * rows].reshape(wide_count, rows)
    tables = jnp.transpose(jnp.sum(tables, axis=1).reshape(HEADS, table_rows))
    group = jnp.sum(group_all, axis=0).reshape(-1)[:group_used].reshape(group_count, rows)
    late_up_wide, project_wide, filter_up_wide = giveback(
        n, [late_slope, mixer_slope, filter_slope], [(1, hidden), (3, inner), (2, inner)], 13
    )
    (early_up_wide,) = giveback(n, [early_slope], [(1, hidden)], 14)

    def rejoin(value, low):
        return final(jnp.transpose(value[:, :, low:], (1, 0, 2)).reshape(rows, D))

    def final(value):
        return value.astype(jnp.float32)

    lift_slopes = KW + 5
    return (
        layer_out,
        slope_frames,
        wide[12],
        wide[13],
        final(early_up_wide),
        jnp.transpose(group[lift_slopes : lift_slopes + spans]).reshape(-1),
        final(early_slope[n:]).reshape(spans * rows, D),
        wide[11],
        wide[9],
        wide[10],
        final(project_wide),
        group[0],
        group[1],
        rejoin(mixer_slope, 3 * inner),
        wide[8],
        tables,
        wide[6],
        wide[7],
        final(filter_up_wide),
        lift_total,
        jnp.transpose(group[4 : 4 + KW]),
        group[4 + KW],
        group[2],
        group[3],
        rejoin(filter_slope, 2 * inner),
        wide[5],
        wide[3],
        wide[4],
        final(late_up_wide),
        jnp.transpose(group[lift_slopes + spans : lift_slopes + 2 * spans]).reshape(-1),
        final(late_slope[n:]).reshape(spans * rows, D),
        wide[2],
        wide[0],
        wide[1],
    )


def solution(mesh):
    in_specs = (
        P(("dp", "fsdp"), None),
        P(("dp", "fsdp")),
        P(("dp", "fsdp"), None),
        P(("dp", "fsdp")),
        P(("dp", "fsdp")),
        P(("dp", "fsdp"), None),
        P(("dp", "fsdp")),
        P(("dp", "fsdp"), None),
        P(("dp", "fsdp")),
        P(("dp", "fsdp")),
        P(("dp", "fsdp")),
        P(("dp", "fsdp"), None),
        P(("dp", "fsdp")),
        P(("dp", "fsdp")),
        P(("dp", "fsdp"), None),
        P(("dp", "fsdp")),
        P(("dp", "fsdp"), None),
        P(("dp", "fsdp")),
        P(("dp", "fsdp")),
        P(("dp", "fsdp"), None),
        P(("dp", "fsdp")),
        P(("dp", "fsdp"), None),
        P(("dp", "fsdp")),
        P(("dp", "fsdp")),
        P(("dp", "fsdp")),
        P(("dp", "fsdp"), None),
        P(("dp", "fsdp")),
        P(("dp", "fsdp")),
        P(("dp", "fsdp")),
        P(("dp", "fsdp"), None),
        P(("dp", "fsdp")),
        P(("dp", "fsdp"), None),
        P(("dp", "fsdp")),
        P(("dp", "fsdp")),
        P(("dp", "fsdp")),
    )
    out_specs = (
        P(("dp", "fsdp"), None),
        P(("dp", "fsdp"), None),
        P(("dp", "fsdp")),
        P(("dp", "fsdp")),
        P(("dp", "fsdp"), None),
        P(("dp", "fsdp")),
        P(("dp", "fsdp"), None),
        P(("dp", "fsdp")),
        P(("dp", "fsdp")),
        P(("dp", "fsdp")),
        P(("dp", "fsdp"), None),
        P(("dp", "fsdp")),
        P(("dp", "fsdp")),
        P(("dp", "fsdp"), None),
        P(("dp", "fsdp")),
        P(("dp", "fsdp"), None),
        P(("dp", "fsdp")),
        P(("dp", "fsdp")),
        P(("dp", "fsdp"), None),
        P(("dp", "fsdp")),
        P(("dp", "fsdp"), None),
        P(("dp", "fsdp")),
        P(("dp", "fsdp")),
        P(("dp", "fsdp")),
        P(("dp", "fsdp"), None),
        P(("dp", "fsdp")),
        P(("dp", "fsdp")),
        P(("dp", "fsdp")),
        P(("dp", "fsdp"), None),
        P(("dp", "fsdp")),
        P(("dp", "fsdp"), None),
        P(("dp", "fsdp")),
        P(("dp", "fsdp")),
        P(("dp", "fsdp")),
    )
    n, m = mesh.shape["dp"], mesh.shape["fsdp"]
    run = functools.partial(split_body, n, m) if n == 4 and D // (n * m) == 32 else body
    return jax.shard_map(run, mesh=mesh, in_specs=in_specs, out_specs=out_specs, check_vma=False)
```

```python
import functools

import jax
import jax.numpy as jnp
from jax import lax
from jax.experimental import pallas as pl
from jax.experimental.pallas import tpu as pltpu
from jax.sharding import PartitionSpec as P

D = 1024
HEADS = 16
HEAD = 64
KW = 31
NREL = 256


EPSILON = 1e-05
MASKED = -1e30
UTTERANCE_LIMIT = 4
MESH = pl.DeviceIdType.MESH
PIECES = 2
LAG = 2
BLOCK = 16
MARGIN = 16
LANES = 128


def flat_dot(left_rows, right_rows):
    return jnp.dot(left_rows, right_rows, preferred_element_type=jnp.float32)


def lead_dot(left_rows, right_rows):
    return lax.dot_general(
        left_rows, right_rows, (((0,), (0,)), ((), ())), preferred_element_type=jnp.float32
    )


def back_dot(left_rows, right_rows):
    return lax.dot_general(
        left_rows, right_rows, (((1,), (1,)), ((), ())), preferred_element_type=jnp.float32
    )


def norm_apply(values, norm_gain, norm_shift):
    centered = values - jnp.mean(values, axis=-1, keepdims=True)
    inverse = lax.rsqrt(jnp.mean(centered * centered, axis=-1, keepdims=True) + EPSILON)
    normed_unit = centered * inverse
    return (
        normed_unit * norm_gain.astype(jnp.float32) + norm_shift.astype(jnp.float32),
        normed_unit,
        inverse,
    )


def norm_back(upstream, normed_unit, inverse, norm_gain):
    scaled = upstream * norm_gain.astype(jnp.float32)
    adjusted = scaled - jnp.mean(scaled, axis=-1, keepdims=True)
    adjusted = adjusted - normed_unit * jnp.mean(scaled * normed_unit, axis=-1, keepdims=True)
    return (inverse * adjusted, jnp.sum(upstream * normed_unit, axis=0), jnp.sum(upstream, axis=0))


def swish_back(upstream, before):
    sigmoid_rows = jax.nn.sigmoid(before)
    return upstream * sigmoid_rows * (1.0 + before * (1.0 - sigmoid_rows))


def depthwise(gated_rows, kernel, segment_ids):
    margin = (KW - 1) // 2
    channels = gated_rows.shape[1]
    taps = jnp.transpose(kernel)[:, None, :]
    running = jnp.zeros_like(gated_rows)
    for utterance in range(UTTERANCE_LIMIT):
        inside = (segment_ids == utterance)[:, None]
        masked_rows = jnp.where(inside, gated_rows, 0.0)
        convolved = lax.conv_general_dilated(
            masked_rows[None],
            taps,
            (1,),
            ((margin, margin),),
            dimension_numbers=("NWC", "WIO", "NWC"),
            feature_group_count=channels,
            precision=lax.Precision.HIGHEST,
        )[0]
        running = running + jnp.where(inside, convolved, 0.0)
    return running


def fetch_feed(norm_gain, norm_shift, w_up, up_shift, w_down, down_shift):
    return (
        lax.all_gather(norm_gain, ("dp", "fsdp"), axis=0, tiled=True),
        lax.all_gather(norm_shift, ("dp", "fsdp"), axis=0, tiled=True),
        lax.all_gather(w_up, ("dp", "fsdp"), axis=0, tiled=True),
        lax.all_gather(up_shift, ("dp", "fsdp"), axis=0, tiled=True),
        lax.all_gather(w_down, ("dp", "fsdp"), axis=0, tiled=True),
        lax.all_gather(down_shift, ("dp", "fsdp"), axis=0, tiled=True),
    )


def reduce_feed(norm_gain, norm_shift, w_up, up_shift, w_down, down_shift):
    return (
        lax.psum_scatter(norm_gain, ("dp", "fsdp"), scatter_dimension=0, tiled=True),
        lax.psum_scatter(norm_shift, ("dp", "fsdp"), scatter_dimension=0, tiled=True),
        lax.psum_scatter(w_up, ("dp", "fsdp"), scatter_dimension=0, tiled=True),
        lax.psum_scatter(up_shift, ("dp", "fsdp"), scatter_dimension=0, tiled=True),
        lax.psum_scatter(w_down, ("dp", "fsdp"), scatter_dimension=0, tiled=True),
        lax.psum_scatter(down_shift, ("dp", "fsdp"), scatter_dimension=0, tiled=True),
    )


def fetch_mixer(
    norm_gain, norm_shift, w_project, query_shift, value_shift, w_output, output_shift, table_rows
):
    return (
        lax.all_gather(norm_gain, ("dp", "fsdp"), axis=0, tiled=True),
        lax.all_gather(norm_shift, ("dp", "fsdp"), axis=0, tiled=True),
        lax.all_gather(w_project, ("dp", "fsdp"), axis=0, tiled=True),
        lax.all_gather(query_shift, ("dp", "fsdp"), axis=0, tiled=True),
        lax.all_gather(value_shift, ("dp", "fsdp"), axis=0, tiled=True),
        lax.all_gather(w_output, ("dp", "fsdp"), axis=0, tiled=True),
        lax.all_gather(output_shift, ("dp", "fsdp"), axis=0, tiled=True),
        lax.all_gather(table_rows, ("dp", "fsdp"), axis=0, tiled=True),
    )


def reduce_mixer(
    norm_gain, norm_shift, w_project, query_shift, value_shift, w_output, output_shift, table_rows
):
    return (
        lax.psum_scatter(norm_gain, ("dp", "fsdp"), scatter_dimension=0, tiled=True),
        lax.psum_scatter(norm_shift, ("dp", "fsdp"), scatter_dimension=0, tiled=True),
        lax.psum_scatter(w_project, ("dp", "fsdp"), scatter_dimension=0, tiled=True),
        lax.psum_scatter(query_shift, ("dp", "fsdp"), scatter_dimension=0, tiled=True),
        lax.psum_scatter(value_shift, ("dp", "fsdp"), scatter_dimension=0, tiled=True),
        lax.psum_scatter(w_output, ("dp", "fsdp"), scatter_dimension=0, tiled=True),
        lax.psum_scatter(output_shift, ("dp", "fsdp"), scatter_dimension=0, tiled=True),
        lax.psum_scatter(table_rows, ("dp", "fsdp"), scatter_dimension=0, tiled=True),
    )


def fetch_filter(
    norm_gain,
    norm_shift,
    w_up,
    up_shift,
    depth_taps,
    depth_shift,
    middle_gain,
    middle_shift,
    w_down,
    down_shift,
    last_gain,
    last_shift,
):
    return (
        lax.all_gather(norm_gain, ("dp", "fsdp"), axis=0, tiled=True),
        lax.all_gather(norm_shift, ("dp", "fsdp"), axis=0, tiled=True),
        lax.all_gather(w_up, ("dp", "fsdp"), axis=0, tiled=True),
        lax.all_gather(up_shift, ("dp", "fsdp"), axis=0, tiled=True),
        lax.all_gather(depth_taps, ("dp", "fsdp"), axis=0, tiled=True),
        lax.all_gather(depth_shift, ("dp", "fsdp"), axis=0, tiled=True),
        lax.all_gather(middle_gain, ("dp", "fsdp"), axis=0, tiled=True),
        lax.all_gather(middle_shift, ("dp", "fsdp"), axis=0, tiled=True),
        lax.all_gather(w_down, ("dp", "fsdp"), axis=0, tiled=True),
        lax.all_gather(down_shift, ("dp", "fsdp"), axis=0, tiled=True),
        lax.all_gather(last_gain, ("dp", "fsdp"), axis=0, tiled=True),
        lax.all_gather(last_shift, ("dp", "fsdp"), axis=0, tiled=True),
    )


def reduce_filter(
    norm_gain,
    norm_shift,
    w_up,
    up_shift,
    depth_taps,
    depth_shift,
    middle_gain,
    middle_shift,
    w_down,
    down_shift,
    last_gain,
    last_shift,
):
    return (
        lax.psum_scatter(norm_gain, ("dp", "fsdp"), scatter_dimension=0, tiled=True),
        lax.psum_scatter(norm_shift, ("dp", "fsdp"), scatter_dimension=0, tiled=True),
        lax.psum_scatter(w_up, ("dp", "fsdp"), scatter_dimension=0, tiled=True),
        lax.psum_scatter(up_shift, ("dp", "fsdp"), scatter_dimension=0, tiled=True),
        lax.psum_scatter(depth_taps, ("dp", "fsdp"), scatter_dimension=0, tiled=True),
        lax.psum_scatter(depth_shift, ("dp", "fsdp"), scatter_dimension=0, tiled=True),
        lax.psum_scatter(middle_gain, ("dp", "fsdp"), scatter_dimension=0, tiled=True),
        lax.psum_scatter(middle_shift, ("dp", "fsdp"), scatter_dimension=0, tiled=True),
        lax.psum_scatter(w_down, ("dp", "fsdp"), scatter_dimension=0, tiled=True),
        lax.psum_scatter(down_shift, ("dp", "fsdp"), scatter_dimension=0, tiled=True),
        lax.psum_scatter(last_gain, ("dp", "fsdp"), scatter_dimension=0, tiled=True),
        lax.psum_scatter(last_shift, ("dp", "fsdp"), scatter_dimension=0, tiled=True),
    )


def feed_forward(values, weights):
    normed, normed_unit, inverse = norm_apply(values, weights[0], weights[1])
    hidden = normed.astype(jnp.bfloat16)
    widened = flat_dot(hidden, weights[2]) + weights[3].astype(jnp.float32)
    active = (widened * jax.nn.sigmoid(widened)).astype(jnp.bfloat16)
    result = values + 0.5 * (flat_dot(active, weights[4]) + weights[5].astype(jnp.float32))
    return (result, (normed_unit, inverse, hidden, widened, active))


def feed_backward(upstream, saved, weights):
    normed_unit, inverse, hidden, widened, active = saved
    half_grad = 0.5 * upstream
    half_low = half_grad.astype(jnp.bfloat16)
    down_slope = lead_dot(active, half_low)
    widened_grad = swish_back(back_dot(half_low, weights[4]), widened)
    widened_low = widened_grad.astype(jnp.bfloat16)
    up_slope = lead_dot(hidden, widened_low)
    hidden_grad = back_dot(widened_low, weights[2])
    input_grad, gain_slope, shift_slope = norm_back(hidden_grad, normed_unit, inverse, weights[0])
    slopes = (
        gain_slope,
        shift_slope,
        up_slope,
        jnp.sum(widened_grad, axis=0),
        down_slope,
        jnp.sum(half_grad, axis=0),
    )
    return (upstream + input_grad, slopes)


def bucket_table(frame_count):
    offsets = jnp.arange(2 * frame_count - 1, dtype=jnp.int32) - (frame_count - 1)
    buckets = jnp.clip(offsets, -(NREL // 2), NREL // 2 - 1) + NREL // 2
    return (buckets[:, None] == jnp.arange(NREL, dtype=jnp.int32)[None, :]).astype(jnp.float32)


def relative_bias(table_rows, frame_count):
    diagonals = jnp.dot(
        bucket_table(frame_count),
        table_rows.astype(jnp.float32),
        precision=lax.Precision.HIGHEST,
        preferred_element_type=jnp.float32,
    )
    flipped = jnp.concatenate(
        [jnp.transpose(diagonals[::-1]), jnp.zeros((HEADS, 1), jnp.float32)], axis=1
    )
    spread = jnp.broadcast_to(flipped[:, None, :], (HEADS, frame_count, 2 * frame_count))
    spread = spread.reshape(HEADS, 2 * frame_count * frame_count)
    sheared = spread[:, : frame_count * (2 * frame_count - 1)].reshape(
        HEADS, frame_count, 2 * frame_count - 1
    )
    return sheared[:, :, frame_count - 1 :]


def relative_slope(score_grad, frame_count):
    placed = jnp.pad(score_grad, ((0, 0), (0, 0), (frame_count - 1, 0)))
    flattened = jnp.pad(
        placed.reshape(HEADS, frame_count * (2 * frame_count - 1)), ((0, 0), (0, frame_count))
    )
    columns = jnp.sum(flattened.reshape(HEADS, frame_count, 2 * frame_count), axis=1)
    diagonals = columns[:, 2 * frame_count - 2 :: -1]
    return lax.dot_general(
        bucket_table(frame_count),
        diagonals,
        (((0,), (1,)), ((), ())),
        precision=lax.Precision.HIGHEST,
        preferred_element_type=jnp.float32,
    )


def mixer_scores(query_rows, key_matrix_rows, relative, same_utterance):
    unnormalized_scores = jnp.einsum(
        "jug,fug->ujf", query_rows, key_matrix_rows, preferred_element_type=jnp.float32
    )
    return jnp.where(same_utterance[None], HEAD ** (-0.5) * unnormalized_scores + relative, MASKED)


def mixer_forward(values, segment_ids, weights):
    frame_count = values.shape[0]
    normed, normed_unit, inverse = norm_apply(values, weights[0], weights[1])
    hidden = normed.astype(jnp.bfloat16)
    projected = flat_dot(hidden, weights[2])
    query_rows = (projected[:, :D] + weights[3].astype(jnp.float32)).astype(jnp.bfloat16)
    query_rows = query_rows.reshape(frame_count, HEADS, HEAD)
    key_matrix_rows = projected[:, D : 2 * D].astype(jnp.bfloat16).reshape(frame_count, HEADS, HEAD)
    value_matrix_rows = (projected[:, 2 * D :] + weights[4].astype(jnp.float32)).astype(
        jnp.bfloat16
    )
    value_matrix_rows = value_matrix_rows.reshape(frame_count, HEADS, HEAD)
    relative = relative_bias(weights[7], frame_count)
    same_utterance = segment_ids[:, None] == segment_ids[None, :]
    scores = mixer_scores(query_rows, key_matrix_rows, relative, same_utterance)
    row_peak = jnp.max(scores, axis=-1, keepdims=True)
    powered = jnp.exp(scores - row_peak)
    row_total = jnp.sum(powered, axis=-1, keepdims=True)
    log_total = row_peak + jnp.log(row_total)
    softmax_rows = (powered / row_total).astype(jnp.bfloat16)
    attention_blend = jnp.einsum(
        "ief,fiv->eiv", softmax_rows, value_matrix_rows, preferred_element_type=jnp.float32
    )
    attention_blend = attention_blend.reshape(frame_count, D).astype(jnp.bfloat16)
    result = values + (flat_dot(attention_blend, weights[5]) + weights[6].astype(jnp.float32))
    return (
        result,
        (
            normed_unit,
            inverse,
            hidden,
            query_rows,
            key_matrix_rows,
            value_matrix_rows,
            log_total,
            attention_blend,
            relative,
            same_utterance,
        ),
    )


def mixer_backward(upstream, saved, weights):
    (
        normed_unit,
        inverse,
        hidden,
        query_rows,
        key_matrix_rows,
        value_matrix_rows,
        log_total,
        attention_blend,
        relative,
        same_utterance,
    ) = saved
    frame_count = upstream.shape[0]
    upstream_low = upstream.astype(jnp.bfloat16)
    output_slope = lead_dot(attention_blend, upstream_low)
    attention_blend_gradient = (
        back_dot(upstream_low, weights[5]).astype(jnp.bfloat16).reshape(frame_count, HEADS, HEAD)
    )
    scores = mixer_scores(query_rows, key_matrix_rows, relative, same_utterance)
    soft_full = jnp.exp(scores - log_total)
    value_grad = jnp.einsum(
        "ybr,byq->ryq",
        soft_full.astype(jnp.bfloat16),
        attention_blend_gradient,
        preferred_element_type=jnp.float32,
    ).reshape(frame_count, D)
    soft_grad = jnp.einsum(
        "jug,fug->ujf",
        attention_blend_gradient,
        value_matrix_rows,
        preferred_element_type=jnp.float32,
    )
    score_grad = soft_full * (soft_grad - jnp.sum(soft_full * soft_grad, axis=-1, keepdims=True))
    table_slope = relative_slope(score_grad, frame_count)
    score_reduced_precision = (HEAD ** (-0.5) * score_grad).astype(jnp.bfloat16)
    query_grad = jnp.einsum(
        "ief,fiv->eiv", score_reduced_precision, key_matrix_rows, preferred_element_type=jnp.float32
    ).reshape(frame_count, D)
    key_grad = jnp.einsum(
        "ybr,byq->ryq", score_reduced_precision, query_rows, preferred_element_type=jnp.float32
    ).reshape(frame_count, D)
    projected_low = jnp.concatenate([query_grad, key_grad, value_grad], axis=1).astype(jnp.bfloat16)
    project_slope = lead_dot(hidden, projected_low)
    hidden_grad = back_dot(projected_low, weights[2])
    input_grad, gain_slope, shift_slope = norm_back(hidden_grad, normed_unit, inverse, weights[0])
    slopes = (
        gain_slope,
        shift_slope,
        project_slope,
        jnp.sum(query_grad, axis=0),
        jnp.sum(value_grad, axis=0),
        output_slope,
        jnp.sum(upstream, axis=0),
        table_slope,
    )
    return (upstream + input_grad, slopes)


def filter_forward(values, segment_ids, weights):
    normed, normed_unit, inverse = norm_apply(values, weights[0], weights[1])
    hidden = normed.astype(jnp.bfloat16)
    widened = flat_dot(hidden, weights[2]) + weights[3].astype(jnp.float32)
    gated_rows = widened[:, :D] * jax.nn.sigmoid(widened[:, D:])
    filtered = depthwise(gated_rows, weights[4].astype(jnp.float32), segment_ids) + weights[
        5
    ].astype(jnp.float32)
    middle, middle_unit, middle_inverse = norm_apply(filtered, weights[6], weights[7])
    swished = (middle * jax.nn.sigmoid(middle)).astype(jnp.bfloat16)
    result = values + (flat_dot(swished, weights[8]) + weights[9].astype(jnp.float32))
    return (
        result,
        (
            normed_unit,
            inverse,
            hidden,
            widened,
            gated_rows,
            middle_unit,
            middle_inverse,
            middle,
            swished,
        ),
    )


def filter_backward(upstream, saved, weights, segment_ids):
    (
        normed_unit,
        inverse,
        hidden,
        widened,
        gated_rows,
        middle_unit,
        middle_inverse,
        middle,
        swished,
    ) = saved
    upstream_low = upstream.astype(jnp.bfloat16)
    down_slope = lead_dot(swished, upstream_low)
    middle_grad = swish_back(back_dot(upstream_low, weights[8]), middle)
    filtered_grad, middle_gain_slope, middle_shift_slope = norm_back(
        middle_grad, middle_unit, middle_inverse, weights[6]
    )

    def local_filter(local_rows, local_kernel):
        return depthwise(local_rows, local_kernel, segment_ids)

    unused, pullback = jax.vjp(local_filter, gated_rows, weights[4].astype(jnp.float32))
    gated_grad, kernel_slope = pullback(filtered_grad)
    opened = jax.nn.sigmoid(widened[:, D:])
    widened_grad = jnp.concatenate(
        [gated_grad * opened, gated_grad * widened[:, :D] * opened * (1.0 - opened)], axis=1
    )
    widened_low = widened_grad.astype(jnp.bfloat16)
    up_slope = lead_dot(hidden, widened_low)
    hidden_grad = back_dot(widened_low, weights[2])
    input_grad, gain_slope, shift_slope = norm_back(hidden_grad, normed_unit, inverse, weights[0])
    slopes = (
        gain_slope,
        shift_slope,
        up_slope,
        jnp.sum(widened_grad, axis=0),
        kernel_slope,
        jnp.sum(filtered_grad, axis=0),
        middle_gain_slope,
        middle_shift_slope,
        down_slope,
        jnp.sum(upstream, axis=0),
    )
    return (upstream + input_grad, slopes)


def body(
    frames,
    segments,
    cotangent,
    early_gain,
    early_shift,
    early_up,
    early_lift,
    early_down,
    early_drop,
    mixer_gain,
    mixer_shift,
    mixer_project,
    query_bias,
    value_bias,
    mixer_output,
    mixer_drop,
    distance_table,
    filter_gain,
    filter_shift,
    filter_up,
    filter_lift,
    depth_weight,
    depth_bias,
    middle_gain,
    middle_shift,
    filter_down,
    filter_drop,
    late_gain,
    late_shift,
    late_up,
    late_lift,
    late_down,
    late_drop,
    final_gain,
    final_shift,
):
    start_rows = frames.astype(jnp.float32)
    final_upstream = cotangent.astype(jnp.float32)
    early_full = fetch_feed(early_gain, early_shift, early_up, early_lift, early_down, early_drop)
    first_rows, early_kept = feed_forward(start_rows, early_full)
    mixer_full = fetch_mixer(
        mixer_gain,
        mixer_shift,
        mixer_project,
        query_bias,
        value_bias,
        mixer_output,
        mixer_drop,
        distance_table,
    )
    second_rows, mixer_kept = mixer_forward(first_rows, segments, mixer_full)
    filter_full = fetch_filter(
        filter_gain,
        filter_shift,
        filter_up,
        filter_lift,
        depth_weight,
        depth_bias,
        middle_gain,
        middle_shift,
        filter_down,
        filter_drop,
        final_gain,
        final_shift,
    )
    third_rows, filter_kept = filter_forward(second_rows, segments, filter_full)
    late_full = fetch_feed(late_gain, late_shift, late_up, late_lift, late_down, late_drop)
    fourth_rows, late_kept = feed_forward(third_rows, late_full)
    layer_out, final_unit, final_inverse = norm_apply(fourth_rows, filter_full[10], filter_full[11])
    final_stats = (final_unit, final_inverse)
    upstream, final_gain_slope, final_shift_slope = norm_back(
        final_upstream, final_stats[0], final_stats[1], filter_full[10]
    )
    upstream, late_slopes = feed_backward(upstream, late_kept, late_full)
    late_summed = reduce_feed(
        late_slopes[0],
        late_slopes[1],
        late_slopes[2],
        late_slopes[3],
        late_slopes[4],
        late_slopes[5],
    )
    upstream, filter_grads = filter_backward(upstream, filter_kept, filter_full, segments)
    filter_summed = reduce_filter(
        filter_grads[0],
        filter_grads[1],
        filter_grads[2],
        filter_grads[3],
        filter_grads[4],
        filter_grads[5],
        filter_grads[6],
        filter_grads[7],
        filter_grads[8],
        filter_grads[9],
        final_gain_slope,
        final_shift_slope,
    )
    upstream, mixer_grads = mixer_backward(upstream, mixer_kept, mixer_full)
    mixer_summed = reduce_mixer(
        mixer_grads[0],
        mixer_grads[1],
        mixer_grads[2],
        mixer_grads[3],
        mixer_grads[4],
        mixer_grads[5],
        mixer_grads[6],
        mixer_grads[7],
    )
    upstream, early_slopes = feed_backward(upstream, early_kept, early_full)
    early_summed = reduce_feed(
        early_slopes[0],
        early_slopes[1],
        early_slopes[2],
        early_slopes[3],
        early_slopes[4],
        early_slopes[5],
    )
    return (
        layer_out,
        upstream,
        early_summed[0],
        early_summed[1],
        early_summed[2],
        early_summed[3],
        early_summed[4],
        early_summed[5],
        mixer_summed[0],
        mixer_summed[1],
        mixer_summed[2],
        mixer_summed[3],
        mixer_summed[4],
        mixer_summed[5],
        mixer_summed[6],
        mixer_summed[7],
        filter_summed[0],
        filter_summed[1],
        filter_summed[2],
        filter_summed[3],
        filter_summed[4],
        filter_summed[5],
        filter_summed[6],
        filter_summed[7],
        filter_summed[8],
        filter_summed[9],
        late_summed[0],
        late_summed[1],
        late_summed[2],
        late_summed[3],
        late_summed[4],
        late_summed[5],
        filter_summed[10],
        filter_summed[11],
    )


def near(me, n):
    if n == 4:
        row, column = me // 2, me % 2
        flip_row, flip_column = (1 - row) * 2 + column, row * 2 + 1 - column
        across = (1 - row) * 2 + 1 - column
        return [(flip_column, flip_column), (flip_row, flip_row), (across, across)]
    return [((me + step) % n, (me + n - step) % n) for step in range(1, n)]


def greet(targets):
    barrier = pltpu.get_barrier_semaphore()
    for target in targets:
        pl.semaphore_signal(barrier, inc=1, device_id={"dp": target}, device_id_type=MESH)
    pl.semaphore_wait(barrier, len(targets))


def greet_all(n, m):
    me, lane = lax.axis_index("dp"), lax.axis_index("fsdp")
    barrier = pltpu.get_barrier_semaphore()

    def say(step, carry):
        target = {"dp": (me + step // m) % n, "fsdp": (lane + step % m) % m}
        pl.semaphore_signal(barrier, inc=1, device_id=target, device_id_type=MESH)
        return carry

    lax.fori_loop(1, n * m, say, 0)
    pl.semaphore_wait(barrier, n * m - 1)


def remote(src, dst, send, recv, target):
    return pltpu.make_async_remote_copy(
        src_ref=src, dst_ref=dst, send_sem=send, recv_sem=recv, device_id=target, device_id_type=MESH
    )


def columns(start, width):
    return pl.ds(pl.multiple_of(start * width, width), width)


def column_pieces(index, n, sizes):
    pieces = []
    for place, (groups, width) in enumerate(sizes):
        for group in range(groups):
            wide = pl.ds(pl.multiple_of((group * n + index) * width, width), width)
            pieces.append((place, wide, pl.ds(group * width, width)))
    return pieces


def row_of(shards, line, first):
    rows = shards.shape[0]
    lines = shards[:, line, :]
    lanes = lax.broadcasted_iota(jnp.int32, lines.shape, 1) // 32
    places = lax.broadcasted_iota(jnp.int32, lines.shape, 0) % 4
    merged = jnp.zeros_like(lines)
    for quarter in range(4):
        shift = (32 * quarter - 32 * first) % LANES
        moved = pltpu.roll(lines, shift, 1) if shift else lines
        merged = merged + jnp.where((lanes == quarter) & (places == quarter), moved, 0.0)
    return [
        jnp.sum(merged[4 * tile : 4 * tile + 4], axis=0, keepdims=True) for tile in range(rows // 4)
    ]


def pack_small(small, singles, lifts, table):
    rows = singles[0].shape[0]
    small[...] = jnp.zeros_like(small)
    for at, single in enumerate(singles):
        line, low = at * rows // LANES, at * rows % LANES
        small[line : line + 1, low : low + rows] = single[...].astype(jnp.float32).reshape(1, rows)
    for at, lift in enumerate(lifts):
        line, count = 5 + at, lift.shape[0]
        small[line : line + 1, 0:count] = lift[...].astype(jnp.float32).reshape(1, count)
    small[8 : 8 + table.shape[0], 0 : table.shape[1]] = table[...].astype(jnp.float32)


def spread_vectors(n, m, inner, me, single_count, small_all, gains, own, lifts, wide_lifts):
    for index in range(single_count):
        for tile, line in enumerate(row_of(small_all, index // 4, index % 4)):
            gains[index : index + 1, tile * LANES : (tile + 1) * LANES] = line
    own[...] = gains[:, columns(me, inner)]
    for index in range(2):
        lines = small_all[pl.ds(me * m, m), 5 + index, :]
        for tile in range(m):
            lifts[index : index + 1, tile * LANES : (tile + 1) * LANES] = lines[tile : tile + 1, :]
    lanes = lax.broadcasted_iota(jnp.int32, (1, LANES), 1)
    for group in range(2):
        for tile in range(inner // LANES):
            first = group * n * m // 2 + me * n + 2 * tile
            left, right = small_all[pl.ds(first, 1), 7, :], small_all[pl.ds(first + 1, 1), 7, :]
            low = group * inner + tile * LANES
            wide_lifts[0:1, low : low + LANES] = jnp.where(
                lanes < LANES // 2, left, pltpu.roll(right, LANES // 2, 1)
            )


def exchange_kernel(n, m, width, inner, *refs):
    early_up, early_down, late_up, project, filter_up, output, filter_down, depth, segs, frames = refs[:10]
    singles, lift_shards, table = refs[10:29], refs[29:32], refs[32]
    up_full, down_full, late_split, mixer_split, filter_split, small_all = refs[33:39]
    gains, own, lifts, wide_lifts, depth_all, segs_all, spread = refs[39:46]
    gathered, small, held, local, send, recv, small_send, small_recv, up_send, up_recv = refs[46:56]
    climb_send, climb_recv, pass_send, pass_recv, out_send, out_recv, depth_send, depth_recv = refs[56:]
    pack_small(gathered.at[0], singles, lift_shards, table)
    small[...] = gathered[0].astype(jnp.bfloat16)
    me, lane = lax.axis_index("dp"), lax.axis_index("fsdp")
    here = me * m + lane
    levels = m // 2
    level = lane // 2
    units = early_down.shape[0]
    beside = lane + 1 - 2 * (lane % 2)
    others = near(me, n)
    ways = (1, -1)
    greet_all(n, m)

    def place(kind, unit, source):
        if kind:
            return up_full.at[((me + n - unit) % n) * m + source]
        return down_full.at[source, unit]

    def climb(kind, way, distance, unit, src=None):
        block = place(kind, unit, (lane + m - 2 * ways[way] * (distance - 1)) % m)
        return remote(
            block if src is None else src,
            block,
            climb_send.at[kind, way, distance - 1, unit],
            climb_recv.at[kind, way, distance - 1, unit],
            {"fsdp": (lane + m + 2 * ways[way]) % m},
        )

    def across(kind, offset, unit, src=None):
        block = place(kind, unit, (lane + 2 * offset) % m)
        return remote(
            block if src is None else src,
            block,
            pass_send.at[kind, offset, unit],
            pass_recv.at[kind, offset, unit],
            {"fsdp": beside},
        )

    def open_way(way):
        return level < levels - 1 if ways[way] > 0 else level > 0

    def reached(way, distance):
        return level >= distance if ways[way] > 0 else level + distance < levels

    def launch(kind, unit, src=None):
        for way in range(2):

            @pl.when(open_way(way))
            def _():
                climb(kind, way, 1, unit, src).start()

        across(kind, 0, unit, src).start()

    def to_device(step):
        target = {"dp": (me + step // m) % n, "fsdp": (lane + step % m) % m}
        return remote(small, small_all.at[here], small_send.at[step], small_recv.at[step], target)

    def to_lane(step):
        return remote(
            depth, depth_all.at[lane], depth_send.at[step], depth_recv.at[step], {"fsdp": (lane + step) % m}
        )

    def to_column(step):
        other = (me + step) % n
        return remote(
            early_up.at[:, columns(other, width)], up_full.at[here], up_send.at[step], up_recv.at[step], {"dp": other}
        )

    def each(call):
        def turn(step, carry):
            call(step)
            return carry

        return turn

    def pieces(index):
        found = [(late_up.at[:, columns(index, width)], late_split.at[me])]
        for group in range(3):
            wide = pl.ds(pl.multiple_of(group * inner * n + index * inner, inner), inner)
            found.append((project.at[:, wide], mixer_split.at[me, :, pl.ds(group * inner, inner)]))
        for group in range(2):
            wide = pl.ds(pl.multiple_of(group * inner * n + index * inner, inner), inner)
            found.append((filter_up.at[:, wide], filter_split.at[me, :, pl.ds(group * inner, inner)]))
        found.append((segs, segs_all.at[me]))
        return found

    lax.fori_loop(1, n * m, each(lambda step: to_device(step).start()), 0)
    lax.fori_loop(1, n, each(lambda step: to_column(step).start()), 0)
    lax.fori_loop(0, units, each(lambda unit: launch(0, unit, early_down.at[unit])), 0)
    mine = early_up.at[:, columns(me, width)]
    launch(1, 0, mine)
    copies = []
    for peer, (target, unused) in enumerate(others):
        for at, (src, dst) in enumerate(pieces(target)):
            copies.append(remote(src, dst, send.at[peer, at], recv.at[peer, at], {"dp": target}))
    owns = [(small, small_all.at[here]), (mine, up_full.at[here]), (early_down, down_full.at[lane])]
    owns += pieces(me)
    for group in range(n):
        wide = pl.ds(group * inner, inner)
        owns.append((output.at[:, wide], mixer_split.at[group, :, pl.ds(3 * inner, inner)]))
        owns.append((filter_down.at[:, wide], filter_split.at[group, :, pl.ds(2 * inner, inner)]))
    owns.append((depth, depth_all.at[lane]))
    owns = [pltpu.make_async_copy(src, dst, local.at[at]) for at, (src, dst) in enumerate(owns)]
    for copy in owns:
        copy.start()
    for step in range(1, n):
        to_column(step).wait_recv()
        launch(1, step)
    for copy in copies:
        copy.start()
    lax.fori_loop(1, m, each(lambda step: to_lane(step).start()), 0)
    def carry_on(kind, distance, unit):
        for way in range(2):

            @pl.when(reached(way, distance))
            def _():
                climb(kind, way, distance, unit).wait_recv()
                offset = levels - distance if ways[way] > 0 else distance
                across(kind, offset, unit).start()
                if distance < levels - 1:

                    @pl.when(open_way(way))
                    def _():
                        climb(kind, way, distance + 1, unit).start()

    def finish(kind, unit):
        for offset in range(levels):
            across(kind, offset, unit).wait()
        for way in range(2):
            for distance in range(1, levels):
                begun = open_way(way)
                if distance > 1:
                    begun = begun & reached(way, distance - 1)

                @pl.when(begun)
                def _():
                    climb(kind, way, distance, unit).wait_send()

    for kind in range(2):
        lax.fori_loop(0, units, each(functools.partial(carry_on, kind, 1)), 0)
    owns[0].wait()
    lax.fori_loop(1, n * m, each(lambda step: to_device(step).wait()), 0)
    gathered[...] = small_all[...].astype(jnp.float32)
    spread_vectors(n, m, inner, me, len(singles), gathered, gains, own, lifts, wide_lifts)
    gain, shift = gains[0:1, :], gains[1:2, :]

    def work(block, carry):
        span = pl.ds(pl.multiple_of(block * BLOCK, BLOCK), BLOCK)
        unit, inverse = unit_of(frames[span, :].astype(jnp.float32))
        held[span, :] = (unit * gain + shift).astype(jnp.bfloat16)
        return carry

    lax.fori_loop(0, frames.shape[0] // BLOCK, work, 0)
    keep = pltpu.make_async_copy(held, spread.at[me], local.at[len(owns)])
    keep.start()
    outgoing = []
    for peer, (target, unused) in enumerate(others):
        outgoing.append(remote(held, spread.at[me], out_send.at[peer], out_recv.at[peer], {"dp": target}))
    for copy in outgoing:
        copy.start()

    for distance in range(2, levels):
        for kind in range(2):
            lax.fori_loop(0, units, each(functools.partial(carry_on, kind, distance)), 0)
    for copy in owns[1:] + copies + outgoing:
        copy.wait()
    keep.wait()
    for kind in range(2):
        lax.fori_loop(0, units, each(functools.partial(finish, kind)), 0)
    lax.fori_loop(1, n, each(lambda step: to_column(step).wait_send()), 0)
    lax.fori_loop(1, m, each(lambda step: to_lane(step).wait()), 0)


def exchange(n, m, early_up, early_down, late_up, project, filter_up, output, filter_down, depth, segs, frames, singles, lifts, table):
    rows, width = early_up.shape[0], early_up.shape[1] // n
    inner = output.shape[1] // n
    frame_count, deep = frames.shape
    units, levels = early_down.shape[0], m // 2
    low, full = jnp.bfloat16, jnp.float32
    packed = (16, LANES)
    struct = jax.ShapeDtypeStruct
    outs = [
        struct((n * m, rows, width), low),
        struct((m,) + early_down.shape, low),
        struct((n, rows, width), low),
        struct((n, rows, 4 * inner), low),
        struct((n, rows, 3 * inner), low),
        struct((n * m,) + packed, low),
        struct((len(singles), deep), full),
        struct((len(singles), inner), full),
        struct((2, width), full),
        struct((1, 2 * inner), full),
        struct((m,) + depth.shape, low),
        struct((n,) + segs.shape, segs.dtype),
        struct((n, frame_count, deep), low),
    ]
    anywhere = pl.BlockSpec(memory_space=pl.ANY)
    inside = pl.BlockSpec(memory_space=pltpu.VMEM)
    dma = pltpu.SemaphoreType.DMA
    return pl.pallas_call(
        functools.partial(exchange_kernel, n, m, width, inner),
        out_shape=outs,
        in_specs=[anywhere] * 9 + [inside] * (2 + len(singles) + len(lifts)),
        out_specs=[anywhere] * 5 + [inside] * 5 + [anywhere] * 3,
        scratch_shapes=[
            pltpu.VMEM((n * m,) + packed, full),
            pltpu.VMEM(packed, low),
            pltpu.VMEM((frame_count, deep), low),
            dma((2 * n + 12,)),
            dma((n - 1, 7)),
            dma((n - 1, 7)),
            dma((n * m,)),
            dma((n * m,)),
            dma((n,)),
            dma((n,)),
            dma((2, 2, levels - 1, units)),
            dma((2, 2, levels - 1, units)),
            dma((2, levels, units)),
            dma((2, levels, units)),
            dma((n - 1,)),
            dma((n - 1,)),
            dma((m,)),
            dma((m,)),
        ],
        compiler_params=pltpu.CompilerParams(collective_id=0, has_side_effects=True),
        name="exchange",
    )(
        early_up, early_down, late_up, project, filter_up, output, filter_down, depth, segs, frames,
        *singles, *lifts, table,
    )


def return_copies(n, sizes, narrows, wides, local, send, recv):
    me = lax.axis_index("dp")
    copies = []
    for peer, (target, unused) in enumerate(near(me, n)):
        for at, (place, wide, narrow) in enumerate(column_pieces(me, n, sizes)):
            copies.append(
                remote(narrows[place].at[target, :, narrow], wides[place].at[:, wide], send.at[peer, at], recv.at[peer, at], {"dp": target})
            )
    for at, (place, wide, narrow) in enumerate(column_pieces(me, n, sizes)):
        copies.append(pltpu.make_async_copy(narrows[place].at[me, :, narrow], wides[place].at[:, wide], local.at[at]))
    return copies


def giveback_kernel(n, sizes, *refs):
    count = len(sizes)
    narrows, wides = refs[:count], refs[count : 2 * count]
    local, send, recv = refs[2 * count :]
    greet([target for target, unused in near(lax.axis_index("dp"), n)])
    copies = return_copies(n, sizes, narrows, wides, local, send, recv)
    for copy in copies:
        copy.start()
    for copy in copies:
        copy.wait()


def giveback(n, narrows, sizes, number):
    rows = narrows[0].shape[1]
    total = sum(groups for groups, width in sizes)
    outs = [jax.ShapeDtypeStruct((rows, groups * width * n), jnp.bfloat16) for groups, width in sizes]
    anywhere = pl.BlockSpec(memory_space=pl.ANY)
    return pl.pallas_call(
        functools.partial(giveback_kernel, n, sizes),
        out_shape=outs,
        in_specs=[anywhere] * len(narrows),
        out_specs=[anywhere] * len(outs),
        scratch_shapes=[
            pltpu.SemaphoreType.DMA((total,)),
            pltpu.SemaphoreType.DMA((n - 1, total)),
            pltpu.SemaphoreType.DMA((n - 1, total)),
        ],
        compiler_params=pltpu.CompilerParams(collective_id=number, has_side_effects=True),
        name="giveback",
    )(*narrows)


def share_kernel(n, mine, shared, local, send, recv):
    me = lax.axis_index("dp")
    others = near(me, n)
    greet([target for target, unused in others])
    copies = [pltpu.make_async_copy(mine, shared.at[me], local)]
    for peer, (target, unused) in enumerate(others):
        copies.append(remote(mine, shared.at[me], send.at[peer], recv.at[peer], {"dp": target}))
    for copy in copies:
        copy.start()
    for copy in copies:
        copy.wait()


def share(n, mine, number):
    inside = pl.BlockSpec(memory_space=pltpu.VMEM)
    return pl.pallas_call(
        functools.partial(share_kernel, n),
        out_shape=jax.ShapeDtypeStruct((n,) + mine.shape, mine.dtype),
        in_specs=[inside],
        out_specs=inside,
        scratch_shapes=[
            pltpu.SemaphoreType.DMA,
            pltpu.SemaphoreType.DMA((n - 1,)),
            pltpu.SemaphoreType.DMA((n - 1,)),
        ],
        compiler_params=pltpu.CompilerParams(collective_id=number, has_side_effects=True),
        name="share",
    )(mine)


def collect_kernel(n, m, sizes, *refs):
    count = len(sizes)
    wide, group = refs[:2]
    narrows, wides = refs[2 : 2 + count], refs[4 + count : 4 + 2 * count]
    wide_all, group_all = refs[2 + count : 4 + count]
    local, send, recv, group_send, group_recv, back_local, back_send, back_recv = refs[4 + 2 * count :]
    me, lane = lax.axis_index("dp"), lax.axis_index("fsdp")
    here = me * m + lane
    greet_all(n, m)

    def to_device(step):
        other, beside = (me + step // m) % n, (lane + step % m) % m
        return remote(
            wide.at[other * m + beside], wide_all.at[here], send.at[step], recv.at[step], {"dp": other, "fsdp": beside}
        )

    def to_group(step):
        beside = (lane + step) % m
        return remote(group.at[beside], group_all.at[lane], group_send.at[step], group_recv.at[step], {"fsdp": beside})

    def start_wide(step, carry):
        to_device(step).start()
        return carry

    def start_group(step, carry):
        to_group(step).start()
        return carry

    def wait_wide(step, carry):
        to_device(step).wait()
        return carry

    def wait_group(step, carry):
        to_group(step).wait()
        return carry

    own = pltpu.make_async_copy(wide.at[here], wide_all.at[here], local.at[0])
    own_group = pltpu.make_async_copy(group.at[lane], group_all.at[lane], local.at[1])
    own.start()
    own_group.start()
    lax.fori_loop(1, n * m, start_wide, 0)
    lax.fori_loop(1, m, start_group, 0)
    copies = return_copies(n, sizes, narrows, wides, back_local, back_send, back_recv)
    for copy in copies:
        copy.start()
    own.wait()
    own_group.wait()
    lax.fori_loop(1, n * m, wait_wide, 0)
    lax.fori_loop(1, m, wait_group, 0)
    for copy in copies:
        copy.wait()


def collect(n, m, wide, group, narrows, sizes, number):
    inside = pl.BlockSpec(memory_space=pltpu.VMEM)
    anywhere = pl.BlockSpec(memory_space=pl.ANY)
    rows = narrows[0].shape[1]
    total = sum(groups for groups, width in sizes)
    outs = [jax.ShapeDtypeStruct(wide.shape, wide.dtype), jax.ShapeDtypeStruct(group.shape, group.dtype)]
    outs += [jax.ShapeDtypeStruct((rows, groups * width * n), jnp.bfloat16) for groups, width in sizes]
    return pl.pallas_call(
        functools.partial(collect_kernel, n, m, sizes),
        out_shape=outs,
        in_specs=[inside] * 2 + [anywhere] * len(sizes),
        out_specs=[inside] * 2 + [anywhere] * len(sizes),
        scratch_shapes=[
            pltpu.SemaphoreType.DMA((2,)),
            pltpu.SemaphoreType.DMA((n * m,)),
            pltpu.SemaphoreType.DMA((n * m,)),
            pltpu.SemaphoreType.DMA((m,)),
            pltpu.SemaphoreType.DMA((m,)),
            pltpu.SemaphoreType.DMA((total,)),
            pltpu.SemaphoreType.DMA((n - 1, total)),
            pltpu.SemaphoreType.DMA((n - 1, total)),
        ],
        compiler_params=pltpu.CompilerParams(collective_id=number, has_side_effects=True),
        name="collect",
    )(wide, group, *narrows)


def keep_kernel(first, second, first_out, second_out):
    first_out[...] = first[...]
    second_out[...] = second[...]


def keep(first, second):
    inside = pl.BlockSpec(memory_space=pltpu.VMEM)
    return pl.pallas_call(
        keep_kernel,
        out_shape=[jax.ShapeDtypeStruct(value.shape, value.dtype) for value in (first, second)],
        in_specs=[inside] * 2,
        out_specs=[inside] * 2,
        name="keep",
    )(first, second)


def unit_of(values):
    centered = values - jnp.mean(values, axis=-1, keepdims=True)
    inverse = lax.rsqrt(jnp.mean(centered * centered, axis=-1, keepdims=True) + EPSILON)
    return centered * inverse, inverse


def unit_back(upstream, unit, inverse, gain):
    scaled = upstream * gain
    adjusted = scaled - jnp.mean(scaled, axis=-1, keepdims=True)
    return inverse * (adjusted - unit * jnp.mean(scaled * unit, axis=-1, keepdims=True))


def step_forward(scale, total, states, vectors):
    values = states[0] + scale * (total + vectors[0])
    unit, inverse = unit_of(values)
    return [values], unit * vectors[1] + vectors[2], []


def step_turn(total, states, vectors):
    values = states[0] + 0.5 * (total + vectors[0])
    upstream = states[1]
    unit, inverse = unit_of(values)
    layer_out = unit * vectors[1] + vectors[2]
    grad = unit_back(upstream, unit, inverse, vectors[1])
    half = 0.5 * grad
    return [layer_out, grad], half, [upstream * unit, upstream, half]


def step_backward(scale, total, states, vectors):
    unit, inverse = unit_of(states[1])
    grad = states[0] + unit_back(total, unit, inverse, vectors[0])
    sent = scale * grad
    return [grad], sent, [total * unit, total, sent]


def step_last(total, states, vectors):
    unit, inverse = unit_of(states[1])
    grad = states[0] + unit_back(total, unit, inverse, vectors[0])
    return [grad], None, [total * unit, total]


def boundary_kernel(step, shape, *refs):
    gathered, state_count, out_count, sum_count, picked = shape
    refs = list(refs)
    take = lambda count: [refs.pop(0) for unused in range(count)]
    part = take(1)[0]
    states = take(state_count)
    vectors = take(1)[0]
    outs = take(out_count)
    spread = take(1)[0] if gathered else None
    sums = take(1)[0] if sum_count else None
    arrived, passing, mine, merged, own, local = take(6)
    relay_send, relay_recv, direct_send, direct_recv, merge_send, merge_recv = take(6)
    if gathered:
        held, held_sem, out_send, out_recv, pass_send, pass_recv = take(6)
    partials = take(1)[0] if sum_count else None
    me = lax.axis_index("dp")
    row, column = me // 2, me % 2
    sides = [row * 2 + 1 - column, (1 - row) * 2 + column]
    across = (1 - row) * 2 + 1 - column
    half = own.shape[0] // 2
    height = half // PIECES
    both, places = range(2), range(PIECES)

    def span(axis, piece):
        return pl.ds(axis * half + piece * height, height)

    def inner(piece):
        return pl.ds(piece * height, height)

    def relay(axis, piece):
        return remote(
            part.at[across, span(axis, piece)],
            passing.at[axis, inner(piece)],
            relay_send.at[axis, piece],
            relay_recv.at[axis, piece],
            {"dp": sides[axis]},
        )

    def direct(axis, piece):
        return remote(
            part.at[sides[axis], span(axis, piece)],
            arrived.at[axis, span(axis, piece)],
            direct_send.at[axis, piece],
            direct_recv.at[axis, piece],
            {"dp": sides[axis]},
        )

    def merge(axis, piece):
        return remote(
            merged.at[axis, inner(piece)],
            arrived.at[1 - axis, span(axis, piece)],
            merge_send.at[axis, piece],
            merge_recv.at[axis, piece],
            {"dp": sides[1 - axis]},
        )

    def hand(target, axis, piece):
        return remote(
            held.at[span(axis, piece)],
            spread.at[me, span(axis, piece)],
            out_send.at[target, axis, piece],
            out_recv.at[target, axis, piece],
            {"dp": sides[target]},
        )

    def onward(axis, piece):
        block = spread.at[sides[axis], span(axis, piece)]
        return remote(
            block, block, pass_send.at[axis, piece], pass_recv.at[axis, piece], {"dp": sides[1 - axis]}
        )

    def forward(axis, piece):
        hand(axis, axis, piece).wait_recv()
        onward(axis, piece).start()

    greet(sides)
    for piece in places:
        for axis in both:
            relay(axis, piece).start()
    locals_ = [
        pltpu.make_async_copy(part.at[sides[1 - axis], pl.ds(axis * half, half)], mine.at[axis], local.at[axis])
        for axis in both
    ]
    locals_.append(pltpu.make_async_copy(part.at[me], own, local.at[2]))
    for copy in locals_:
        copy.start()
    for piece in places:
        for axis in both:
            direct(axis, piece).start()
    if sum_count:
        partials[...] = jnp.zeros_like(partials)
    for copy in locals_:
        copy.wait()
    for piece in places:
        for axis in both:
            relay(axis, piece).wait_recv()

            def join(block, carry):
                rows = pl.ds(pl.multiple_of(piece * height + block * BLOCK, BLOCK), BLOCK)
                total = passing[axis, rows, :].astype(jnp.float32) + mine[axis, rows, :].astype(jnp.float32)
                merged[axis, rows, :] = total.astype(jnp.bfloat16)
                return carry

            lax.fori_loop(0, height // BLOCK, join, 0)
            merge(axis, piece).start()
    rows_of = [vectors[pl.ds(index, 1), :] for index in picked]
    order = [(axis, piece) for piece in places for axis in both]
    for at, (axis, piece) in enumerate(order):
        direct(axis, piece).wait_recv()
        merge(axis, piece).wait_recv()

        def work(block, carry):
            rows = pl.ds(pl.multiple_of(axis * half + piece * height + block * BLOCK, BLOCK), BLOCK)
            total = own[rows, :].astype(jnp.float32)
            for side in both:
                total = total + arrived[side, rows, :].astype(jnp.float32)
            made, sent, terms = step(total, [state[rows, :].astype(jnp.float32) for state in states], rows_of)
            for out, value in zip(outs, made):
                out[rows, :] = value
            if gathered:
                held[rows, :] = sent.astype(jnp.bfloat16)
            for index, term in enumerate(terms):
                partials[index] += sum(term[8 * low : 8 * low + 8] for low in range(BLOCK // 8))
            return carry

        lax.fori_loop(0, height // BLOCK, work, 0)
        if gathered:
            for target in both:
                hand(target, axis, piece).start()
            if at >= LAG:
                forward(*order[at - LAG])
    if gathered:
        keep = pltpu.make_async_copy(held, spread.at[me], held_sem)
        keep.start()
        for axis, piece in order[len(order) - LAG :]:
            forward(axis, piece)
    for index in range(sum_count):
        sums[pl.ds(index, 1), :] = jnp.sum(partials[index], axis=0, keepdims=True)
    for axis, piece in order:
        relay(axis, piece).wait_send()
        direct(axis, piece).wait_send()
        merge(axis, piece).wait_send()
    if gathered:
        for axis, piece in order:
            hand(axis, axis, piece).wait_send()
            hand(1 - axis, axis, piece).wait()
        for axis, piece in order:
            onward(axis, piece).wait()
        keep.wait()


def boundary(step, part, states, vectors, picked, out_count, sum_count, number, gathered=True):
    n, rows, width = part.shape
    inside = pl.BlockSpec(memory_space=pltpu.VMEM)
    anywhere = pl.BlockSpec(memory_space=pl.ANY)
    dma = pltpu.SemaphoreType.DMA
    shape = (gathered, len(states), out_count, sum_count, picked)
    low = jnp.bfloat16
    scratch = [
        pltpu.VMEM((2, rows, width), low),
        pltpu.VMEM((2, rows // 2, width), low),
        pltpu.VMEM((2, rows // 2, width), low),
        pltpu.VMEM((2, rows // 2, width), low),
        pltpu.VMEM((rows, width), low),
        dma((3,)),
    ]
    scratch += [dma((2, PIECES))] * 6
    outs = [jax.ShapeDtypeStruct((rows, width), jnp.float32)] * out_count
    out_specs = [inside] * out_count
    if gathered:
        outs.append(jax.ShapeDtypeStruct((n, rows, width), low))
        out_specs.append(anywhere)
        scratch += [pltpu.VMEM((rows, width), low), dma]
        scratch += [dma((2, 2, PIECES))] * 2 + [dma((2, PIECES))] * 2
    if sum_count:
        outs.append(jax.ShapeDtypeStruct((sum_count, width), jnp.float32))
        out_specs.append(inside)
        scratch.append(pltpu.VMEM((sum_count, 8, width), jnp.float32))
    return pl.pallas_call(
        functools.partial(boundary_kernel, step, shape),
        out_shape=outs,
        in_specs=[anywhere] + [inside] * (len(states) + 1),
        out_specs=out_specs,
        scratch_shapes=scratch,
        compiler_params=pltpu.CompilerParams(collective_id=number, has_side_effects=True),
        name="boundary",
    )(part, *states, vectors)


def toeplitz(line, frame_count):
    wide = jnp.broadcast_to(line, (frame_count, NREL))
    return pltpu.roll(wide, NREL - frame_count + 1, 1, stride=1, stride_axis=0)[:, :frame_count]


def head_scores(packed, head, heads, same, bias):
    size = heads * HEAD
    query_rows = packed[:, head * HEAD : (head + 1) * HEAD]
    key_rows = packed[:, size + head * HEAD : size + (head + 1) * HEAD]
    value_rows = packed[:, 2 * size + head * HEAD : 2 * size + (head + 1) * HEAD]
    scores = jnp.where(same, HEAD ** (-0.5) * back_dot(query_rows, key_rows) + bias, MASKED)
    powered = jnp.exp(scores - jnp.max(scores, axis=-1, keepdims=True))
    soft = powered / jnp.sum(powered, axis=-1, keepdims=True)
    return query_rows, key_rows, value_rows, soft


def attend_kernel(heads, packed, segment_rows, segment_columns, table, blended, bias):
    frame_count = packed.shape[1]

    @pl.when(pl.program_id(0) == 0)
    def _():
        for head in range(heads):
            bias[head] = toeplitz(table[pl.ds(head, 1), :], frame_count)

    same = segment_columns[0] == segment_rows[0]
    block = packed[0]
    results = []
    for head in range(heads):
        unused, unused_too, value_rows, soft = head_scores(block, head, heads, same, bias[head])
        results.append(flat_dot(soft.astype(jnp.bfloat16), value_rows).astype(jnp.bfloat16))
    blended[0] = jnp.concatenate(results, axis=1)


def attend(packed, segment_rows, segment_columns, table):
    blocks, frame_count, width = packed.shape
    heads = table.shape[0]
    return pl.pallas_call(
        functools.partial(attend_kernel, heads),
        grid=(blocks,),
        out_shape=jax.ShapeDtypeStruct((blocks, frame_count, width // 3), jnp.bfloat16),
        in_specs=[
            pl.BlockSpec((1, frame_count, width), lambda i: (i, 0, 0)),
            pl.BlockSpec((1, 1, frame_count), lambda i: (i, 0, 0)),
            pl.BlockSpec((1, frame_count, 1), lambda i: (i, 0, 0)),
            pl.BlockSpec((heads, NREL), lambda i: (0, 0)),
        ],
        out_specs=pl.BlockSpec((1, frame_count, width // 3), lambda i: (i, 0, 0)),
        scratch_shapes=[pltpu.VMEM((heads, frame_count, frame_count), jnp.float32)],
        name="attend",
    )(packed, segment_rows, segment_columns, table)


def unattend_kernel(heads, packed, upstream, segment_rows, segment_columns, table, grads, sums, slope, bias, gathered):
    frame_count = packed.shape[1]
    size = heads * HEAD
    at = pl.program_id(0)

    @pl.when(at == 0)
    def _():
        for head in range(heads):
            bias[head] = toeplitz(table[pl.ds(head, 1), :], frame_count)
        gathered[...] = jnp.zeros_like(gathered)
        sums[...] = jnp.zeros_like(sums)

    same = segment_columns[0] == segment_rows[0]
    block = packed[0]
    above = upstream[0]
    query_grads, key_grads, value_grads = [], [], []
    for head in range(heads):
        query_rows, key_rows, value_rows, soft = head_scores(block, head, heads, same, bias[head])
        blend_grad = above[:, head * HEAD : (head + 1) * HEAD]
        value_grads.append(lead_dot(soft.astype(jnp.bfloat16), blend_grad))
        soft_grad = back_dot(blend_grad, value_rows)
        score_grad = soft * (soft_grad - jnp.sum(soft * soft_grad, axis=-1, keepdims=True))
        gathered[head] += score_grad
        low = (HEAD ** (-0.5) * score_grad).astype(jnp.bfloat16)
        query_grads.append(flat_dot(low, key_rows))
        key_grads.append(lead_dot(low, query_rows))
    query_grad = jnp.concatenate(query_grads, axis=1)
    value_grad = jnp.concatenate(value_grads, axis=1)
    grads[0, :, 0:size] = query_grad.astype(jnp.bfloat16)
    grads[0, :, size : 2 * size] = jnp.concatenate(key_grads, axis=1).astype(jnp.bfloat16)
    grads[0, :, 2 * size :] = value_grad.astype(jnp.bfloat16)
    sums[0:1, :] += jnp.sum(query_grad, axis=0, keepdims=True)
    sums[1:2, :] += jnp.sum(value_grad, axis=0, keepdims=True)

    @pl.when(at == pl.num_programs(0) - 1)
    def _():
        places = lax.broadcasted_iota(jnp.int32, (frame_count, NREL), 0)
        for head in range(heads):
            wide = jnp.concatenate(
                [gathered[head], jnp.zeros((frame_count, NREL - frame_count), jnp.float32)], axis=1
            )
            stride = 1
            while stride < frame_count:
                moved = pltpu.roll(wide, NREL - stride, 1)
                wide = jnp.where((places // stride) % 2 == 1, moved, wide)
                stride *= 2
            slope[pl.ds(head, 1), :] = jnp.sum(wide, axis=0, keepdims=True)


def unattend(packed, upstream, segment_rows, segment_columns, table):
    blocks, frame_count, width = packed.shape
    heads = table.shape[0]
    return pl.pallas_call(
        functools.partial(unattend_kernel, heads),
        grid=(blocks,),
        out_shape=[
            jax.ShapeDtypeStruct((blocks, frame_count, width), jnp.bfloat16),
            jax.ShapeDtypeStruct((2, width // 3), jnp.float32),
            jax.ShapeDtypeStruct((heads, NREL), jnp.float32),
        ],
        in_specs=[
            pl.BlockSpec((1, frame_count, width), lambda i: (i, 0, 0)),
            pl.BlockSpec((1, frame_count, width // 3), lambda i: (i, 0, 0)),
            pl.BlockSpec((1, 1, frame_count), lambda i: (i, 0, 0)),
            pl.BlockSpec((1, frame_count, 1), lambda i: (i, 0, 0)),
            pl.BlockSpec((heads, NREL), lambda i: (0, 0)),
        ],
        out_specs=[
            pl.BlockSpec((1, frame_count, width), lambda i: (i, 0, 0)),
            pl.BlockSpec((2, width // 3), lambda i: (0, 0)),
            pl.BlockSpec((heads, NREL), lambda i: (0, 0)),
        ],
        scratch_shapes=[
            pltpu.VMEM((heads, frame_count, frame_count), jnp.float32),
            pltpu.VMEM((heads, frame_count, frame_count), jnp.float32),
        ],
        name="unattend",
    )(packed, upstream, segment_rows, segment_columns, table)


def reach_mask(offset, behind, ahead):
    if offset < 0:
        return behind >= -offset
    return ahead >= offset


def convolve_kernel(opened, behind, ahead, taps, bias, gated, filtered, padded):
    frame_count, channels = gated.shape[1:]
    gates = opened[0, :, 0:channels] * jax.nn.sigmoid(opened[0, :, channels:])
    gated[0] = gates
    padded[pl.ds(0, MARGIN), :] = jnp.zeros((MARGIN, channels), jnp.float32)
    padded[pl.ds(MARGIN + frame_count, MARGIN), :] = jnp.zeros((MARGIN, channels), jnp.float32)
    padded[pl.ds(MARGIN, frame_count), :] = gates
    back = jnp.broadcast_to(behind[0], (frame_count, LANES))
    front = jnp.broadcast_to(ahead[0], (frame_count, LANES))
    for low in range(0, channels, LANES):
        lanes = slice(low, low + LANES)
        running = jnp.broadcast_to(bias[:, lanes], (frame_count, LANES))
        for tap in range(KW):
            offset = tap - (KW - 1) // 2
            moved = padded[pl.ds(MARGIN + offset, frame_count), lanes]
            if offset:
                moved = jnp.where(reach_mask(offset, back, front), moved, 0.0)
            running = running + moved * taps[pl.ds(tap, 1), lanes]
        filtered[0, :, lanes] = running


def convolve(opened, behind, ahead, taps, bias):
    blocks, frame_count, width = opened.shape
    channels = width // 2
    rows = pl.BlockSpec((1, frame_count, channels), lambda i: (i, 0, 0))
    places = pl.BlockSpec((1, frame_count, 1), lambda i: (i, 0, 0))
    return pl.pallas_call(
        convolve_kernel,
        grid=(blocks,),
        out_shape=[jax.ShapeDtypeStruct((blocks, frame_count, channels), jnp.float32)] * 2,
        in_specs=[
            pl.BlockSpec((1, frame_count, width), lambda i: (i, 0, 0)),
            places,
            places,
            pl.BlockSpec((KW, channels), lambda i: (0, 0)),
            pl.BlockSpec((1, channels), lambda i: (0, 0)),
        ],
        out_specs=[rows, rows],
        scratch_shapes=[pltpu.VMEM((frame_count + 2 * MARGIN, channels), jnp.float32)],
        name="convolve",
    )(opened, behind, ahead, taps, bias)


def unconvolve_kernel(opened, gated, upstream, behind, ahead, taps, grads, lifts, slopes, padded, padded_grad):
    frame_count, channels = gated.shape[1:]

    @pl.when(pl.program_id(0) == 0)
    def _():
        lifts[...] = jnp.zeros_like(lifts)
        slopes[...] = jnp.zeros_like(slopes)

    for store, value in ((padded, gated[0]), (padded_grad, upstream[0])):
        store[pl.ds(0, MARGIN), :] = jnp.zeros((MARGIN, channels), jnp.float32)
        store[pl.ds(MARGIN + frame_count, MARGIN), :] = jnp.zeros((MARGIN, channels), jnp.float32)
        store[pl.ds(MARGIN, frame_count), :] = value
    back = jnp.broadcast_to(behind[0], (frame_count, LANES))
    front = jnp.broadcast_to(ahead[0], (frame_count, LANES))
    for low in range(0, channels, LANES):
        lanes = slice(low, low + LANES)
        above = upstream[0, :, lanes]
        running = jnp.zeros((frame_count, LANES), jnp.float32)
        for tap in range(KW):
            offset = tap - (KW - 1) // 2
            moved = padded[pl.ds(MARGIN + offset, frame_count), lanes]
            moved_grad = padded_grad[pl.ds(MARGIN + offset, frame_count), lanes]
            if offset:
                mask = reach_mask(offset, back, front)
                moved = jnp.where(mask, moved, 0.0)
                moved_grad = jnp.where(mask, moved_grad, 0.0)
            running = running + moved_grad * taps[pl.ds(KW - 1 - tap, 1), lanes]
            slopes[pl.ds(tap, 1), lanes] += jnp.sum(moved * above, axis=0, keepdims=True)
        slopes[pl.ds(KW, 1), lanes] += jnp.sum(above, axis=0, keepdims=True)
        wide = slice(channels + low, channels + low + LANES)
        left, gate = opened[0, :, lanes], jax.nn.sigmoid(opened[0, :, wide])
        left_grad = running * gate
        gate_grad = running * left * gate * (1.0 - gate)
        grads[0, :, lanes] = left_grad.astype(jnp.bfloat16)
        grads[0, :, wide] = gate_grad.astype(jnp.bfloat16)
        lifts[:, lanes] += jnp.sum(left_grad, axis=0, keepdims=True)
        lifts[:, wide] += jnp.sum(gate_grad, axis=0, keepdims=True)


def unconvolve(opened, gated, upstream, behind, ahead, taps):
    blocks, frame_count, width = opened.shape
    channels = width // 2
    wide = pl.BlockSpec((1, frame_count, width), lambda i: (i, 0, 0))
    rows = pl.BlockSpec((1, frame_count, channels), lambda i: (i, 0, 0))
    places = pl.BlockSpec((1, frame_count, 1), lambda i: (i, 0, 0))
    return pl.pallas_call(
        unconvolve_kernel,
        grid=(blocks,),
        out_shape=[
            jax.ShapeDtypeStruct((blocks, frame_count, width), jnp.bfloat16),
            jax.ShapeDtypeStruct((1, width), jnp.float32),
            jax.ShapeDtypeStruct((KW + 1, channels), jnp.float32),
        ],
        in_specs=[wide, rows, rows, places, places, pl.BlockSpec((KW, channels), lambda i: (0, 0))],
        out_specs=[
            wide,
            pl.BlockSpec((1, width), lambda i: (0, 0)),
            pl.BlockSpec((KW + 1, channels), lambda i: (0, 0)),
        ],
        scratch_shapes=[pltpu.VMEM((frame_count + 2 * MARGIN, channels), jnp.float32)] * 2,
        name="unconvolve",
    )(opened, gated, upstream, behind, ahead, taps)


def gather_rows(value):
    return lax.all_gather(value, "fsdp", axis=0, tiled=True)


def gather_split(value):
    full = lax.all_gather(value, "fsdp", axis=1, tiled=True)
    return full.reshape(-1, full.shape[-1])


def scatter_rows(value):
    return lax.psum_scatter(value.astype(jnp.bfloat16), "fsdp", scatter_dimension=0, tiled=True)


def scatter_split(value, n):
    value = value.astype(jnp.bfloat16).reshape(n, value.shape[0] // n, value.shape[1])
    return lax.psum_scatter(value, "fsdp", scatter_dimension=1, tiled=True)


def pair_slopes(up_slope, down_slope, n):
    inner = down_slope.shape[0]
    up_slope = up_slope.reshape(n, inner, -1)
    down_slope = jnp.transpose(down_slope.reshape(inner, n, inner), (1, 0, 2))
    return jnp.concatenate([up_slope, down_slope], axis=2)


def flat(value):
    return value.reshape(-1, value.shape[-1])


def split_body(
    n,
    m,
    frames,
    segments,
    cotangent,
    early_gain,
    early_shift,
    early_up,
    early_lift,
    early_down,
    early_drop,
    mixer_gain,
    mixer_shift,
    mixer_project,
    query_bias,
    value_bias,
    mixer_output,
    mixer_drop,
    distance_table,
    filter_gain,
    filter_shift,
    filter_up,
    filter_lift,
    depth_weight,
    depth_bias,
    middle_gain,
    middle_shift,
    filter_down,
    filter_drop,
    late_gain,
    late_shift,
    late_up,
    late_lift,
    late_down,
    late_drop,
    final_gain,
    final_shift,
):
    me = lax.axis_index("dp")
    frame_count = frames.shape[0]
    rows = early_gain.shape[0]
    hidden = early_up.shape[1] // n
    inner = D // n
    heads = HEADS // n
    singles = [
        early_gain, early_shift, early_drop, mixer_gain, mixer_shift, query_bias, value_bias, mixer_drop,
        filter_gain, filter_shift, depth_bias, middle_gain, middle_shift, filter_drop, late_gain, late_shift,
        late_drop, final_gain, final_shift,
    ]
    spans = hidden * n // D
    (
        w_early_up, w_early_down, late_up_split, mixer_split, filter_split, small_all, vectors, own_vectors, lifts,
        filter_lifts, depth_all, segments_all, early_hidden,
    ) = exchange(
        n, m, early_up, early_down.reshape(spans, rows, D), late_up, mixer_project, filter_up, mixer_output,
        filter_down, depth_weight, segments.reshape(1, frame_count), frames, singles,
        [early_lift, late_lift, filter_lift], distance_table,
    )
    w_early_up = w_early_up.reshape(D, hidden)
    w_early_down = w_early_down.reshape(hidden, D)
    w_mixer = lax.all_gather(mixer_split, "fsdp", axis=1, tiled=True)
    w_filter = lax.all_gather(filter_split, "fsdp", axis=1, tiled=True)
    w_late_up = gather_split(late_up_split)
    w_late_down = gather_rows(late_down)

    early_lifts, late_lifts = lifts[0], lifts[1]
    table = small_all[:, 8 : 8 + distance_table.shape[0], :HEADS].astype(jnp.float32).reshape(NREL, HEADS)
    table = jnp.transpose(lax.dynamic_slice(table, (0, me * heads), (NREL, heads)))[:, ::-1]
    taps = jnp.transpose(depth_all.reshape(inner, KW)).astype(jnp.float32)
    attention_shift = jnp.concatenate([own_vectors[5], jnp.zeros((inner,), jnp.float32), own_vectors[6]])
    segment_rows = segments_all
    segment_columns = segments_all.reshape(n, frame_count, 1)
    places = jnp.arange(frame_count, dtype=jnp.int32)[None, :]
    lower = (segment_rows < segment_columns).astype(jnp.int32)
    upto = (segment_rows <= segment_columns).astype(jnp.int32)
    behind = (places - jnp.sum(lower, axis=-1)).reshape(n, frame_count, 1)
    ahead = (jnp.sum(upto, axis=-1) - 1 - places).reshape(n, frame_count, 1)

    def blocks(value):
        return value.reshape(n, frame_count, value.shape[-1])

    def feed(hidden_rows, w_up, lifts, w_down):
        widened = flat_dot(flat(hidden_rows), w_up) + lifts
        active = (widened * jax.nn.sigmoid(widened)).astype(jnp.bfloat16)
        return widened, active, blocks(flat_dot(active, w_down).astype(jnp.bfloat16))

    def feed_back(low, hidden_rows, widened, active, w_up, w_down):
        low = flat(low)
        down_slope = lead_dot(active, low).astype(jnp.bfloat16)
        widened_grad = swish_back(back_dot(low, w_down), widened)
        widened_low = widened_grad.astype(jnp.bfloat16)
        up_slope = lead_dot(flat(hidden_rows), widened_low).astype(jnp.bfloat16)
        part = blocks(back_dot(widened_low, w_up).astype(jnp.bfloat16))
        down_slope = jnp.transpose(down_slope.reshape(m, spans, rows, D), (1, 0, 2, 3)).reshape(spans, m * rows, D)
        slope = jnp.concatenate([up_slope.reshape(n, D // n, hidden), down_slope])
        part, slope = lax.optimization_barrier((part, slope))
        return part, slope, jnp.sum(widened_grad, axis=0)

    early_wide, early_active, part = feed(early_hidden, w_early_up, early_lifts, w_early_down)
    first_rows, mixer_hidden = boundary(
        functools.partial(step_forward, 0.5), part, [frames], vectors, (2, 3, 4), 1, 0, 2
    )
    mixer_hidden, w_mixer = lax.optimization_barrier((mixer_hidden, w_mixer))
    w_project = w_mixer[:, :, : 3 * inner].reshape(D, 3 * inner)
    w_output = jnp.transpose(w_mixer[:, :, 3 * inner :], (1, 0, 2)).reshape(inner, D)
    packed = blocks((flat_dot(flat(mixer_hidden), w_project) + attention_shift).astype(jnp.bfloat16))
    blended = attend(packed, segment_rows, segment_columns, table)
    part = blocks(flat_dot(flat(blended), w_output).astype(jnp.bfloat16))
    second_rows, filter_hidden = boundary(
        functools.partial(step_forward, 1.0), part, [first_rows], vectors, (7, 8, 9), 1, 0, 3
    )
    filter_hidden, w_filter = lax.optimization_barrier((filter_hidden, w_filter))
    w_filter_up = w_filter[:, :, : 2 * inner].reshape(D, 2 * inner)
    w_filter_down = jnp.transpose(w_filter[:, :, 2 * inner :], (1, 0, 2)).reshape(inner, D)
    opened = blocks(flat_dot(flat(filter_hidden), w_filter_up) + filter_lifts)
    gated, filtered = convolve(opened, behind, ahead, taps, own_vectors[10:11])
    filtered = flat(filtered)
    local_mean = jnp.mean(filtered, axis=-1)
    local_square = jnp.sum((filtered - local_mean[:, None]) ** 2, axis=-1)
    shared = share(
        n, jnp.concatenate([local_mean.reshape(n, frame_count), local_square.reshape(n, frame_count)]), 4
    )
    means, squares = shared[:, :n], shared[:, n:]
    middle_mean = jnp.mean(means, axis=0)
    spread = jnp.sum(squares, axis=0) + inner * jnp.sum((means - middle_mean) ** 2, axis=0)
    middle_inverse = lax.rsqrt(spread / D + EPSILON).reshape(-1, 1)
    middle_unit = (filtered - middle_mean.reshape(-1, 1)) * middle_inverse
    middle = middle_unit * own_vectors[11] + own_vectors[12]
    swished = (middle * jax.nn.sigmoid(middle)).astype(jnp.bfloat16)
    part = blocks(flat_dot(swished, w_filter_down).astype(jnp.bfloat16))
    third_rows, late_hidden = boundary(
        functools.partial(step_forward, 1.0), part, [second_rows], vectors, (13, 14, 15), 1, 0, 5
    )
    late_hidden, w_late_up, w_late_down = lax.optimization_barrier((late_hidden, w_late_up, w_late_down))
    late_wide, late_active, part = feed(late_hidden, w_late_up, late_lifts, w_late_down)
    layer_out, grad, low, turn_sums = boundary(
        step_turn, part, [third_rows, cotangent], vectors, (16, 17, 18), 2, 3, 6
    )

    part, late_slope, late_lift_slope = feed_back(
        low, late_hidden, late_wide, late_active, w_late_up, w_late_down
    )
    late_slope = lax.psum_scatter(late_slope, "fsdp", scatter_dimension=1, tiled=True)
    grad, low, late_sums = boundary(
        functools.partial(step_backward, 1.0), part, [grad, third_rows], vectors, (14,), 1, 3, 7
    )
    low = flat(low)
    filter_down_slope = lead_dot(swished, low).astype(jnp.bfloat16)
    middle_grad = swish_back(back_dot(low, w_filter_down), middle)
    middle_gain_slope = jnp.sum(middle_grad * middle_unit, axis=0)
    middle_shift_slope = jnp.sum(middle_grad, axis=0)
    scaled = middle_grad * own_vectors[11]
    shared = share(
        n,
        jnp.concatenate(
            [
                jnp.sum(scaled, axis=-1).reshape(n, frame_count),
                jnp.sum(scaled * middle_unit, axis=-1).reshape(n, frame_count),
            ]
        ),
        8,
    )
    totals = jnp.sum(shared, axis=0) / D
    filtered_grad = middle_inverse * (
        scaled - totals[:n].reshape(-1, 1) - middle_unit * totals[n:].reshape(-1, 1)
    )
    opened_low, filter_lift_slope, depth_slope = unconvolve(
        opened, gated, blocks(filtered_grad), behind, ahead, taps
    )
    opened_low = flat(opened_low)
    filter_up_slope = lead_dot(flat(filter_hidden), opened_low).astype(jnp.bfloat16)
    part = blocks(back_dot(opened_low, w_filter_up).astype(jnp.bfloat16))
    part, filter_slope = lax.optimization_barrier((part, pair_slopes(filter_up_slope, filter_down_slope, n)))
    filter_slope = lax.psum_scatter(filter_slope, "fsdp", scatter_dimension=1, tiled=True)
    grad, low, filter_sums = boundary(
        functools.partial(step_backward, 1.0), part, [grad, second_rows], vectors, (8,), 1, 3, 9
    )
    low = flat(low)
    output_slope = lead_dot(flat(blended), low).astype(jnp.bfloat16)
    blend_grad = blocks(back_dot(low, w_output).astype(jnp.bfloat16))
    packed_low, shift_sums, table_slope = unattend(packed, blend_grad, segment_rows, segment_columns, table)
    packed_low = flat(packed_low)
    project_slope = lead_dot(flat(mixer_hidden), packed_low).astype(jnp.bfloat16)
    part = blocks(back_dot(packed_low, w_project).astype(jnp.bfloat16))
    part, mixer_slope, late_slope = lax.optimization_barrier(
        (part, pair_slopes(project_slope, output_slope, n), late_slope)
    )
    mixer_slope = lax.psum_scatter(mixer_slope, "fsdp", scatter_dimension=1, tiled=True)
    grad, low, mixer_sums = boundary(
        functools.partial(step_backward, 0.5), part, [grad, first_rows], vectors, (3,), 1, 3, 10
    )
    part, early_slope, early_lift_slope = feed_back(
        low, early_hidden, early_wide, early_active, w_early_up, w_early_down
    )
    part, early_slope, filter_slope = lax.optimization_barrier((part, early_slope, filter_slope))
    early_slope = lax.psum_scatter(early_slope, "fsdp", scatter_dimension=1, tiled=True)
    slope_frames, early_sums = boundary(
        step_last, part, [grad, frames], vectors, (0,), 1, 2, 11, gathered=False
    )

    table_slope = jnp.roll(table_slope[:, ::-1], 1 - NREL // 2, axis=1)
    table_rows = NREL // (n * m)
    wide = jnp.concatenate([turn_sums, late_sums, filter_sums, mixer_sums, early_sums])
    wide_count = wide.shape[0]
    wide = jnp.transpose(wide.reshape(wide_count, n * m, rows), (1, 0, 2)).reshape(n * m, wide_count * rows)
    wide = jnp.concatenate(
        [wide, jnp.transpose(table_slope.reshape(heads, n * m, table_rows), (1, 0, 2)).reshape(n * m, -1)], axis=1
    )
    lift_full = lax.dynamic_update_slice(
        jnp.zeros((2, D), jnp.float32), filter_lift_slope.reshape(2, inner), (0, me * inner)
    ).reshape(n * m, -1)
    table_used = wide.shape[1]
    wide = jnp.concatenate([wide, lift_full], axis=1)
    wide_used = wide.shape[1]
    wide = jnp.pad(wide, ((0, 0), (0, -wide_used % LANES))).reshape(n * m, -1, LANES)
    group = jnp.concatenate(
        [
            shift_sums,
            middle_gain_slope[None],
            middle_shift_slope[None],
            depth_slope,
            jnp.transpose(early_lift_slope.reshape(inner, spans)),
            jnp.transpose(late_lift_slope.reshape(inner, spans)),
        ]
    )
    group_count = group.shape[0]
    group = jnp.transpose(group.reshape(group_count, m, rows), (1, 0, 2)).reshape(m, group_count * rows)
    group_used = group.shape[1]
    group = jnp.pad(group, ((0, 0), (0, -group_used % LANES))).reshape(m, -1, LANES)
    wide_all, group_all, late_up_wide, project_wide, filter_up_wide = collect(
        n, m, wide, group, [late_slope, mixer_slope, filter_slope], [(1, hidden), (3, inner), (2, inner)], 12
    )
    tables = wide_all.reshape(n, m, -1)[:, :, wide_count * rows : table_used]
    wide = jnp.sum(wide_all, axis=0).reshape(-1)
    lift_total = wide[table_used:wide_used]
    wide = wide[: wide_count * rows].reshape(wide_count, rows)
    tables = jnp.transpose(jnp.sum(tables, axis=1).reshape(HEADS, table_rows))
    group = jnp.sum(group_all, axis=0).reshape(-1)[:group_used].reshape(group_count, rows)
    def rejoin(value, low):
        return final(jnp.transpose(value[:, :, low:], (1, 0, 2)).reshape(rows, D))

    def final(value):
        return value.astype(jnp.float32)

    lift_slopes = KW + 5
    results = [
        layer_out,
        slope_frames,
        wide[12],
        wide[13],
        jnp.transpose(group[lift_slopes : lift_slopes + spans]).reshape(-1),
        wide[11],
        wide[9],
        wide[10],
        final(project_wide),
        group[0],
        group[1],
        rejoin(mixer_slope, 3 * inner),
        wide[8],
        tables,
        wide[6],
        wide[7],
        final(filter_up_wide),
        lift_total,
        jnp.transpose(group[4 : 4 + KW]),
        group[4 + KW],
        group[2],
        group[3],
        rejoin(filter_slope, 2 * inner),
        wide[5],
        wide[3],
        wide[4],
        final(late_up_wide),
        jnp.transpose(group[lift_slopes + spans : lift_slopes + 2 * spans]).reshape(-1),
        final(late_slope[n:]).reshape(spans * rows, D),
        wide[2],
        wide[0],
        wide[1],
    ]
    results[:2] = keep(layer_out, slope_frames)
    *results, early_slope = lax.optimization_barrier((*results, early_slope))
    (early_up_wide,) = giveback(n, [early_slope], [(1, hidden)], 14)
    results.insert(4, final(early_up_wide))
    results.insert(6, final(early_slope[n:]).reshape(spans * rows, D))
    return tuple(results)


def solution(mesh):
    in_specs = (
        P(("dp", "fsdp"), None),
        P(("dp", "fsdp")),
        P(("dp", "fsdp"), None),
        P(("dp", "fsdp")),
        P(("dp", "fsdp")),
        P(("dp", "fsdp"), None),
        P(("dp", "fsdp")),
        P(("dp", "fsdp"), None),
        P(("dp", "fsdp")),
        P(("dp", "fsdp")),
        P(("dp", "fsdp")),
        P(("dp", "fsdp"), None),
        P(("dp", "fsdp")),
        P(("dp", "fsdp")),
        P(("dp", "fsdp"), None),
        P(("dp", "fsdp")),
        P(("dp", "fsdp"), None),
        P(("dp", "fsdp")),
        P(("dp", "fsdp")),
        P(("dp", "fsdp"), None),
        P(("dp", "fsdp")),
        P(("dp", "fsdp"), None),
        P(("dp", "fsdp")),
        P(("dp", "fsdp")),
        P(("dp", "fsdp")),
        P(("dp", "fsdp"), None),
        P(("dp", "fsdp")),
        P(("dp", "fsdp")),
        P(("dp", "fsdp")),
        P(("dp", "fsdp"), None),
        P(("dp", "fsdp")),
        P(("dp", "fsdp"), None),
        P(("dp", "fsdp")),
        P(("dp", "fsdp")),
        P(("dp", "fsdp")),
    )
    out_specs = (
        P(("dp", "fsdp"), None),
        P(("dp", "fsdp"), None),
        P(("dp", "fsdp")),
        P(("dp", "fsdp")),
        P(("dp", "fsdp"), None),
        P(("dp", "fsdp")),
        P(("dp", "fsdp"), None),
        P(("dp", "fsdp")),
        P(("dp", "fsdp")),
        P(("dp", "fsdp")),
        P(("dp", "fsdp"), None),
        P(("dp", "fsdp")),
        P(("dp", "fsdp")),
        P(("dp", "fsdp"), None),
        P(("dp", "fsdp")),
        P(("dp", "fsdp"), None),
        P(("dp", "fsdp")),
        P(("dp", "fsdp")),
        P(("dp", "fsdp"), None),
        P(("dp", "fsdp")),
        P(("dp", "fsdp"), None),
        P(("dp", "fsdp")),
        P(("dp", "fsdp")),
        P(("dp", "fsdp")),
        P(("dp", "fsdp"), None),
        P(("dp", "fsdp")),
        P(("dp", "fsdp")),
        P(("dp", "fsdp")),
        P(("dp", "fsdp"), None),
        P(("dp", "fsdp")),
        P(("dp", "fsdp"), None),
        P(("dp", "fsdp")),
        P(("dp", "fsdp")),
        P(("dp", "fsdp")),
    )
    n, m = mesh.shape["dp"], mesh.shape["fsdp"]
    run = functools.partial(split_body, n, m) if n == 4 and D // (n * m) == 32 else body
    return jax.shard_map(run, mesh=mesh, in_specs=in_specs, out_specs=out_specs, check_vma=False)
```

```python
import functools

import jax
import jax.numpy as jnp
from jax import lax
from jax.experimental import pallas as pl
from jax.experimental.pallas import tpu as pltpu
from jax.sharding import PartitionSpec as P

D = 1024
HEADS = 16
HEAD = 64
KW = 31
NREL = 256


EPSILON = 1e-05
MASKED = -1e30
UTTERANCE_LIMIT = 4
MESH = pl.DeviceIdType.MESH
PIECES = 2
LAG = 2
BLOCK = 16
MARGIN = 16
LANES = 128


def flat_dot(left_rows, right_rows):
    return jnp.dot(left_rows, right_rows, preferred_element_type=jnp.float32)


def lead_dot(left_rows, right_rows):
    return lax.dot_general(
        left_rows, right_rows, (((0,), (0,)), ((), ())), preferred_element_type=jnp.float32
    )


def back_dot(left_rows, right_rows):
    return lax.dot_general(
        left_rows, right_rows, (((1,), (1,)), ((), ())), preferred_element_type=jnp.float32
    )


def norm_apply(values, norm_gain, norm_shift):
    centered = values - jnp.mean(values, axis=-1, keepdims=True)
    inverse = lax.rsqrt(jnp.mean(centered * centered, axis=-1, keepdims=True) + EPSILON)
    normed_unit = centered * inverse
    return (
        normed_unit * norm_gain.astype(jnp.float32) + norm_shift.astype(jnp.float32),
        normed_unit,
        inverse,
    )


def norm_back(upstream, normed_unit, inverse, norm_gain):
    scaled = upstream * norm_gain.astype(jnp.float32)
    adjusted = scaled - jnp.mean(scaled, axis=-1, keepdims=True)
    adjusted = adjusted - normed_unit * jnp.mean(scaled * normed_unit, axis=-1, keepdims=True)
    return (inverse * adjusted, jnp.sum(upstream * normed_unit, axis=0), jnp.sum(upstream, axis=0))


def swish_back(upstream, before):
    sigmoid_rows = jax.nn.sigmoid(before)
    return upstream * sigmoid_rows * (1.0 + before * (1.0 - sigmoid_rows))


def depthwise(gated_rows, kernel, segment_ids):
    margin = (KW - 1) // 2
    channels = gated_rows.shape[1]
    taps = jnp.transpose(kernel)[:, None, :]
    running = jnp.zeros_like(gated_rows)
    for utterance in range(UTTERANCE_LIMIT):
        inside = (segment_ids == utterance)[:, None]
        masked_rows = jnp.where(inside, gated_rows, 0.0)
        convolved = lax.conv_general_dilated(
            masked_rows[None],
            taps,
            (1,),
            ((margin, margin),),
            dimension_numbers=("NWC", "WIO", "NWC"),
            feature_group_count=channels,
            precision=lax.Precision.HIGHEST,
        )[0]
        running = running + jnp.where(inside, convolved, 0.0)
    return running


def fetch_feed(norm_gain, norm_shift, w_up, up_shift, w_down, down_shift):
    return (
        lax.all_gather(norm_gain, ("dp", "fsdp"), axis=0, tiled=True),
        lax.all_gather(norm_shift, ("dp", "fsdp"), axis=0, tiled=True),
        lax.all_gather(w_up, ("dp", "fsdp"), axis=0, tiled=True),
        lax.all_gather(up_shift, ("dp", "fsdp"), axis=0, tiled=True),
        lax.all_gather(w_down, ("dp", "fsdp"), axis=0, tiled=True),
        lax.all_gather(down_shift, ("dp", "fsdp"), axis=0, tiled=True),
    )


def reduce_feed(norm_gain, norm_shift, w_up, up_shift, w_down, down_shift):
    return (
        lax.psum_scatter(norm_gain, ("dp", "fsdp"), scatter_dimension=0, tiled=True),
        lax.psum_scatter(norm_shift, ("dp", "fsdp"), scatter_dimension=0, tiled=True),
        lax.psum_scatter(w_up, ("dp", "fsdp"), scatter_dimension=0, tiled=True),
        lax.psum_scatter(up_shift, ("dp", "fsdp"), scatter_dimension=0, tiled=True),
        lax.psum_scatter(w_down, ("dp", "fsdp"), scatter_dimension=0, tiled=True),
        lax.psum_scatter(down_shift, ("dp", "fsdp"), scatter_dimension=0, tiled=True),
    )


def fetch_mixer(
    norm_gain, norm_shift, w_project, query_shift, value_shift, w_output, output_shift, table_rows
):
    return (
        lax.all_gather(norm_gain, ("dp", "fsdp"), axis=0, tiled=True),
        lax.all_gather(norm_shift, ("dp", "fsdp"), axis=0, tiled=True),
        lax.all_gather(w_project, ("dp", "fsdp"), axis=0, tiled=True),
        lax.all_gather(query_shift, ("dp", "fsdp"), axis=0, tiled=True),
        lax.all_gather(value_shift, ("dp", "fsdp"), axis=0, tiled=True),
        lax.all_gather(w_output, ("dp", "fsdp"), axis=0, tiled=True),
        lax.all_gather(output_shift, ("dp", "fsdp"), axis=0, tiled=True),
        lax.all_gather(table_rows, ("dp", "fsdp"), axis=0, tiled=True),
    )


def reduce_mixer(
    norm_gain, norm_shift, w_project, query_shift, value_shift, w_output, output_shift, table_rows
):
    return (
        lax.psum_scatter(norm_gain, ("dp", "fsdp"), scatter_dimension=0, tiled=True),
        lax.psum_scatter(norm_shift, ("dp", "fsdp"), scatter_dimension=0, tiled=True),
        lax.psum_scatter(w_project, ("dp", "fsdp"), scatter_dimension=0, tiled=True),
        lax.psum_scatter(query_shift, ("dp", "fsdp"), scatter_dimension=0, tiled=True),
        lax.psum_scatter(value_shift, ("dp", "fsdp"), scatter_dimension=0, tiled=True),
        lax.psum_scatter(w_output, ("dp", "fsdp"), scatter_dimension=0, tiled=True),
        lax.psum_scatter(output_shift, ("dp", "fsdp"), scatter_dimension=0, tiled=True),
        lax.psum_scatter(table_rows, ("dp", "fsdp"), scatter_dimension=0, tiled=True),
    )


def fetch_filter(
    norm_gain,
    norm_shift,
    w_up,
    up_shift,
    depth_taps,
    depth_shift,
    middle_gain,
    middle_shift,
    w_down,
    down_shift,
    last_gain,
    last_shift,
):
    return (
        lax.all_gather(norm_gain, ("dp", "fsdp"), axis=0, tiled=True),
        lax.all_gather(norm_shift, ("dp", "fsdp"), axis=0, tiled=True),
        lax.all_gather(w_up, ("dp", "fsdp"), axis=0, tiled=True),
        lax.all_gather(up_shift, ("dp", "fsdp"), axis=0, tiled=True),
        lax.all_gather(depth_taps, ("dp", "fsdp"), axis=0, tiled=True),
        lax.all_gather(depth_shift, ("dp", "fsdp"), axis=0, tiled=True),
        lax.all_gather(middle_gain, ("dp", "fsdp"), axis=0, tiled=True),
        lax.all_gather(middle_shift, ("dp", "fsdp"), axis=0, tiled=True),
        lax.all_gather(w_down, ("dp", "fsdp"), axis=0, tiled=True),
        lax.all_gather(down_shift, ("dp", "fsdp"), axis=0, tiled=True),
        lax.all_gather(last_gain, ("dp", "fsdp"), axis=0, tiled=True),
        lax.all_gather(last_shift, ("dp", "fsdp"), axis=0, tiled=True),
    )


def reduce_filter(
    norm_gain,
    norm_shift,
    w_up,
    up_shift,
    depth_taps,
    depth_shift,
    middle_gain,
    middle_shift,
    w_down,
    down_shift,
    last_gain,
    last_shift,
):
    return (
        lax.psum_scatter(norm_gain, ("dp", "fsdp"), scatter_dimension=0, tiled=True),
        lax.psum_scatter(norm_shift, ("dp", "fsdp"), scatter_dimension=0, tiled=True),
        lax.psum_scatter(w_up, ("dp", "fsdp"), scatter_dimension=0, tiled=True),
        lax.psum_scatter(up_shift, ("dp", "fsdp"), scatter_dimension=0, tiled=True),
        lax.psum_scatter(depth_taps, ("dp", "fsdp"), scatter_dimension=0, tiled=True),
        lax.psum_scatter(depth_shift, ("dp", "fsdp"), scatter_dimension=0, tiled=True),
        lax.psum_scatter(middle_gain, ("dp", "fsdp"), scatter_dimension=0, tiled=True),
        lax.psum_scatter(middle_shift, ("dp", "fsdp"), scatter_dimension=0, tiled=True),
        lax.psum_scatter(w_down, ("dp", "fsdp"), scatter_dimension=0, tiled=True),
        lax.psum_scatter(down_shift, ("dp", "fsdp"), scatter_dimension=0, tiled=True),
        lax.psum_scatter(last_gain, ("dp", "fsdp"), scatter_dimension=0, tiled=True),
        lax.psum_scatter(last_shift, ("dp", "fsdp"), scatter_dimension=0, tiled=True),
    )


def feed_forward(values, weights):
    normed, normed_unit, inverse = norm_apply(values, weights[0], weights[1])
    hidden = normed.astype(jnp.bfloat16)
    widened = flat_dot(hidden, weights[2]) + weights[3].astype(jnp.float32)
    active = (widened * jax.nn.sigmoid(widened)).astype(jnp.bfloat16)
    result = values + 0.5 * (flat_dot(active, weights[4]) + weights[5].astype(jnp.float32))
    return (result, (normed_unit, inverse, hidden, widened, active))


def feed_backward(upstream, saved, weights):
    normed_unit, inverse, hidden, widened, active = saved
    half_grad = 0.5 * upstream
    half_low = half_grad.astype(jnp.bfloat16)
    down_slope = lead_dot(active, half_low)
    widened_grad = swish_back(back_dot(half_low, weights[4]), widened)
    widened_low = widened_grad.astype(jnp.bfloat16)
    up_slope = lead_dot(hidden, widened_low)
    hidden_grad = back_dot(widened_low, weights[2])
    input_grad, gain_slope, shift_slope = norm_back(hidden_grad, normed_unit, inverse, weights[0])
    slopes = (
        gain_slope,
        shift_slope,
        up_slope,
        jnp.sum(widened_grad, axis=0),
        down_slope,
        jnp.sum(half_grad, axis=0),
    )
    return (upstream + input_grad, slopes)


def bucket_table(frame_count):
    offsets = jnp.arange(2 * frame_count - 1, dtype=jnp.int32) - (frame_count - 1)
    buckets = jnp.clip(offsets, -(NREL // 2), NREL // 2 - 1) + NREL // 2
    return (buckets[:, None] == jnp.arange(NREL, dtype=jnp.int32)[None, :]).astype(jnp.float32)


def relative_bias(table_rows, frame_count):
    diagonals = jnp.dot(
        bucket_table(frame_count),
        table_rows.astype(jnp.float32),
        precision=lax.Precision.HIGHEST,
        preferred_element_type=jnp.float32,
    )
    flipped = jnp.concatenate(
        [jnp.transpose(diagonals[::-1]), jnp.zeros((HEADS, 1), jnp.float32)], axis=1
    )
    spread = jnp.broadcast_to(flipped[:, None, :], (HEADS, frame_count, 2 * frame_count))
    spread = spread.reshape(HEADS, 2 * frame_count * frame_count)
    sheared = spread[:, : frame_count * (2 * frame_count - 1)].reshape(
        HEADS, frame_count, 2 * frame_count - 1
    )
    return sheared[:, :, frame_count - 1 :]


def relative_slope(score_grad, frame_count):
    placed = jnp.pad(score_grad, ((0, 0), (0, 0), (frame_count - 1, 0)))
    flattened = jnp.pad(
        placed.reshape(HEADS, frame_count * (2 * frame_count - 1)), ((0, 0), (0, frame_count))
    )
    columns = jnp.sum(flattened.reshape(HEADS, frame_count, 2 * frame_count), axis=1)
    diagonals = columns[:, 2 * frame_count - 2 :: -1]
    return lax.dot_general(
        bucket_table(frame_count),
        diagonals,
        (((0,), (1,)), ((), ())),
        precision=lax.Precision.HIGHEST,
        preferred_element_type=jnp.float32,
    )


def mixer_scores(query_rows, key_matrix_rows, relative, same_utterance):
    unnormalized_scores = jnp.einsum(
        "jug,fug->ujf", query_rows, key_matrix_rows, preferred_element_type=jnp.float32
    )
    return jnp.where(same_utterance[None], HEAD ** (-0.5) * unnormalized_scores + relative, MASKED)


def mixer_forward(values, segment_ids, weights):
    frame_count = values.shape[0]
    normed, normed_unit, inverse = norm_apply(values, weights[0], weights[1])
    hidden = normed.astype(jnp.bfloat16)
    projected = flat_dot(hidden, weights[2])
    query_rows = (projected[:, :D] + weights[3].astype(jnp.float32)).astype(jnp.bfloat16)
    query_rows = query_rows.reshape(frame_count, HEADS, HEAD)
    key_matrix_rows = projected[:, D : 2 * D].astype(jnp.bfloat16).reshape(frame_count, HEADS, HEAD)
    value_matrix_rows = (projected[:, 2 * D :] + weights[4].astype(jnp.float32)).astype(
        jnp.bfloat16
    )
    value_matrix_rows = value_matrix_rows.reshape(frame_count, HEADS, HEAD)
    relative = relative_bias(weights[7], frame_count)
    same_utterance = segment_ids[:, None] == segment_ids[None, :]
    scores = mixer_scores(query_rows, key_matrix_rows, relative, same_utterance)
    row_peak = jnp.max(scores, axis=-1, keepdims=True)
    powered = jnp.exp(scores - row_peak)
    row_total = jnp.sum(powered, axis=-1, keepdims=True)
    log_total = row_peak + jnp.log(row_total)
    softmax_rows = (powered / row_total).astype(jnp.bfloat16)
    attention_blend = jnp.einsum(
        "ief,fiv->eiv", softmax_rows, value_matrix_rows, preferred_element_type=jnp.float32
    )
    attention_blend = attention_blend.reshape(frame_count, D).astype(jnp.bfloat16)
    result = values + (flat_dot(attention_blend, weights[5]) + weights[6].astype(jnp.float32))
    return (
        result,
        (
            normed_unit,
            inverse,
            hidden,
            query_rows,
            key_matrix_rows,
            value_matrix_rows,
            log_total,
            attention_blend,
            relative,
            same_utterance,
        ),
    )


def mixer_backward(upstream, saved, weights):
    (
        normed_unit,
        inverse,
        hidden,
        query_rows,
        key_matrix_rows,
        value_matrix_rows,
        log_total,
        attention_blend,
        relative,
        same_utterance,
    ) = saved
    frame_count = upstream.shape[0]
    upstream_low = upstream.astype(jnp.bfloat16)
    output_slope = lead_dot(attention_blend, upstream_low)
    attention_blend_gradient = (
        back_dot(upstream_low, weights[5]).astype(jnp.bfloat16).reshape(frame_count, HEADS, HEAD)
    )
    scores = mixer_scores(query_rows, key_matrix_rows, relative, same_utterance)
    soft_full = jnp.exp(scores - log_total)
    value_grad = jnp.einsum(
        "ybr,byq->ryq",
        soft_full.astype(jnp.bfloat16),
        attention_blend_gradient,
        preferred_element_type=jnp.float32,
    ).reshape(frame_count, D)
    soft_grad = jnp.einsum(
        "jug,fug->ujf",
        attention_blend_gradient,
        value_matrix_rows,
        preferred_element_type=jnp.float32,
    )
    score_grad = soft_full * (soft_grad - jnp.sum(soft_full * soft_grad, axis=-1, keepdims=True))
    table_slope = relative_slope(score_grad, frame_count)
    score_reduced_precision = (HEAD ** (-0.5) * score_grad).astype(jnp.bfloat16)
    query_grad = jnp.einsum(
        "ief,fiv->eiv", score_reduced_precision, key_matrix_rows, preferred_element_type=jnp.float32
    ).reshape(frame_count, D)
    key_grad = jnp.einsum(
        "ybr,byq->ryq", score_reduced_precision, query_rows, preferred_element_type=jnp.float32
    ).reshape(frame_count, D)
    projected_low = jnp.concatenate([query_grad, key_grad, value_grad], axis=1).astype(jnp.bfloat16)
    project_slope = lead_dot(hidden, projected_low)
    hidden_grad = back_dot(projected_low, weights[2])
    input_grad, gain_slope, shift_slope = norm_back(hidden_grad, normed_unit, inverse, weights[0])
    slopes = (
        gain_slope,
        shift_slope,
        project_slope,
        jnp.sum(query_grad, axis=0),
        jnp.sum(value_grad, axis=0),
        output_slope,
        jnp.sum(upstream, axis=0),
        table_slope,
    )
    return (upstream + input_grad, slopes)


def filter_forward(values, segment_ids, weights):
    normed, normed_unit, inverse = norm_apply(values, weights[0], weights[1])
    hidden = normed.astype(jnp.bfloat16)
    widened = flat_dot(hidden, weights[2]) + weights[3].astype(jnp.float32)
    gated_rows = widened[:, :D] * jax.nn.sigmoid(widened[:, D:])
    filtered = depthwise(gated_rows, weights[4].astype(jnp.float32), segment_ids) + weights[
        5
    ].astype(jnp.float32)
    middle, middle_unit, middle_inverse = norm_apply(filtered, weights[6], weights[7])
    swished = (middle * jax.nn.sigmoid(middle)).astype(jnp.bfloat16)
    result = values + (flat_dot(swished, weights[8]) + weights[9].astype(jnp.float32))
    return (
        result,
        (
            normed_unit,
            inverse,
            hidden,
            widened,
            gated_rows,
            middle_unit,
            middle_inverse,
            middle,
            swished,
        ),
    )


def filter_backward(upstream, saved, weights, segment_ids):
    (
        normed_unit,
        inverse,
        hidden,
        widened,
        gated_rows,
        middle_unit,
        middle_inverse,
        middle,
        swished,
    ) = saved
    upstream_low = upstream.astype(jnp.bfloat16)
    down_slope = lead_dot(swished, upstream_low)
    middle_grad = swish_back(back_dot(upstream_low, weights[8]), middle)
    filtered_grad, middle_gain_slope, middle_shift_slope = norm_back(
        middle_grad, middle_unit, middle_inverse, weights[6]
    )

    def local_filter(local_rows, local_kernel):
        return depthwise(local_rows, local_kernel, segment_ids)

    unused, pullback = jax.vjp(local_filter, gated_rows, weights[4].astype(jnp.float32))
    gated_grad, kernel_slope = pullback(filtered_grad)
    opened = jax.nn.sigmoid(widened[:, D:])
    widened_grad = jnp.concatenate(
        [gated_grad * opened, gated_grad * widened[:, :D] * opened * (1.0 - opened)], axis=1
    )
    widened_low = widened_grad.astype(jnp.bfloat16)
    up_slope = lead_dot(hidden, widened_low)
    hidden_grad = back_dot(widened_low, weights[2])
    input_grad, gain_slope, shift_slope = norm_back(hidden_grad, normed_unit, inverse, weights[0])
    slopes = (
        gain_slope,
        shift_slope,
        up_slope,
        jnp.sum(widened_grad, axis=0),
        kernel_slope,
        jnp.sum(filtered_grad, axis=0),
        middle_gain_slope,
        middle_shift_slope,
        down_slope,
        jnp.sum(upstream, axis=0),
    )
    return (upstream + input_grad, slopes)


def body(
    frames,
    segments,
    cotangent,
    early_gain,
    early_shift,
    early_up,
    early_lift,
    early_down,
    early_drop,
    mixer_gain,
    mixer_shift,
    mixer_project,
    query_bias,
    value_bias,
    mixer_output,
    mixer_drop,
    distance_table,
    filter_gain,
    filter_shift,
    filter_up,
    filter_lift,
    depth_weight,
    depth_bias,
    middle_gain,
    middle_shift,
    filter_down,
    filter_drop,
    late_gain,
    late_shift,
    late_up,
    late_lift,
    late_down,
    late_drop,
    final_gain,
    final_shift,
):
    start_rows = frames.astype(jnp.float32)
    final_upstream = cotangent.astype(jnp.float32)
    early_full = fetch_feed(early_gain, early_shift, early_up, early_lift, early_down, early_drop)
    first_rows, early_kept = feed_forward(start_rows, early_full)
    mixer_full = fetch_mixer(
        mixer_gain,
        mixer_shift,
        mixer_project,
        query_bias,
        value_bias,
        mixer_output,
        mixer_drop,
        distance_table,
    )
    second_rows, mixer_kept = mixer_forward(first_rows, segments, mixer_full)
    filter_full = fetch_filter(
        filter_gain,
        filter_shift,
        filter_up,
        filter_lift,
        depth_weight,
        depth_bias,
        middle_gain,
        middle_shift,
        filter_down,
        filter_drop,
        final_gain,
        final_shift,
    )
    third_rows, filter_kept = filter_forward(second_rows, segments, filter_full)
    late_full = fetch_feed(late_gain, late_shift, late_up, late_lift, late_down, late_drop)
    fourth_rows, late_kept = feed_forward(third_rows, late_full)
    layer_out, final_unit, final_inverse = norm_apply(fourth_rows, filter_full[10], filter_full[11])
    final_stats = (final_unit, final_inverse)
    upstream, final_gain_slope, final_shift_slope = norm_back(
        final_upstream, final_stats[0], final_stats[1], filter_full[10]
    )
    upstream, late_slopes = feed_backward(upstream, late_kept, late_full)
    late_summed = reduce_feed(
        late_slopes[0],
        late_slopes[1],
        late_slopes[2],
        late_slopes[3],
        late_slopes[4],
        late_slopes[5],
    )
    upstream, filter_grads = filter_backward(upstream, filter_kept, filter_full, segments)
    filter_summed = reduce_filter(
        filter_grads[0],
        filter_grads[1],
        filter_grads[2],
        filter_grads[3],
        filter_grads[4],
        filter_grads[5],
        filter_grads[6],
        filter_grads[7],
        filter_grads[8],
        filter_grads[9],
        final_gain_slope,
        final_shift_slope,
    )
    upstream, mixer_grads = mixer_backward(upstream, mixer_kept, mixer_full)
    mixer_summed = reduce_mixer(
        mixer_grads[0],
        mixer_grads[1],
        mixer_grads[2],
        mixer_grads[3],
        mixer_grads[4],
        mixer_grads[5],
        mixer_grads[6],
        mixer_grads[7],
    )
    upstream, early_slopes = feed_backward(upstream, early_kept, early_full)
    early_summed = reduce_feed(
        early_slopes[0],
        early_slopes[1],
        early_slopes[2],
        early_slopes[3],
        early_slopes[4],
        early_slopes[5],
    )
    return (
        layer_out,
        upstream,
        early_summed[0],
        early_summed[1],
        early_summed[2],
        early_summed[3],
        early_summed[4],
        early_summed[5],
        mixer_summed[0],
        mixer_summed[1],
        mixer_summed[2],
        mixer_summed[3],
        mixer_summed[4],
        mixer_summed[5],
        mixer_summed[6],
        mixer_summed[7],
        filter_summed[0],
        filter_summed[1],
        filter_summed[2],
        filter_summed[3],
        filter_summed[4],
        filter_summed[5],
        filter_summed[6],
        filter_summed[7],
        filter_summed[8],
        filter_summed[9],
        late_summed[0],
        late_summed[1],
        late_summed[2],
        late_summed[3],
        late_summed[4],
        late_summed[5],
        filter_summed[10],
        filter_summed[11],
    )


def near(me, n):
    if n == 4:
        row, column = me // 2, me % 2
        flip_row, flip_column = (1 - row) * 2 + column, row * 2 + 1 - column
        across = (1 - row) * 2 + 1 - column
        return [(flip_column, flip_column), (flip_row, flip_row), (across, across)]
    return [((me + step) % n, (me + n - step) % n) for step in range(1, n)]


def greet(targets):
    barrier = pltpu.get_barrier_semaphore()
    for target in targets:
        pl.semaphore_signal(barrier, inc=1, device_id={"dp": target}, device_id_type=MESH)
    pl.semaphore_wait(barrier, len(targets))


def greet_all(n, m):
    me, lane = lax.axis_index("dp"), lax.axis_index("fsdp")
    barrier = pltpu.get_barrier_semaphore()

    def say(step, carry):
        target = {"dp": (me + step // m) % n, "fsdp": (lane + step % m) % m}
        pl.semaphore_signal(barrier, inc=1, device_id=target, device_id_type=MESH)
        return carry

    lax.fori_loop(1, n * m, say, 0)
    pl.semaphore_wait(barrier, n * m - 1)


def remote(src, dst, send, recv, target):
    return pltpu.make_async_remote_copy(
        src_ref=src, dst_ref=dst, send_sem=send, recv_sem=recv, device_id=target, device_id_type=MESH
    )


def columns(start, width):
    return pl.ds(pl.multiple_of(start * width, width), width)


def column_pieces(index, n, sizes):
    pieces = []
    for place, (groups, width) in enumerate(sizes):
        for group in range(groups):
            wide = pl.ds(pl.multiple_of((group * n + index) * width, width), width)
            pieces.append((place, wide, pl.ds(group * width, width)))
    return pieces


def row_of(shards, line, first):
    rows = shards.shape[0]
    lines = shards[:, line, :]
    lanes = lax.broadcasted_iota(jnp.int32, lines.shape, 1) // 32
    places = lax.broadcasted_iota(jnp.int32, lines.shape, 0) % 4
    merged = jnp.zeros_like(lines)
    for quarter in range(4):
        shift = (32 * quarter - 32 * first) % LANES
        moved = pltpu.roll(lines, shift, 1) if shift else lines
        merged = merged + jnp.where((lanes == quarter) & (places == quarter), moved, 0.0)
    return [
        jnp.sum(merged[4 * tile : 4 * tile + 4], axis=0, keepdims=True) for tile in range(rows // 4)
    ]


def pack_small(small, singles, lifts, table):
    rows = singles[0].shape[0]
    small[...] = jnp.zeros_like(small)
    for at, single in enumerate(singles):
        line, low = at * rows // LANES, at * rows % LANES
        small[line : line + 1, low : low + rows] = single[...].astype(jnp.float32).reshape(1, rows)
    for at, lift in enumerate(lifts):
        line, count = 5 + at, lift.shape[0]
        small[line : line + 1, 0:count] = lift[...].astype(jnp.float32).reshape(1, count)
    small[8 : 8 + table.shape[0], 0 : table.shape[1]] = table[...].astype(jnp.float32)


def spread_vectors(n, m, inner, me, single_count, small_all, gains, own, lifts, wide_lifts):
    for index in range(single_count):
        for tile, line in enumerate(row_of(small_all, index // 4, index % 4)):
            gains[index : index + 1, tile * LANES : (tile + 1) * LANES] = line
    own[...] = gains[:, columns(me, inner)]
    for index in range(2):
        lines = small_all[pl.ds(me * m, m), 5 + index, :]
        for tile in range(m):
            lifts[index : index + 1, tile * LANES : (tile + 1) * LANES] = lines[tile : tile + 1, :]
    lanes = lax.broadcasted_iota(jnp.int32, (1, LANES), 1)
    for group in range(2):
        for tile in range(inner // LANES):
            first = group * n * m // 2 + me * n + 2 * tile
            left, right = small_all[pl.ds(first, 1), 7, :], small_all[pl.ds(first + 1, 1), 7, :]
            low = group * inner + tile * LANES
            wide_lifts[0:1, low : low + LANES] = jnp.where(
                lanes < LANES // 2, left, pltpu.roll(right, LANES // 2, 1)
            )


def exchange_kernel(n, m, width, inner, *refs):
    early_up, early_down, late_up, project, filter_up, output, filter_down, depth, segs, frames = refs[:10]
    singles, lift_shards, table = refs[10:29], refs[29:32], refs[32]
    up_full, down_full, late_split, mixer_split, filter_split, small_all = refs[33:39]
    gains, own, lifts, wide_lifts, depth_all, segs_all, spread = refs[39:46]
    gathered, small, held, local, send, recv, small_send, small_recv, up_send, up_recv = refs[46:56]
    climb_send, climb_recv, pass_send, pass_recv, out_send, out_recv, depth_send, depth_recv = refs[56:]
    pack_small(gathered.at[0], singles, lift_shards, table)
    small[...] = gathered[0].astype(jnp.bfloat16)
    me, lane = lax.axis_index("dp"), lax.axis_index("fsdp")
    here = me * m + lane
    levels = m // 2
    level = lane // 2
    units = early_down.shape[0]
    beside = lane + 1 - 2 * (lane % 2)
    others = near(me, n)
    ways = (1, -1)
    greet_all(n, m)

    def place(kind, unit, source):
        if kind:
            return up_full.at[((me + n - unit) % n) * m + source]
        return down_full.at[source, unit]

    def climb(kind, way, distance, unit, src=None):
        block = place(kind, unit, (lane + m - 2 * ways[way] * (distance - 1)) % m)
        return remote(
            block if src is None else src,
            block,
            climb_send.at[kind, way, distance - 1, unit],
            climb_recv.at[kind, way, distance - 1, unit],
            {"fsdp": (lane + m + 2 * ways[way]) % m},
        )

    def across(kind, offset, unit, src=None):
        block = place(kind, unit, (lane + 2 * offset) % m)
        return remote(
            block if src is None else src,
            block,
            pass_send.at[kind, offset, unit],
            pass_recv.at[kind, offset, unit],
            {"fsdp": beside},
        )

    def open_way(way):
        return level < levels - 1 if ways[way] > 0 else level > 0

    def reached(way, distance):
        return level >= distance if ways[way] > 0 else level + distance < levels

    def launch(kind, unit, src=None):
        for way in range(2):

            @pl.when(open_way(way))
            def _():
                climb(kind, way, 1, unit, src).start()

        across(kind, 0, unit, src).start()

    def to_device(step):
        target = {"dp": (me + step // m) % n, "fsdp": (lane + step % m) % m}
        return remote(small, small_all.at[here], small_send.at[step], small_recv.at[step], target)

    def to_lane(step):
        return remote(
            depth, depth_all.at[lane], depth_send.at[step], depth_recv.at[step], {"fsdp": (lane + step) % m}
        )

    def to_column(step):
        other = (me + step) % n
        return remote(
            early_up.at[:, columns(other, width)], up_full.at[here], up_send.at[step], up_recv.at[step], {"dp": other}
        )

    def each(call):
        def turn(step, carry):
            call(step)
            return carry

        return turn

    def pieces(index):
        found = [(late_up.at[:, columns(index, width)], late_split.at[me])]
        for group in range(3):
            wide = pl.ds(pl.multiple_of(group * inner * n + index * inner, inner), inner)
            found.append((project.at[:, wide], mixer_split.at[me, :, pl.ds(group * inner, inner)]))
        for group in range(2):
            wide = pl.ds(pl.multiple_of(group * inner * n + index * inner, inner), inner)
            found.append((filter_up.at[:, wide], filter_split.at[me, :, pl.ds(group * inner, inner)]))
        found.append((segs, segs_all.at[me]))
        return found

    lax.fori_loop(1, n * m, each(lambda step: to_device(step).start()), 0)
    lax.fori_loop(1, n, each(lambda step: to_column(step).start()), 0)
    lax.fori_loop(0, units, each(lambda unit: launch(0, unit, early_down.at[unit])), 0)
    mine = early_up.at[:, columns(me, width)]
    launch(1, 0, mine)
    copies = []
    for peer, (target, unused) in enumerate(others):
        for at, (src, dst) in enumerate(pieces(target)):
            copies.append(remote(src, dst, send.at[peer, at], recv.at[peer, at], {"dp": target}))
    owns = [(small, small_all.at[here]), (mine, up_full.at[here]), (early_down, down_full.at[lane])]
    owns += pieces(me)
    for group in range(n):
        wide = pl.ds(group * inner, inner)
        owns.append((output.at[:, wide], mixer_split.at[group, :, pl.ds(3 * inner, inner)]))
        owns.append((filter_down.at[:, wide], filter_split.at[group, :, pl.ds(2 * inner, inner)]))
    owns.append((depth, depth_all.at[lane]))
    owns = [pltpu.make_async_copy(src, dst, local.at[at]) for at, (src, dst) in enumerate(owns)]
    for copy in owns:
        copy.start()
    for step in range(1, n):
        to_column(step).wait_recv()
        launch(1, step)
    for copy in copies:
        copy.start()
    lax.fori_loop(1, m, each(lambda step: to_lane(step).start()), 0)
    def carry_on(kind, distance, unit):
        for way in range(2):

            @pl.when(reached(way, distance))
            def _():
                climb(kind, way, distance, unit).wait_recv()
                offset = levels - distance if ways[way] > 0 else distance
                across(kind, offset, unit).start()
                if distance < levels - 1:

                    @pl.when(open_way(way))
                    def _():
                        climb(kind, way, distance + 1, unit).start()

    def finish(kind, unit):
        for offset in range(levels):
            across(kind, offset, unit).wait()
        for way in range(2):
            for distance in range(1, levels):
                begun = open_way(way)
                if distance > 1:
                    begun = begun & reached(way, distance - 1)

                @pl.when(begun)
                def _():
                    climb(kind, way, distance, unit).wait_send()

    for kind in range(2):
        lax.fori_loop(0, units, each(functools.partial(carry_on, kind, 1)), 0)
    owns[0].wait()
    lax.fori_loop(1, n * m, each(lambda step: to_device(step).wait()), 0)
    gathered[...] = small_all[...].astype(jnp.float32)
    spread_vectors(n, m, inner, me, len(singles), gathered, gains, own, lifts, wide_lifts)
    gain, shift = gains[0:1, :], gains[1:2, :]

    def work(block, carry):
        span = pl.ds(pl.multiple_of(block * BLOCK, BLOCK), BLOCK)
        unit, inverse = unit_of(frames[span, :].astype(jnp.float32))
        held[span, :] = (unit * gain + shift).astype(jnp.bfloat16)
        return carry

    lax.fori_loop(0, frames.shape[0] // BLOCK, work, 0)
    keep = pltpu.make_async_copy(held, spread.at[me], local.at[len(owns)])
    keep.start()
    outgoing = []
    for peer, (target, unused) in enumerate(others):
        outgoing.append(remote(held, spread.at[me], out_send.at[peer], out_recv.at[peer], {"dp": target}))
    for copy in outgoing:
        copy.start()

    for distance in range(2, levels):
        for kind in range(2):
            lax.fori_loop(0, units, each(functools.partial(carry_on, kind, distance)), 0)
    for copy in owns[1:] + copies + outgoing:
        copy.wait()
    keep.wait()
    for kind in range(2):
        lax.fori_loop(0, units, each(functools.partial(finish, kind)), 0)
    lax.fori_loop(1, n, each(lambda step: to_column(step).wait_send()), 0)
    lax.fori_loop(1, m, each(lambda step: to_lane(step).wait()), 0)


def exchange(n, m, early_up, early_down, late_up, project, filter_up, output, filter_down, depth, segs, frames, singles, lifts, table):
    rows, width = early_up.shape[0], early_up.shape[1] // n
    inner = output.shape[1] // n
    frame_count, deep = frames.shape
    units, levels = early_down.shape[0], m // 2
    low, full = jnp.bfloat16, jnp.float32
    packed = (16, LANES)
    struct = jax.ShapeDtypeStruct
    outs = [
        struct((n * m, rows, width), low),
        struct((m,) + early_down.shape, low),
        struct((n, rows, width), low),
        struct((n, rows, 4 * inner), low),
        struct((n, rows, 3 * inner), low),
        struct((n * m,) + packed, low),
        struct((len(singles), deep), full),
        struct((len(singles), inner), full),
        struct((2, width), full),
        struct((1, 2 * inner), full),
        struct((m,) + depth.shape, low),
        struct((n,) + segs.shape, segs.dtype),
        struct((n, frame_count, deep), low),
    ]
    anywhere = pl.BlockSpec(memory_space=pl.ANY)
    inside = pl.BlockSpec(memory_space=pltpu.VMEM)
    dma = pltpu.SemaphoreType.DMA
    return pl.pallas_call(
        functools.partial(exchange_kernel, n, m, width, inner),
        out_shape=outs,
        in_specs=[anywhere] * 9 + [inside] * (2 + len(singles) + len(lifts)),
        out_specs=[anywhere] * 5 + [inside] * 5 + [anywhere] * 3,
        scratch_shapes=[
            pltpu.VMEM((n * m,) + packed, full),
            pltpu.VMEM(packed, low),
            pltpu.VMEM((frame_count, deep), low),
            dma((2 * n + 12,)),
            dma((n - 1, 7)),
            dma((n - 1, 7)),
            dma((n * m,)),
            dma((n * m,)),
            dma((n,)),
            dma((n,)),
            dma((2, 2, levels - 1, units)),
            dma((2, 2, levels - 1, units)),
            dma((2, levels, units)),
            dma((2, levels, units)),
            dma((n - 1,)),
            dma((n - 1,)),
            dma((m,)),
            dma((m,)),
        ],
        compiler_params=pltpu.CompilerParams(collective_id=0, has_side_effects=True),
        name="exchange",
    )(
        early_up, early_down, late_up, project, filter_up, output, filter_down, depth, segs, frames,
        *singles, *lifts, table,
    )


def return_copies(n, sizes, narrows, wides, local, send, recv):
    me = lax.axis_index("dp")
    copies = []
    for peer, (target, unused) in enumerate(near(me, n)):
        for at, (place, wide, narrow) in enumerate(column_pieces(me, n, sizes)):
            copies.append(
                remote(narrows[place].at[target, :, narrow], wides[place].at[:, wide], send.at[peer, at], recv.at[peer, at], {"dp": target})
            )
    for at, (place, wide, narrow) in enumerate(column_pieces(me, n, sizes)):
        copies.append(pltpu.make_async_copy(narrows[place].at[me, :, narrow], wides[place].at[:, wide], local.at[at]))
    return copies


def giveback_kernel(n, sizes, *refs):
    count = len(sizes)
    narrows, wides = refs[:count], refs[count : 2 * count]
    local, send, recv = refs[2 * count :]
    greet([target for target, unused in near(lax.axis_index("dp"), n)])
    copies = return_copies(n, sizes, narrows, wides, local, send, recv)
    for copy in copies:
        copy.start()
    for copy in copies:
        copy.wait()


def giveback(n, narrows, sizes, number):
    rows = narrows[0].shape[1]
    total = sum(groups for groups, width in sizes)
    outs = [jax.ShapeDtypeStruct((rows, groups * width * n), jnp.bfloat16) for groups, width in sizes]
    anywhere = pl.BlockSpec(memory_space=pl.ANY)
    return pl.pallas_call(
        functools.partial(giveback_kernel, n, sizes),
        out_shape=outs,
        in_specs=[anywhere] * len(narrows),
        out_specs=[anywhere] * len(outs),
        scratch_shapes=[
            pltpu.SemaphoreType.DMA((total,)),
            pltpu.SemaphoreType.DMA((n - 1, total)),
            pltpu.SemaphoreType.DMA((n - 1, total)),
        ],
        compiler_params=pltpu.CompilerParams(collective_id=number, has_side_effects=True),
        name="giveback",
    )(*narrows)


def collect_kernel(n, m, sizes, *refs):
    count = len(sizes)
    wide, group = refs[:2]
    narrows, wides = refs[2 : 2 + count], refs[4 + count : 4 + 2 * count]
    wide_all, group_all = refs[2 + count : 4 + count]
    local, send, recv, group_send, group_recv, back_local, back_send, back_recv = refs[4 + 2 * count :]
    me, lane = lax.axis_index("dp"), lax.axis_index("fsdp")
    here = me * m + lane
    greet_all(n, m)

    def to_device(step):
        other, beside = (me + step // m) % n, (lane + step % m) % m
        return remote(
            wide.at[other * m + beside], wide_all.at[here], send.at[step], recv.at[step], {"dp": other, "fsdp": beside}
        )

    def to_group(step):
        beside = (lane + step) % m
        return remote(group.at[beside], group_all.at[lane], group_send.at[step], group_recv.at[step], {"fsdp": beside})

    def start_wide(step, carry):
        to_device(step).start()
        return carry

    def start_group(step, carry):
        to_group(step).start()
        return carry

    def wait_wide(step, carry):
        to_device(step).wait()
        return carry

    def wait_group(step, carry):
        to_group(step).wait()
        return carry

    own = pltpu.make_async_copy(wide.at[here], wide_all.at[here], local.at[0])
    own_group = pltpu.make_async_copy(group.at[lane], group_all.at[lane], local.at[1])
    own.start()
    own_group.start()
    lax.fori_loop(1, n * m, start_wide, 0)
    lax.fori_loop(1, m, start_group, 0)
    copies = return_copies(n, sizes, narrows, wides, back_local, back_send, back_recv)
    for copy in copies:
        copy.start()
    own.wait()
    own_group.wait()
    lax.fori_loop(1, n * m, wait_wide, 0)
    lax.fori_loop(1, m, wait_group, 0)
    for copy in copies:
        copy.wait()


def collect(n, m, wide, group, narrows, sizes, number):
    inside = pl.BlockSpec(memory_space=pltpu.VMEM)
    anywhere = pl.BlockSpec(memory_space=pl.ANY)
    rows = narrows[0].shape[1]
    total = sum(groups for groups, width in sizes)
    outs = [jax.ShapeDtypeStruct(wide.shape, wide.dtype), jax.ShapeDtypeStruct(group.shape, group.dtype)]
    outs += [jax.ShapeDtypeStruct((rows, groups * width * n), jnp.bfloat16) for groups, width in sizes]
    return pl.pallas_call(
        functools.partial(collect_kernel, n, m, sizes),
        out_shape=outs,
        in_specs=[inside] * 2 + [anywhere] * len(sizes),
        out_specs=[inside] * 2 + [anywhere] * len(sizes),
        scratch_shapes=[
            pltpu.SemaphoreType.DMA((2,)),
            pltpu.SemaphoreType.DMA((n * m,)),
            pltpu.SemaphoreType.DMA((n * m,)),
            pltpu.SemaphoreType.DMA((m,)),
            pltpu.SemaphoreType.DMA((m,)),
            pltpu.SemaphoreType.DMA((total,)),
            pltpu.SemaphoreType.DMA((n - 1, total)),
            pltpu.SemaphoreType.DMA((n - 1, total)),
        ],
        compiler_params=pltpu.CompilerParams(collective_id=number, has_side_effects=True),
        name="collect",
    )(wide, group, *narrows)


def keep_kernel(first, second, first_out, second_out):
    first_out[...] = first[...]
    second_out[...] = second[...]


def keep(first, second):
    inside = pl.BlockSpec(memory_space=pltpu.VMEM)
    return pl.pallas_call(
        keep_kernel,
        out_shape=[jax.ShapeDtypeStruct(value.shape, value.dtype) for value in (first, second)],
        in_specs=[inside] * 2,
        out_specs=[inside] * 2,
        name="keep",
    )(first, second)


def unit_of(values):
    centered = values - jnp.mean(values, axis=-1, keepdims=True)
    inverse = lax.rsqrt(jnp.mean(centered * centered, axis=-1, keepdims=True) + EPSILON)
    return centered * inverse, inverse


def unit_back(upstream, unit, inverse, gain):
    scaled = upstream * gain
    adjusted = scaled - jnp.mean(scaled, axis=-1, keepdims=True)
    return inverse * (adjusted - unit * jnp.mean(scaled * unit, axis=-1, keepdims=True))


def step_forward(scale, total, states, vectors):
    values = states[0] + scale * (total + vectors[0])
    unit, inverse = unit_of(values)
    return [values], unit * vectors[1] + vectors[2], []


def step_turn(total, states, vectors):
    values = states[0] + 0.5 * (total + vectors[0])
    upstream = states[1]
    unit, inverse = unit_of(values)
    layer_out = unit * vectors[1] + vectors[2]
    grad = unit_back(upstream, unit, inverse, vectors[1])
    half = 0.5 * grad
    return [layer_out, grad], half, [upstream * unit, upstream, half]


def step_backward(scale, total, states, vectors):
    unit, inverse = unit_of(states[1])
    grad = states[0] + unit_back(total, unit, inverse, vectors[0])
    sent = scale * grad
    return [grad], sent, [total * unit, total, sent]


def step_last(total, states, vectors):
    unit, inverse = unit_of(states[1])
    grad = states[0] + unit_back(total, unit, inverse, vectors[0])
    return [grad], None, [total * unit, total]


def boundary_kernel(step, shape, *refs):
    gathered, state_count, out_count, sum_count, picked = shape
    refs = list(refs)
    take = lambda count: [refs.pop(0) for unused in range(count)]
    part = take(1)[0]
    states = take(state_count)
    vectors = take(1)[0]
    outs = take(out_count)
    spread = take(1)[0] if gathered else None
    sums = take(1)[0] if sum_count else None
    arrived, passing, mine, merged, own, local = take(6)
    relay_send, relay_recv, direct_send, direct_recv, merge_send, merge_recv = take(6)
    if gathered:
        held, held_sem, out_send, out_recv, pass_send, pass_recv = take(6)
    partials = take(1)[0] if sum_count else None
    me = lax.axis_index("dp")
    row, column = me // 2, me % 2
    sides = [row * 2 + 1 - column, (1 - row) * 2 + column]
    across = (1 - row) * 2 + 1 - column
    half = own.shape[0] // 2
    height = half // PIECES
    both, places = range(2), range(PIECES)

    def span(axis, piece):
        return pl.ds(axis * half + piece * height, height)

    def inner(piece):
        return pl.ds(piece * height, height)

    def relay(axis, piece):
        return remote(
            part.at[across, span(axis, piece)],
            passing.at[axis, inner(piece)],
            relay_send.at[axis, piece],
            relay_recv.at[axis, piece],
            {"dp": sides[axis]},
        )

    def direct(axis, piece):
        return remote(
            part.at[sides[axis], span(axis, piece)],
            arrived.at[axis, span(axis, piece)],
            direct_send.at[axis, piece],
            direct_recv.at[axis, piece],
            {"dp": sides[axis]},
        )

    def merge(axis, piece):
        return remote(
            merged.at[axis, inner(piece)],
            arrived.at[1 - axis, span(axis, piece)],
            merge_send.at[axis, piece],
            merge_recv.at[axis, piece],
            {"dp": sides[1 - axis]},
        )

    def hand(target, axis, piece):
        return remote(
            held.at[span(axis, piece)],
            spread.at[me, span(axis, piece)],
            out_send.at[target, axis, piece],
            out_recv.at[target, axis, piece],
            {"dp": sides[target]},
        )

    def onward(axis, piece):
        block = spread.at[sides[axis], span(axis, piece)]
        return remote(
            block, block, pass_send.at[axis, piece], pass_recv.at[axis, piece], {"dp": sides[1 - axis]}
        )

    def forward(axis, piece):
        hand(axis, axis, piece).wait_recv()
        onward(axis, piece).start()

    greet(sides)
    for piece in places:
        for axis in both:
            relay(axis, piece).start()
    locals_ = [
        pltpu.make_async_copy(part.at[sides[1 - axis], pl.ds(axis * half, half)], mine.at[axis], local.at[axis])
        for axis in both
    ]
    locals_.append(pltpu.make_async_copy(part.at[me], own, local.at[2]))
    for copy in locals_:
        copy.start()
    for piece in places:
        for axis in both:
            direct(axis, piece).start()
    if sum_count:
        partials[...] = jnp.zeros_like(partials)
    for copy in locals_:
        copy.wait()
    for piece in places:
        for axis in both:
            relay(axis, piece).wait_recv()

            def join(block, carry):
                rows = pl.ds(pl.multiple_of(piece * height + block * BLOCK, BLOCK), BLOCK)
                total = passing[axis, rows, :].astype(jnp.float32) + mine[axis, rows, :].astype(jnp.float32)
                merged[axis, rows, :] = total.astype(jnp.bfloat16)
                return carry

            lax.fori_loop(0, height // BLOCK, join, 0)
            merge(axis, piece).start()
    rows_of = [vectors[pl.ds(index, 1), :] for index in picked]
    order = [(axis, piece) for piece in places for axis in both]
    for at, (axis, piece) in enumerate(order):
        direct(axis, piece).wait_recv()
        merge(axis, piece).wait_recv()

        def work(block, carry):
            rows = pl.ds(pl.multiple_of(axis * half + piece * height + block * BLOCK, BLOCK), BLOCK)
            total = own[rows, :].astype(jnp.float32)
            for side in both:
                total = total + arrived[side, rows, :].astype(jnp.float32)
            made, sent, terms = step(total, [state[rows, :].astype(jnp.float32) for state in states], rows_of)
            for out, value in zip(outs, made):
                out[rows, :] = value
            if gathered:
                held[rows, :] = sent.astype(jnp.bfloat16)
            for index, term in enumerate(terms):
                partials[index] += sum(term[8 * low : 8 * low + 8] for low in range(BLOCK // 8))
            return carry

        lax.fori_loop(0, height // BLOCK, work, 0)
        if gathered:
            for target in both:
                hand(target, axis, piece).start()
            if at >= LAG:
                forward(*order[at - LAG])
    if gathered:
        keep = pltpu.make_async_copy(held, spread.at[me], held_sem)
        keep.start()
        for axis, piece in order[len(order) - LAG :]:
            forward(axis, piece)
    for index in range(sum_count):
        sums[pl.ds(index, 1), :] = jnp.sum(partials[index], axis=0, keepdims=True)
    for axis, piece in order:
        relay(axis, piece).wait_send()
        direct(axis, piece).wait_send()
        merge(axis, piece).wait_send()
    if gathered:
        for axis, piece in order:
            hand(axis, axis, piece).wait_send()
            hand(1 - axis, axis, piece).wait()
        for axis, piece in order:
            onward(axis, piece).wait()
        keep.wait()


def boundary(step, part, states, vectors, picked, out_count, sum_count, number, gathered=True):
    n, rows, width = part.shape
    inside = pl.BlockSpec(memory_space=pltpu.VMEM)
    anywhere = pl.BlockSpec(memory_space=pl.ANY)
    dma = pltpu.SemaphoreType.DMA
    shape = (gathered, len(states), out_count, sum_count, picked)
    low = jnp.bfloat16
    scratch = [
        pltpu.VMEM((2, rows, width), low),
        pltpu.VMEM((2, rows // 2, width), low),
        pltpu.VMEM((2, rows // 2, width), low),
        pltpu.VMEM((2, rows // 2, width), low),
        pltpu.VMEM((rows, width), low),
        dma((3,)),
    ]
    scratch += [dma((2, PIECES))] * 6
    outs = [jax.ShapeDtypeStruct((rows, width), jnp.float32)] * out_count
    out_specs = [inside] * out_count
    if gathered:
        outs.append(jax.ShapeDtypeStruct((n, rows, width), low))
        out_specs.append(anywhere)
        scratch += [pltpu.VMEM((rows, width), low), dma]
        scratch += [dma((2, 2, PIECES))] * 2 + [dma((2, PIECES))] * 2
    if sum_count:
        outs.append(jax.ShapeDtypeStruct((sum_count, width), jnp.float32))
        out_specs.append(inside)
        scratch.append(pltpu.VMEM((sum_count, 8, width), jnp.float32))
    return pl.pallas_call(
        functools.partial(boundary_kernel, step, shape),
        out_shape=outs,
        in_specs=[anywhere] + [inside] * (len(states) + 1),
        out_specs=out_specs,
        scratch_shapes=scratch,
        compiler_params=pltpu.CompilerParams(collective_id=number, has_side_effects=True),
        name="boundary",
    )(part, *states, vectors)


def toeplitz(line, frame_count):
    wide = jnp.broadcast_to(line, (frame_count, NREL))
    return pltpu.roll(wide, NREL - frame_count + 1, 1, stride=1, stride_axis=0)[:, :frame_count]


def head_scores(packed, head, heads, same, bias):
    size = heads * HEAD
    query_rows = packed[:, head * HEAD : (head + 1) * HEAD]
    key_rows = packed[:, size + head * HEAD : size + (head + 1) * HEAD]
    value_rows = packed[:, 2 * size + head * HEAD : 2 * size + (head + 1) * HEAD]
    scores = jnp.where(same, HEAD ** (-0.5) * back_dot(query_rows, key_rows) + bias, MASKED)
    powered = jnp.exp(scores - jnp.max(scores, axis=-1, keepdims=True))
    soft = powered / jnp.sum(powered, axis=-1, keepdims=True)
    return query_rows, key_rows, value_rows, soft


def attend_kernel(heads, packed, segment_rows, segment_columns, table, blended, bias):
    frame_count = packed.shape[1]

    @pl.when(pl.program_id(0) == 0)
    def _():
        for head in range(heads):
            bias[head] = toeplitz(table[pl.ds(head, 1), :], frame_count)

    same = segment_columns[0] == segment_rows[0]
    block = packed[0]
    results = []
    for head in range(heads):
        unused, unused_too, value_rows, soft = head_scores(block, head, heads, same, bias[head])
        results.append(flat_dot(soft.astype(jnp.bfloat16), value_rows).astype(jnp.bfloat16))
    blended[0] = jnp.concatenate(results, axis=1)


def attend(packed, segment_rows, segment_columns, table):
    blocks, frame_count, width = packed.shape
    heads = table.shape[0]
    return pl.pallas_call(
        functools.partial(attend_kernel, heads),
        grid=(blocks,),
        out_shape=jax.ShapeDtypeStruct((blocks, frame_count, width // 3), jnp.bfloat16),
        in_specs=[
            pl.BlockSpec((1, frame_count, width), lambda i: (i, 0, 0)),
            pl.BlockSpec((1, 1, frame_count), lambda i: (i, 0, 0)),
            pl.BlockSpec((1, frame_count, 1), lambda i: (i, 0, 0)),
            pl.BlockSpec((heads, NREL), lambda i: (0, 0)),
        ],
        out_specs=pl.BlockSpec((1, frame_count, width // 3), lambda i: (i, 0, 0)),
        scratch_shapes=[pltpu.VMEM((heads, frame_count, frame_count), jnp.float32)],
        name="attend",
    )(packed, segment_rows, segment_columns, table)


def unattend_kernel(heads, packed, upstream, segment_rows, segment_columns, table, grads, sums, slope, bias, gathered):
    frame_count = packed.shape[1]
    size = heads * HEAD
    at = pl.program_id(0)

    @pl.when(at == 0)
    def _():
        for head in range(heads):
            bias[head] = toeplitz(table[pl.ds(head, 1), :], frame_count)
        gathered[...] = jnp.zeros_like(gathered)
        sums[...] = jnp.zeros_like(sums)

    same = segment_columns[0] == segment_rows[0]
    block = packed[0]
    above = upstream[0]
    query_grads, key_grads, value_grads = [], [], []
    for head in range(heads):
        query_rows, key_rows, value_rows, soft = head_scores(block, head, heads, same, bias[head])
        blend_grad = above[:, head * HEAD : (head + 1) * HEAD]
        value_grads.append(lead_dot(soft.astype(jnp.bfloat16), blend_grad))
        soft_grad = back_dot(blend_grad, value_rows)
        score_grad = soft * (soft_grad - jnp.sum(soft * soft_grad, axis=-1, keepdims=True))
        gathered[head] += score_grad
        low = (HEAD ** (-0.5) * score_grad).astype(jnp.bfloat16)
        query_grads.append(flat_dot(low, key_rows))
        key_grads.append(lead_dot(low, query_rows))
    query_grad = jnp.concatenate(query_grads, axis=1)
    value_grad = jnp.concatenate(value_grads, axis=1)
    grads[0, :, 0:size] = query_grad.astype(jnp.bfloat16)
    grads[0, :, size : 2 * size] = jnp.concatenate(key_grads, axis=1).astype(jnp.bfloat16)
    grads[0, :, 2 * size :] = value_grad.astype(jnp.bfloat16)
    sums[0:1, :] += jnp.sum(query_grad, axis=0, keepdims=True)
    sums[1:2, :] += jnp.sum(value_grad, axis=0, keepdims=True)

    @pl.when(at == pl.num_programs(0) - 1)
    def _():
        places = lax.broadcasted_iota(jnp.int32, (frame_count, NREL), 0)
        for head in range(heads):
            wide = jnp.concatenate(
                [gathered[head], jnp.zeros((frame_count, NREL - frame_count), jnp.float32)], axis=1
            )
            stride = 1
            while stride < frame_count:
                moved = pltpu.roll(wide, NREL - stride, 1)
                wide = jnp.where((places // stride) % 2 == 1, moved, wide)
                stride *= 2
            slope[pl.ds(head, 1), :] = jnp.sum(wide, axis=0, keepdims=True)


def unattend(packed, upstream, segment_rows, segment_columns, table):
    blocks, frame_count, width = packed.shape
    heads = table.shape[0]
    return pl.pallas_call(
        functools.partial(unattend_kernel, heads),
        grid=(blocks,),
        out_shape=[
            jax.ShapeDtypeStruct((blocks, frame_count, width), jnp.bfloat16),
            jax.ShapeDtypeStruct((2, width // 3), jnp.float32),
            jax.ShapeDtypeStruct((heads, NREL), jnp.float32),
        ],
        in_specs=[
            pl.BlockSpec((1, frame_count, width), lambda i: (i, 0, 0)),
            pl.BlockSpec((1, frame_count, width // 3), lambda i: (i, 0, 0)),
            pl.BlockSpec((1, 1, frame_count), lambda i: (i, 0, 0)),
            pl.BlockSpec((1, frame_count, 1), lambda i: (i, 0, 0)),
            pl.BlockSpec((heads, NREL), lambda i: (0, 0)),
        ],
        out_specs=[
            pl.BlockSpec((1, frame_count, width), lambda i: (i, 0, 0)),
            pl.BlockSpec((2, width // 3), lambda i: (0, 0)),
            pl.BlockSpec((heads, NREL), lambda i: (0, 0)),
        ],
        scratch_shapes=[
            pltpu.VMEM((heads, frame_count, frame_count), jnp.float32),
            pltpu.VMEM((heads, frame_count, frame_count), jnp.float32),
        ],
        name="unattend",
    )(packed, upstream, segment_rows, segment_columns, table)


def reach_mask(offset, behind, ahead):
    if offset < 0:
        return behind >= -offset
    return ahead >= offset


def to_rows(wide, count):
    return jnp.transpose(wide)[:count]


def to_columns(rows):
    count, length = rows.shape
    wide = jnp.transpose(jnp.concatenate([rows, jnp.zeros((LANES - count, length), rows.dtype)]))
    return [wide[:, at : at + 1] for at in range(count)]


def swap(n, mine, shared, send, recv):
    me = lax.axis_index("dp")
    shared[me] = mine[...]
    copies = []
    for peer, (target, unused) in enumerate(near(me, n)):
        copies.append(remote(mine, shared.at[me], send.at[peer], recv.at[peer], {"dp": target}))
    for copy in copies:
        copy.start()
    for copy in copies:
        copy.wait()


def fill(store, value):
    frame_count, channels = value.shape
    store[pl.ds(0, MARGIN), :] = jnp.zeros((MARGIN, channels), jnp.float32)
    store[pl.ds(MARGIN + frame_count, MARGIN), :] = jnp.zeros((MARGIN, channels), jnp.float32)
    store[pl.ds(MARGIN, frame_count), :] = value


def convolve_kernel(
    n, opened, behind, ahead, taps, vectors, gated, unit, inverse, swished, padded, mine, shared, send, recv
):
    frame_count, channels = gated.shape[1:]
    greet([target for target, unused in near(lax.axis_index("dp"), n)])
    places = lax.broadcasted_iota(jnp.int32, (frame_count, LANES), 1)

    def filter_block(block, wide):
        gates = opened[block, :, 0:channels] * jax.nn.sigmoid(opened[block, :, channels:])
        gated[block] = gates
        fill(padded, gates)
        back = jnp.broadcast_to(behind[block], (frame_count, LANES))
        front = jnp.broadcast_to(ahead[block], (frame_count, LANES))
        for low in range(0, channels, LANES):
            lanes = slice(low, low + LANES)
            running = jnp.broadcast_to(vectors[10:11, lanes], (frame_count, LANES))
            for tap in range(KW):
                offset = tap - (KW - 1) // 2
                moved = padded[pl.ds(MARGIN + offset, frame_count), lanes]
                if offset:
                    moved = jnp.where(reach_mask(offset, back, front), moved, 0.0)
                running = running + moved * taps[pl.ds(tap, 1), lanes]
            unit[block, :, lanes] = running
        filtered = unit[block]
        mean = jnp.mean(filtered, axis=-1, keepdims=True)
        square = jnp.sum((filtered - mean) ** 2, axis=-1, keepdims=True)
        return jnp.where(places == block, mean, jnp.where(places == n + block, square, wide))

    wide = lax.fori_loop(0, n, filter_block, jnp.zeros((frame_count, LANES), jnp.float32))
    mine[...] = to_rows(wide, 2 * n)
    swap(n, mine, shared, send, recv)
    everyone = [shared[at] for at in range(n)]
    middle_mean = sum(rows[:n] for rows in everyone) / n
    total = sum(rows[n:] + channels * (rows[:n] - middle_mean) ** 2 for rows in everyone)
    scale = lax.rsqrt(total / (n * channels) + EPSILON)
    found = to_columns(jnp.concatenate([middle_mean, scale]))
    for block in range(n):
        values = (unit[block] - found[block]) * found[n + block]
        unit[block] = values
        inverse[block] = found[n + block]
        middle = values * vectors[11:12, :] + vectors[12:13, :]
        swished[block] = (middle * jax.nn.sigmoid(middle)).astype(jnp.bfloat16)


def swap_scratch(n, frame_count):
    return [
        pltpu.VMEM((2 * n, frame_count), jnp.float32),
        pltpu.VMEM((n, 2 * n, frame_count), jnp.float32),
        pltpu.SemaphoreType.DMA((n - 1,)),
        pltpu.SemaphoreType.DMA((n - 1,)),
    ]


def convolve(opened, behind, ahead, taps, vectors, number):
    blocks, frame_count, width = opened.shape
    channels = width // 2
    inside = pl.BlockSpec(memory_space=pltpu.VMEM)
    wide = (blocks, frame_count, channels)
    return pl.pallas_call(
        functools.partial(convolve_kernel, blocks),
        out_shape=[
            jax.ShapeDtypeStruct(wide, jnp.float32),
            jax.ShapeDtypeStruct(wide, jnp.float32),
            jax.ShapeDtypeStruct((blocks, frame_count, 1), jnp.float32),
            jax.ShapeDtypeStruct(wide, jnp.bfloat16),
        ],
        in_specs=[inside] * 5,
        out_specs=[inside] * 4,
        scratch_shapes=[pltpu.VMEM((frame_count + 2 * MARGIN, channels), jnp.float32)] + swap_scratch(blocks, frame_count),
        compiler_params=pltpu.CompilerParams(collective_id=number, has_side_effects=True),
        name="convolve",
    )(opened, behind, ahead, taps, vectors)


def unconvolve_kernel(
    n, opened, gated, upstream, unit, inverse, behind, ahead, taps, vectors, grads, lifts, slopes, *scratch
):
    padded, padded_grad, turned, mine, shared, send, recv = scratch
    frame_count, channels = gated.shape[1:]
    greet([target for target, unused in near(lax.axis_index("dp"), n)])
    places = lax.broadcasted_iota(jnp.int32, (frame_count, LANES), 1)
    lifts[...] = jnp.zeros_like(lifts)
    slopes[...] = jnp.zeros_like(slopes)
    wide = jnp.zeros((frame_count, LANES), jnp.float32)
    for block in range(n):
        scaled = upstream[block] * vectors[11:12, :]
        plain = jnp.sum(scaled, axis=-1, keepdims=True)
        along = jnp.sum(scaled * unit[block], axis=-1, keepdims=True)
        wide = jnp.where(places == block, plain, jnp.where(places == n + block, along, wide))
    mine[...] = to_rows(wide, 2 * n)
    swap(n, mine, shared, send, recv)
    found = to_columns(sum(shared[at] for at in range(n)) / (n * channels))
    for block in range(n):
        scaled = upstream[block] * vectors[11:12, :]
        turned[block] = inverse[block] * (scaled - found[block] - unit[block] * found[n + block])

    def block_back(block, carry):
        fill(padded, gated[block])
        fill(padded_grad, turned[block])
        back = jnp.broadcast_to(behind[block], (frame_count, LANES))
        front = jnp.broadcast_to(ahead[block], (frame_count, LANES))
        for low in range(0, channels, LANES):
            lanes = slice(low, low + LANES)
            above = turned[block, :, lanes]
            running = jnp.zeros((frame_count, LANES), jnp.float32)
            for tap in range(KW):
                offset = tap - (KW - 1) // 2
                moved = padded[pl.ds(MARGIN + offset, frame_count), lanes]
                moved_grad = padded_grad[pl.ds(MARGIN + offset, frame_count), lanes]
                if offset:
                    mask = reach_mask(offset, back, front)
                    moved = jnp.where(mask, moved, 0.0)
                    moved_grad = jnp.where(mask, moved_grad, 0.0)
                running = running + moved_grad * taps[pl.ds(KW - 1 - tap, 1), lanes]
                slopes[pl.ds(tap, 1), lanes] += jnp.sum(moved * above, axis=0, keepdims=True)
            slopes[pl.ds(KW, 1), lanes] += jnp.sum(above, axis=0, keepdims=True)
            far = slice(channels + low, channels + low + LANES)
            left, gate = opened[block, :, lanes], jax.nn.sigmoid(opened[block, :, far])
            left_grad = running * gate
            gate_grad = running * left * gate * (1.0 - gate)
            grads[block, :, lanes] = left_grad.astype(jnp.bfloat16)
            grads[block, :, far] = gate_grad.astype(jnp.bfloat16)
            lifts[:, lanes] += jnp.sum(left_grad, axis=0, keepdims=True)
            lifts[:, far] += jnp.sum(gate_grad, axis=0, keepdims=True)
        return carry

    lax.fori_loop(0, n, block_back, 0)


def unconvolve(opened, gated, upstream, unit, inverse, behind, ahead, taps, vectors, number):
    blocks, frame_count, width = opened.shape
    channels = width // 2
    inside = pl.BlockSpec(memory_space=pltpu.VMEM)
    return pl.pallas_call(
        functools.partial(unconvolve_kernel, blocks),
        out_shape=[
            jax.ShapeDtypeStruct((blocks, frame_count, width), jnp.bfloat16),
            jax.ShapeDtypeStruct((1, width), jnp.float32),
            jax.ShapeDtypeStruct((KW + 1, channels), jnp.float32),
        ],
        in_specs=[inside] * 9,
        out_specs=[inside] * 3,
        scratch_shapes=[
            pltpu.VMEM((frame_count + 2 * MARGIN, channels), jnp.float32),
            pltpu.VMEM((frame_count + 2 * MARGIN, channels), jnp.float32),
            pltpu.VMEM((blocks, frame_count, channels), jnp.float32),
        ]
        + swap_scratch(blocks, frame_count),
        compiler_params=pltpu.CompilerParams(collective_id=number, has_side_effects=True),
        name="unconvolve",
    )(opened, gated, upstream, unit, inverse, behind, ahead, taps, vectors)


def gather_rows(value):
    return lax.all_gather(value, "fsdp", axis=0, tiled=True)


def gather_split(value):
    full = lax.all_gather(value, "fsdp", axis=1, tiled=True)
    return full.reshape(-1, full.shape[-1])


def scatter_rows(value):
    return lax.psum_scatter(value.astype(jnp.bfloat16), "fsdp", scatter_dimension=0, tiled=True)


def scatter_split(value, n):
    value = value.astype(jnp.bfloat16).reshape(n, value.shape[0] // n, value.shape[1])
    return lax.psum_scatter(value, "fsdp", scatter_dimension=1, tiled=True)


def pair_slopes(up_slope, down_slope, n):
    inner = down_slope.shape[0]
    up_slope = up_slope.reshape(n, inner, -1)
    down_slope = jnp.transpose(down_slope.reshape(inner, n, inner), (1, 0, 2))
    return jnp.concatenate([up_slope, down_slope], axis=2)


def flat(value):
    return value.reshape(-1, value.shape[-1])


def split_body(
    n,
    m,
    frames,
    segments,
    cotangent,
    early_gain,
    early_shift,
    early_up,
    early_lift,
    early_down,
    early_drop,
    mixer_gain,
    mixer_shift,
    mixer_project,
    query_bias,
    value_bias,
    mixer_output,
    mixer_drop,
    distance_table,
    filter_gain,
    filter_shift,
    filter_up,
    filter_lift,
    depth_weight,
    depth_bias,
    middle_gain,
    middle_shift,
    filter_down,
    filter_drop,
    late_gain,
    late_shift,
    late_up,
    late_lift,
    late_down,
    late_drop,
    final_gain,
    final_shift,
):
    me = lax.axis_index("dp")
    frame_count = frames.shape[0]
    rows = early_gain.shape[0]
    hidden = early_up.shape[1] // n
    inner = D // n
    heads = HEADS // n
    singles = [
        early_gain, early_shift, early_drop, mixer_gain, mixer_shift, query_bias, value_bias, mixer_drop,
        filter_gain, filter_shift, depth_bias, middle_gain, middle_shift, filter_drop, late_gain, late_shift,
        late_drop, final_gain, final_shift,
    ]
    spans = hidden * n // D
    (
        w_early_up, w_early_down, late_up_split, mixer_split, filter_split, small_all, vectors, own_vectors, lifts,
        filter_lifts, depth_all, segments_all, early_hidden,
    ) = exchange(
        n, m, early_up, early_down.reshape(spans, rows, D), late_up, mixer_project, filter_up, mixer_output,
        filter_down, depth_weight, segments.reshape(1, frame_count), frames, singles,
        [early_lift, late_lift, filter_lift], distance_table,
    )
    w_early_up = w_early_up.reshape(D, hidden)
    w_early_down = w_early_down.reshape(hidden, D)
    w_mixer = lax.all_gather(mixer_split, "fsdp", axis=1, tiled=True)
    w_filter = lax.all_gather(filter_split, "fsdp", axis=1, tiled=True)
    w_late_up = gather_split(late_up_split)
    w_late_down = gather_rows(late_down)

    early_lifts, late_lifts = lifts[0], lifts[1]
    table = small_all[:, 8 : 8 + distance_table.shape[0], :HEADS].astype(jnp.float32).reshape(NREL, HEADS)
    table = jnp.transpose(lax.dynamic_slice(table, (0, me * heads), (NREL, heads)))[:, ::-1]
    taps = jnp.transpose(depth_all.reshape(inner, KW)).astype(jnp.float32)
    attention_shift = jnp.concatenate([own_vectors[5], jnp.zeros((inner,), jnp.float32), own_vectors[6]])
    segment_rows = segments_all
    segment_columns = segments_all.reshape(n, frame_count, 1)
    places = jnp.arange(frame_count, dtype=jnp.int32)[None, :]
    lower = (segment_rows < segment_columns).astype(jnp.int32)
    upto = (segment_rows <= segment_columns).astype(jnp.int32)
    behind = (places - jnp.sum(lower, axis=-1)).reshape(n, frame_count, 1)
    ahead = (jnp.sum(upto, axis=-1) - 1 - places).reshape(n, frame_count, 1)

    def blocks(value):
        return value.reshape(n, frame_count, value.shape[-1])

    def feed(hidden_rows, w_up, lifts, w_down):
        widened = flat_dot(flat(hidden_rows), w_up) + lifts
        active = (widened * jax.nn.sigmoid(widened)).astype(jnp.bfloat16)
        return widened, active, blocks(flat_dot(active, w_down).astype(jnp.bfloat16))

    def feed_back(low, hidden_rows, widened, active, w_up, w_down):
        low = flat(low)
        down_slope = lead_dot(active, low).astype(jnp.bfloat16)
        widened_grad = swish_back(back_dot(low, w_down), widened)
        widened_low = widened_grad.astype(jnp.bfloat16)
        up_slope = lead_dot(flat(hidden_rows), widened_low).astype(jnp.bfloat16)
        part = blocks(back_dot(widened_low, w_up).astype(jnp.bfloat16))
        down_slope = jnp.transpose(down_slope.reshape(m, spans, rows, D), (1, 0, 2, 3)).reshape(spans, m * rows, D)
        slope = jnp.concatenate([up_slope.reshape(n, D // n, hidden), down_slope])
        part, slope = lax.optimization_barrier((part, slope))
        return part, slope, jnp.sum(widened_grad, axis=0)

    early_wide, early_active, part = feed(early_hidden, w_early_up, early_lifts, w_early_down)
    first_rows, mixer_hidden = boundary(
        functools.partial(step_forward, 0.5), part, [frames], vectors, (2, 3, 4), 1, 0, 2
    )
    mixer_hidden, w_mixer = lax.optimization_barrier((mixer_hidden, w_mixer))
    w_project = w_mixer[:, :, : 3 * inner].reshape(D, 3 * inner)
    w_output = jnp.transpose(w_mixer[:, :, 3 * inner :], (1, 0, 2)).reshape(inner, D)
    packed = blocks((flat_dot(flat(mixer_hidden), w_project) + attention_shift).astype(jnp.bfloat16))
    blended = attend(packed, segment_rows, segment_columns, table)
    part = blocks(flat_dot(flat(blended), w_output).astype(jnp.bfloat16))
    second_rows, filter_hidden = boundary(
        functools.partial(step_forward, 1.0), part, [first_rows], vectors, (7, 8, 9), 1, 0, 3
    )
    filter_hidden, w_filter = lax.optimization_barrier((filter_hidden, w_filter))
    w_filter_up = w_filter[:, :, : 2 * inner].reshape(D, 2 * inner)
    w_filter_down = jnp.transpose(w_filter[:, :, 2 * inner :], (1, 0, 2)).reshape(inner, D)
    opened = blocks(flat_dot(flat(filter_hidden), w_filter_up) + filter_lifts)
    gated, middle_unit, middle_inverse, swished = convolve(opened, behind, ahead, taps, own_vectors, 4)
    swished = flat(swished)
    part = blocks(flat_dot(swished, w_filter_down).astype(jnp.bfloat16))
    third_rows, late_hidden = boundary(
        functools.partial(step_forward, 1.0), part, [second_rows], vectors, (13, 14, 15), 1, 0, 5
    )
    late_hidden, w_late_up, w_late_down = lax.optimization_barrier((late_hidden, w_late_up, w_late_down))
    late_wide, late_active, part = feed(late_hidden, w_late_up, late_lifts, w_late_down)
    layer_out, grad, low, turn_sums = boundary(
        step_turn, part, [third_rows, cotangent], vectors, (16, 17, 18), 2, 3, 6
    )

    part, late_slope, late_lift_slope = feed_back(
        low, late_hidden, late_wide, late_active, w_late_up, w_late_down
    )
    late_slope = lax.psum_scatter(late_slope, "fsdp", scatter_dimension=1, tiled=True)
    grad, low, late_sums = boundary(
        functools.partial(step_backward, 1.0), part, [grad, third_rows], vectors, (14,), 1, 3, 7
    )
    low = flat(low)
    filter_down_slope = lead_dot(swished, low).astype(jnp.bfloat16)
    flat_unit = flat(middle_unit)
    middle = flat_unit * own_vectors[11] + own_vectors[12]
    middle_grad = swish_back(back_dot(low, w_filter_down), middle)
    middle_gain_slope = jnp.sum(middle_grad * flat_unit, axis=0)
    middle_shift_slope = jnp.sum(middle_grad, axis=0)
    opened_low, filter_lift_slope, depth_slope = unconvolve(
        opened, gated, blocks(middle_grad), middle_unit, middle_inverse, behind, ahead, taps, own_vectors, 8
    )
    opened_low = flat(opened_low)
    filter_up_slope = lead_dot(flat(filter_hidden), opened_low).astype(jnp.bfloat16)
    part = blocks(back_dot(opened_low, w_filter_up).astype(jnp.bfloat16))
    part, filter_slope = lax.optimization_barrier((part, pair_slopes(filter_up_slope, filter_down_slope, n)))
    filter_slope = lax.psum_scatter(filter_slope, "fsdp", scatter_dimension=1, tiled=True)
    grad, low, filter_sums = boundary(
        functools.partial(step_backward, 1.0), part, [grad, second_rows], vectors, (8,), 1, 3, 9
    )
    low = flat(low)
    output_slope = lead_dot(flat(blended), low).astype(jnp.bfloat16)
    blend_grad = blocks(back_dot(low, w_output).astype(jnp.bfloat16))
    packed_low, shift_sums, table_slope = unattend(packed, blend_grad, segment_rows, segment_columns, table)
    packed_low = flat(packed_low)
    project_slope = lead_dot(flat(mixer_hidden), packed_low).astype(jnp.bfloat16)
    part = blocks(back_dot(packed_low, w_project).astype(jnp.bfloat16))
    part, mixer_slope, late_slope = lax.optimization_barrier(
        (part, pair_slopes(project_slope, output_slope, n), late_slope)
    )
    mixer_slope = lax.psum_scatter(mixer_slope, "fsdp", scatter_dimension=1, tiled=True)
    grad, low, mixer_sums = boundary(
        functools.partial(step_backward, 0.5), part, [grad, first_rows], vectors, (3,), 1, 3, 10
    )
    part, early_slope, early_lift_slope = feed_back(
        low, early_hidden, early_wide, early_active, w_early_up, w_early_down
    )
    part, early_slope, filter_slope = lax.optimization_barrier((part, early_slope, filter_slope))
    early_slope = lax.psum_scatter(early_slope, "fsdp", scatter_dimension=1, tiled=True)
    slope_frames, early_sums = boundary(
        step_last, part, [grad, frames], vectors, (0,), 1, 2, 11, gathered=False
    )

    table_slope = jnp.roll(table_slope[:, ::-1], 1 - NREL // 2, axis=1)
    table_rows = NREL // (n * m)
    wide = jnp.concatenate([turn_sums, late_sums, filter_sums, mixer_sums, early_sums])
    wide_count = wide.shape[0]
    wide = jnp.transpose(wide.reshape(wide_count, n * m, rows), (1, 0, 2)).reshape(n * m, wide_count * rows)
    wide = jnp.concatenate(
        [wide, jnp.transpose(table_slope.reshape(heads, n * m, table_rows), (1, 0, 2)).reshape(n * m, -1)], axis=1
    )
    lift_full = lax.dynamic_update_slice(
        jnp.zeros((2, D), jnp.float32), filter_lift_slope.reshape(2, inner), (0, me * inner)
    ).reshape(n * m, -1)
    table_used = wide.shape[1]
    wide = jnp.concatenate([wide, lift_full], axis=1)
    wide_used = wide.shape[1]
    wide = jnp.pad(wide, ((0, 0), (0, -wide_used % LANES))).reshape(n * m, -1, LANES)
    group = jnp.concatenate(
        [
            shift_sums,
            middle_gain_slope[None],
            middle_shift_slope[None],
            depth_slope,
            jnp.transpose(early_lift_slope.reshape(inner, spans)),
            jnp.transpose(late_lift_slope.reshape(inner, spans)),
        ]
    )
    group_count = group.shape[0]
    group = jnp.transpose(group.reshape(group_count, m, rows), (1, 0, 2)).reshape(m, group_count * rows)
    group_used = group.shape[1]
    group = jnp.pad(group, ((0, 0), (0, -group_used % LANES))).reshape(m, -1, LANES)
    wide_all, group_all, late_up_wide, project_wide, filter_up_wide = collect(
        n, m, wide, group, [late_slope, mixer_slope, filter_slope], [(1, hidden), (3, inner), (2, inner)], 12
    )
    tables = wide_all.reshape(n, m, -1)[:, :, wide_count * rows : table_used]
    wide = jnp.sum(wide_all, axis=0).reshape(-1)
    lift_total = wide[table_used:wide_used]
    wide = wide[: wide_count * rows].reshape(wide_count, rows)
    tables = jnp.transpose(jnp.sum(tables, axis=1).reshape(HEADS, table_rows))
    group = jnp.sum(group_all, axis=0).reshape(-1)[:group_used].reshape(group_count, rows)
    def rejoin(value, low):
        return final(jnp.transpose(value[:, :, low:], (1, 0, 2)).reshape(rows, D))

    def final(value):
        return value.astype(jnp.float32)

    lift_slopes = KW + 5
    results = [
        layer_out,
        slope_frames,
        wide[12],
        wide[13],
        jnp.transpose(group[lift_slopes : lift_slopes + spans]).reshape(-1),
        wide[11],
        wide[9],
        wide[10],
        final(project_wide),
        group[0],
        group[1],
        rejoin(mixer_slope, 3 * inner),
        wide[8],
        tables,
        wide[6],
        wide[7],
        final(filter_up_wide),
        lift_total,
        jnp.transpose(group[4 : 4 + KW]),
        group[4 + KW],
        group[2],
        group[3],
        rejoin(filter_slope, 2 * inner),
        wide[5],
        wide[3],
        wide[4],
        final(late_up_wide),
        jnp.transpose(group[lift_slopes + spans : lift_slopes + 2 * spans]).reshape(-1),
        final(late_slope[n:]).reshape(spans * rows, D),
        wide[2],
        wide[0],
        wide[1],
    ]
    results[:2] = keep(layer_out, slope_frames)
    *results, early_slope = lax.optimization_barrier((*results, early_slope))
    (early_up_wide,) = giveback(n, [early_slope], [(1, hidden)], 14)
    results.insert(4, final(early_up_wide))
    results.insert(6, final(early_slope[n:]).reshape(spans * rows, D))
    return tuple(results)


def solution(mesh):
    in_specs = (
        P(("dp", "fsdp"), None),
        P(("dp", "fsdp")),
        P(("dp", "fsdp"), None),
        P(("dp", "fsdp")),
        P(("dp", "fsdp")),
        P(("dp", "fsdp"), None),
        P(("dp", "fsdp")),
        P(("dp", "fsdp"), None),
        P(("dp", "fsdp")),
        P(("dp", "fsdp")),
        P(("dp", "fsdp")),
        P(("dp", "fsdp"), None),
        P(("dp", "fsdp")),
        P(("dp", "fsdp")),
        P(("dp", "fsdp"), None),
        P(("dp", "fsdp")),
        P(("dp", "fsdp"), None),
        P(("dp", "fsdp")),
        P(("dp", "fsdp")),
        P(("dp", "fsdp"), None),
        P(("dp", "fsdp")),
        P(("dp", "fsdp"), None),
        P(("dp", "fsdp")),
        P(("dp", "fsdp")),
        P(("dp", "fsdp")),
        P(("dp", "fsdp"), None),
        P(("dp", "fsdp")),
        P(("dp", "fsdp")),
        P(("dp", "fsdp")),
        P(("dp", "fsdp"), None),
        P(("dp", "fsdp")),
        P(("dp", "fsdp"), None),
        P(("dp", "fsdp")),
        P(("dp", "fsdp")),
        P(("dp", "fsdp")),
    )
    out_specs = (
        P(("dp", "fsdp"), None),
        P(("dp", "fsdp"), None),
        P(("dp", "fsdp")),
        P(("dp", "fsdp")),
        P(("dp", "fsdp"), None),
        P(("dp", "fsdp")),
        P(("dp", "fsdp"), None),
        P(("dp", "fsdp")),
        P(("dp", "fsdp")),
        P(("dp", "fsdp")),
        P(("dp", "fsdp"), None),
        P(("dp", "fsdp")),
        P(("dp", "fsdp")),
        P(("dp", "fsdp"), None),
        P(("dp", "fsdp")),
        P(("dp", "fsdp"), None),
        P(("dp", "fsdp")),
        P(("dp", "fsdp")),
        P(("dp", "fsdp"), None),
        P(("dp", "fsdp")),
        P(("dp", "fsdp"), None),
        P(("dp", "fsdp")),
        P(("dp", "fsdp")),
        P(("dp", "fsdp")),
        P(("dp", "fsdp"), None),
        P(("dp", "fsdp")),
        P(("dp", "fsdp")),
        P(("dp", "fsdp")),
        P(("dp", "fsdp"), None),
        P(("dp", "fsdp")),
        P(("dp", "fsdp"), None),
        P(("dp", "fsdp")),
        P(("dp", "fsdp")),
        P(("dp", "fsdp")),
    )
    n, m = mesh.shape["dp"], mesh.shape["fsdp"]
    run = functools.partial(split_body, n, m) if n == 4 and D // (n * m) == 32 else body
    return jax.shard_map(run, mesh=mesh, in_specs=in_specs, out_specs=out_specs, check_vma=False)
```

```python
import functools

import jax
import jax.numpy as jnp
from jax import lax
from jax.experimental import pallas as pl
from jax.experimental.pallas import tpu as pltpu
from jax.sharding import PartitionSpec as P

D = 1024
HEADS = 16
HEAD = 64
KW = 31
NREL = 256


EPSILON = 1e-05
MASKED = -1e30
UTTERANCE_LIMIT = 4
MESH = pl.DeviceIdType.MESH
PIECES = 2
LAG = 2
BLOCK = 16
MARGIN = 16
LANES = 128


def flat_dot(left_rows, right_rows):
    return jnp.dot(left_rows, right_rows, preferred_element_type=jnp.float32)


def lead_dot(left_rows, right_rows):
    return lax.dot_general(
        left_rows, right_rows, (((0,), (0,)), ((), ())), preferred_element_type=jnp.float32
    )


def back_dot(left_rows, right_rows):
    return lax.dot_general(
        left_rows, right_rows, (((1,), (1,)), ((), ())), preferred_element_type=jnp.float32
    )


def norm_apply(values, norm_gain, norm_shift):
    centered = values - jnp.mean(values, axis=-1, keepdims=True)
    inverse = lax.rsqrt(jnp.mean(centered * centered, axis=-1, keepdims=True) + EPSILON)
    normed_unit = centered * inverse
    return (
        normed_unit * norm_gain.astype(jnp.float32) + norm_shift.astype(jnp.float32),
        normed_unit,
        inverse,
    )


def norm_back(upstream, normed_unit, inverse, norm_gain):
    scaled = upstream * norm_gain.astype(jnp.float32)
    adjusted = scaled - jnp.mean(scaled, axis=-1, keepdims=True)
    adjusted = adjusted - normed_unit * jnp.mean(scaled * normed_unit, axis=-1, keepdims=True)
    return (inverse * adjusted, jnp.sum(upstream * normed_unit, axis=0), jnp.sum(upstream, axis=0))


def swish_back(upstream, before):
    sigmoid_rows = jax.nn.sigmoid(before)
    return upstream * sigmoid_rows * (1.0 + before * (1.0 - sigmoid_rows))


def depthwise(gated_rows, kernel, segment_ids):
    margin = (KW - 1) // 2
    channels = gated_rows.shape[1]
    taps = jnp.transpose(kernel)[:, None, :]
    running = jnp.zeros_like(gated_rows)
    for utterance in range(UTTERANCE_LIMIT):
        inside = (segment_ids == utterance)[:, None]
        masked_rows = jnp.where(inside, gated_rows, 0.0)
        convolved = lax.conv_general_dilated(
            masked_rows[None],
            taps,
            (1,),
            ((margin, margin),),
            dimension_numbers=("NWC", "WIO", "NWC"),
            feature_group_count=channels,
            precision=lax.Precision.HIGHEST,
        )[0]
        running = running + jnp.where(inside, convolved, 0.0)
    return running


def fetch_feed(norm_gain, norm_shift, w_up, up_shift, w_down, down_shift):
    return (
        lax.all_gather(norm_gain, ("dp", "fsdp"), axis=0, tiled=True),
        lax.all_gather(norm_shift, ("dp", "fsdp"), axis=0, tiled=True),
        lax.all_gather(w_up, ("dp", "fsdp"), axis=0, tiled=True),
        lax.all_gather(up_shift, ("dp", "fsdp"), axis=0, tiled=True),
        lax.all_gather(w_down, ("dp", "fsdp"), axis=0, tiled=True),
        lax.all_gather(down_shift, ("dp", "fsdp"), axis=0, tiled=True),
    )


def reduce_feed(norm_gain, norm_shift, w_up, up_shift, w_down, down_shift):
    return (
        lax.psum_scatter(norm_gain, ("dp", "fsdp"), scatter_dimension=0, tiled=True),
        lax.psum_scatter(norm_shift, ("dp", "fsdp"), scatter_dimension=0, tiled=True),
        lax.psum_scatter(w_up, ("dp", "fsdp"), scatter_dimension=0, tiled=True),
        lax.psum_scatter(up_shift, ("dp", "fsdp"), scatter_dimension=0, tiled=True),
        lax.psum_scatter(w_down, ("dp", "fsdp"), scatter_dimension=0, tiled=True),
        lax.psum_scatter(down_shift, ("dp", "fsdp"), scatter_dimension=0, tiled=True),
    )


def fetch_mixer(
    norm_gain, norm_shift, w_project, query_shift, value_shift, w_output, output_shift, table_rows
):
    return (
        lax.all_gather(norm_gain, ("dp", "fsdp"), axis=0, tiled=True),
        lax.all_gather(norm_shift, ("dp", "fsdp"), axis=0, tiled=True),
        lax.all_gather(w_project, ("dp", "fsdp"), axis=0, tiled=True),
        lax.all_gather(query_shift, ("dp", "fsdp"), axis=0, tiled=True),
        lax.all_gather(value_shift, ("dp", "fsdp"), axis=0, tiled=True),
        lax.all_gather(w_output, ("dp", "fsdp"), axis=0, tiled=True),
        lax.all_gather(output_shift, ("dp", "fsdp"), axis=0, tiled=True),
        lax.all_gather(table_rows, ("dp", "fsdp"), axis=0, tiled=True),
    )


def reduce_mixer(
    norm_gain, norm_shift, w_project, query_shift, value_shift, w_output, output_shift, table_rows
):
    return (
        lax.psum_scatter(norm_gain, ("dp", "fsdp"), scatter_dimension=0, tiled=True),
        lax.psum_scatter(norm_shift, ("dp", "fsdp"), scatter_dimension=0, tiled=True),
        lax.psum_scatter(w_project, ("dp", "fsdp"), scatter_dimension=0, tiled=True),
        lax.psum_scatter(query_shift, ("dp", "fsdp"), scatter_dimension=0, tiled=True),
        lax.psum_scatter(value_shift, ("dp", "fsdp"), scatter_dimension=0, tiled=True),
        lax.psum_scatter(w_output, ("dp", "fsdp"), scatter_dimension=0, tiled=True),
        lax.psum_scatter(output_shift, ("dp", "fsdp"), scatter_dimension=0, tiled=True),
        lax.psum_scatter(table_rows, ("dp", "fsdp"), scatter_dimension=0, tiled=True),
    )


def fetch_filter(
    norm_gain,
    norm_shift,
    w_up,
    up_shift,
    depth_taps,
    depth_shift,
    middle_gain,
    middle_shift,
    w_down,
    down_shift,
    last_gain,
    last_shift,
):
    return (
        lax.all_gather(norm_gain, ("dp", "fsdp"), axis=0, tiled=True),
        lax.all_gather(norm_shift, ("dp", "fsdp"), axis=0, tiled=True),
        lax.all_gather(w_up, ("dp", "fsdp"), axis=0, tiled=True),
        lax.all_gather(up_shift, ("dp", "fsdp"), axis=0, tiled=True),
        lax.all_gather(depth_taps, ("dp", "fsdp"), axis=0, tiled=True),
        lax.all_gather(depth_shift, ("dp", "fsdp"), axis=0, tiled=True),
        lax.all_gather(middle_gain, ("dp", "fsdp"), axis=0, tiled=True),
        lax.all_gather(middle_shift, ("dp", "fsdp"), axis=0, tiled=True),
        lax.all_gather(w_down, ("dp", "fsdp"), axis=0, tiled=True),
        lax.all_gather(down_shift, ("dp", "fsdp"), axis=0, tiled=True),
        lax.all_gather(last_gain, ("dp", "fsdp"), axis=0, tiled=True),
        lax.all_gather(last_shift, ("dp", "fsdp"), axis=0, tiled=True),
    )


def reduce_filter(
    norm_gain,
    norm_shift,
    w_up,
    up_shift,
    depth_taps,
    depth_shift,
    middle_gain,
    middle_shift,
    w_down,
    down_shift,
    last_gain,
    last_shift,
):
    return (
        lax.psum_scatter(norm_gain, ("dp", "fsdp"), scatter_dimension=0, tiled=True),
        lax.psum_scatter(norm_shift, ("dp", "fsdp"), scatter_dimension=0, tiled=True),
        lax.psum_scatter(w_up, ("dp", "fsdp"), scatter_dimension=0, tiled=True),
        lax.psum_scatter(up_shift, ("dp", "fsdp"), scatter_dimension=0, tiled=True),
        lax.psum_scatter(depth_taps, ("dp", "fsdp"), scatter_dimension=0, tiled=True),
        lax.psum_scatter(depth_shift, ("dp", "fsdp"), scatter_dimension=0, tiled=True),
        lax.psum_scatter(middle_gain, ("dp", "fsdp"), scatter_dimension=0, tiled=True),
        lax.psum_scatter(middle_shift, ("dp", "fsdp"), scatter_dimension=0, tiled=True),
        lax.psum_scatter(w_down, ("dp", "fsdp"), scatter_dimension=0, tiled=True),
        lax.psum_scatter(down_shift, ("dp", "fsdp"), scatter_dimension=0, tiled=True),
        lax.psum_scatter(last_gain, ("dp", "fsdp"), scatter_dimension=0, tiled=True),
        lax.psum_scatter(last_shift, ("dp", "fsdp"), scatter_dimension=0, tiled=True),
    )


def feed_forward(values, weights):
    normed, normed_unit, inverse = norm_apply(values, weights[0], weights[1])
    hidden = normed.astype(jnp.bfloat16)
    widened = flat_dot(hidden, weights[2]) + weights[3].astype(jnp.float32)
    active = (widened * jax.nn.sigmoid(widened)).astype(jnp.bfloat16)
    result = values + 0.5 * (flat_dot(active, weights[4]) + weights[5].astype(jnp.float32))
    return (result, (normed_unit, inverse, hidden, widened, active))


def feed_backward(upstream, saved, weights):
    normed_unit, inverse, hidden, widened, active = saved
    half_grad = 0.5 * upstream
    half_low = half_grad.astype(jnp.bfloat16)
    down_slope = lead_dot(active, half_low)
    widened_grad = swish_back(back_dot(half_low, weights[4]), widened)
    widened_low = widened_grad.astype(jnp.bfloat16)
    up_slope = lead_dot(hidden, widened_low)
    hidden_grad = back_dot(widened_low, weights[2])
    input_grad, gain_slope, shift_slope = norm_back(hidden_grad, normed_unit, inverse, weights[0])
    slopes = (
        gain_slope,
        shift_slope,
        up_slope,
        jnp.sum(widened_grad, axis=0),
        down_slope,
        jnp.sum(half_grad, axis=0),
    )
    return (upstream + input_grad, slopes)


def bucket_table(frame_count):
    offsets = jnp.arange(2 * frame_count - 1, dtype=jnp.int32) - (frame_count - 1)
    buckets = jnp.clip(offsets, -(NREL // 2), NREL // 2 - 1) + NREL // 2
    return (buckets[:, None] == jnp.arange(NREL, dtype=jnp.int32)[None, :]).astype(jnp.float32)


def relative_bias(table_rows, frame_count):
    diagonals = jnp.dot(
        bucket_table(frame_count),
        table_rows.astype(jnp.float32),
        precision=lax.Precision.HIGHEST,
        preferred_element_type=jnp.float32,
    )
    flipped = jnp.concatenate(
        [jnp.transpose(diagonals[::-1]), jnp.zeros((HEADS, 1), jnp.float32)], axis=1
    )
    spread = jnp.broadcast_to(flipped[:, None, :], (HEADS, frame_count, 2 * frame_count))
    spread = spread.reshape(HEADS, 2 * frame_count * frame_count)
    sheared = spread[:, : frame_count * (2 * frame_count - 1)].reshape(
        HEADS, frame_count, 2 * frame_count - 1
    )
    return sheared[:, :, frame_count - 1 :]


def relative_slope(score_grad, frame_count):
    placed = jnp.pad(score_grad, ((0, 0), (0, 0), (frame_count - 1, 0)))
    flattened = jnp.pad(
        placed.reshape(HEADS, frame_count * (2 * frame_count - 1)), ((0, 0), (0, frame_count))
    )
    columns = jnp.sum(flattened.reshape(HEADS, frame_count, 2 * frame_count), axis=1)
    diagonals = columns[:, 2 * frame_count - 2 :: -1]
    return lax.dot_general(
        bucket_table(frame_count),
        diagonals,
        (((0,), (1,)), ((), ())),
        precision=lax.Precision.HIGHEST,
        preferred_element_type=jnp.float32,
    )


def mixer_scores(query_rows, key_matrix_rows, relative, same_utterance):
    unnormalized_scores = jnp.einsum(
        "jug,fug->ujf", query_rows, key_matrix_rows, preferred_element_type=jnp.float32
    )
    return jnp.where(same_utterance[None], HEAD ** (-0.5) * unnormalized_scores + relative, MASKED)


def mixer_forward(values, segment_ids, weights):
    frame_count = values.shape[0]
    normed, normed_unit, inverse = norm_apply(values, weights[0], weights[1])
    hidden = normed.astype(jnp.bfloat16)
    projected = flat_dot(hidden, weights[2])
    query_rows = (projected[:, :D] + weights[3].astype(jnp.float32)).astype(jnp.bfloat16)
    query_rows = query_rows.reshape(frame_count, HEADS, HEAD)
    key_matrix_rows = projected[:, D : 2 * D].astype(jnp.bfloat16).reshape(frame_count, HEADS, HEAD)
    value_matrix_rows = (projected[:, 2 * D :] + weights[4].astype(jnp.float32)).astype(
        jnp.bfloat16
    )
    value_matrix_rows = value_matrix_rows.reshape(frame_count, HEADS, HEAD)
    relative = relative_bias(weights[7], frame_count)
    same_utterance = segment_ids[:, None] == segment_ids[None, :]
    scores = mixer_scores(query_rows, key_matrix_rows, relative, same_utterance)
    row_peak = jnp.max(scores, axis=-1, keepdims=True)
    powered = jnp.exp(scores - row_peak)
    row_total = jnp.sum(powered, axis=-1, keepdims=True)
    log_total = row_peak + jnp.log(row_total)
    softmax_rows = (powered / row_total).astype(jnp.bfloat16)
    attention_blend = jnp.einsum(
        "ief,fiv->eiv", softmax_rows, value_matrix_rows, preferred_element_type=jnp.float32
    )
    attention_blend = attention_blend.reshape(frame_count, D).astype(jnp.bfloat16)
    result = values + (flat_dot(attention_blend, weights[5]) + weights[6].astype(jnp.float32))
    return (
        result,
        (
            normed_unit,
            inverse,
            hidden,
            query_rows,
            key_matrix_rows,
            value_matrix_rows,
            log_total,
            attention_blend,
            relative,
            same_utterance,
        ),
    )


def mixer_backward(upstream, saved, weights):
    (
        normed_unit,
        inverse,
        hidden,
        query_rows,
        key_matrix_rows,
        value_matrix_rows,
        log_total,
        attention_blend,
        relative,
        same_utterance,
    ) = saved
    frame_count = upstream.shape[0]
    upstream_low = upstream.astype(jnp.bfloat16)
    output_slope = lead_dot(attention_blend, upstream_low)
    attention_blend_gradient = (
        back_dot(upstream_low, weights[5]).astype(jnp.bfloat16).reshape(frame_count, HEADS, HEAD)
    )
    scores = mixer_scores(query_rows, key_matrix_rows, relative, same_utterance)
    soft_full = jnp.exp(scores - log_total)
    value_grad = jnp.einsum(
        "ybr,byq->ryq",
        soft_full.astype(jnp.bfloat16),
        attention_blend_gradient,
        preferred_element_type=jnp.float32,
    ).reshape(frame_count, D)
    soft_grad = jnp.einsum(
        "jug,fug->ujf",
        attention_blend_gradient,
        value_matrix_rows,
        preferred_element_type=jnp.float32,
    )
    score_grad = soft_full * (soft_grad - jnp.sum(soft_full * soft_grad, axis=-1, keepdims=True))
    table_slope = relative_slope(score_grad, frame_count)
    score_reduced_precision = (HEAD ** (-0.5) * score_grad).astype(jnp.bfloat16)
    query_grad = jnp.einsum(
        "ief,fiv->eiv", score_reduced_precision, key_matrix_rows, preferred_element_type=jnp.float32
    ).reshape(frame_count, D)
    key_grad = jnp.einsum(
        "ybr,byq->ryq", score_reduced_precision, query_rows, preferred_element_type=jnp.float32
    ).reshape(frame_count, D)
    projected_low = jnp.concatenate([query_grad, key_grad, value_grad], axis=1).astype(jnp.bfloat16)
    project_slope = lead_dot(hidden, projected_low)
    hidden_grad = back_dot(projected_low, weights[2])
    input_grad, gain_slope, shift_slope = norm_back(hidden_grad, normed_unit, inverse, weights[0])
    slopes = (
        gain_slope,
        shift_slope,
        project_slope,
        jnp.sum(query_grad, axis=0),
        jnp.sum(value_grad, axis=0),
        output_slope,
        jnp.sum(upstream, axis=0),
        table_slope,
    )
    return (upstream + input_grad, slopes)


def filter_forward(values, segment_ids, weights):
    normed, normed_unit, inverse = norm_apply(values, weights[0], weights[1])
    hidden = normed.astype(jnp.bfloat16)
    widened = flat_dot(hidden, weights[2]) + weights[3].astype(jnp.float32)
    gated_rows = widened[:, :D] * jax.nn.sigmoid(widened[:, D:])
    filtered = depthwise(gated_rows, weights[4].astype(jnp.float32), segment_ids) + weights[
        5
    ].astype(jnp.float32)
    middle, middle_unit, middle_inverse = norm_apply(filtered, weights[6], weights[7])
    swished = (middle * jax.nn.sigmoid(middle)).astype(jnp.bfloat16)
    result = values + (flat_dot(swished, weights[8]) + weights[9].astype(jnp.float32))
    return (
        result,
        (
            normed_unit,
            inverse,
            hidden,
            widened,
            gated_rows,
            middle_unit,
            middle_inverse,
            middle,
            swished,
        ),
    )


def filter_backward(upstream, saved, weights, segment_ids):
    (
        normed_unit,
        inverse,
        hidden,
        widened,
        gated_rows,
        middle_unit,
        middle_inverse,
        middle,
        swished,
    ) = saved
    upstream_low = upstream.astype(jnp.bfloat16)
    down_slope = lead_dot(swished, upstream_low)
    middle_grad = swish_back(back_dot(upstream_low, weights[8]), middle)
    filtered_grad, middle_gain_slope, middle_shift_slope = norm_back(
        middle_grad, middle_unit, middle_inverse, weights[6]
    )

    def local_filter(local_rows, local_kernel):
        return depthwise(local_rows, local_kernel, segment_ids)

    unused, pullback = jax.vjp(local_filter, gated_rows, weights[4].astype(jnp.float32))
    gated_grad, kernel_slope = pullback(filtered_grad)
    opened = jax.nn.sigmoid(widened[:, D:])
    widened_grad = jnp.concatenate(
        [gated_grad * opened, gated_grad * widened[:, :D] * opened * (1.0 - opened)], axis=1
    )
    widened_low = widened_grad.astype(jnp.bfloat16)
    up_slope = lead_dot(hidden, widened_low)
    hidden_grad = back_dot(widened_low, weights[2])
    input_grad, gain_slope, shift_slope = norm_back(hidden_grad, normed_unit, inverse, weights[0])
    slopes = (
        gain_slope,
        shift_slope,
        up_slope,
        jnp.sum(widened_grad, axis=0),
        kernel_slope,
        jnp.sum(filtered_grad, axis=0),
        middle_gain_slope,
        middle_shift_slope,
        down_slope,
        jnp.sum(upstream, axis=0),
    )
    return (upstream + input_grad, slopes)


def body(
    frames,
    segments,
    cotangent,
    early_gain,
    early_shift,
    early_up,
    early_lift,
    early_down,
    early_drop,
    mixer_gain,
    mixer_shift,
    mixer_project,
    query_bias,
    value_bias,
    mixer_output,
    mixer_drop,
    distance_table,
    filter_gain,
    filter_shift,
    filter_up,
    filter_lift,
    depth_weight,
    depth_bias,
    middle_gain,
    middle_shift,
    filter_down,
    filter_drop,
    late_gain,
    late_shift,
    late_up,
    late_lift,
    late_down,
    late_drop,
    final_gain,
    final_shift,
):
    start_rows = frames.astype(jnp.float32)
    final_upstream = cotangent.astype(jnp.float32)
    early_full = fetch_feed(early_gain, early_shift, early_up, early_lift, early_down, early_drop)
    first_rows, early_kept = feed_forward(start_rows, early_full)
    mixer_full = fetch_mixer(
        mixer_gain,
        mixer_shift,
        mixer_project,
        query_bias,
        value_bias,
        mixer_output,
        mixer_drop,
        distance_table,
    )
    second_rows, mixer_kept = mixer_forward(first_rows, segments, mixer_full)
    filter_full = fetch_filter(
        filter_gain,
        filter_shift,
        filter_up,
        filter_lift,
        depth_weight,
        depth_bias,
        middle_gain,
        middle_shift,
        filter_down,
        filter_drop,
        final_gain,
        final_shift,
    )
    third_rows, filter_kept = filter_forward(second_rows, segments, filter_full)
    late_full = fetch_feed(late_gain, late_shift, late_up, late_lift, late_down, late_drop)
    fourth_rows, late_kept = feed_forward(third_rows, late_full)
    layer_out, final_unit, final_inverse = norm_apply(fourth_rows, filter_full[10], filter_full[11])
    final_stats = (final_unit, final_inverse)
    upstream, final_gain_slope, final_shift_slope = norm_back(
        final_upstream, final_stats[0], final_stats[1], filter_full[10]
    )
    upstream, late_slopes = feed_backward(upstream, late_kept, late_full)
    late_summed = reduce_feed(
        late_slopes[0],
        late_slopes[1],
        late_slopes[2],
        late_slopes[3],
        late_slopes[4],
        late_slopes[5],
    )
    upstream, filter_grads = filter_backward(upstream, filter_kept, filter_full, segments)
    filter_summed = reduce_filter(
        filter_grads[0],
        filter_grads[1],
        filter_grads[2],
        filter_grads[3],
        filter_grads[4],
        filter_grads[5],
        filter_grads[6],
        filter_grads[7],
        filter_grads[8],
        filter_grads[9],
        final_gain_slope,
        final_shift_slope,
    )
    upstream, mixer_grads = mixer_backward(upstream, mixer_kept, mixer_full)
    mixer_summed = reduce_mixer(
        mixer_grads[0],
        mixer_grads[1],
        mixer_grads[2],
        mixer_grads[3],
        mixer_grads[4],
        mixer_grads[5],
        mixer_grads[6],
        mixer_grads[7],
    )
    upstream, early_slopes = feed_backward(upstream, early_kept, early_full)
    early_summed = reduce_feed(
        early_slopes[0],
        early_slopes[1],
        early_slopes[2],
        early_slopes[3],
        early_slopes[4],
        early_slopes[5],
    )
    return (
        layer_out,
        upstream,
        early_summed[0],
        early_summed[1],
        early_summed[2],
        early_summed[3],
        early_summed[4],
        early_summed[5],
        mixer_summed[0],
        mixer_summed[1],
        mixer_summed[2],
        mixer_summed[3],
        mixer_summed[4],
        mixer_summed[5],
        mixer_summed[6],
        mixer_summed[7],
        filter_summed[0],
        filter_summed[1],
        filter_summed[2],
        filter_summed[3],
        filter_summed[4],
        filter_summed[5],
        filter_summed[6],
        filter_summed[7],
        filter_summed[8],
        filter_summed[9],
        late_summed[0],
        late_summed[1],
        late_summed[2],
        late_summed[3],
        late_summed[4],
        late_summed[5],
        filter_summed[10],
        filter_summed[11],
    )


def near(me, n):
    if n == 4:
        row, column = me // 2, me % 2
        flip_row, flip_column = (1 - row) * 2 + column, row * 2 + 1 - column
        across = (1 - row) * 2 + 1 - column
        return [(flip_column, flip_column), (flip_row, flip_row), (across, across)]
    return [((me + step) % n, (me + n - step) % n) for step in range(1, n)]


def greet(targets):
    barrier = pltpu.get_barrier_semaphore()
    for target in targets:
        pl.semaphore_signal(barrier, inc=1, device_id={"dp": target}, device_id_type=MESH)
    pl.semaphore_wait(barrier, len(targets))


def greet_all(n, m):
    me, lane = lax.axis_index("dp"), lax.axis_index("fsdp")
    barrier = pltpu.get_barrier_semaphore()

    def say(step, carry):
        target = {"dp": (me + step // m) % n, "fsdp": (lane + step % m) % m}
        pl.semaphore_signal(barrier, inc=1, device_id=target, device_id_type=MESH)
        return carry

    lax.fori_loop(1, n * m, say, 0)
    pl.semaphore_wait(barrier, n * m - 1)


def remote(src, dst, send, recv, target):
    return pltpu.make_async_remote_copy(
        src_ref=src, dst_ref=dst, send_sem=send, recv_sem=recv, device_id=target, device_id_type=MESH
    )


def columns(start, width):
    return pl.ds(pl.multiple_of(start * width, width), width)


def column_pieces(index, n, sizes):
    pieces = []
    for place, (groups, width) in enumerate(sizes):
        for group in range(groups):
            wide = pl.ds(pl.multiple_of((group * n + index) * width, width), width)
            pieces.append((place, wide, pl.ds(group * width, width)))
    return pieces


def row_of(shards, line, first):
    rows = shards.shape[0]
    lines = shards[:, line, :]
    lanes = lax.broadcasted_iota(jnp.int32, lines.shape, 1) // 32
    places = lax.broadcasted_iota(jnp.int32, lines.shape, 0) % 4
    merged = jnp.zeros_like(lines)
    for quarter in range(4):
        shift = (32 * quarter - 32 * first) % LANES
        moved = pltpu.roll(lines, shift, 1) if shift else lines
        merged = merged + jnp.where((lanes == quarter) & (places == quarter), moved, 0.0)
    return [
        jnp.sum(merged[4 * tile : 4 * tile + 4], axis=0, keepdims=True) for tile in range(rows // 4)
    ]


def pack_small(small, singles, lifts, table):
    rows = singles[0].shape[0]
    small[...] = jnp.zeros_like(small)
    for at, single in enumerate(singles):
        line, low = at * rows // LANES, at * rows % LANES
        small[line : line + 1, low : low + rows] = single[...].astype(jnp.float32).reshape(1, rows)
    for at, lift in enumerate(lifts):
        line, count = 5 + at, lift.shape[0]
        small[line : line + 1, 0:count] = lift[...].astype(jnp.float32).reshape(1, count)
    small[8 : 8 + table.shape[0], 0 : table.shape[1]] = table[...].astype(jnp.float32)


def spread_vectors(n, m, inner, me, single_count, small_all, gains, own, lifts, wide_lifts):
    for index in range(single_count):
        for tile, line in enumerate(row_of(small_all, index // 4, index % 4)):
            gains[index : index + 1, tile * LANES : (tile + 1) * LANES] = line
    own[...] = gains[:, columns(me, inner)]
    for index in range(2):
        lines = small_all[pl.ds(me * m, m), 5 + index, :]
        for tile in range(m):
            lifts[index : index + 1, tile * LANES : (tile + 1) * LANES] = lines[tile : tile + 1, :]
    lanes = lax.broadcasted_iota(jnp.int32, (1, LANES), 1)
    for group in range(2):
        for tile in range(inner // LANES):
            first = group * n * m // 2 + me * n + 2 * tile
            left, right = small_all[pl.ds(first, 1), 7, :], small_all[pl.ds(first + 1, 1), 7, :]
            low = group * inner + tile * LANES
            wide_lifts[0:1, low : low + LANES] = jnp.where(
                lanes < LANES // 2, left, pltpu.roll(right, LANES // 2, 1)
            )


def pack_info(info, segs):
    count = segs.shape[1]
    row = segs[...].astype(jnp.float32)
    wide = jnp.broadcast_to(row, (count, count))
    tall = jnp.transpose(wide)
    places = lax.broadcasted_iota(jnp.int32, (1, count), 1).astype(jnp.float32)
    info[...] = jnp.zeros_like(info)
    info[0:1, :] = row
    info[1:2, :] = places - jnp.sum(jnp.where(tall < wide, 1.0, 0.0), axis=0, keepdims=True)
    info[2:3, :] = jnp.sum(jnp.where(tall <= wide, 1.0, 0.0), axis=0, keepdims=True) - 1.0 - places


def spread_info(infos, seg_rows, seg_columns, behind, ahead):
    for block in range(infos.shape[0]):
        found = to_columns(infos[block])
        seg_rows[block] = infos[block, 0:1, :]
        seg_columns[block], behind[block], ahead[block] = found[0], found[1], found[2]


def spread_table(heads, me, gathered, table_all, own_table):
    buckets = gathered[:, 8:16, :].reshape(NREL, LANES).astype(jnp.bfloat16)
    sides = lax.broadcasted_iota(jnp.int32, (NREL, NREL), 0) + lax.broadcasted_iota(jnp.int32, (NREL, NREL), 1)
    turned = jnp.where(sides == NREL - 1, 1.0, 0.0).astype(jnp.bfloat16)
    table_all[...] = lead_dot(buckets, turned)
    for head in range(heads):
        own_table[head : head + 1, :] = table_all[pl.ds(me * heads + head, 1), :]


def exchange_kernel(n, m, width, inner, *refs):
    early_up, early_down, late_up, project, filter_up, output, filter_down, depth, segs, frames = refs[:10]
    singles, lift_shards, table = refs[10:29], refs[29:32], refs[32]
    up_full, down_full, late_split, mixer_split, filter_split, small_all = refs[33:39]
    gains, own, lifts, wide_lifts, seg_rows, seg_columns, behind, ahead, own_table, depth_all, spread = refs[39:50]
    info, infos, table_all = refs[50:53]
    gathered, small, held, local, send, recv, small_send, small_recv, up_send, up_recv = refs[53:63]
    climb_send, climb_recv, pass_send, pass_recv, out_send, out_recv, depth_send, depth_recv = refs[63:]
    pack_info(info, segs)
    pack_small(gathered.at[0], singles, lift_shards, table)
    small[...] = gathered[0].astype(jnp.bfloat16)
    me, lane = lax.axis_index("dp"), lax.axis_index("fsdp")
    here = me * m + lane
    levels = m // 2
    level = lane // 2
    units = early_down.shape[0]
    beside = lane + 1 - 2 * (lane % 2)
    others = near(me, n)
    ways = (1, -1)
    greet_all(n, m)

    def place(kind, unit, source):
        if kind:
            return up_full.at[((me + n - unit) % n) * m + source]
        return down_full.at[source, unit]

    def climb(kind, way, distance, unit, src=None):
        block = place(kind, unit, (lane + m - 2 * ways[way] * (distance - 1)) % m)
        return remote(
            block if src is None else src,
            block,
            climb_send.at[kind, way, distance - 1, unit],
            climb_recv.at[kind, way, distance - 1, unit],
            {"fsdp": (lane + m + 2 * ways[way]) % m},
        )

    def across(kind, offset, unit, src=None):
        block = place(kind, unit, (lane + 2 * offset) % m)
        return remote(
            block if src is None else src,
            block,
            pass_send.at[kind, offset, unit],
            pass_recv.at[kind, offset, unit],
            {"fsdp": beside},
        )

    def open_way(way):
        return level < levels - 1 if ways[way] > 0 else level > 0

    def reached(way, distance):
        return level >= distance if ways[way] > 0 else level + distance < levels

    def launch(kind, unit, src=None):
        for way in range(2):

            @pl.when(open_way(way))
            def _():
                climb(kind, way, 1, unit, src).start()

        across(kind, 0, unit, src).start()

    def to_device(step):
        target = {"dp": (me + step // m) % n, "fsdp": (lane + step % m) % m}
        return remote(small, small_all.at[here], small_send.at[step], small_recv.at[step], target)

    def to_lane(step):
        return remote(
            depth, depth_all.at[lane], depth_send.at[step], depth_recv.at[step], {"fsdp": (lane + step) % m}
        )

    def to_column(step):
        other = (me + step) % n
        return remote(
            early_up.at[:, columns(other, width)], up_full.at[here], up_send.at[step], up_recv.at[step], {"dp": other}
        )

    def each(call):
        def turn(step, carry):
            call(step)
            return carry

        return turn

    def pieces(index):
        found = [(late_up.at[:, columns(index, width)], late_split.at[me])]
        for group in range(3):
            wide = pl.ds(pl.multiple_of(group * inner * n + index * inner, inner), inner)
            found.append((project.at[:, wide], mixer_split.at[me, :, pl.ds(group * inner, inner)]))
        for group in range(2):
            wide = pl.ds(pl.multiple_of(group * inner * n + index * inner, inner), inner)
            found.append((filter_up.at[:, wide], filter_split.at[me, :, pl.ds(group * inner, inner)]))
        return found

    lax.fori_loop(1, n * m, each(lambda step: to_device(step).start()), 0)
    infos[me] = info[...]
    info_copies = []
    for peer, (target, unused) in enumerate(others):
        info_copies.append(remote(info, infos.at[me], send.at[peer, 6], recv.at[peer, 6], {"dp": target}))
    for copy in info_copies:
        copy.start()
    lax.fori_loop(1, n, each(lambda step: to_column(step).start()), 0)
    lax.fori_loop(0, units, each(lambda unit: launch(0, unit, early_down.at[unit])), 0)
    mine = early_up.at[:, columns(me, width)]
    launch(1, 0, mine)
    copies = []
    for peer, (target, unused) in enumerate(others):
        for at, (src, dst) in enumerate(pieces(target)):
            copies.append(remote(src, dst, send.at[peer, at], recv.at[peer, at], {"dp": target}))
    owns = [(small, small_all.at[here]), (mine, up_full.at[here]), (early_down, down_full.at[lane])]
    owns += pieces(me)
    for group in range(n):
        wide = pl.ds(group * inner, inner)
        owns.append((output.at[:, wide], mixer_split.at[group, :, pl.ds(3 * inner, inner)]))
        owns.append((filter_down.at[:, wide], filter_split.at[group, :, pl.ds(2 * inner, inner)]))
    owns.append((depth, depth_all.at[lane]))
    owns = [pltpu.make_async_copy(src, dst, local.at[at]) for at, (src, dst) in enumerate(owns)]
    for copy in owns:
        copy.start()
    for step in range(1, n):
        to_column(step).wait_recv()
        launch(1, step)
    for copy in copies:
        copy.start()
    lax.fori_loop(1, m, each(lambda step: to_lane(step).start()), 0)
    def carry_on(kind, distance, unit):
        for way in range(2):

            @pl.when(reached(way, distance))
            def _():
                climb(kind, way, distance, unit).wait_recv()
                offset = levels - distance if ways[way] > 0 else distance
                across(kind, offset, unit).start()
                if distance < levels - 1:

                    @pl.when(open_way(way))
                    def _():
                        climb(kind, way, distance + 1, unit).start()

    def finish(kind, unit):
        for offset in range(levels):
            across(kind, offset, unit).wait()
        for way in range(2):
            for distance in range(1, levels):
                begun = open_way(way)
                if distance > 1:
                    begun = begun & reached(way, distance - 1)

                @pl.when(begun)
                def _():
                    climb(kind, way, distance, unit).wait_send()

    for kind in range(2):
        lax.fori_loop(0, units, each(functools.partial(carry_on, kind, 1)), 0)
    owns[0].wait()
    lax.fori_loop(1, n * m, each(lambda step: to_device(step).wait()), 0)
    gathered[...] = small_all[...].astype(jnp.float32)
    spread_vectors(n, m, inner, me, len(singles), gathered, gains, own, lifts, wide_lifts)
    gain, shift = gains[0:1, :], gains[1:2, :]

    def work(block, carry):
        span = pl.ds(pl.multiple_of(block * BLOCK, BLOCK), BLOCK)
        unit, inverse = unit_of(frames[span, :].astype(jnp.float32))
        held[span, :] = (unit * gain + shift).astype(jnp.bfloat16)
        return carry

    lax.fori_loop(0, frames.shape[0] // BLOCK, work, 0)
    keep = pltpu.make_async_copy(held, spread.at[me], local.at[len(owns)])
    keep.start()
    outgoing = []
    for peer, (target, unused) in enumerate(others):
        outgoing.append(remote(held, spread.at[me], out_send.at[peer], out_recv.at[peer], {"dp": target}))
    for copy in outgoing:
        copy.start()
    for copy in info_copies:
        copy.wait()
    spread_info(infos, seg_rows, seg_columns, behind, ahead)
    spread_table(HEADS // n, me, gathered, table_all, own_table)
    for distance in range(2, levels):
        for kind in range(2):
            lax.fori_loop(0, units, each(functools.partial(carry_on, kind, distance)), 0)
    for copy in owns[1:] + copies + outgoing:
        copy.wait()
    keep.wait()
    for kind in range(2):
        lax.fori_loop(0, units, each(functools.partial(finish, kind)), 0)
    lax.fori_loop(1, n, each(lambda step: to_column(step).wait_send()), 0)
    lax.fori_loop(1, m, each(lambda step: to_lane(step).wait()), 0)


def exchange(n, m, early_up, early_down, late_up, project, filter_up, output, filter_down, depth, segs, frames, singles, lifts, table):
    rows, width = early_up.shape[0], early_up.shape[1] // n
    inner = output.shape[1] // n
    frame_count, deep = frames.shape
    units, levels = early_down.shape[0], m // 2
    low, full = jnp.bfloat16, jnp.float32
    packed = (16, LANES)
    struct = jax.ShapeDtypeStruct
    outs = [
        struct((n * m, rows, width), low),
        struct((m,) + early_down.shape, low),
        struct((n, rows, width), low),
        struct((n, rows, 4 * inner), low),
        struct((n, rows, 3 * inner), low),
        struct((n * m,) + packed, low),
        struct((len(singles), deep), full),
        struct((len(singles), inner), full),
        struct((2, width), full),
        struct((1, 2 * inner), full),
        struct((n, 1, frame_count), full),
        struct((n, frame_count, 1), full),
        struct((n, frame_count, 1), full),
        struct((n, frame_count, 1), full),
        struct((HEADS // n, NREL), full),
        struct((m,) + depth.shape, low),
        struct((n, frame_count, deep), low),
    ]
    anywhere = pl.BlockSpec(memory_space=pl.ANY)
    inside = pl.BlockSpec(memory_space=pltpu.VMEM)
    dma = pltpu.SemaphoreType.DMA
    return pl.pallas_call(
        functools.partial(exchange_kernel, n, m, width, inner),
        out_shape=outs,
        in_specs=[anywhere] * 8 + [inside] * (3 + len(singles) + len(lifts)),
        out_specs=[anywhere] * 5 + [inside] * 10 + [anywhere] * 2,
        scratch_shapes=[
            pltpu.VMEM((8, frame_count), full),
            pltpu.VMEM((n, 8, frame_count), full),
            pltpu.VMEM((LANES, NREL), full),
            pltpu.VMEM((n * m,) + packed, full),
            pltpu.VMEM(packed, low),
            pltpu.VMEM((frame_count, deep), low),
            dma((2 * n + 12,)),
            dma((n - 1, 7)),
            dma((n - 1, 7)),
            dma((n * m,)),
            dma((n * m,)),
            dma((n,)),
            dma((n,)),
            dma((2, 2, levels - 1, units)),
            dma((2, 2, levels - 1, units)),
            dma((2, levels, units)),
            dma((2, levels, units)),
            dma((n - 1,)),
            dma((n - 1,)),
            dma((m,)),
            dma((m,)),
        ],
        compiler_params=pltpu.CompilerParams(collective_id=0, has_side_effects=True),
        name="exchange",
    )(
        early_up, early_down, late_up, project, filter_up, output, filter_down, depth, segs, frames,
        *singles, *lifts, table,
    )


def return_copies(n, sizes, narrows, wides, local, send, recv):
    me = lax.axis_index("dp")
    copies = []
    for peer, (target, unused) in enumerate(near(me, n)):
        for at, (place, wide, narrow) in enumerate(column_pieces(me, n, sizes)):
            copies.append(
                remote(narrows[place].at[target, :, narrow], wides[place].at[:, wide], send.at[peer, at], recv.at[peer, at], {"dp": target})
            )
    for at, (place, wide, narrow) in enumerate(column_pieces(me, n, sizes)):
        copies.append(pltpu.make_async_copy(narrows[place].at[me, :, narrow], wides[place].at[:, wide], local.at[at]))
    return copies


def giveback_kernel(n, sizes, *refs):
    count = len(sizes)
    narrows, wides = refs[:count], refs[count : 2 * count]
    local, send, recv = refs[2 * count :]
    greet([target for target, unused in near(lax.axis_index("dp"), n)])
    copies = return_copies(n, sizes, narrows, wides, local, send, recv)
    for copy in copies:
        copy.start()
    for copy in copies:
        copy.wait()


def giveback(n, narrows, sizes, number):
    rows = narrows[0].shape[1]
    total = sum(groups for groups, width in sizes)
    outs = [jax.ShapeDtypeStruct((rows, groups * width * n), jnp.bfloat16) for groups, width in sizes]
    anywhere = pl.BlockSpec(memory_space=pl.ANY)
    return pl.pallas_call(
        functools.partial(giveback_kernel, n, sizes),
        out_shape=outs,
        in_specs=[anywhere] * len(narrows),
        out_specs=[anywhere] * len(outs),
        scratch_shapes=[
            pltpu.SemaphoreType.DMA((total,)),
            pltpu.SemaphoreType.DMA((n - 1, total)),
            pltpu.SemaphoreType.DMA((n - 1, total)),
        ],
        compiler_params=pltpu.CompilerParams(collective_id=number, has_side_effects=True),
        name="giveback",
    )(*narrows)


def collect_kernel(n, m, sizes, *refs):
    count = len(sizes)
    wide, group = refs[:2]
    narrows, wides = refs[2 : 2 + count], refs[4 + count : 4 + 2 * count]
    wide_all, group_all = refs[2 + count : 4 + count]
    local, send, recv, group_send, group_recv, back_local, back_send, back_recv = refs[4 + 2 * count :]
    me, lane = lax.axis_index("dp"), lax.axis_index("fsdp")
    here = me * m + lane
    greet_all(n, m)

    def to_device(step):
        other, beside = (me + step // m) % n, (lane + step % m) % m
        return remote(
            wide.at[other * m + beside], wide_all.at[here], send.at[step], recv.at[step], {"dp": other, "fsdp": beside}
        )

    def to_group(step):
        beside = (lane + step) % m
        return remote(group.at[beside], group_all.at[lane], group_send.at[step], group_recv.at[step], {"fsdp": beside})

    def start_wide(step, carry):
        to_device(step).start()
        return carry

    def start_group(step, carry):
        to_group(step).start()
        return carry

    def wait_wide(step, carry):
        to_device(step).wait()
        return carry

    def wait_group(step, carry):
        to_group(step).wait()
        return carry

    own = pltpu.make_async_copy(wide.at[here], wide_all.at[here], local.at[0])
    own_group = pltpu.make_async_copy(group.at[lane], group_all.at[lane], local.at[1])
    own.start()
    own_group.start()
    lax.fori_loop(1, n * m, start_wide, 0)
    lax.fori_loop(1, m, start_group, 0)
    copies = return_copies(n, sizes, narrows, wides, back_local, back_send, back_recv)
    for copy in copies:
        copy.start()
    own.wait()
    own_group.wait()
    lax.fori_loop(1, n * m, wait_wide, 0)
    lax.fori_loop(1, m, wait_group, 0)
    for copy in copies:
        copy.wait()


def collect(n, m, wide, group, narrows, sizes, number):
    inside = pl.BlockSpec(memory_space=pltpu.VMEM)
    anywhere = pl.BlockSpec(memory_space=pl.ANY)
    rows = narrows[0].shape[1]
    total = sum(groups for groups, width in sizes)
    outs = [jax.ShapeDtypeStruct(wide.shape, wide.dtype), jax.ShapeDtypeStruct(group.shape, group.dtype)]
    outs += [jax.ShapeDtypeStruct((rows, groups * width * n), jnp.bfloat16) for groups, width in sizes]
    return pl.pallas_call(
        functools.partial(collect_kernel, n, m, sizes),
        out_shape=outs,
        in_specs=[inside] * 2 + [anywhere] * len(sizes),
        out_specs=[inside] * 2 + [anywhere] * len(sizes),
        scratch_shapes=[
            pltpu.SemaphoreType.DMA((2,)),
            pltpu.SemaphoreType.DMA((n * m,)),
            pltpu.SemaphoreType.DMA((n * m,)),
            pltpu.SemaphoreType.DMA((m,)),
            pltpu.SemaphoreType.DMA((m,)),
            pltpu.SemaphoreType.DMA((total,)),
            pltpu.SemaphoreType.DMA((n - 1, total)),
            pltpu.SemaphoreType.DMA((n - 1, total)),
        ],
        compiler_params=pltpu.CompilerParams(collective_id=number, has_side_effects=True),
        name="collect",
    )(wide, group, *narrows)


def keep_kernel(first, second, first_out, second_out):
    first_out[...] = first[...]
    second_out[...] = second[...]


def keep(first, second):
    inside = pl.BlockSpec(memory_space=pltpu.VMEM)
    return pl.pallas_call(
        keep_kernel,
        out_shape=[jax.ShapeDtypeStruct(value.shape, value.dtype) for value in (first, second)],
        in_specs=[inside] * 2,
        out_specs=[inside] * 2,
        name="keep",
    )(first, second)


def unit_of(values):
    centered = values - jnp.mean(values, axis=-1, keepdims=True)
    inverse = lax.rsqrt(jnp.mean(centered * centered, axis=-1, keepdims=True) + EPSILON)
    return centered * inverse, inverse


def unit_back(upstream, unit, inverse, gain):
    scaled = upstream * gain
    adjusted = scaled - jnp.mean(scaled, axis=-1, keepdims=True)
    return inverse * (adjusted - unit * jnp.mean(scaled * unit, axis=-1, keepdims=True))


def step_forward(scale, total, states, vectors):
    values = states[0] + scale * (total + vectors[0])
    unit, inverse = unit_of(values)
    return [values], unit * vectors[1] + vectors[2], []


def step_turn(total, states, vectors):
    values = states[0] + 0.5 * (total + vectors[0])
    upstream = states[1]
    unit, inverse = unit_of(values)
    layer_out = unit * vectors[1] + vectors[2]
    grad = unit_back(upstream, unit, inverse, vectors[1])
    half = 0.5 * grad
    return [layer_out, grad], half, [upstream * unit, upstream, half]


def step_backward(scale, total, states, vectors):
    unit, inverse = unit_of(states[1])
    grad = states[0] + unit_back(total, unit, inverse, vectors[0])
    sent = scale * grad
    return [grad], sent, [total * unit, total, sent]


def step_last(total, states, vectors):
    unit, inverse = unit_of(states[1])
    grad = states[0] + unit_back(total, unit, inverse, vectors[0])
    return [grad], None, [total * unit, total]


def boundary_kernel(step, shape, *refs):
    gathered, state_count, out_count, sum_count, picked = shape
    refs = list(refs)
    take = lambda count: [refs.pop(0) for unused in range(count)]
    part = take(1)[0]
    states = take(state_count)
    vectors = take(1)[0]
    outs = take(out_count)
    spread = take(1)[0] if gathered else None
    sums = take(1)[0] if sum_count else None
    arrived, passing, mine, merged, own, local = take(6)
    relay_send, relay_recv, direct_send, direct_recv, merge_send, merge_recv = take(6)
    if gathered:
        held, held_sem, out_send, out_recv, pass_send, pass_recv = take(6)
    partials = take(1)[0] if sum_count else None
    me = lax.axis_index("dp")
    row, column = me // 2, me % 2
    sides = [row * 2 + 1 - column, (1 - row) * 2 + column]
    across = (1 - row) * 2 + 1 - column
    half = own.shape[0] // 2
    height = half // PIECES
    both, places = range(2), range(PIECES)

    def span(axis, piece):
        return pl.ds(axis * half + piece * height, height)

    def inner(piece):
        return pl.ds(piece * height, height)

    def relay(axis, piece):
        return remote(
            part.at[across, span(axis, piece)],
            passing.at[axis, inner(piece)],
            relay_send.at[axis, piece],
            relay_recv.at[axis, piece],
            {"dp": sides[axis]},
        )

    def direct(axis, piece):
        return remote(
            part.at[sides[axis], span(axis, piece)],
            arrived.at[axis, span(axis, piece)],
            direct_send.at[axis, piece],
            direct_recv.at[axis, piece],
            {"dp": sides[axis]},
        )

    def merge(axis, piece):
        return remote(
            merged.at[axis, inner(piece)],
            arrived.at[1 - axis, span(axis, piece)],
            merge_send.at[axis, piece],
            merge_recv.at[axis, piece],
            {"dp": sides[1 - axis]},
        )

    def hand(target, axis, piece):
        return remote(
            held.at[span(axis, piece)],
            spread.at[me, span(axis, piece)],
            out_send.at[target, axis, piece],
            out_recv.at[target, axis, piece],
            {"dp": sides[target]},
        )

    def onward(axis, piece):
        block = spread.at[sides[axis], span(axis, piece)]
        return remote(
            block, block, pass_send.at[axis, piece], pass_recv.at[axis, piece], {"dp": sides[1 - axis]}
        )

    def forward(axis, piece):
        hand(axis, axis, piece).wait_recv()
        onward(axis, piece).start()

    greet(sides)
    for piece in places:
        for axis in both:
            relay(axis, piece).start()
    locals_ = [
        pltpu.make_async_copy(part.at[sides[1 - axis], pl.ds(axis * half, half)], mine.at[axis], local.at[axis])
        for axis in both
    ]
    locals_.append(pltpu.make_async_copy(part.at[me], own, local.at[2]))
    for copy in locals_:
        copy.start()
    for piece in places:
        for axis in both:
            direct(axis, piece).start()
    if sum_count:
        partials[...] = jnp.zeros_like(partials)
    for copy in locals_:
        copy.wait()
    for piece in places:
        for axis in both:
            relay(axis, piece).wait_recv()

            def join(block, carry):
                rows = pl.ds(pl.multiple_of(piece * height + block * BLOCK, BLOCK), BLOCK)
                total = passing[axis, rows, :].astype(jnp.float32) + mine[axis, rows, :].astype(jnp.float32)
                merged[axis, rows, :] = total.astype(jnp.bfloat16)
                return carry

            lax.fori_loop(0, height // BLOCK, join, 0)
            merge(axis, piece).start()
    rows_of = [vectors[pl.ds(index, 1), :] for index in picked]
    order = [(axis, piece) for piece in places for axis in both]
    for at, (axis, piece) in enumerate(order):
        direct(axis, piece).wait_recv()
        merge(axis, piece).wait_recv()

        def work(block, carry):
            rows = pl.ds(pl.multiple_of(axis * half + piece * height + block * BLOCK, BLOCK), BLOCK)
            total = own[rows, :].astype(jnp.float32)
            for side in both:
                total = total + arrived[side, rows, :].astype(jnp.float32)
            made, sent, terms = step(total, [state[rows, :].astype(jnp.float32) for state in states], rows_of)
            for out, value in zip(outs, made):
                out[rows, :] = value
            if gathered:
                held[rows, :] = sent.astype(jnp.bfloat16)
            for index, term in enumerate(terms):
                partials[index] += sum(term[8 * low : 8 * low + 8] for low in range(BLOCK // 8))
            return carry

        lax.fori_loop(0, height // BLOCK, work, 0)
        if gathered:
            for target in both:
                hand(target, axis, piece).start()
            if at >= LAG:
                forward(*order[at - LAG])
    if gathered:
        keep = pltpu.make_async_copy(held, spread.at[me], held_sem)
        keep.start()
        for axis, piece in order[len(order) - LAG :]:
            forward(axis, piece)
    for index in range(sum_count):
        sums[pl.ds(index, 1), :] = jnp.sum(partials[index], axis=0, keepdims=True)
    for axis, piece in order:
        relay(axis, piece).wait_send()
        direct(axis, piece).wait_send()
        merge(axis, piece).wait_send()
    if gathered:
        for axis, piece in order:
            hand(axis, axis, piece).wait_send()
            hand(1 - axis, axis, piece).wait()
        for axis, piece in order:
            onward(axis, piece).wait()
        keep.wait()


def boundary(step, part, states, vectors, picked, out_count, sum_count, number, gathered=True):
    n, rows, width = part.shape
    inside = pl.BlockSpec(memory_space=pltpu.VMEM)
    anywhere = pl.BlockSpec(memory_space=pl.ANY)
    dma = pltpu.SemaphoreType.DMA
    shape = (gathered, len(states), out_count, sum_count, picked)
    low = jnp.bfloat16
    scratch = [
        pltpu.VMEM((2, rows, width), low),
        pltpu.VMEM((2, rows // 2, width), low),
        pltpu.VMEM((2, rows // 2, width), low),
        pltpu.VMEM((2, rows // 2, width), low),
        pltpu.VMEM((rows, width), low),
        dma((3,)),
    ]
    scratch += [dma((2, PIECES))] * 6
    outs = [jax.ShapeDtypeStruct((rows, width), jnp.float32)] * out_count
    out_specs = [inside] * out_count
    if gathered:
        outs.append(jax.ShapeDtypeStruct((n, rows, width), low))
        out_specs.append(anywhere)
        scratch += [pltpu.VMEM((rows, width), low), dma]
        scratch += [dma((2, 2, PIECES))] * 2 + [dma((2, PIECES))] * 2
    if sum_count:
        outs.append(jax.ShapeDtypeStruct((sum_count, width), jnp.float32))
        out_specs.append(inside)
        scratch.append(pltpu.VMEM((sum_count, 8, width), jnp.float32))
    return pl.pallas_call(
        functools.partial(boundary_kernel, step, shape),
        out_shape=outs,
        in_specs=[anywhere] + [inside] * (len(states) + 1),
        out_specs=out_specs,
        scratch_shapes=scratch,
        compiler_params=pltpu.CompilerParams(collective_id=number, has_side_effects=True),
        name="boundary",
    )(part, *states, vectors)


def toeplitz(line, frame_count):
    wide = jnp.broadcast_to(line, (frame_count, NREL))
    return pltpu.roll(wide, NREL - frame_count + 1, 1, stride=1, stride_axis=0)[:, :frame_count]


def head_scores(packed, head, heads, same, bias):
    size = heads * HEAD
    query_rows = packed[:, head * HEAD : (head + 1) * HEAD]
    key_rows = packed[:, size + head * HEAD : size + (head + 1) * HEAD]
    value_rows = packed[:, 2 * size + head * HEAD : 2 * size + (head + 1) * HEAD]
    scores = jnp.where(same, HEAD ** (-0.5) * back_dot(query_rows, key_rows) + bias, MASKED)
    powered = jnp.exp(scores - jnp.max(scores, axis=-1, keepdims=True))
    soft = powered / jnp.sum(powered, axis=-1, keepdims=True)
    return query_rows, key_rows, value_rows, soft


def attend_kernel(heads, packed, segment_rows, segment_columns, table, blended, bias):
    frame_count = packed.shape[1]

    @pl.when(pl.program_id(0) == 0)
    def _():
        for head in range(heads):
            bias[head] = toeplitz(table[pl.ds(head, 1), :], frame_count)

    same = segment_columns[0] == segment_rows[0]
    block = packed[0]
    results = []
    for head in range(heads):
        unused, unused_too, value_rows, soft = head_scores(block, head, heads, same, bias[head])
        results.append(flat_dot(soft.astype(jnp.bfloat16), value_rows).astype(jnp.bfloat16))
    blended[0] = jnp.concatenate(results, axis=1)


def attend(packed, segment_rows, segment_columns, table):
    blocks, frame_count, width = packed.shape
    heads = table.shape[0]
    return pl.pallas_call(
        functools.partial(attend_kernel, heads),
        grid=(blocks,),
        out_shape=jax.ShapeDtypeStruct((blocks, frame_count, width // 3), jnp.bfloat16),
        in_specs=[
            pl.BlockSpec((1, frame_count, width), lambda i: (i, 0, 0)),
            pl.BlockSpec((1, 1, frame_count), lambda i: (i, 0, 0)),
            pl.BlockSpec((1, frame_count, 1), lambda i: (i, 0, 0)),
            pl.BlockSpec((heads, NREL), lambda i: (0, 0)),
        ],
        out_specs=pl.BlockSpec((1, frame_count, width // 3), lambda i: (i, 0, 0)),
        scratch_shapes=[pltpu.VMEM((heads, frame_count, frame_count), jnp.float32)],
        name="attend",
    )(packed, segment_rows, segment_columns, table)


def unattend_kernel(heads, packed, upstream, segment_rows, segment_columns, table, grads, sums, slope, bias, gathered):
    frame_count = packed.shape[1]
    size = heads * HEAD
    at = pl.program_id(0)

    @pl.when(at == 0)
    def _():
        for head in range(heads):
            bias[head] = toeplitz(table[pl.ds(head, 1), :], frame_count)
        gathered[...] = jnp.zeros_like(gathered)
        sums[...] = jnp.zeros_like(sums)

    same = segment_columns[0] == segment_rows[0]
    block = packed[0]
    above = upstream[0]
    query_grads, key_grads, value_grads = [], [], []
    for head in range(heads):
        query_rows, key_rows, value_rows, soft = head_scores(block, head, heads, same, bias[head])
        blend_grad = above[:, head * HEAD : (head + 1) * HEAD]
        value_grads.append(lead_dot(soft.astype(jnp.bfloat16), blend_grad))
        soft_grad = back_dot(blend_grad, value_rows)
        score_grad = soft * (soft_grad - jnp.sum(soft * soft_grad, axis=-1, keepdims=True))
        gathered[head] += score_grad
        low = (HEAD ** (-0.5) * score_grad).astype(jnp.bfloat16)
        query_grads.append(flat_dot(low, key_rows))
        key_grads.append(lead_dot(low, query_rows))
    query_grad = jnp.concatenate(query_grads, axis=1)
    value_grad = jnp.concatenate(value_grads, axis=1)
    grads[0, :, 0:size] = query_grad.astype(jnp.bfloat16)
    grads[0, :, size : 2 * size] = jnp.concatenate(key_grads, axis=1).astype(jnp.bfloat16)
    grads[0, :, 2 * size :] = value_grad.astype(jnp.bfloat16)
    sums[0:1, :] += jnp.sum(query_grad, axis=0, keepdims=True)
    sums[1:2, :] += jnp.sum(value_grad, axis=0, keepdims=True)

    @pl.when(at == pl.num_programs(0) - 1)
    def _():
        places = lax.broadcasted_iota(jnp.int32, (frame_count, NREL), 0)
        for head in range(heads):
            wide = jnp.concatenate(
                [gathered[head], jnp.zeros((frame_count, NREL - frame_count), jnp.float32)], axis=1
            )
            stride = 1
            while stride < frame_count:
                moved = pltpu.roll(wide, NREL - stride, 1)
                wide = jnp.where((places // stride) % 2 == 1, moved, wide)
                stride *= 2
            slope[pl.ds(head, 1), :] = jnp.sum(wide, axis=0, keepdims=True)


def unattend(packed, upstream, segment_rows, segment_columns, table):
    blocks, frame_count, width = packed.shape
    heads = table.shape[0]
    return pl.pallas_call(
        functools.partial(unattend_kernel, heads),
        grid=(blocks,),
        out_shape=[
            jax.ShapeDtypeStruct((blocks, frame_count, width), jnp.bfloat16),
            jax.ShapeDtypeStruct((2, width // 3), jnp.float32),
            jax.ShapeDtypeStruct((heads, NREL), jnp.float32),
        ],
        in_specs=[
            pl.BlockSpec((1, frame_count, width), lambda i: (i, 0, 0)),
            pl.BlockSpec((1, frame_count, width // 3), lambda i: (i, 0, 0)),
            pl.BlockSpec((1, 1, frame_count), lambda i: (i, 0, 0)),
            pl.BlockSpec((1, frame_count, 1), lambda i: (i, 0, 0)),
            pl.BlockSpec((heads, NREL), lambda i: (0, 0)),
        ],
        out_specs=[
            pl.BlockSpec((1, frame_count, width), lambda i: (i, 0, 0)),
            pl.BlockSpec((2, width // 3), lambda i: (0, 0)),
            pl.BlockSpec((heads, NREL), lambda i: (0, 0)),
        ],
        scratch_shapes=[
            pltpu.VMEM((heads, frame_count, frame_count), jnp.float32),
            pltpu.VMEM((heads, frame_count, frame_count), jnp.float32),
        ],
        name="unattend",
    )(packed, upstream, segment_rows, segment_columns, table)


def reach_mask(offset, behind, ahead):
    if offset < 0:
        return behind >= -offset
    return ahead >= offset


def to_rows(wide, count):
    return jnp.transpose(wide)[:count]


def to_columns(rows):
    count, length = rows.shape
    wide = jnp.transpose(jnp.concatenate([rows, jnp.zeros((LANES - count, length), rows.dtype)]))
    return [wide[:, at : at + 1] for at in range(count)]


def swap(n, mine, shared, send, recv):
    me = lax.axis_index("dp")
    shared[me] = mine[...]
    copies = []
    for peer, (target, unused) in enumerate(near(me, n)):
        copies.append(remote(mine, shared.at[me], send.at[peer], recv.at[peer], {"dp": target}))
    for copy in copies:
        copy.start()
    for copy in copies:
        copy.wait()


def fill(store, value):
    frame_count, channels = value.shape
    store[pl.ds(0, MARGIN), :] = jnp.zeros((MARGIN, channels), jnp.float32)
    store[pl.ds(MARGIN + frame_count, MARGIN), :] = jnp.zeros((MARGIN, channels), jnp.float32)
    store[pl.ds(MARGIN, frame_count), :] = value


def convolve_kernel(
    n, opened, behind, ahead, taps, vectors, gated, unit, inverse, swished, padded, mine, shared, send, recv
):
    frame_count, channels = gated.shape[1:]
    greet([target for target, unused in near(lax.axis_index("dp"), n)])
    places = lax.broadcasted_iota(jnp.int32, (frame_count, LANES), 1)

    def filter_block(block, wide):
        gates = opened[block, :, 0:channels] * jax.nn.sigmoid(opened[block, :, channels:])
        gated[block] = gates
        fill(padded, gates)
        back = jnp.broadcast_to(behind[block], (frame_count, LANES))
        front = jnp.broadcast_to(ahead[block], (frame_count, LANES))
        for low in range(0, channels, LANES):
            lanes = slice(low, low + LANES)
            running = jnp.broadcast_to(vectors[10:11, lanes], (frame_count, LANES))
            for tap in range(KW):
                offset = tap - (KW - 1) // 2
                moved = padded[pl.ds(MARGIN + offset, frame_count), lanes]
                if offset:
                    moved = jnp.where(reach_mask(offset, back, front), moved, 0.0)
                running = running + moved * taps[pl.ds(tap, 1), lanes]
            unit[block, :, lanes] = running
        filtered = unit[block]
        mean = jnp.mean(filtered, axis=-1, keepdims=True)
        square = jnp.sum((filtered - mean) ** 2, axis=-1, keepdims=True)
        return jnp.where(places == block, mean, jnp.where(places == n + block, square, wide))

    wide = lax.fori_loop(0, n, filter_block, jnp.zeros((frame_count, LANES), jnp.float32))
    mine[...] = to_rows(wide, 2 * n)
    swap(n, mine, shared, send, recv)
    everyone = [shared[at] for at in range(n)]
    middle_mean = sum(rows[:n] for rows in everyone) / n
    total = sum(rows[n:] + channels * (rows[:n] - middle_mean) ** 2 for rows in everyone)
    scale = lax.rsqrt(total / (n * channels) + EPSILON)
    found = to_columns(jnp.concatenate([middle_mean, scale]))
    for block in range(n):
        values = (unit[block] - found[block]) * found[n + block]
        unit[block] = values
        inverse[block] = found[n + block]
        middle = values * vectors[11:12, :] + vectors[12:13, :]
        swished[block] = (middle * jax.nn.sigmoid(middle)).astype(jnp.bfloat16)


def swap_scratch(n, frame_count):
    return [
        pltpu.VMEM((2 * n, frame_count), jnp.float32),
        pltpu.VMEM((n, 2 * n, frame_count), jnp.float32),
        pltpu.SemaphoreType.DMA((n - 1,)),
        pltpu.SemaphoreType.DMA((n - 1,)),
    ]


def convolve(opened, behind, ahead, taps, vectors, number):
    blocks, frame_count, width = opened.shape
    channels = width // 2
    inside = pl.BlockSpec(memory_space=pltpu.VMEM)
    wide = (blocks, frame_count, channels)
    return pl.pallas_call(
        functools.partial(convolve_kernel, blocks),
        out_shape=[
            jax.ShapeDtypeStruct(wide, jnp.float32),
            jax.ShapeDtypeStruct(wide, jnp.float32),
            jax.ShapeDtypeStruct((blocks, frame_count, 1), jnp.float32),
            jax.ShapeDtypeStruct(wide, jnp.bfloat16),
        ],
        in_specs=[inside] * 5,
        out_specs=[inside] * 4,
        scratch_shapes=[pltpu.VMEM((frame_count + 2 * MARGIN, channels), jnp.float32)] + swap_scratch(blocks, frame_count),
        compiler_params=pltpu.CompilerParams(collective_id=number, has_side_effects=True),
        name="convolve",
    )(opened, behind, ahead, taps, vectors)


def unconvolve_kernel(
    n, opened, gated, upstream, unit, inverse, behind, ahead, taps, vectors, grads, lifts, slopes, *scratch
):
    padded, padded_grad, turned, mine, shared, send, recv = scratch
    frame_count, channels = gated.shape[1:]
    greet([target for target, unused in near(lax.axis_index("dp"), n)])
    places = lax.broadcasted_iota(jnp.int32, (frame_count, LANES), 1)
    lifts[...] = jnp.zeros_like(lifts)
    slopes[...] = jnp.zeros_like(slopes)
    wide = jnp.zeros((frame_count, LANES), jnp.float32)
    for block in range(n):
        scaled = upstream[block] * vectors[11:12, :]
        plain = jnp.sum(scaled, axis=-1, keepdims=True)
        along = jnp.sum(scaled * unit[block], axis=-1, keepdims=True)
        wide = jnp.where(places == block, plain, jnp.where(places == n + block, along, wide))
    mine[...] = to_rows(wide, 2 * n)
    swap(n, mine, shared, send, recv)
    found = to_columns(sum(shared[at] for at in range(n)) / (n * channels))
    for block in range(n):
        scaled = upstream[block] * vectors[11:12, :]
        turned[block] = inverse[block] * (scaled - found[block] - unit[block] * found[n + block])

    def block_back(block, carry):
        fill(padded, gated[block])
        fill(padded_grad, turned[block])
        back = jnp.broadcast_to(behind[block], (frame_count, LANES))
        front = jnp.broadcast_to(ahead[block], (frame_count, LANES))
        for low in range(0, channels, LANES):
            lanes = slice(low, low + LANES)
            above = turned[block, :, lanes]
            running = jnp.zeros((frame_count, LANES), jnp.float32)
            for tap in range(KW):
                offset = tap - (KW - 1) // 2
                moved = padded[pl.ds(MARGIN + offset, frame_count), lanes]
                moved_grad = padded_grad[pl.ds(MARGIN + offset, frame_count), lanes]
                if offset:
                    mask = reach_mask(offset, back, front)
                    moved = jnp.where(mask, moved, 0.0)
                    moved_grad = jnp.where(mask, moved_grad, 0.0)
                running = running + moved_grad * taps[pl.ds(KW - 1 - tap, 1), lanes]
                slopes[pl.ds(tap, 1), lanes] += jnp.sum(moved * above, axis=0, keepdims=True)
            slopes[pl.ds(KW, 1), lanes] += jnp.sum(above, axis=0, keepdims=True)
            far = slice(channels + low, channels + low + LANES)
            left, gate = opened[block, :, lanes], jax.nn.sigmoid(opened[block, :, far])
            left_grad = running * gate
            gate_grad = running * left * gate * (1.0 - gate)
            grads[block, :, lanes] = left_grad.astype(jnp.bfloat16)
            grads[block, :, far] = gate_grad.astype(jnp.bfloat16)
            lifts[:, lanes] += jnp.sum(left_grad, axis=0, keepdims=True)
            lifts[:, far] += jnp.sum(gate_grad, axis=0, keepdims=True)
        return carry

    lax.fori_loop(0, n, block_back, 0)


def unconvolve(opened, gated, upstream, unit, inverse, behind, ahead, taps, vectors, number):
    blocks, frame_count, width = opened.shape
    channels = width // 2
    inside = pl.BlockSpec(memory_space=pltpu.VMEM)
    return pl.pallas_call(
        functools.partial(unconvolve_kernel, blocks),
        out_shape=[
            jax.ShapeDtypeStruct((blocks, frame_count, width), jnp.bfloat16),
            jax.ShapeDtypeStruct((1, width), jnp.float32),
            jax.ShapeDtypeStruct((KW + 1, channels), jnp.float32),
        ],
        in_specs=[inside] * 9,
        out_specs=[inside] * 3,
        scratch_shapes=[
            pltpu.VMEM((frame_count + 2 * MARGIN, channels), jnp.float32),
            pltpu.VMEM((frame_count + 2 * MARGIN, channels), jnp.float32),
            pltpu.VMEM((blocks, frame_count, channels), jnp.float32),
        ]
        + swap_scratch(blocks, frame_count),
        compiler_params=pltpu.CompilerParams(collective_id=number, has_side_effects=True),
        name="unconvolve",
    )(opened, gated, upstream, unit, inverse, behind, ahead, taps, vectors)


def gather_rows(value):
    return lax.all_gather(value, "fsdp", axis=0, tiled=True)


def gather_split(value):
    full = lax.all_gather(value, "fsdp", axis=1, tiled=True)
    return full.reshape(-1, full.shape[-1])


def scatter_rows(value):
    return lax.psum_scatter(value.astype(jnp.bfloat16), "fsdp", scatter_dimension=0, tiled=True)


def scatter_split(value, n):
    value = value.astype(jnp.bfloat16).reshape(n, value.shape[0] // n, value.shape[1])
    return lax.psum_scatter(value, "fsdp", scatter_dimension=1, tiled=True)


def pair_slopes(up_slope, down_slope, n):
    inner = down_slope.shape[0]
    up_slope = up_slope.reshape(n, inner, -1)
    down_slope = jnp.transpose(down_slope.reshape(inner, n, inner), (1, 0, 2))
    return jnp.concatenate([up_slope, down_slope], axis=2)


def flat(value):
    return value.reshape(-1, value.shape[-1])


def split_body(
    n,
    m,
    frames,
    segments,
    cotangent,
    early_gain,
    early_shift,
    early_up,
    early_lift,
    early_down,
    early_drop,
    mixer_gain,
    mixer_shift,
    mixer_project,
    query_bias,
    value_bias,
    mixer_output,
    mixer_drop,
    distance_table,
    filter_gain,
    filter_shift,
    filter_up,
    filter_lift,
    depth_weight,
    depth_bias,
    middle_gain,
    middle_shift,
    filter_down,
    filter_drop,
    late_gain,
    late_shift,
    late_up,
    late_lift,
    late_down,
    late_drop,
    final_gain,
    final_shift,
):
    me = lax.axis_index("dp")
    frame_count = frames.shape[0]
    rows = early_gain.shape[0]
    hidden = early_up.shape[1] // n
    inner = D // n
    heads = HEADS // n
    singles = [
        early_gain, early_shift, early_drop, mixer_gain, mixer_shift, query_bias, value_bias, mixer_drop,
        filter_gain, filter_shift, depth_bias, middle_gain, middle_shift, filter_drop, late_gain, late_shift,
        late_drop, final_gain, final_shift,
    ]
    spans = hidden * n // D
    (
        w_early_up, w_early_down, late_up_split, mixer_split, filter_split, small_all, vectors, own_vectors, lifts,
        filter_lifts, segment_rows, segment_columns, behind, ahead, table, depth_all, early_hidden,
    ) = exchange(
        n, m, early_up, early_down.reshape(spans, rows, D), late_up, mixer_project, filter_up, mixer_output,
        filter_down, depth_weight, segments.reshape(1, frame_count), frames, singles,
        [early_lift, late_lift, filter_lift], distance_table,
    )
    w_early_up = w_early_up.reshape(D, hidden)
    w_early_down = w_early_down.reshape(hidden, D)
    w_mixer = lax.all_gather(mixer_split, "fsdp", axis=1, tiled=True)
    w_filter = lax.all_gather(filter_split, "fsdp", axis=1, tiled=True)
    w_late_up = gather_split(late_up_split)
    w_late_down = gather_rows(late_down)

    early_lifts, late_lifts = lifts[0], lifts[1]
    taps = jnp.transpose(depth_all.reshape(inner, KW)).astype(jnp.float32)
    attention_shift = jnp.concatenate([own_vectors[5], jnp.zeros((inner,), jnp.float32), own_vectors[6]])

    def blocks(value):
        return value.reshape(n, frame_count, value.shape[-1])

    def feed(hidden_rows, w_up, lifts, w_down):
        widened = flat_dot(flat(hidden_rows), w_up) + lifts
        active = (widened * jax.nn.sigmoid(widened)).astype(jnp.bfloat16)
        return widened, active, blocks(flat_dot(active, w_down).astype(jnp.bfloat16))

    def feed_back(low, hidden_rows, widened, active, w_up, w_down):
        low = flat(low)
        down_slope = lead_dot(active, low).astype(jnp.bfloat16)
        widened_grad = swish_back(back_dot(low, w_down), widened)
        widened_low = widened_grad.astype(jnp.bfloat16)
        up_slope = lead_dot(flat(hidden_rows), widened_low).astype(jnp.bfloat16)
        down_slope = jnp.transpose(down_slope.reshape(m, spans, rows, D), (1, 0, 2, 3)).reshape(spans, m * rows, D)
        slope = jnp.concatenate([up_slope.reshape(n, D // n, hidden), down_slope])
        widened_low, slope = lax.optimization_barrier((widened_low, slope))
        part = blocks(back_dot(widened_low, w_up).astype(jnp.bfloat16))
        return part, slope, jnp.sum(widened_grad, axis=0)

    early_wide, early_active, part = feed(early_hidden, w_early_up, early_lifts, w_early_down)
    first_rows, mixer_hidden = boundary(
        functools.partial(step_forward, 0.5), part, [frames], vectors, (2, 3, 4), 1, 0, 2
    )
    mixer_hidden, w_mixer = lax.optimization_barrier((mixer_hidden, w_mixer))
    w_project = w_mixer[:, :, : 3 * inner].reshape(D, 3 * inner)
    w_output = jnp.transpose(w_mixer[:, :, 3 * inner :], (1, 0, 2)).reshape(inner, D)
    packed = blocks((flat_dot(flat(mixer_hidden), w_project) + attention_shift).astype(jnp.bfloat16))
    blended = attend(packed, segment_rows, segment_columns, table)
    part = blocks(flat_dot(flat(blended), w_output).astype(jnp.bfloat16))
    second_rows, filter_hidden = boundary(
        functools.partial(step_forward, 1.0), part, [first_rows], vectors, (7, 8, 9), 1, 0, 3
    )
    filter_hidden, w_filter = lax.optimization_barrier((filter_hidden, w_filter))
    w_filter_up = w_filter[:, :, : 2 * inner].reshape(D, 2 * inner)
    w_filter_down = jnp.transpose(w_filter[:, :, 2 * inner :], (1, 0, 2)).reshape(inner, D)
    opened = blocks(flat_dot(flat(filter_hidden), w_filter_up) + filter_lifts)
    gated, middle_unit, middle_inverse, swished = convolve(opened, behind, ahead, taps, own_vectors, 4)
    swished = flat(swished)
    part = blocks(flat_dot(swished, w_filter_down).astype(jnp.bfloat16))
    third_rows, late_hidden = boundary(
        functools.partial(step_forward, 1.0), part, [second_rows], vectors, (13, 14, 15), 1, 0, 5
    )
    late_hidden, w_late_up, w_late_down = lax.optimization_barrier((late_hidden, w_late_up, w_late_down))
    late_wide, late_active, part = feed(late_hidden, w_late_up, late_lifts, w_late_down)
    layer_out, grad, low, turn_sums = boundary(
        step_turn, part, [third_rows, cotangent], vectors, (16, 17, 18), 2, 3, 6
    )

    part, late_slope, late_lift_slope = feed_back(
        low, late_hidden, late_wide, late_active, w_late_up, w_late_down
    )
    late_slope = lax.psum_scatter(late_slope, "fsdp", scatter_dimension=1, tiled=True)
    grad, low, late_sums = boundary(
        functools.partial(step_backward, 1.0), part, [grad, third_rows], vectors, (14,), 1, 3, 7
    )
    low = flat(low)
    filter_down_slope = lead_dot(swished, low).astype(jnp.bfloat16)
    flat_unit = flat(middle_unit)
    middle = flat_unit * own_vectors[11] + own_vectors[12]
    middle_grad = swish_back(back_dot(low, w_filter_down), middle)
    middle_gain_slope = jnp.sum(middle_grad * flat_unit, axis=0)
    middle_shift_slope = jnp.sum(middle_grad, axis=0)
    opened_low, filter_lift_slope, depth_slope = unconvolve(
        opened, gated, blocks(middle_grad), middle_unit, middle_inverse, behind, ahead, taps, own_vectors, 8
    )
    opened_low = flat(opened_low)
    filter_up_slope = lead_dot(flat(filter_hidden), opened_low).astype(jnp.bfloat16)
    part = blocks(back_dot(opened_low, w_filter_up).astype(jnp.bfloat16))
    part, filter_slope = lax.optimization_barrier((part, pair_slopes(filter_up_slope, filter_down_slope, n)))
    filter_slope = lax.psum_scatter(filter_slope, "fsdp", scatter_dimension=1, tiled=True)
    grad, low, filter_sums = boundary(
        functools.partial(step_backward, 1.0), part, [grad, second_rows], vectors, (8,), 1, 3, 9
    )
    low = flat(low)
    output_slope = lead_dot(flat(blended), low).astype(jnp.bfloat16)
    blend_grad = blocks(back_dot(low, w_output).astype(jnp.bfloat16))
    packed_low, shift_sums, table_slope = unattend(packed, blend_grad, segment_rows, segment_columns, table)
    packed_low = flat(packed_low)
    project_slope = lead_dot(flat(mixer_hidden), packed_low).astype(jnp.bfloat16)
    part = blocks(back_dot(packed_low, w_project).astype(jnp.bfloat16))
    part, mixer_slope, late_slope = lax.optimization_barrier(
        (part, pair_slopes(project_slope, output_slope, n), late_slope)
    )
    mixer_slope = lax.psum_scatter(mixer_slope, "fsdp", scatter_dimension=1, tiled=True)
    grad, low, mixer_sums = boundary(
        functools.partial(step_backward, 0.5), part, [grad, first_rows], vectors, (3,), 1, 3, 10
    )
    part, early_slope, early_lift_slope = feed_back(
        low, early_hidden, early_wide, early_active, w_early_up, w_early_down
    )
    early_slope, filter_slope = lax.optimization_barrier((early_slope, filter_slope))
    early_slope = lax.psum_scatter(early_slope, "fsdp", scatter_dimension=1, tiled=True)
    slope_frames, early_sums = boundary(
        step_last, part, [grad, frames], vectors, (0,), 1, 2, 11, gathered=False
    )

    table_slope = jnp.roll(table_slope[:, ::-1], 1 - NREL // 2, axis=1)
    table_rows = NREL // (n * m)
    wide = jnp.concatenate([turn_sums, late_sums, filter_sums, mixer_sums, early_sums])
    wide_count = wide.shape[0]
    wide = jnp.transpose(wide.reshape(wide_count, n * m, rows), (1, 0, 2)).reshape(n * m, wide_count * rows)
    wide = jnp.concatenate(
        [wide, jnp.transpose(table_slope.reshape(heads, n * m, table_rows), (1, 0, 2)).reshape(n * m, -1)], axis=1
    )
    lift_full = lax.dynamic_update_slice(
        jnp.zeros((2, D), jnp.float32), filter_lift_slope.reshape(2, inner), (0, me * inner)
    ).reshape(n * m, -1)
    table_used = wide.shape[1]
    wide = jnp.concatenate([wide, lift_full], axis=1)
    wide_used = wide.shape[1]
    wide = jnp.pad(wide, ((0, 0), (0, -wide_used % LANES))).reshape(n * m, -1, LANES)
    group = jnp.concatenate(
        [
            shift_sums,
            middle_gain_slope[None],
            middle_shift_slope[None],
            depth_slope,
            jnp.transpose(early_lift_slope.reshape(inner, spans)),
            jnp.transpose(late_lift_slope.reshape(inner, spans)),
        ]
    )
    group_count = group.shape[0]
    group = jnp.transpose(group.reshape(group_count, m, rows), (1, 0, 2)).reshape(m, group_count * rows)
    group_used = group.shape[1]
    group = jnp.pad(group, ((0, 0), (0, -group_used % LANES))).reshape(m, -1, LANES)
    wide_all, group_all, late_up_wide, project_wide, filter_up_wide = collect(
        n, m, wide, group, [late_slope, mixer_slope, filter_slope], [(1, hidden), (3, inner), (2, inner)], 12
    )
    tables = wide_all.reshape(n, m, -1)[:, :, wide_count * rows : table_used]
    wide = jnp.sum(wide_all, axis=0).reshape(-1)
    lift_total = wide[table_used:wide_used]
    wide = wide[: wide_count * rows].reshape(wide_count, rows)
    tables = jnp.transpose(jnp.sum(tables, axis=1).reshape(HEADS, table_rows))
    group = jnp.sum(group_all, axis=0).reshape(-1)[:group_used].reshape(group_count, rows)
    def rejoin(value, low):
        return final(jnp.transpose(value[:, :, low:], (1, 0, 2)).reshape(rows, D))

    def final(value):
        return value.astype(jnp.float32)

    lift_slopes = KW + 5
    results = [
        layer_out,
        slope_frames,
        wide[12],
        wide[13],
        jnp.transpose(group[lift_slopes : lift_slopes + spans]).reshape(-1),
        wide[11],
        wide[9],
        wide[10],
        final(project_wide),
        group[0],
        group[1],
        rejoin(mixer_slope, 3 * inner),
        wide[8],
        tables,
        wide[6],
        wide[7],
        final(filter_up_wide),
        lift_total,
        jnp.transpose(group[4 : 4 + KW]),
        group[4 + KW],
        group[2],
        group[3],
        rejoin(filter_slope, 2 * inner),
        wide[5],
        wide[3],
        wide[4],
        final(late_up_wide),
        jnp.transpose(group[lift_slopes + spans : lift_slopes + 2 * spans]).reshape(-1),
        final(late_slope[n:]).reshape(spans * rows, D),
        wide[2],
        wide[0],
        wide[1],
    ]
    results[:2] = keep(layer_out, slope_frames)
    *results, early_slope = lax.optimization_barrier((*results, early_slope))
    (early_up_wide,) = giveback(n, [early_slope], [(1, hidden)], 14)
    results.insert(4, final(early_up_wide))
    results.insert(6, final(early_slope[n:]).reshape(spans * rows, D))
    return tuple(results)


def solution(mesh):
    in_specs = (
        P(("dp", "fsdp"), None),
        P(("dp", "fsdp")),
        P(("dp", "fsdp"), None),
        P(("dp", "fsdp")),
        P(("dp", "fsdp")),
        P(("dp", "fsdp"), None),
        P(("dp", "fsdp")),
        P(("dp", "fsdp"), None),
        P(("dp", "fsdp")),
        P(("dp", "fsdp")),
        P(("dp", "fsdp")),
        P(("dp", "fsdp"), None),
        P(("dp", "fsdp")),
        P(("dp", "fsdp")),
        P(("dp", "fsdp"), None),
        P(("dp", "fsdp")),
        P(("dp", "fsdp"), None),
        P(("dp", "fsdp")),
        P(("dp", "fsdp")),
        P(("dp", "fsdp"), None),
        P(("dp", "fsdp")),
        P(("dp", "fsdp"), None),
        P(("dp", "fsdp")),
        P(("dp", "fsdp")),
        P(("dp", "fsdp")),
        P(("dp", "fsdp"), None),
        P(("dp", "fsdp")),
        P(("dp", "fsdp")),
        P(("dp", "fsdp")),
        P(("dp", "fsdp"), None),
        P(("dp", "fsdp")),
        P(("dp", "fsdp"), None),
        P(("dp", "fsdp")),
        P(("dp", "fsdp")),
        P(("dp", "fsdp")),
    )
    out_specs = (
        P(("dp", "fsdp"), None),
        P(("dp", "fsdp"), None),
        P(("dp", "fsdp")),
        P(("dp", "fsdp")),
        P(("dp", "fsdp"), None),
        P(("dp", "fsdp")),
        P(("dp", "fsdp"), None),
        P(("dp", "fsdp")),
        P(("dp", "fsdp")),
        P(("dp", "fsdp")),
        P(("dp", "fsdp"), None),
        P(("dp", "fsdp")),
        P(("dp", "fsdp")),
        P(("dp", "fsdp"), None),
        P(("dp", "fsdp")),
        P(("dp", "fsdp"), None),
        P(("dp", "fsdp")),
        P(("dp", "fsdp")),
        P(("dp", "fsdp"), None),
        P(("dp", "fsdp")),
        P(("dp", "fsdp"), None),
        P(("dp", "fsdp")),
        P(("dp", "fsdp")),
        P(("dp", "fsdp")),
        P(("dp", "fsdp"), None),
        P(("dp", "fsdp")),
        P(("dp", "fsdp")),
        P(("dp", "fsdp")),
        P(("dp", "fsdp"), None),
        P(("dp", "fsdp")),
        P(("dp", "fsdp"), None),
        P(("dp", "fsdp")),
        P(("dp", "fsdp")),
        P(("dp", "fsdp")),
    )
    n, m = mesh.shape["dp"], mesh.shape["fsdp"]
    run = functools.partial(split_body, n, m) if n == 4 and D // (n * m) == 32 else body
    return jax.shard_map(run, mesh=mesh, in_specs=in_specs, out_specs=out_specs, check_vma=False)
```
